256 devices in a mesh: dp: 4 (over x), seq: 64 (over y, z, core).
Axes of the slice: x: 4, y: 4, z: 8, core: 2. Of those that a mesh axis runs over, the one named last changes fastest.
Arguments:
- tokens: bfloat16 [4, 8192, 2048], P('dp', 'seq'), may hold values from -6 to 6
- values: bfloat16 [4, 8192, 1024], P('dp', 'seq'), may hold values from -6 to 6
- cotangent: bfloat16 [4, 8192, 1024], P('dp', 'seq'), may hold values from -6 to 6
- sel_weight: bfloat16 [2048, 128], P(('dp', 'seq')), may hold values from -0.03125 to 0.03125
- step_weight: bfloat16 [2048, 32], P(('dp', 'seq')), may hold values from -0.125 to 0.125
- sel_dir: bfloat16 [2048, 128], P(('dp', 'seq')), may hold values from -0.03125 to 0.03125
- step_dir: bfloat16 [2048, 32], P(('dp', 'seq')), may hold values from -0.125 to 0.125
- conv_weight: float32 [4, 128], replicated, may hold values from -3 to 3
- step_bias: float32 [32], replicated, may hold values from -1 to 0.5
- decay_rate: float32 [32], replicated, may hold values from 0 to 1
Outputs:
- sel_grad: float32 [2048, 128], P(('dp', 'seq'))
- step_grad: float32 [2048, 32], P(('dp', 'seq'))
- sel_hvp: float32 [2048, 128], P(('dp', 'seq'))
- step_hvp: float32 [2048, 32], P(('dp', 'seq'))
The draws below stay inside these ranges and needn't reach their ends.
All inputs are finite; a program needn't handle non-finite values.
Results may differ from the reference program's by a relative error of at most 0.0003.
Values may be sent and summed in bfloat16 or wider, within the bound.
A program may use at most 192 MiB of HBM per device.

```python
import math
import jax
import jax.numpy as jnp
from jax import lax

D = 2048
N = 64
P_SIZE = 32
H = 32
KCONV = 4
TOK_DEV = 128
SEQLEN = 8192
SEQS = 4


def draw_decay_rate(key, part):
    first_key, second_key = jax.random.split(jax.random.fold_in(key, 11))
    ranking = jax.random.permutation(first_key, H)
    spread = jax.random.uniform(second_key, (H,), jnp.float32)
    slow_heads = ranking < H // 2
    slow_rate = (0.3 + 1.7 * spread) / SEQLEN
    fast_rate = jnp.exp(jnp.log(0.02) + spread * jnp.log(7.5))
    return jnp.where(slow_heads, slow_rate, fast_rate).astype(jnp.float32)


def shard_levels(key, extent, shards, low, high):
    def one(dim, parts):
        heights = jax.random.uniform(jax.random.fold_in(jax.random.fold_in(key, 6), dim), (parts,), jnp.float32, low / len(shards), high / len(shards))
        return jnp.repeat(jnp.exp(heights), extent[dim] // parts).reshape((-1,) + (1,) * (len(extent) - dim - 1))

    factor_of = one(*shards[0])
    for cut in shards[1:]:
        factor_of = factor_of * one(*cut)
    return factor_of


def normal_values(rng, extent, scale, limit, cuts=(), dtype=jnp.bfloat16):
    loudness = shard_levels(rng, extent, cuts, -0.22, 0.18) if cuts else 1.0
    result = jax.random.normal(rng, extent, jnp.float32) * scale * loudness
    return jnp.minimum(jnp.maximum(result, -limit), limit).astype(dtype)


def setup_inputs(seed: int = 0) -> dict:
    key_of = jax.random.split(jax.random.key(seed), 11)
    return {
        "tokens": normal_values(key_of[0], (SEQS, SEQLEN, D), 1.0, 6.0, ((0, 4), (1, 64))),
        "values": normal_values(key_of[1], (SEQS, SEQLEN, H * P_SIZE), 1.0, 6.0, ((0, 4), (1, 64))),
        "cotangent": normal_values(key_of[2], (SEQS, SEQLEN, H * P_SIZE), 1.0, 6.0, ((0, 4), (1, 64))),
        "sel_weight": normal_values(key_of[3], (D, 2 * N), (16 * D) ** -0.5, 0.03125, ((0, 256),)),
        "step_weight": normal_values(key_of[4], (D, H), D ** -0.5, 0.125, ((0, 256),)),
        "sel_dir": normal_values(key_of[5], (D, 2 * N), (16 * D) ** -0.5, 0.03125, ((0, 256),)),
        "step_dir": normal_values(key_of[6], (D, H), D ** -0.5, 0.125, ((0, 256),)),
        "conv_weight": normal_values(key_of[7], (KCONV, 2 * N), 0.5, 3.0, (), jnp.float32),
        "step_bias": jnp.clip(jax.random.uniform(key_of[8], (H,), jnp.float32, -1.0, 0.5), -1.0, 0.5),
        "decay_rate": draw_decay_rate(jax.random.fold_in(key_of[10], 71), 0),
    }


HIGHEST = lax.Precision.HIGHEST

def state_space(in_map, out_map, step_size, head_values, decay_rate, state_in):
    cumulated = jnp.cumsum(-step_size * decay_rate[None, :], axis=0)
    cumulated_heads = cumulated.T
    spans = cumulated_heads[:, :, None] - cumulated_heads[:, None, :]
    length = in_map.shape[0]
    causal = jnp.arange(length)[:, None] >= jnp.arange(length)[None, :]
    decays = jnp.exp(jnp.where(causal[None], spans, -1e+30))
    intersection = jnp.dot(out_map, in_map.T, precision=HIGHEST)
    mixing = decays * intersection[None] * step_size.T[:, None, :]
    within = jnp.einsum('hts,shp->thp', mixing, head_values, precision=HIGHEST)
    carried = jnp.exp(cumulated)[:, :, None] * jnp.einsum('tn,hpn->thp', out_map, state_in, precision=HIGHEST)
    whole_decay = cumulated[-1]
    tail_weight = jnp.exp(whole_decay[None, :] - cumulated) * step_size
    local_state = jnp.einsum('thp,tn->hpn', head_values * tail_weight[:, :, None], in_map, precision=HIGHEST)
    state_out = jnp.exp(whole_decay)[:, None, None] * state_in + local_state
    return (within + carried, state_out)

def features(sel_float, step_float, extended, conv_weight, step_bias, length):
    projected = jnp.dot(extended, sel_float, precision=HIGHEST)
    convolved = conv_weight[0][None, :] * projected[0:length]
    for offset in range(1, KCONV):
        convolved = convolved + conv_weight[offset][None, :] * projected[offset:offset + length]
    activated = jax.nn.silu(convolved)
    step_size = jax.nn.softplus(jnp.dot(extended[KCONV - 1:], step_float, precision=HIGHEST) + step_bias[None, :])
    return (activated[:, :N], activated[:, N:], step_size)

def reference(tokens, values, cotangent, sel_weight, step_weight, sel_dir, step_dir, conv_weight, step_bias, decay_rate):
    scale_factor = 1.0 / math.sqrt(tokens.shape[0] * tokens.shape[1])
    blocks = SEQLEN // TOK_DEV

    def objective(parameters):
        total_loss = jnp.zeros((), jnp.float32)
        for sequence in range(tokens.shape[0]):
            extended = jnp.concatenate([jnp.zeros((KCONV - 1, D), jnp.float32), tokens[sequence].astype(jnp.float32)], axis=0)
            in_map, out_map, step_size = features(parameters[0], parameters[1], extended, conv_weight, step_bias, SEQLEN)
            head_values = values[sequence].reshape(blocks, TOK_DEV, H, P_SIZE).astype(jnp.float32)
            head_cotangent = cotangent[sequence].reshape(blocks, TOK_DEV, H, P_SIZE).astype(jnp.float32)

            def block_loss(state, inputs):
                outputs, state_next = state_space(inputs[0], inputs[1], inputs[2], inputs[3], decay_rate, state)
                return (state_next, jnp.sum(inputs[4] * outputs))
            _, pieces = lax.scan(jax.checkpoint(block_loss), jnp.zeros((H, P_SIZE, N), jnp.float32), (in_map.reshape(blocks, TOK_DEV, N), out_map.reshape(blocks, TOK_DEV, N), step_size.reshape(blocks, TOK_DEV, H), head_values, head_cotangent))
            total_loss = total_loss + jnp.sum(pieces)
        return total_loss * scale_factor
    parameters = (sel_weight.astype(jnp.float32), step_weight.astype(jnp.float32))
    directions = (sel_dir.astype(jnp.float32), step_dir.astype(jnp.float32))
    gradients, curvature = jax.jvp(jax.grad(objective), (parameters,), (directions,))
    return (gradients[0], gradients[1], curvature[0], curvature[1])
```

```python
import functools
import math

import jax
import jax.numpy as jnp
from jax import lax
from jax.experimental import pallas as pl
from jax.experimental.pallas import tpu as pltpu
from jax.sharding import PartitionSpec as P

N = 64
P_SIZE = 32
H = 32
KCONV = 4
L = 128
HALO = 16
HP = H * P_SIZE
HALF = HP // 2
WIDE = 384
NX, NY, NZ = 4, 4, 8
CHIPS = NY * NZ
MESH = pl.DeviceIdType.MESH
F32 = jnp.float32
BF16 = jnp.bfloat16
VMEM_LIMIT = 56 * 1024 * 1024


def roll64(x):
    return pltpu.roll(x, 64, 1)


def split(x):
    high = x.astype(BF16)
    low = (x - high.astype(F32)).astype(BF16)
    return high, low


def split3(x):
    high = x.astype(BF16)
    rest = x - high.astype(F32)
    mid = rest.astype(BF16)
    low = (rest - mid.astype(F32)).astype(BF16)
    return high, mid, low


def dg(a, b, ca, cb):
    return lax.dot_general(a, b, (((ca,), (cb,)), ((), ())), preferred_element_type=F32)


def dot_split(a, b, ca, cb):
    ah, al = split(a)
    bh, bl = split(b)
    return dg(ah, bh, ca, cb) + (dg(ah, bl, ca, cb) + dg(al, bh, ca, cb))


def dot_left(a, b, ca, cb):
    ah, al = split(a)
    return dg(ah, b, ca, cb) + dg(al, b, ca, cb)


def iota(shape, dim):
    return lax.broadcasted_iota(jnp.int32, shape, dim)


def low_lanes():
    return iota((L, 128), 1) < 64


def head_spread():
    return (iota((H, HP), 0) == iota((H, HP), 1) // P_SIZE).astype(F32).astype(BF16)


def triangle(reverse):
    row, column = iota((L, L), 0), iota((L, L), 1)
    keep = (column >= row) if reverse else (row >= column)
    return keep.astype(F32).astype(BF16)


def cumulate(x, reverse):
    tri = triangle(reverse)
    a, b, c = split3(x)
    return dg(tri, a, 1, 0) + (dg(tri, b, 1, 0) + dg(tri, c, 1, 0))


def features(proj, conv2, bias, rate):
    z = jnp.zeros((L, 128), F32)
    zd = jnp.zeros((L, 128), F32)
    for k in range(KCONV):
        rows = HALO - (KCONV - 1) + k
        z = z + conv2[k : k + 1, :128] * proj(rows, 0, 128)
        zd = zd + conv2[k : k + 1, :128] * proj(rows, 128, 128)
    sg = jax.nn.sigmoid(z)
    act = z * sg
    first = sg * (1.0 + z * (1.0 - sg))
    second = sg * (1.0 - sg) * (2.0 + z * (1.0 - 2.0 * sg))
    actd = first * zd
    steps = proj(HALO, 256, 128)
    q = steps[:, :H] + bias
    qd = steps[:, H : 2 * H]
    delta = jnp.maximum(q, 0.0) + jnp.log1p(jnp.exp(-jnp.abs(q)))
    sq = jax.nn.sigmoid(q)
    deltad = sq * qd
    cum = cumulate(-(delta * rate), False)
    cumd = cumulate(-(deltad * rate), False)
    return dict(
        zd=zd, act=act, actd=actd, first=first, second=second,
        qd=qd, sq=sq, delta=delta, deltad=deltad, cum=cum, cumd=cumd,
    )


def weights_of(ft):
    cum, cumd = ft["cum"], ft["cumd"]
    last, lastd = cum[L - 1 :, :], cumd[L - 1 :, :]
    e = jnp.exp(cum)
    ed = e * cumd
    f = jnp.exp(last - cum)
    fd = f * (lastd - cumd)
    w = f * ft["delta"]
    wd = fd * ft["delta"] + f * ft["deltad"]
    return e, ed, f, fd, w, wd


def pair_parts(ft):
    act, actd = ft["act"], ft["actd"]
    actr, actdr = roll64(act), roll64(actd)
    m = low_lanes()
    return dict(
        b_bd=jnp.where(m, act, actdr),
        o_b=jnp.where(m, 0.0, actr),
        c_cd=jnp.where(m, actr, actd),
        o_c=jnp.where(m, 0.0, act),
        b_o=jnp.where(m, act, 0.0),
        bd_b=jnp.where(m, actd, actr),
        c_o=jnp.where(m, actr, 0.0),
        cd_c=jnp.where(m, actdr, act),
        b_c=act,
        c_b=actr,
    )


def spread_rows(rows):
    return dot_left(rows, head_spread(), 1, 0)


def streams(wts, values, cotangent):
    e, ed, _, _, w, wd = wts
    v = values.astype(F32)
    u = cotangent.astype(F32)
    we = spread_rows(w) * v
    wde = spread_rows(wd) * v
    es = spread_rows(e)
    eds = spread_rows(ed)
    return we, wde, es, eds, es * u, eds * u


def local_states(pp, we, wde, eu, edu):
    left = jnp.concatenate([pp["b_bd"], pp["o_b"]], 0)
    right = jnp.concatenate([we, wde], 0)
    forward = dot_split(left, right, 0, 0)
    left = jnp.concatenate([pp["c_cd"], pp["o_c"]], 0)
    right = jnp.concatenate([eu, edu], 0)
    backward = dot_split(left, right, 0, 0)
    return forward, backward


def intra(ft, pp, v_of, u_of, cols_ref, rows_ref, row1_ref, row2_ref, colq_ref, colqd_ref):
    g = dot_split(pp["c_o"], pp["b_c"], 1, 1)
    gd = dot_split(pp["cd_c"], pp["b_bd"], 1, 1)
    eta = ft["deltad"] - ft["delta"] * ft["cumd"]
    rows_ref[0:H, :] = ft["cum"].T
    rows_ref[H : 2 * H, :] = ft["delta"].T
    rows_ref[2 * H : 3 * H, :] = eta.T
    parts = split3(ft["cum"])
    partsd = split(ft["cumd"])
    row, lane = iota((L, L), 0), iota((L, L), 1)
    causal = row >= lane
    row1_ref[...] = jnp.zeros((L, L), F32)
    row2_ref[...] = jnp.zeros((L, L), F32)

    def one(i, carry):
        dgm, dgd = carry
        pick = (iota((H, 512), 0) == (4 * i + iota((H, 512), 1) // 128)).astype(F32).astype(BF16)
        ct4 = dg(parts[0], pick, 1, 0) + (dg(parts[1], pick, 1, 0) + dg(parts[2], pick, 1, 0))
        cd4 = dg(partsd[0], pick, 1, 0) + dg(partsd[1], pick, 1, 0)
        v_tile, u_tile = v_of(i), u_of(i)
        row1, row2 = row1_ref[...], row2_ref[...]
        for j in range(4):
            h = 4 * i + j
            mask = (iota((L, 128), 1) // P_SIZE == j).astype(F32)
            w = dg((u_tile.astype(F32) * mask).astype(BF16), v_tile, 1, 1)
            ct = ct4[:, 128 * j : 128 * j + 128]
            cd = cd4[:, 128 * j : 128 * j + 128]
            cs = rows_ref[pl.ds(h, 1), :]
            ds = rows_ref[pl.ds(H + h, 1), :]
            et = rows_ref[pl.ds(2 * H + h, 1), :]
            x = jnp.exp(jnp.where(causal, ct - cs, -1e30)) * w
            xd = x * ds
            dgm = dgm + xd
            dgd = dgd + (x * et + cd * xd)
            q = x * g
            xgd = x * gd
            colq_ref[pl.ds(h, 1), :] = jnp.sum(q, axis=0, keepdims=True)
            colqd_ref[pl.ds(h, 1), :] = jnp.sum(xgd + q * cd, axis=0, keepdims=True)
            r1 = jnp.sum(q * ds, axis=1, keepdims=True)
            r2 = jnp.sum(xgd * ds + q * et, axis=1, keepdims=True)
            here = lane == h
            row1 = jnp.where(here, r1, row1)
            row2 = jnp.where(here, r2, row2)
        row1_ref[...] = row1
        row2_ref[...] = row2
        return dgm, dgd

    zero = jnp.zeros((L, L), F32)
    return lax.fori_loop(0, H // 4, one, (zero, zero))


def head_sums(x):
    return dot_left(x, head_spread(), 1, 1)


def finish(ft, wts, pp, dgm, dgd, row1, row2, colq, colqd, we, wde, eu, edu, values, cotangent, xf, xb, rate, scale):
    e, ed, f, fd, w, wd = wts
    v = values.astype(F32)
    u = cotangent.astype(F32)
    zz = dot_split(jnp.concatenate([pp["c_o"], pp["cd_c"]], 0), xf, 1, 0)
    yy = dot_split(jnp.concatenate([pp["b_o"], pp["bd_b"]], 0), xb, 1, 0)
    g = head_sums(zz[:L] * u)
    gdot = head_sums(zz[L:] * u)
    kk = head_sums(yy[:L] * v)
    kdot = head_sums(yy[L:] * v)
    kap = jnp.sum(xb[:64] * xf[:64], axis=0, keepdims=True)
    kapd = jnp.sum(xb[64:] * xf[:64] + xb[:64] * xf[64:], axis=0, keepdims=True)
    both = head_sums(jnp.concatenate([jnp.broadcast_to(kap, (8, HP)), jnp.broadcast_to(kapd, (8, HP))], 0))
    kap, kapd = both[0:1], both[8:9]

    pc = dot_split(jnp.concatenate([eu, edu], 0), xf, 1, 1)
    pb = dot_split(jnp.concatenate([we, wde], 0), xb, 1, 1)
    m = low_lanes()
    t1 = dot_split(dgm, pp["b_bd"], 1, 0)
    t2 = dot_split(dgd, pp["b_c"], 1, 0)
    t3 = dot_split(dgm, pp["c_cd"], 0, 0)
    t4 = dot_split(dgd, pp["c_b"], 0, 0)
    pair_c = t1 + pc[:L] + jnp.where(m, 0.0, roll64(t2 + pc[L:]))
    pair_b = t3 + pb[:L] + jnp.where(m, 0.0, roll64(t4 + pb[L:]))
    dact = jnp.where(m, pair_b, roll64(pair_c))
    dactd = jnp.where(m, roll64(pair_b), pair_c)
    dz = scale * (ft["first"] * dact)
    dzd = scale * (ft["second"] * ft["zd"] * dact + ft["first"] * dactd)

    delta, deltad, cum, cumd = ft["delta"], ft["deltad"], ft["cum"], ft["cumd"]
    colq, colqd = colq.T, colqd.T
    colqd = colqd - cumd * colq
    row1, row2 = row1[:, :H], row2[:, :H]
    row2 = row2 + cumd * row1
    wk = w * kk
    wkd = wd * kk + w * kdot
    dc = row1 - delta * colq + e * g - wk
    dcd = row2 - (deltad * colq + delta * colqd) + ed * g + e * gdot - wkd
    el, edl = e[L - 1 :, :], ed[L - 1 :, :]
    extra = el * kap + jnp.sum(wk, axis=0, keepdims=True)
    extrad = edl * kap + el * kapd + jnp.sum(wkd, axis=0, keepdims=True)
    ddelta = colq + f * kk - rate * (cumulate(dc, True) + extra)
    ddeltad = colqd + fd * kk + f * kdot - rate * (cumulate(dcd, True) + extrad)
    sq = ft["sq"]
    dq = scale * (sq * ddelta)
    dqd = scale * (sq * (1.0 - sq) * ft["qd"] * ddelta + sq * ddeltad)
    return dz, dzd, dq, dqd


def place():
    x = lax.axis_index("dp")
    s = lax.axis_index("seq")
    chip = s // 2
    return x, chip // NZ, lax.rem(chip, NZ), lax.rem(s, 2), chip


def device(x, y, z, k):
    return (x, (y * NZ + z) * 2 + k)


def remote(src, dst, send_sem, recv_sem, dev):
    return pltpu.make_async_remote_copy(
        src_ref=src, dst_ref=dst, send_sem=send_sem, recv_sem=recv_sem,
        device_id=dev, device_id_type=MESH,
    )


def hello(partners):
    barrier = pltpu.get_barrier_semaphore()
    for dev in partners:
        pl.semaphore_signal(barrier, inc=1, device_id=dev, device_id_type=MESH)
    pl.semaphore_wait(barrier, len(partners))


def line_partners():
    x, y, z, k, _ = place()
    out = [device(x, y, z, 1 - k)]
    out += [device(lax.rem(x + d, NX), y, z, k) for d in range(1, NX)]
    out += [device(x, lax.rem(y + d, NY), z, k) for d in range(1, NY)]
    out += [device(x, y, lax.rem(z + d, NZ), k) for d in range(1, NZ)]
    return out


def gather_kernel(shard_ref, tok_ref, proj_ref, ext, pair, wbuf, s_send, s_pair, s_halo, s_tok, s_z, s_slab, s_swap):
    x, y, z, k, chip = place()
    s = 2 * chip + k
    seq = CHIPS * 2
    own = pltpu.make_async_copy(tok_ref, ext.at[pl.ds(HALO, L)], s_tok)
    own.start()
    partners = line_partners()
    barrier = pltpu.get_barrier_semaphore()
    for dev in partners + [(x, lax.rem(s + 1, seq)), (x, lax.rem(s + seq - 1, seq))]:
        pl.semaphore_signal(barrier, inc=1, device_id=dev, device_id_type=MESH)
    pl.semaphore_wait(barrier, len(partners) + 2)

    mate = device(x, y, z, 1 - k)
    to_mate = remote(shard_ref, pair, s_send.at[0], s_pair, mate)
    to_mate.start()
    halo = remote(
        tok_ref.at[pl.ds(L - HALO, HALO)], ext.at[pl.ds(0, HALO)], s_send.at[1], s_halo,
        (x, lax.rem(s + 1, seq)),
    )
    halo.start()
    to_mate.wait()
    first = k == 0
    mine, other = shard_ref[...], pair[...]
    block = jnp.concatenate([jnp.where(first, mine, other), jnp.where(first, other, mine)], 0)
    half = z // 2
    source = lax.rem(z, 2) == k

    @pl.when(source)
    def _():
        wbuf[x, y, half, k] = block.astype(BF16)

    def z_copy(d):
        return remote(
            wbuf.at[x, y, half, k], wbuf.at[x, y, half, k], s_send.at[1 + d], s_z.at[half],
            device(x, y, lax.rem(z + d, NZ), k),
        )

    @pl.when(source)
    def _():
        for d in range(1, NZ):
            z_copy(d).start()

    for i in range(NZ // 2):

        @pl.when(2 * i + k != z)
        def _(i=i):
            remote(
                wbuf.at[x, y, i, k], wbuf.at[x, y, i, k], s_send.at[0], s_z.at[i], mate
            ).wait_recv()

    def slab(sx, sy):
        return wbuf.at[sx, sy, :, k]

    def slab_copy(sx, sy, tx, ty, sem):
        return remote(slab(sx, sy), slab(sx, sy), s_send.at[sem], s_slab.at[sx * NY + sy], device(tx, ty, z, k))

    def swap(sx, sy, kk):
        return remote(
            wbuf.at[sx, sy, :, kk], wbuf.at[sx, sy, :, kk], s_send.at[24 + 0], s_swap.at[sx * NY + sy], mate
        )

    def swap_out(sx, sy, n):
        return remote(
            wbuf.at[sx, sy, :, k], wbuf.at[sx, sy, :, k], s_send.at[24 + n], s_swap.at[sx * NY + sy], mate
        )

    sent = []

    def start(copy):
        copy.start()
        sent.append(copy)

    def near(d):
        return lax.rem(x + d * k, NX), lax.rem(y + d * (1 - k), NY)

    def far(d):
        return lax.rem(x + d * (1 - k), NX), lax.rem(y + d * k, NY)

    for d in range(1, 4):
        tx, ty = near(d)
        start(slab_copy(x, y, tx, ty, 8 + d))
    for d in range(1, 4):
        tx, ty = far(d)
        start(slab_copy(x, y, tx, ty, 11 + d))
    start(swap_out(x, y, 0))
    n = 0
    for d in range(1, 4):
        sx, sy = near(4 - d)
        slab_copy(sx, sy, x, y, 0).wait_recv()
        for t in range(1, 4):
            tx = lax.rem(x + t * (1 - k), NX)
            ty = lax.rem(y + t * k, NY)
            start(slab_copy(sx, sy, tx, ty, 15 + n))
            n += 1
        start(swap_out(sx, sy, d))
    n = 4
    for e in range(4):
        for d in range(1, 4):
            dx, dy = far(4 - d)
            sx = lax.rem(dx + e * k, NX)
            sy = lax.rem(dy + e * (1 - k), NY)
            slab_copy(sx, sy, x, y, 0).wait_recv()
            start(swap_out(sx, sy, n))
            n += 1
    halo.wait()
    own.wait()

    @pl.when(s == 0)
    def _():
        ext[0:HALO, :] = jnp.zeros((HALO, ext.shape[1]), BF16)

    for sx in range(NX):
        for sy in range(NY):
            swap(sx, sy, 1 - k).wait_recv()
    depth = ext.shape[1]
    proj_ref[...] = dg(ext[...], wbuf[...].reshape(depth, WIDE), 1, 0)
    for copy in sent:
        copy.wait_send()

    @pl.when(source)
    def _():
        for d in range(1, NZ):
            z_copy(d).wait_send()


def proj_reader(ref):
    def read(row, lane, lanes):
        return ref[row : row + L, lane : lane + lanes]

    return read


def states_kernel(proj_ref, v_ref, u_ref, conv_ref, bias_ref, rate_ref, out_ref):
    ft = features(proj_reader(proj_ref), conv_ref[...], bias_ref[...], rate_ref[...])
    wts = weights_of(ft)
    pp = pair_parts(ft)
    we, wde, es, eds, eu, edu = streams(wts, v_ref[...], u_ref[...])
    forward, backward = local_states(pp, we, wde, eu, edu)
    row = iota((8, HP), 0)
    dec = jnp.where(row == 0, es[L - 1 :, :], jnp.where(row == 1, eds[L - 1 :, :], 0.0))
    for half in range(2):
        lanes = slice(HALF * half, HALF * half + HALF)
        out_ref[half, 0:128, :] = forward[:, lanes]
        out_ref[half, 128:256, :] = backward[:, lanes]
        out_ref[half, 256:264, :] = dec[:, lanes]


def scan_kernel(loc_ref, out_ref, part, snd, rcv, snd2, rcv2, mine_in, other_in, s_send, s_part, s_one, s_two, s_fin):
    x, y, z, k, chip = place()
    mate = device(x, y, z, 1 - k)

    def peer(d):
        c = lax.rem(chip + d, CHIPS)
        return c, (x, 2 * c + k)

    barrier = pltpu.get_barrier_semaphore()
    pl.semaphore_signal(barrier, inc=1, device_id=mate, device_id_type=MESH)

    def greet(d, carry):
        pl.semaphore_signal(barrier, inc=1, device_id=peer(d)[1], device_id_type=MESH)
        return carry

    lax.fori_loop(1, CHIPS, greet, 0)
    pl.semaphore_wait(barrier, CHIPS)

    to_mate = remote(loc_ref.at[1 - k], part, s_send.at[0], s_part, mate)
    to_mate.start()
    to_mate.wait()
    first = k == 0
    own, other = loc_ref[k], part[...]
    one0 = jnp.where(first, own, other)
    one1 = jnp.where(first, other, own)
    a0, ad0 = one0[256:257], one0[257:258]
    a1, ad1 = one1[256:257], one1[257:258]
    fs = a1 * one0[0:64] + one1[0:64]
    ft = a1 * one0[64:128] + ad1 * one0[0:64] + one1[64:128]
    bs = a0 * one1[128:192] + one0[128:192]
    bt = a0 * one1[192:256] + ad0 * one1[128:192] + one0[192:256]
    a, ad = a0 * a1, ad0 * a1 + a0 * ad1
    row = iota((8, HALF), 0)
    dec = jnp.where(row == 0, a, jnp.where(row == 1, ad, 0.0))
    for g in range(8):
        for i in range(4):
            j = 4 * g + i
            lanes = slice(128 * i, 128 * i + 128)
            rows = slice(8 * g, 8 * g + 8)
            snd[j, 0] = fs[rows, lanes]
            snd[j, 1] = ft[rows, lanes]
            snd[j, 2] = bs[rows, lanes]
            snd[j, 3] = bt[rows, lanes]
            snd[j, 4] = dec[:, lanes]

    def first_copy(d):
        c, dev = peer(d)
        return remote(snd.at[c], rcv.at[chip], s_send.at[d], s_one.at[chip], dev)

    def second_copy(d):
        c, dev = peer(d)
        return remote(snd2.at[c], rcv2.at[chip], s_send.at[CHIPS + d], s_two.at[chip], dev)

    def loop(fn):
        def body(d, carry):
            fn(d)
            return carry

        lax.fori_loop(1, CHIPS, body, 0)

    loop(lambda d: first_copy(d).start())
    rcv[chip] = snd[chip]

    def first_arrived(d):
        c, dev = peer(d)
        remote(snd.at[c], rcv.at[c], s_send.at[d], s_one.at[c], dev).wait_recv()

    loop(first_arrived)
    zero = jnp.zeros((8, 128), F32)

    s, t = zero, zero
    for c in range(CHIPS):
        snd2[c, 0] = s
        snd2[c, 1] = t
        ca, cad = rcv[c, 4, 0:1, :], rcv[c, 4, 1:2, :]
        s, t = ca * s + rcv[c, 0], ca * t + (cad * s + rcv[c, 1])
    s, t = zero, zero
    for c in range(CHIPS - 1, -1, -1):
        snd2[c, 2] = s
        snd2[c, 3] = t
        ca, cad = rcv[c, 4, 0:1, :], rcv[c, 4, 1:2, :]
        s, t = ca * s + rcv[c, 2], ca * t + (cad * s + rcv[c, 3])

    loop(lambda d: second_copy(d).start())
    rcv2[chip] = snd2[chip]

    def second_arrived(d):
        c, dev = peer(d)
        remote(snd2.at[c], rcv2.at[c], s_send.at[CHIPS + d], s_two.at[c], dev).wait_recv()

    loop(second_arrived)
    for g in range(8):
        for i in range(4):
            j = 4 * g + i
            lanes = slice(128 * i, 128 * i + 128)
            for part_index in range(4):
                base = 64 * part_index + 8 * g
                mine_in[base : base + 8, lanes] = rcv2[j, part_index]
    fs, ft, bs, bt = (mine_in[64 * i : 64 * i + 64, :] for i in range(4))
    later_s = a0 * fs + one0[0:64]
    later_t = a0 * ft + ad0 * fs + one0[64:128]
    early_s = a1 * bs + one1[128:192]
    early_t = a1 * bt + ad1 * bs + one1[192:256]
    out_ref[k, 0:64, :] = jnp.where(first, fs, later_s)
    out_ref[k, 64:128, :] = jnp.where(first, ft, later_t)
    out_ref[k, 128:192, :] = jnp.where(first, early_s, bs)
    out_ref[k, 192:256, :] = jnp.where(first, early_t, bt)
    other_in[0:64, :] = jnp.where(first, later_s, fs)
    other_in[64:128, :] = jnp.where(first, later_t, ft)
    other_in[128:192, :] = jnp.where(first, bs, early_s)
    other_in[192:256, :] = jnp.where(first, bt, early_t)
    back = remote(other_in, out_ref.at[k], s_send.at[2 * CHIPS], s_fin, mate)
    back.start()
    loop(lambda d: first_copy(d).wait_send())
    loop(lambda d: second_copy(d).wait_send())
    back.wait_send()
    remote(other_in, out_ref.at[1 - k], s_send.at[2 * CHIPS], s_fin, mate).wait_recv()


def grads_kernel(scale, proj_ref, v_ref, u_ref, st_ref, conv_ref, bias_ref, rate_ref, dp_ref,
                 rows_ref, row1_ref, row2_ref, colq_ref, colqd_ref, zp_ref):
    rate = rate_ref[...]
    ft = features(proj_reader(proj_ref), conv_ref[...], bias_ref[...], rate)
    wts = weights_of(ft)
    pp = pair_parts(ft)

    def tile(ref):
        return lambda i: ref[:, pl.ds(pl.multiple_of(i * 128, 128), 128)]

    dgm, dgd = intra(ft, pp, tile(v_ref), tile(u_ref), None, rows_ref, row1_ref, row2_ref, colq_ref, colqd_ref)
    we, wde, es, eds, eu, edu = streams(wts, v_ref[...], u_ref[...])
    xf = jnp.concatenate([st_ref[0, 0:128, :], st_ref[1, 0:128, :]], 1)
    xb = jnp.concatenate([st_ref[0, 128:256, :], st_ref[1, 128:256, :]], 1)
    dz, dzd, dq, dqd = finish(
        ft, wts, pp, dgm, dgd, row1_ref[...], row2_ref[...], colq_ref[...], colqd_ref[...],
        we, wde, eu, edu, v_ref[...], u_ref[...], xf, xb, rate, scale,
    )
    zp_ref[...] = jnp.zeros(zp_ref.shape, F32)
    zp_ref[HALO : HALO + L, 0:128] = dz
    zp_ref[HALO : HALO + L, 128:256] = dzd
    conv = conv_ref[...]
    for half in range(2):
        lanes = slice(128 * half, 128 * half + 128)
        total = conv[0:1, :128] * zp_ref[3 : 3 + HALO + L, lanes]
        for k in range(1, KCONV):
            total = total + conv[k : k + 1, :128] * zp_ref[3 - k : 3 - k + HALO + L, lanes]
        dp_ref[:, lanes] = total
    dp_ref[:, 256:384] = jnp.zeros((HALO + L, 128), F32)
    dp_ref[HALO:, 256 : 256 + H] = dq
    dp_ref[HALO:, 256 + H : 256 + 2 * H] = dqd


def reduce_kernel(ext_ref, dp_ref, out_ref, full, mate_in, a0, a1, a2, r0, r1, r2, b0, b1, b2,
                  q0, q1, q2, c0, c1, c2, p0, p1, p2, s_send, s_mate, s_a, s_b, s_c):
    x, y, z, k, chip = place()
    mate = device(x, y, z, 1 - k)
    hello(line_partners())

    def x_to(d):
        return device(lax.rem(x + d, NX), y, z, k)

    def y_to(d):
        return device(x, lax.rem(y + d, NY), z, k)

    def z_to(d):
        return device(x, y, lax.rem(z + d, NZ), k)

    high, low = split(dp_ref[...])
    ext = ext_ref[...]
    rows = NX * NY * NZ
    for tile in range(3):
        lanes = slice(128 * tile, 128 * tile + 128)
        part = dg(ext, high[:, lanes], 0, 0) + dg(ext, low[:, lanes], 0, 0)
        full[tile] = part.reshape(NX, NY, NZ, 2, 8, 128)
    to_mate = remote(full.at[:, :, :, :, 1 - k], mate_in, s_send.at[0], s_mate, mate)
    to_mate.start()
    to_mate.wait()
    for tile, acc in enumerate((a0, a1, a2)):
        acc[...] = full[tile, :, :, :, k] + mate_in[tile]

    first = []
    for d in range(1, NX):
        first.append(remote(a0.at[lax.rem(x + d, NX)], r0.at[d - 1], s_send.at[d], s_a.at[d], x_to(d)))
    for d in range(1, NY):
        first.append(remote(a1.at[:, lax.rem(y + d, NY)], r1.at[d - 1], s_send.at[3 + d], s_a.at[3 + d], y_to(d)))
    for d in range(1, NZ):
        first.append(remote(a2.at[:, :, lax.rem(z + d, NZ)], r2.at[d - 1], s_send.at[6 + d], s_a.at[6 + d], z_to(d)))
    for copy in first:
        copy.start()

    second = []
    for copy in first[0:3]:
        copy.wait_recv()
    b0[...] = (a0[x] + r0[0]) + (r0[1] + r0[2])
    for d in range(1, NY):
        second.append(remote(b0.at[lax.rem(y + d, NY)], q0.at[d - 1], s_send.at[13 + d], s_b.at[d], y_to(d)))
        second[-1].start()
    for copy in first[3:6]:
        copy.wait_recv()
    b1[...] = (a1[:, y] + r1[0]) + (r1[1] + r1[2])
    for d in range(1, NZ):
        second.append(remote(b1.at[:, lax.rem(z + d, NZ)], q1.at[d - 1], s_send.at[16 + d], s_b.at[3 + d], z_to(d)))
        second[-1].start()
    for copy in first[6:13]:
        copy.wait_recv()
    b2[...] = a2[:, :, z] + ((r2[0] + r2[1]) + (r2[2] + r2[3])) + ((r2[4] + r2[5]) + r2[6])
    for d in range(1, NX):
        second.append(remote(b2.at[lax.rem(x + d, NX)], q2.at[d - 1], s_send.at[23 + d], s_b.at[10 + d], x_to(d)))
        second[-1].start()

    third = []
    for copy in second[0:3]:
        copy.wait_recv()
    c0[...] = (b0[y] + q0[0]) + (q0[1] + q0[2])
    for d in range(1, NZ):
        third.append(remote(c0.at[lax.rem(z + d, NZ)], p0.at[d - 1], s_send.at[26 + d], s_c.at[d], z_to(d)))
        third[-1].start()
    for copy in second[3:10]:
        copy.wait_recv()
    c1[...] = b1[:, z] + ((q1[0] + q1[1]) + (q1[2] + q1[3])) + ((q1[4] + q1[5]) + q1[6])
    for d in range(1, NX):
        third.append(remote(c1.at[lax.rem(x + d, NX)], p1.at[d - 1], s_send.at[33 + d], s_c.at[7 + d], x_to(d)))
        third[-1].start()
    for copy in second[10:13]:
        copy.wait_recv()
    c2[...] = (b2[x] + q2[0]) + (q2[1] + q2[2])
    for d in range(1, NY):
        third.append(remote(c2.at[lax.rem(y + d, NY)], p2.at[d - 1], s_send.at[36 + d], s_c.at[10 + d], y_to(d)))
        third[-1].start()
    for copy in third[0:7]:
        copy.wait_recv()
    out_ref[:, 0:128] = c0[z] + ((p0[0] + p0[1]) + (p0[2] + p0[3])) + ((p0[4] + p0[5]) + p0[6])
    for copy in third[7:10]:
        copy.wait_recv()
    out_ref[:, 128:256] = (c1[x] + p1[0]) + (p1[1] + p1[2])
    for copy in third[10:13]:
        copy.wait_recv()
    out_ref[:, 256:384] = (c2[y] + p2[0]) + (p2[1] + p2[2])
    for copy in first + second + third:
        copy.wait_send()


def vmem(shape, dtype=F32):
    return pltpu.VMEM(shape, dtype)


def dma(*shape):
    return pltpu.SemaphoreType.DMA(shape)


def call(kernel, out_shape, in_specs, scratch, out_specs=None, cid=None):
    spec = pl.BlockSpec(memory_space=pltpu.VMEM)
    n_out = len(out_shape) if isinstance(out_shape, (list, tuple)) else 1
    if out_specs is None:
        out_specs = [spec] * n_out if isinstance(out_shape, (list, tuple)) else spec
    params = dict(vmem_limit_bytes=VMEM_LIMIT)
    if cid is not None:
        params.update(collective_id=cid, has_side_effects=True)
    return pl.pallas_call(
        kernel, out_shape=out_shape, in_specs=in_specs, out_specs=out_specs,
        scratch_shapes=scratch, compiler_params=pltpu.CompilerParams(**params),
    )


def body(tokens, values, cotangent, sel_weight, step_weight, sel_dir, step_dir, conv_weight, step_bias, decay_rate):
    own_tokens, v, u = tokens[0], values[0], cotangent[0]
    depth = own_tokens.shape[1]
    scale = 1.0 / math.sqrt(NX * CHIPS * 2 * L)
    spec = pl.BlockSpec(memory_space=pltpu.VMEM)
    hbm = pl.BlockSpec(memory_space=pl.ANY)
    shard = jnp.concatenate(
        [sel_weight, sel_dir, step_weight, step_dir, jnp.zeros((sel_weight.shape[0], 64), BF16)], 1
    ).astype(F32)
    bias, rate = step_bias[None, :], decay_rate[None, :]
    rows = shard.shape[0]
    ext_shape = (HALO + L, depth)
    proj, ext = call(
        lambda sh, tok, pr, ex, *rest: gather_kernel(sh, tok, pr, ex, *rest),
        [jax.ShapeDtypeStruct((HALO + L, WIDE), F32), jax.ShapeDtypeStruct(ext_shape, BF16)],
        [spec, hbm],
        [vmem((rows, WIDE)), vmem((NX, NY, NZ // 2, 2, 2 * rows, WIDE), BF16),
         dma(40), dma(), dma(), dma(), dma(NZ // 2), dma(NX * NY), dma(NX * NY)],
        cid=0,
    )(shard, own_tokens)
    loc = call(
        states_kernel, jax.ShapeDtypeStruct((2, 264, HALF), F32), [spec] * 6, [],
    )(proj, v, u, conv_weight, bias, rate)
    st = call(
        scan_kernel, jax.ShapeDtypeStruct((2, 256, HALF), F32), [spec],
        [vmem((264, HALF)), vmem((CHIPS, 5, 8, 128)), vmem((CHIPS, 5, 8, 128)),
         vmem((CHIPS, 4, 8, 128)), vmem((CHIPS, 4, 8, 128)), vmem((256, HALF)), vmem((256, HALF)),
         dma(2 * CHIPS + 1), dma(), dma(CHIPS), dma(CHIPS), dma()],
        cid=1,
    )(loc)
    dp = call(
        functools.partial(grads_kernel, scale), jax.ShapeDtypeStruct((HALO + L, WIDE), F32), [spec] * 7,
        [vmem((3 * H, L)), vmem((L, L)), vmem((L, L)), vmem((H, L)), vmem((H, L)), vmem((HALO + L + 8, 256))],
    )(proj, v, u, st, conv_weight, bias, rate)
    out = call(
        reduce_kernel, jax.ShapeDtypeStruct((rows, WIDE), F32), [spec] * 2,
        [vmem((3, NX, NY, NZ, 2, 8, 128)), vmem((3, NX, NY, NZ, 8, 128))]
        + [vmem((NX, NY, NZ, 8, 128))] * 3
        + [vmem((3, NY, NZ, 8, 128)), vmem((3, NX, NZ, 8, 128)), vmem((7, NX, NY, 8, 128))]
        + [vmem((NY, NZ, 8, 128)), vmem((NX, NZ, 8, 128)), vmem((NX, NY, 8, 128))]
        + [vmem((3, NZ, 8, 128)), vmem((7, NX, 8, 128)), vmem((3, NY, 8, 128))]
        + [vmem((NZ, 8, 128)), vmem((NX, 8, 128)), vmem((NY, 8, 128))]
        + [vmem((7, 8, 128)), vmem((3, 8, 128)), vmem((3, 8, 128))]
        + [dma(40), dma(), dma(14), dma(14), dma(14)],
        cid=2,
    )(ext, dp)
    return (
        out[:, 0:128],
        out[:, 256 : 256 + H],
        out[:, 128:256],
        out[:, 256 + H : 256 + 2 * H],
    )


def solution(mesh):
    shards = P(("dp", "seq"), None)
    stream = P("dp", "seq", None)
    return jax.shard_map(
        body,
        mesh=mesh,
        in_specs=(stream, stream, stream, shards, shards, shards, shards, P(), P(), P()),
        out_specs=(shards, shards, shards, shards),
        check_vma=False,
    )
```

```python
import functools
import math

import jax
import jax.numpy as jnp
from jax import lax
from jax.experimental import pallas as pl
from jax.experimental.pallas import tpu as pltpu
from jax.sharding import PartitionSpec as P

N = 64
P_SIZE = 32
H = 32
KCONV = 4
L = 128
HALO = 16
HP = H * P_SIZE
HALF = HP // 2
WIDE = 384
NX, NY, NZ = 4, 4, 8
CHIPS = NY * NZ
MESH = pl.DeviceIdType.MESH
F32 = jnp.float32
BF16 = jnp.bfloat16
VMEM_LIMIT = 56 * 1024 * 1024


def roll64(x):
    return pltpu.roll(x, 64, 1)


def split(x):
    high = x.astype(BF16)
    low = (x - high.astype(F32)).astype(BF16)
    return high, low


def split3(x):
    high = x.astype(BF16)
    rest = x - high.astype(F32)
    mid = rest.astype(BF16)
    low = (rest - mid.astype(F32)).astype(BF16)
    return high, mid, low


def dg(a, b, ca, cb):
    return lax.dot_general(a, b, (((ca,), (cb,)), ((), ())), preferred_element_type=F32)


def dot_split(a, b, ca, cb):
    ah, al = split(a)
    bh, bl = split(b)
    return dg(ah, bh, ca, cb) + (dg(ah, bl, ca, cb) + dg(al, bh, ca, cb))


def dot_left(a, b, ca, cb):
    ah, al = split(a)
    return dg(ah, b, ca, cb) + dg(al, b, ca, cb)


def iota(shape, dim):
    return lax.broadcasted_iota(jnp.int32, shape, dim)


def low_lanes():
    return iota((L, 128), 1) < 64


def head_spread():
    return (iota((H, HP), 0) == iota((H, HP), 1) // P_SIZE).astype(F32).astype(BF16)


def triangle(reverse):
    row, column = iota((L, L), 0), iota((L, L), 1)
    keep = (column >= row) if reverse else (row >= column)
    return keep.astype(F32).astype(BF16)


def cumulate(x, reverse):
    tri = triangle(reverse)
    a, b, c = split3(x)
    return dg(tri, a, 1, 0) + (dg(tri, b, 1, 0) + dg(tri, c, 1, 0))


def features(proj, conv2, bias, rate):
    z = jnp.zeros((L, 128), F32)
    zd = jnp.zeros((L, 128), F32)
    for k in range(KCONV):
        rows = HALO - (KCONV - 1) + k
        z = z + conv2[k : k + 1, :128] * proj(rows, 0, 128)
        zd = zd + conv2[k : k + 1, :128] * proj(rows, 128, 128)
    sg = jax.nn.sigmoid(z)
    act = z * sg
    first = sg * (1.0 + z * (1.0 - sg))
    second = sg * (1.0 - sg) * (2.0 + z * (1.0 - 2.0 * sg))
    actd = first * zd
    steps = proj(HALO, 256, 128)
    q = steps[:, :H] + bias
    qd = steps[:, H : 2 * H]
    delta = jnp.maximum(q, 0.0) + jnp.log1p(jnp.exp(-jnp.abs(q)))
    sq = jax.nn.sigmoid(q)
    deltad = sq * qd
    cum = cumulate(-(delta * rate), False)
    cumd = cumulate(-(deltad * rate), False)
    return dict(
        zd=zd, act=act, actd=actd, first=first, second=second,
        qd=qd, sq=sq, delta=delta, deltad=deltad, cum=cum, cumd=cumd,
    )


def weights_of(ft):
    cum, cumd = ft["cum"], ft["cumd"]
    last, lastd = cum[L - 1 :, :], cumd[L - 1 :, :]
    e = jnp.exp(cum)
    ed = e * cumd
    f = jnp.exp(last - cum)
    fd = f * (lastd - cumd)
    w = f * ft["delta"]
    wd = fd * ft["delta"] + f * ft["deltad"]
    return e, ed, f, fd, w, wd


def pair_parts(ft):
    act, actd = ft["act"], ft["actd"]
    actr, actdr = roll64(act), roll64(actd)
    m = low_lanes()
    return dict(
        b_bd=jnp.where(m, act, actdr),
        o_b=jnp.where(m, 0.0, actr),
        c_cd=jnp.where(m, actr, actd),
        o_c=jnp.where(m, 0.0, act),
        b_o=jnp.where(m, act, 0.0),
        bd_b=jnp.where(m, actd, actr),
        c_o=jnp.where(m, actr, 0.0),
        cd_c=jnp.where(m, actdr, act),
        b_c=act,
        c_b=actr,
    )


def spread_rows(rows):
    return dot_left(rows, head_spread(), 1, 0)


def streams(wts, values, cotangent):
    e, ed, _, _, w, wd = wts
    v = values.astype(F32)
    u = cotangent.astype(F32)
    we = spread_rows(w) * v
    wde = spread_rows(wd) * v
    es = spread_rows(e)
    eds = spread_rows(ed)
    return we, wde, es, eds, es * u, eds * u


def local_states(pp, we, wde, eu, edu):
    left = jnp.concatenate([pp["b_bd"], pp["o_b"]], 0)
    right = jnp.concatenate([we, wde], 0)
    forward = dot_split(left, right, 0, 0)
    left = jnp.concatenate([pp["c_cd"], pp["o_c"]], 0)
    right = jnp.concatenate([eu, edu], 0)
    backward = dot_split(left, right, 0, 0)
    return forward, backward


def intra_setup(ft, pp, rows_ref, row1_ref, row2_ref):
    g = dot_split(pp["c_o"], pp["b_c"], 1, 1)
    gd = dot_split(pp["cd_c"], pp["b_bd"], 1, 1)
    eta = ft["deltad"] - ft["delta"] * ft["cumd"]
    rows_ref[0:H, :] = ft["cum"].T
    rows_ref[H : 2 * H, :] = ft["delta"].T
    rows_ref[2 * H : 3 * H, :] = eta.T
    row1_ref[...] = jnp.zeros((L, L), F32)
    row2_ref[...] = jnp.zeros((L, L), F32)
    return g, gd


def intra(ft, g, gd, v_of, u_of, rows_ref, row1_ref, row2_ref, colq_ref, colqd_ref):
    parts = split3(ft["cum"])
    partsd = split(ft["cumd"])
    row, lane = iota((L, L), 0), iota((L, L), 1)
    causal = row >= lane

    def one(i, carry):
        dgm, dgd = carry
        pick = (iota((H, 512), 0) == (4 * i + iota((H, 512), 1) // 128)).astype(F32).astype(BF16)
        ct4 = dg(parts[0], pick, 1, 0) + (dg(parts[1], pick, 1, 0) + dg(parts[2], pick, 1, 0))
        cd4 = dg(partsd[0], pick, 1, 0) + dg(partsd[1], pick, 1, 0)
        v_tile, u_tile = v_of(i), u_of(i)
        row1, row2 = row1_ref[...], row2_ref[...]
        for j in range(4):
            h = 4 * i + j
            mask = (iota((L, 128), 1) // P_SIZE == j).astype(F32)
            w = dg((u_tile.astype(F32) * mask).astype(BF16), v_tile, 1, 1)
            ct = ct4[:, 128 * j : 128 * j + 128]
            cd = cd4[:, 128 * j : 128 * j + 128]
            cs = rows_ref[pl.ds(h, 1), :]
            ds = rows_ref[pl.ds(H + h, 1), :]
            et = rows_ref[pl.ds(2 * H + h, 1), :]
            x = jnp.exp(jnp.where(causal, ct - cs, -1e30)) * w
            xd = x * ds
            dgm = dgm + xd
            dgd = dgd + (x * et + cd * xd)
            q = x * g
            xgd = x * gd
            colq_ref[pl.ds(h, 1), :] = jnp.sum(q, axis=0, keepdims=True)
            colqd_ref[pl.ds(h, 1), :] = jnp.sum(xgd + q * cd, axis=0, keepdims=True)
            r1 = jnp.sum(q * ds, axis=1, keepdims=True)
            r2 = jnp.sum(xgd * ds + q * et, axis=1, keepdims=True)
            here = lane == h
            row1 = jnp.where(here, r1, row1)
            row2 = jnp.where(here, r2, row2)
        row1_ref[...] = row1
        row2_ref[...] = row2
        return dgm, dgd

    zero = jnp.zeros((L, L), F32)
    return lax.fori_loop(0, H // 4, one, (zero, zero))


def intra_pairs(pp, dgm, dgd):
    return (
        dot_split(dgm, pp["b_bd"], 1, 0),
        dot_split(dgd, pp["b_c"], 1, 0),
        dot_split(dgm, pp["c_cd"], 0, 0),
        dot_split(dgd, pp["c_b"], 0, 0),
    )


def head_sums(x):
    return dot_left(x, head_spread(), 1, 1)


def finish(ft, wts, pp, pairs, row1, row2, colq, colqd, we, wde, eu, edu, values, cotangent, xf, xb, rate, scale):
    e, ed, f, fd, w, wd = wts
    v = values.astype(F32)
    u = cotangent.astype(F32)
    zz = dot_split(jnp.concatenate([pp["c_o"], pp["cd_c"]], 0), xf, 1, 0)
    yy = dot_split(jnp.concatenate([pp["b_o"], pp["bd_b"]], 0), xb, 1, 0)
    g = head_sums(zz[:L] * u)
    gdot = head_sums(zz[L:] * u)
    kk = head_sums(yy[:L] * v)
    kdot = head_sums(yy[L:] * v)
    kap = jnp.sum(xb[:64] * xf[:64], axis=0, keepdims=True)
    kapd = jnp.sum(xb[64:] * xf[:64] + xb[:64] * xf[64:], axis=0, keepdims=True)
    both = head_sums(jnp.concatenate([jnp.broadcast_to(kap, (8, HP)), jnp.broadcast_to(kapd, (8, HP))], 0))
    kap, kapd = both[0:1], both[8:9]

    pc = dot_split(jnp.concatenate([eu, edu], 0), xf, 1, 1)
    pb = dot_split(jnp.concatenate([we, wde], 0), xb, 1, 1)
    m = low_lanes()
    t1, t2, t3, t4 = pairs
    pair_c = t1 + pc[:L] + jnp.where(m, 0.0, roll64(t2 + pc[L:]))
    pair_b = t3 + pb[:L] + jnp.where(m, 0.0, roll64(t4 + pb[L:]))
    dact = jnp.where(m, pair_b, roll64(pair_c))
    dactd = jnp.where(m, roll64(pair_b), pair_c)
    dz = scale * (ft["first"] * dact)
    dzd = scale * (ft["second"] * ft["zd"] * dact + ft["first"] * dactd)

    delta, deltad, cum, cumd = ft["delta"], ft["deltad"], ft["cum"], ft["cumd"]
    colq, colqd = colq.T, colqd.T
    colqd = colqd - cumd * colq
    row1, row2 = row1[:, :H], row2[:, :H]
    row2 = row2 + cumd * row1
    wk = w * kk
    wkd = wd * kk + w * kdot
    dc = row1 - delta * colq + e * g - wk
    dcd = row2 - (deltad * colq + delta * colqd) + ed * g + e * gdot - wkd
    el, edl = e[L - 1 :, :], ed[L - 1 :, :]
    extra = el * kap + jnp.sum(wk, axis=0, keepdims=True)
    extrad = edl * kap + el * kapd + jnp.sum(wkd, axis=0, keepdims=True)
    ddelta = colq + f * kk - rate * (cumulate(dc, True) + extra)
    ddeltad = colqd + fd * kk + f * kdot - rate * (cumulate(dcd, True) + extrad)
    sq = ft["sq"]
    dq = scale * (sq * ddelta)
    dqd = scale * (sq * (1.0 - sq) * ft["qd"] * ddelta + sq * ddeltad)
    return dz, dzd, dq, dqd


def place():
    x = lax.axis_index("dp")
    s = lax.axis_index("seq")
    chip = s // 2
    return x, chip // NZ, lax.rem(chip, NZ), lax.rem(s, 2), chip


def device(x, y, z, k):
    return (x, (y * NZ + z) * 2 + k)


def remote(src, dst, send_sem, recv_sem, dev):
    return pltpu.make_async_remote_copy(
        src_ref=src, dst_ref=dst, send_sem=send_sem, recv_sem=recv_sem,
        device_id=dev, device_id_type=MESH,
    )


def over(first, last, fn):
    def step(d, carry):
        fn(d)
        return carry

    lax.fori_loop(first, last, step, 0)


def enter():
    x, y, z, k, chip = place()
    s = 2 * chip + k
    seq = CHIPS * 2
    partners = [device(x, y, z, 1 - k)]
    partners += [device(lax.rem(x + d, NX), y, z, k) for d in range(1, NX)]
    partners += [device(x, lax.rem(y + d, NY), z, k) for d in range(1, NY)]
    partners += [device(x, y, lax.rem(z + d, NZ), k) for d in range(1, NZ)]
    partners += [(x, lax.rem(s + 1, seq)), (x, lax.rem(s + seq - 1, seq))]
    barrier = pltpu.get_barrier_semaphore()
    for dev in partners:
        pl.semaphore_signal(barrier, inc=1, device_id=dev, device_id_type=MESH)
    pl.semaphore_wait(barrier, len(partners))


def gather(shard, pair, wbuf, ext, ext_t, proj, tok_ref, s_send, s_pair, s_halo, s_z, s_slab, s_swap, landed):
    x, y, z, k, chip = place()
    s = 2 * chip + k
    mate = device(x, y, z, 1 - k)
    to_mate = remote(shard, pair, s_send.at[0], s_pair, mate)
    to_mate.start()
    halo = remote(
        tok_ref.at[pl.ds(L - HALO, HALO)], ext.at[pl.ds(L, HALO)], s_send.at[1], s_halo,
        (x, lax.rem(s + 1, 2 * CHIPS)),
    )
    halo.start()
    ext[L + HALO :, :] = jnp.zeros((ext.shape[0] - L - HALO, ext.shape[1]), BF16)
    to_mate.wait_recv()
    first = k == 0
    mine, other = shard[...], pair[...]
    block = jnp.concatenate([jnp.where(first, mine, other), jnp.where(first, other, mine)], 0)
    half = z // 2
    source = lax.rem(z, 2) == k

    @pl.when(source)
    def _():
        wbuf[x, y, half, k] = block.astype(BF16)

    def z_copy(d):
        return remote(
            wbuf.at[x, y, half, k], wbuf.at[x, y, half, k], s_send.at[1 + d], s_z.at[half],
            device(x, y, lax.rem(z + d, NZ), k),
        )

    @pl.when(source)
    def _():
        for d in range(1, NZ):
            z_copy(d).start()

    for i in range(NZ // 2):

        @pl.when(2 * i + k != z)
        def _(i=i):
            remote(
                wbuf.at[x, y, i, k], wbuf.at[x, y, i, k], s_send.at[0], s_z.at[i], mate
            ).wait_recv()

    sent = []

    def slab_copy(sx, sy, tx, ty, sem):
        ref = wbuf.at[sx, sy, :, k]
        return remote(ref, ref, s_send.at[sem], s_slab.at[sx * NY + sy], device(tx, ty, z, k))

    def swap(sx, sy, kk, sem):
        ref = wbuf.at[sx, sy, :, kk]
        return remote(ref, ref, s_send.at[24 + sem], s_swap.at[sx * NY + sy], mate)

    def start(copy):
        copy.start()
        sent.append(copy)

    def near(d):
        return lax.rem(x + d * k, NX), lax.rem(y + d * (1 - k), NY)

    def far(d):
        return lax.rem(x + d * (1 - k), NX), lax.rem(y + d * k, NY)

    for d in range(1, 4):
        tx, ty = near(d)
        start(slab_copy(x, y, tx, ty, 8 + d))
    for d in range(1, 4):
        tx, ty = far(d)
        start(slab_copy(x, y, tx, ty, 11 + d))
    start(swap(x, y, k, 0))
    n = 0
    for d in range(1, 4):
        sx, sy = near(d)
        slab_copy(sx, sy, x, y, 0).wait_recv()
        for t in range(1, 4):
            tx, ty = far(t)
            start(slab_copy(sx, sy, tx, ty, 15 + n))
            n += 1
        start(swap(sx, sy, k, d))
    landed()
    halo.wait_recv()

    @pl.when(s == 0)
    def _():
        ext[L : L + HALO, :] = jnp.zeros((HALO, ext.shape[1]), BF16)

    ext_t[...] = ext[...].T
    n = 4
    for e in range(4):
        for d in range(1, 4):
            fx, fy = far(d)
            sx = lax.rem(fx + e * k, NX)
            sy = lax.rem(fy + e * (1 - k), NY)
            slab_copy(sx, sy, x, y, 0).wait_recv()
            start(swap(sx, sy, k, n))
            n += 1
    for sx in range(NX):
        for sy in range(NY):
            swap(sx, sy, 1 - k, 0).wait_recv()
    result = dg(ext[0 : L + HALO, :], wbuf[...].reshape(ext.shape[1], WIDE), 1, 0)
    proj[HALO:, :] = result[0:L]
    proj[0:HALO, :] = result[L:]

    def drain():
        to_mate.wait_send()
        halo.wait_send()
        for copy in sent:
            copy.wait_send()

        @pl.when(source)
        def _():
            for d in range(1, NZ):
                z_copy(d).wait_send()

    return drain


def scan(loc, part, snd, rcv, snd2, rcv2, mine_in, other_in, st, s_send, s_part, s_one, s_two, s_fin, meanwhile, meanwhile2):
    x, y, z, k, chip = place()
    mate = device(x, y, z, 1 - k)

    def peer(d):
        c = lax.rem(chip + d, CHIPS)
        return c, (x, 2 * c + k)

    to_mate = remote(loc.at[1 - k], part, s_send.at[0], s_part, mate)
    to_mate.start()
    to_mate.wait_recv()
    first = k == 0
    own, other = loc[k], part[...]
    one0 = jnp.where(first, own, other)
    one1 = jnp.where(first, other, own)
    a0, ad0 = one0[256:257], one0[257:258]
    a1, ad1 = one1[256:257], one1[257:258]
    fs = a1 * one0[0:64] + one1[0:64]
    ft = a1 * one0[64:128] + ad1 * one0[0:64] + one1[64:128]
    bs = a0 * one1[128:192] + one0[128:192]
    bt = a0 * one1[192:256] + ad0 * one1[128:192] + one0[192:256]
    a, ad = a0 * a1, ad0 * a1 + a0 * ad1
    row = iota((8, HALF), 0)
    dec = jnp.where(row == 0, a, jnp.where(row == 1, ad, 0.0))
    for g in range(8):
        for i in range(4):
            j = 4 * g + i
            lanes = slice(128 * i, 128 * i + 128)
            rows = slice(8 * g, 8 * g + 8)
            snd[j, 0] = fs[rows, lanes]
            snd[j, 1] = ft[rows, lanes]
            snd[j, 2] = bs[rows, lanes]
            snd[j, 3] = bt[rows, lanes]
            snd[j, 4] = dec[:, lanes]

    def first_copy(d):
        c, dev = peer(d)
        return remote(snd.at[c], rcv.at[chip], s_send.at[d], s_one.at[chip], dev)

    def second_copy(d):
        c, dev = peer(d)
        return remote(snd2.at[c], rcv2.at[chip], s_send.at[CHIPS + d], s_two.at[chip], dev)

    over(1, CHIPS, lambda d: first_copy(d).start())
    rcv[chip] = snd[chip]
    ready = meanwhile()

    def first_arrived(d):
        c, dev = peer(d)
        remote(snd.at[c], rcv.at[c], s_send.at[d], s_one.at[c], dev).wait_recv()

    over(1, CHIPS, first_arrived)
    zero = jnp.zeros((8, 128), F32)
    s, t = zero, zero
    for c in range(CHIPS):
        snd2[c, 0] = s
        snd2[c, 1] = t
        ca, cad = rcv[c, 4, 0:1, :], rcv[c, 4, 1:2, :]
        s, t = ca * s + rcv[c, 0], ca * t + (cad * s + rcv[c, 1])
    s, t = zero, zero
    for c in range(CHIPS - 1, -1, -1):
        snd2[c, 2] = s
        snd2[c, 3] = t
        ca, cad = rcv[c, 4, 0:1, :], rcv[c, 4, 1:2, :]
        s, t = ca * s + rcv[c, 2], ca * t + (cad * s + rcv[c, 3])

    over(1, CHIPS, lambda d: second_copy(d).start())
    rcv2[chip] = snd2[chip]
    ready = meanwhile2(ready)

    def second_arrived(d):
        c, dev = peer(d)
        remote(snd2.at[c], rcv2.at[c], s_send.at[CHIPS + d], s_two.at[c], dev).wait_recv()

    over(1, CHIPS, second_arrived)
    for g in range(8):
        for i in range(4):
            j = 4 * g + i
            lanes = slice(128 * i, 128 * i + 128)
            for kind in range(4):
                base = 64 * kind + 8 * g
                mine_in[base : base + 8, lanes] = rcv2[j, kind]
    own, other = loc[k], part[...]
    one0 = jnp.where(first, own, other)
    one1 = jnp.where(first, other, own)
    fs, ft, bs, bt = (mine_in[64 * i : 64 * i + 64, :] for i in range(4))
    later_s = a0 * fs + one0[0:64]
    later_t = a0 * ft + ad0 * fs + one0[64:128]
    early_s = a1 * bs + one1[128:192]
    early_t = a1 * bt + ad1 * bs + one1[192:256]
    other_in[0:64, :] = jnp.where(first, later_s, fs)
    other_in[64:128, :] = jnp.where(first, later_t, ft)
    other_in[128:192, :] = jnp.where(first, bs, early_s)
    other_in[192:256, :] = jnp.where(first, bt, early_t)
    back = remote(other_in, st.at[k], s_send.at[2 * CHIPS], s_fin, mate)
    back.start()
    st[k, 0:64, :] = jnp.where(first, fs, later_s)
    st[k, 64:128, :] = jnp.where(first, ft, later_t)
    st[k, 128:192, :] = jnp.where(first, early_s, bs)
    st[k, 192:256, :] = jnp.where(first, early_t, bt)
    remote(other_in, st.at[1 - k], s_send.at[2 * CHIPS], s_fin, mate).wait_recv()

    def drain():
        to_mate.wait_send()
        over(1, CHIPS, lambda d: first_copy(d).wait_send())
        over(1, CHIPS, lambda d: second_copy(d).wait_send())
        back.wait_send()

    return ready, drain


def reduce(dp, ext_t, full, g2, m01, m2, a0, a1, a2, r0, r1, r2, b0, b1, b2, q0, q1, q2, c0, c1, c2, p0, p1, p2,
           e2, f2, s_send, s_mate, s_a, s_b, s_c, s_e, outs):
    x, y, z, k, chip = place()
    mate = device(x, y, z, 1 - k)
    holder = lax.rem(z, 2) == k

    def x_to(d):
        return device(lax.rem(x + d, NX), y, z, k)

    def y_to(d):
        return device(x, lax.rem(y + d, NY), z, k)

    def z_to(d):
        return device(x, y, lax.rem(z + d, NZ), k)

    high, low = split(dp)
    low_half = iota((8, 128), 1) < 64
    block_rows = NY * NZ * 16
    used = [0]

    def copy(src, dst, recv_sem, dev):
        used[0] += 1
        return remote(src, dst, s_send.at[used[0] - 1], recv_sem, dev)

    everything = []
    mates, first0, first1 = [], [], []

    def settle(i):
        xb = lax.rem(x + 1 + i, NX)
        for c in mates[3 * i : 3 * i + 3]:
            c.wait_recv()
        a0[xb] = full[0, xb, :, :, k] + m01[0, xb]
        if i < NX - 1:
            first0.append(copy(a0.at[xb], r0.at[i], s_a.at[i], x_to(1 + i)))
            first0[-1].start()
        a1[xb] = full[1, xb, :, :, k] + m01[1, xb]
        for d in range(1, NY):
            first1.append(copy(a1.at[xb, lax.rem(y + d, NY)], r1.at[d - 1, xb], s_a.at[3 + 3 * i + d - 1], y_to(d)))
            first1[-1].start()
        a2[xb] = g2[k, xb] + m2[xb]

    for i in range(NX):
        xb = lax.rem(x + 1 + i, NX)
        rows = ext_t[pl.ds(pl.multiple_of(xb * block_rows, block_rows), block_rows), :]
        part = dg(rows, high, 1, 0) + dg(rows, low, 1, 0)
        full[0, xb] = part[:, 0:128].reshape(NY, NZ, 2, 8, 128)
        full[1, xb] = part[:, 128:256].reshape(NY, NZ, 2, 8, 128)
        steps = part[:, 256:384].reshape(NY, NZ // 2, 2, 2, 8, 128)
        for zp in range(2):
            g2[zp, xb] = jnp.where(low_half, steps[:, :, zp, 0], steps[:, :, zp, 1])
        for tile in range(2):
            mates.append(copy(full.at[tile, xb, :, :, 1 - k], m01.at[tile, xb], s_mate.at[3 * i + tile], mate))
            mates[-1].start()
        mates.append(copy(g2.at[1 - k, xb], m2.at[xb], s_mate.at[3 * i + 2], mate))
        mates[-1].start()
        if i > 0:
            settle(i - 1)
    settle(NX - 1)

    def z_block(i, slot):
        used[0] += 1
        return remote(a2.at[:, :, i], r2.at[slot], s_send.at[used[0] - 1], s_a.at[16 + slot], device(x, y, 2 * i + k, k))

    zsend = []
    for i in range(NZ // 2):
        gap = lax.rem(z - (2 * i + k) + NZ, NZ)
        zsend.append((2 * i + k != z, z_block(i, gap)))
        pl.when(zsend[-1][0])(zsend[-1][1].start)

    for c in first0:
        c.wait_recv()
    b0[...] = (a0[x] + r0[0]) + (r0[1] + r0[2])
    second0 = []
    for d in range(1, NY):
        second0.append(copy(b0.at[lax.rem(y + d, NY)], q0.at[d - 1], s_b.at[d], y_to(d)))
        second0[-1].start()
    for i in range(NX):
        xb = lax.rem(x + 1 + i, NX)
        for c in first1[3 * i : 3 * i + 3]:
            c.wait_recv()
    b1[...] = (a1[:, y] + r1[0]) + (r1[1] + r1[2])
    second1 = []
    for d in range(1, NZ):
        second1.append(copy(b1.at[:, lax.rem(z + d, NZ)], q1.at[d - 1], s_b.at[3 + d], z_to(d)))
        second1[-1].start()
    second2 = [copy(b2.at[lax.rem(x + d, NX)], q2.at[d - 1], s_b.at[10 + d], x_to(d)) for d in range(1, NX)]

    @pl.when(holder)
    def _():
        for gap in range(1, NZ):
            remote(a2.at[:, :, 0], r2.at[gap], s_send.at[0], s_a.at[16 + gap], mate).wait_recv()
        total = a2[:, :, z // 2] + ((r2[1] + r2[2]) + (r2[3] + r2[4]))
        b2[...] = total + ((r2[5] + r2[6]) + r2[7])
        for c in second2:
            c.start()

    for c in second0:
        c.wait_recv()
    c0[...] = (b0[y] + q0[0]) + (q0[1] + q0[2])
    third0, third1 = [], []
    for d in range(1, NZ):
        third0.append(copy(c0.at[lax.rem(z + d, NZ)], p0.at[d - 1], s_c.at[d], z_to(d)))
        third0[-1].start()
    third2 = [copy(c2.at[lax.rem(y + d, NY)], p2.at[d - 1], s_c.at[10 + d], y_to(d)) for d in range(1, NY)]

    @pl.when(holder)
    def _():
        for c in second2:
            c.wait_recv()
        c2[...] = (b2[x] + q2[0]) + (q2[1] + q2[2])
        for c in third2:
            c.start()

    for c in second1:
        c.wait_recv()
    c1[...] = b1[:, z] + ((q1[0] + q1[1]) + (q1[2] + q1[3])) + ((q1[4] + q1[5]) + q1[6])
    for d in range(1, NX):
        third1.append(copy(c1.at[lax.rem(x + d, NX)], p1.at[d - 1], s_c.at[7 + d], x_to(d)))
        third1[-1].start()
    last = copy(e2, f2, s_e, mate)

    @pl.when(holder)
    def _():
        for c in third2:
            c.wait_recv()
        e2[...] = (c2[y] + p2[0]) + (p2[1] + p2[2])
        last.start()

    for c in third0:
        c.wait_recv()
    outs[0][...] = c0[z] + ((p0[0] + p0[1]) + (p0[2] + p0[3])) + ((p0[4] + p0[5]) + p0[6])
    for c in third1:
        c.wait_recv()
    outs[2][...] = (c1[x] + p1[0]) + (p1[1] + p1[2])

    @pl.when(jnp.logical_not(holder))
    def _():
        last.wait_recv()
        e2[...] = f2[...]

    steps = e2[...]
    mine = jnp.where(k == 0, steps[:, 0:64], steps[:, 64:128])
    outs[1][...] = mine[:, 0:H]
    outs[3][...] = mine[:, H : 2 * H]

    for c in mates + first0 + first1 + second0 + second1 + third0 + third1:
        c.wait_send()
    for used_here, c in zsend:
        pl.when(used_here)(c.wait_send)

    @pl.when(holder)
    def _():
        for c in second2 + third2:
            c.wait_send()
        last.wait_send()


def everything(scale, sw_ref, sd_ref, tw_ref, td_ref, tok_ref, v_hbm, u_hbm, conv_ref, bias_ref, rate_ref,
               o_sel, o_step, o_selh, o_steph, v_ref, u_ref, shard, pair, wbuf, ext, ext_t, proj,
               loc, part, snd, rcv, snd2, rcv2, mine_in, other_in, st,
               rows_ref, row1_ref, row2_ref, colq_ref, colqd_ref, zp_ref, reduce_scratch,
               s_in, gather_sems, scan_sems, reduce_sems):
    local = [
        pltpu.make_async_copy(tok_ref, ext.at[pl.ds(0, L)], s_in.at[0]),
        pltpu.make_async_copy(v_hbm, v_ref, s_in.at[1]),
        pltpu.make_async_copy(u_hbm, u_ref, s_in.at[2]),
    ]
    for c in local:
        c.start()
    shard[:, 0:128] = sw_ref[...].astype(F32)
    shard[:, 128:256] = sd_ref[...].astype(F32)
    shard[:, 256 : 256 + H] = tw_ref[...].astype(F32)
    shard[:, 256 + H : 256 + 2 * H] = td_ref[...].astype(F32)
    shard[:, 256 + 2 * H :] = jnp.zeros((shard.shape[0], 128 - 2 * H), F32)
    enter()

    def landed():
        for c in local:
            c.wait()

    drain_gather = gather(shard, pair, wbuf, ext, ext_t, proj, tok_ref, *gather_sems, landed)

    rate = rate_ref[...]
    ft = features(lambda row, lane, lanes: proj[row : row + L, lane : lane + lanes], conv_ref[...], bias_ref[...], rate)
    wts = weights_of(ft)
    pp = pair_parts(ft)
    we, wde, es, eds, eu, edu = streams(wts, v_ref[...], u_ref[...])
    forward, backward = local_states(pp, we, wde, eu, edu)
    row = iota((8, HP), 0)
    dec = jnp.where(row == 0, es[L - 1 :, :], jnp.where(row == 1, eds[L - 1 :, :], 0.0))
    for half in range(2):
        lanes = slice(HALF * half, HALF * half + HALF)
        loc[half, 0:128, :] = forward[:, lanes]
        loc[half, 128:256, :] = backward[:, lanes]
        loc[half, 256:264, :] = dec[:, lanes]

    def tile(ref):
        return lambda i: ref[:, pl.ds(pl.multiple_of(i * 128, 128), 128)]

    def meanwhile():
        g, gd = intra_setup(ft, pp, rows_ref, row1_ref, row2_ref)
        return intra(ft, g, gd, tile(v_ref), tile(u_ref), rows_ref, row1_ref, row2_ref, colq_ref, colqd_ref)

    def meanwhile2(ready):
        return intra_pairs(pp, *ready)

    pairs, drain_scan = scan(
        loc, part, snd, rcv, snd2, rcv2, mine_in, other_in, st, *scan_sems, meanwhile, meanwhile2
    )
    xf = jnp.concatenate([st[0, 0:128, :], st[1, 0:128, :]], 1)
    xb = jnp.concatenate([st[0, 128:256, :], st[1, 128:256, :]], 1)
    dz, dzd, dq, dqd = finish(
        ft, wts, pp, pairs, row1_ref[...], row2_ref[...], colq_ref[...], colqd_ref[...],
        we, wde, eu, edu, v_ref[...], u_ref[...], xf, xb, rate, scale,
    )
    zp_ref[...] = jnp.zeros(zp_ref.shape, F32)
    zp_ref[HALO : HALO + L, 0:128] = dz
    zp_ref[HALO : HALO + L, 128:256] = dzd
    conv = conv_ref[...]

    def spread(first_row, count, lanes):
        total = conv[0:1, :] * zp_ref[first_row + 3 : first_row + 3 + count, lanes]
        for tap in range(1, KCONV):
            total = total + conv[tap : tap + 1, :] * zp_ref[first_row + 3 - tap : first_row + 3 - tap + count, lanes]
        return total

    pad = jnp.zeros((128 - HALO, 128), F32)
    columns = []
    for half in range(2):
        lanes = slice(128 * half, 128 * half + 128)
        columns.append(jnp.concatenate([spread(HALO, L, lanes), spread(0, HALO, lanes), pad], 0))
    both = jnp.concatenate([dq, dqd, dq, dqd], 1)
    columns.append(jnp.concatenate([both, jnp.zeros((128, 128), F32)], 0))
    dp = jnp.concatenate(columns, 1)
    reduce(dp, ext_t, *reduce_scratch, *reduce_sems, (o_sel, o_step, o_selh, o_steph))
    drain_gather()
    drain_scan()


def vmem(shape, dtype=F32):
    return pltpu.VMEM(shape, dtype)


def dma(*shape):
    return pltpu.SemaphoreType.DMA(shape)


def body(tokens, values, cotangent, sel_weight, step_weight, sel_dir, step_dir, conv_weight, step_bias, decay_rate):
    own_tokens, v, u = tokens[0], values[0], cotangent[0]
    depth = own_tokens.shape[1]
    rows = sel_weight.shape[0]
    scale = 1.0 / math.sqrt(NX * CHIPS * 2 * L)
    spec = pl.BlockSpec(memory_space=pltpu.VMEM)
    hbm = pl.BlockSpec(memory_space=pl.ANY)
    tiles = NX * NY * NZ
    reduce_scratch = (
        [vmem((2, NX, NY, NZ, 2, 8, 128)), vmem((2, NX, NY, NZ // 2, 8, 128)),
         vmem((2, NX, NY, NZ, 8, 128)), vmem((NX, NY, NZ // 2, 8, 128))]
        + [vmem((NX, NY, NZ, 8, 128))] * 2 + [vmem((NX, NY, NZ // 2, 8, 128))]
        + [vmem((3, NY, NZ, 8, 128)), vmem((3, NX, NZ, 8, 128)), vmem((NZ, NX, NY, 8, 128))]
        + [vmem((NY, NZ, 8, 128)), vmem((NX, NZ, 8, 128)), vmem((NX, NY, 8, 128))]
        + [vmem((3, NZ, 8, 128)), vmem((7, NX, 8, 128)), vmem((3, NY, 8, 128))]
        + [vmem((NZ, 8, 128)), vmem((NX, 8, 128)), vmem((NY, 8, 128))]
        + [vmem((7, 8, 128)), vmem((3, 8, 128)), vmem((3, 8, 128))]
        + [vmem((8, 128)), vmem((8, 128))]
    )
    scratch = [
        vmem((L, HP), BF16), vmem((L, HP), BF16),
        vmem((rows, WIDE)), vmem((rows, WIDE)), vmem((NX, NY, NZ // 2, 2, 2 * rows, WIDE), BF16),
        vmem((2 * L, depth), BF16), vmem((depth, 2 * L), BF16), vmem((HALO + L, WIDE)),
        vmem((2, 264, HALF)), vmem((264, HALF)), vmem((CHIPS, 5, 8, 128)), vmem((CHIPS, 5, 8, 128)),
        vmem((CHIPS, 4, 8, 128)), vmem((CHIPS, 4, 8, 128)), vmem((256, HALF)), vmem((256, HALF)),
        vmem((2, 256, HALF)),
        vmem((3 * H, L)), vmem((L, L)), vmem((L, L)), vmem((H, L)), vmem((H, L)), vmem((HALO + L + 8, 256)),
        reduce_scratch,
        dma(3),
        [dma(40), dma(), dma(), dma(NZ // 2), dma(NX * NY), dma(NX * NY)],
        [dma(2 * CHIPS + 1), dma(), dma(CHIPS), dma(CHIPS), dma()],
        [dma(64), dma(12), dma(24), dma(14), dma(14), dma()],
    ]
    return tuple(
        pl.pallas_call(
            functools.partial(everything, scale),
            out_shape=[
                jax.ShapeDtypeStruct((rows, 128), F32), jax.ShapeDtypeStruct((rows, H), F32),
                jax.ShapeDtypeStruct((rows, 128), F32), jax.ShapeDtypeStruct((rows, H), F32),
            ],
            in_specs=[spec] * 4 + [hbm] * 3 + [spec] * 3,
            out_specs=[spec] * 4,
            scratch_shapes=scratch,
            compiler_params=pltpu.CompilerParams(
                vmem_limit_bytes=VMEM_LIMIT, collective_id=0, has_side_effects=True
            ),
        )(sel_weight, sel_dir, step_weight, step_dir, own_tokens, v, u, conv_weight, step_bias[None, :], decay_rate[None, :])
    )


def solution(mesh):
    shards = P(("dp", "seq"), None)
    stream = P("dp", "seq", None)
    return jax.shard_map(
        body,
        mesh=mesh,
        in_specs=(stream, stream, stream, shards, shards, shards, shards, P(), P(), P()),
        out_specs=(shards, shards, shards, shards),
        check_vma=False,
    )
```

```python
import functools
import math

import jax
import jax.numpy as jnp
from jax import lax
from jax.experimental import pallas as pl
from jax.experimental.pallas import tpu as pltpu
from jax.sharding import PartitionSpec as P

N = 64
P_SIZE = 32
H = 32
KCONV = 4
L = 128
HALO = 16
HP = H * P_SIZE
HALF = HP // 2
WIDE = 384
NX, NY, NZ = 4, 4, 8
CHIPS = NY * NZ
MESH = pl.DeviceIdType.MESH
F32 = jnp.float32
BF16 = jnp.bfloat16
VMEM_LIMIT = 56 * 1024 * 1024


def roll64(x):
    return pltpu.roll(x, 64, 1)


def split(x):
    high = x.astype(BF16)
    low = (x - high.astype(F32)).astype(BF16)
    return high, low


def split3(x):
    high = x.astype(BF16)
    rest = x - high.astype(F32)
    mid = rest.astype(BF16)
    low = (rest - mid.astype(F32)).astype(BF16)
    return high, mid, low


def dg(a, b, ca, cb):
    return lax.dot_general(a, b, (((ca,), (cb,)), ((), ())), preferred_element_type=F32)


def dot_split(a, b, ca, cb):
    ah, al = split(a)
    bh, bl = split(b)
    return dg(ah, bh, ca, cb) + (dg(ah, bl, ca, cb) + dg(al, bh, ca, cb))


def dot_left(a, b, ca, cb):
    ah, al = split(a)
    return dg(ah, b, ca, cb) + dg(al, b, ca, cb)


def iota(shape, dim):
    return lax.broadcasted_iota(jnp.int32, shape, dim)


def low_lanes():
    return iota((L, 128), 1) < 64


def head_spread():
    return (iota((H, HP), 0) == iota((H, HP), 1) // P_SIZE).astype(F32).astype(BF16)


def triangle(reverse):
    row, column = iota((L, L), 0), iota((L, L), 1)
    keep = (column >= row) if reverse else (row >= column)
    return keep.astype(F32).astype(BF16)


def cumulate(x, reverse):
    tri = triangle(reverse)
    a, b, c = split3(x)
    return dg(tri, a, 1, 0) + (dg(tri, b, 1, 0) + dg(tri, c, 1, 0))


def features(proj, conv2, bias, rate):
    z = jnp.zeros((L, 128), F32)
    zd = jnp.zeros((L, 128), F32)
    for k in range(KCONV):
        rows = HALO - (KCONV - 1) + k
        z = z + conv2[k : k + 1, :128] * proj(rows, 0, 128)
        zd = zd + conv2[k : k + 1, :128] * proj(rows, 128, 128)
    sg = jax.nn.sigmoid(z)
    act = z * sg
    first = sg * (1.0 + z * (1.0 - sg))
    second = sg * (1.0 - sg) * (2.0 + z * (1.0 - 2.0 * sg))
    actd = first * zd
    steps = proj(HALO, 256, 128)
    q = steps[:, :H] + bias
    qd = steps[:, H : 2 * H]
    delta = jnp.maximum(q, 0.0) + jnp.log1p(jnp.exp(-jnp.abs(q)))
    sq = jax.nn.sigmoid(q)
    deltad = sq * qd
    cum = cumulate(-(delta * rate), False)
    cumd = cumulate(-(deltad * rate), False)
    return dict(
        zd=zd, act=act, actd=actd, first=first, second=second,
        qd=qd, sq=sq, delta=delta, deltad=deltad, cum=cum, cumd=cumd,
    )


def weights_of(ft):
    cum, cumd = ft["cum"], ft["cumd"]
    last, lastd = cum[L - 1 :, :], cumd[L - 1 :, :]
    e = jnp.exp(cum)
    ed = e * cumd
    f = jnp.exp(last - cum)
    fd = f * (lastd - cumd)
    w = f * ft["delta"]
    wd = fd * ft["delta"] + f * ft["deltad"]
    return e, ed, f, fd, w, wd


def pair_parts(ft):
    act, actd = ft["act"], ft["actd"]
    actr, actdr = roll64(act), roll64(actd)
    m = low_lanes()
    return dict(
        b_bd=jnp.where(m, act, actdr),
        o_b=jnp.where(m, 0.0, actr),
        c_cd=jnp.where(m, actr, actd),
        o_c=jnp.where(m, 0.0, act),
        b_o=jnp.where(m, act, 0.0),
        bd_b=jnp.where(m, actd, actr),
        c_o=jnp.where(m, actr, 0.0),
        cd_c=jnp.where(m, actdr, act),
        b_c=act,
        c_b=actr,
    )


def spread_rows(rows):
    return dot_left(rows, head_spread(), 1, 0)


def streams(wts, values, cotangent):
    e, ed, _, _, w, wd = wts
    v = values.astype(F32)
    u = cotangent.astype(F32)
    we = spread_rows(w) * v
    wde = spread_rows(wd) * v
    es = spread_rows(e)
    eds = spread_rows(ed)
    return we, wde, es, eds, es * u, eds * u


def forward_states(pp, we, wde):
    left = jnp.concatenate([pp["b_bd"], pp["o_b"]], 0)
    return dot_split(left, jnp.concatenate([we, wde], 0), 0, 0)


def backward_states(pp, eu, edu):
    left = jnp.concatenate([pp["c_cd"], pp["o_c"]], 0)
    return dot_split(left, jnp.concatenate([eu, edu], 0), 0, 0)


def intra_setup(ft, pp, rows_ref, row1_ref, row2_ref):
    g = dot_split(pp["c_o"], pp["b_c"], 1, 1)
    gd = dot_split(pp["cd_c"], pp["b_bd"], 1, 1)
    eta = ft["deltad"] - ft["delta"] * ft["cumd"]
    rows_ref[0:H, :] = ft["cum"].T
    rows_ref[H : 2 * H, :] = ft["delta"].T
    rows_ref[2 * H : 3 * H, :] = eta.T
    row1_ref[...] = jnp.zeros((L, L), F32)
    row2_ref[...] = jnp.zeros((L, L), F32)
    return g, gd


def intra(ft, g, gd, v_of, u_of, rows_ref, row1_ref, row2_ref, colq_ref, colqd_ref, first, last, carry):
    parts = split3(ft["cum"])
    partsd = split(ft["cumd"])
    row, lane = iota((L, L), 0), iota((L, L), 1)
    causal = row >= lane

    def one(i, carry):
        dgm, dgd = carry
        pick = (iota((H, 512), 0) == (4 * i + iota((H, 512), 1) // 128)).astype(F32).astype(BF16)
        ct4 = dg(parts[0], pick, 1, 0) + (dg(parts[1], pick, 1, 0) + dg(parts[2], pick, 1, 0))
        cd4 = dg(partsd[0], pick, 1, 0) + dg(partsd[1], pick, 1, 0)
        v_tile, u_tile = v_of(i), u_of(i)
        row1, row2 = row1_ref[...], row2_ref[...]
        for j in range(4):
            h = 4 * i + j
            mask = (iota((L, 128), 1) // P_SIZE == j).astype(F32)
            w = dg((u_tile.astype(F32) * mask).astype(BF16), v_tile, 1, 1)
            ct = ct4[:, 128 * j : 128 * j + 128]
            cd = cd4[:, 128 * j : 128 * j + 128]
            cs = rows_ref[pl.ds(h, 1), :]
            ds = rows_ref[pl.ds(H + h, 1), :]
            et = rows_ref[pl.ds(2 * H + h, 1), :]
            x = jnp.exp(jnp.where(causal, ct - cs, -1e30)) * w
            xd = x * ds
            dgm = dgm + xd
            dgd = dgd + (x * et + cd * xd)
            q = x * g
            xgd = x * gd
            colq_ref[pl.ds(h, 1), :] = jnp.sum(q, axis=0, keepdims=True)
            colqd_ref[pl.ds(h, 1), :] = jnp.sum(xgd + q * cd, axis=0, keepdims=True)
            r1 = jnp.sum(q * ds, axis=1, keepdims=True)
            r2 = jnp.sum(xgd * ds + q * et, axis=1, keepdims=True)
            here = lane == h
            row1 = jnp.where(here, r1, row1)
            row2 = jnp.where(here, r2, row2)
        row1_ref[...] = row1
        row2_ref[...] = row2
        return dgm, dgd

    return lax.fori_loop(first, last, one, carry)


def intra_pairs(pp, dgm, dgd):
    return (
        dot_split(dgm, pp["b_bd"], 1, 0),
        dot_split(dgd, pp["b_c"], 1, 0),
        dot_split(dgm, pp["c_cd"], 0, 0),
        dot_split(dgd, pp["c_b"], 0, 0),
    )


def head_sums(x):
    return dot_left(x, head_spread(), 1, 1)


def finish_forward(pp, eu, edu, cotangent, xf):
    u = cotangent.astype(F32)
    zz = dot_split(jnp.concatenate([pp["c_o"], pp["cd_c"]], 0), xf, 1, 0)
    return head_sums(zz[:L] * u), head_sums(zz[L:] * u), dot_split(jnp.concatenate([eu, edu], 0), xf, 1, 1)


def finish_backward(pp, we, wde, values, xb):
    v = values.astype(F32)
    yy = dot_split(jnp.concatenate([pp["b_o"], pp["bd_b"]], 0), xb, 1, 0)
    return head_sums(yy[:L] * v), head_sums(yy[L:] * v), dot_split(jnp.concatenate([we, wde], 0), xb, 1, 1)


def finish(ft, wts, pairs, row1, row2, colq, colqd, from_forward, from_backward, xf, xb, rate, scale):
    e, ed, f, fd, w, wd = wts
    g, gdot, pc = from_forward
    kk, kdot, pb = from_backward
    kap = jnp.sum(xb[:64] * xf[:64], axis=0, keepdims=True)
    kapd = jnp.sum(xb[64:] * xf[:64] + xb[:64] * xf[64:], axis=0, keepdims=True)
    both = head_sums(jnp.concatenate([jnp.broadcast_to(kap, (8, HP)), jnp.broadcast_to(kapd, (8, HP))], 0))
    kap, kapd = both[0:1], both[8:9]

    m = low_lanes()
    t1, t2, t3, t4 = pairs
    pair_c = t1 + pc[:L] + jnp.where(m, 0.0, roll64(t2 + pc[L:]))
    pair_b = t3 + pb[:L] + jnp.where(m, 0.0, roll64(t4 + pb[L:]))
    dact = jnp.where(m, pair_b, roll64(pair_c))
    dactd = jnp.where(m, roll64(pair_b), pair_c)
    dz = scale * (ft["first"] * dact)
    dzd = scale * (ft["second"] * ft["zd"] * dact + ft["first"] * dactd)

    delta, deltad, cum, cumd = ft["delta"], ft["deltad"], ft["cum"], ft["cumd"]
    colq, colqd = colq.T, colqd.T
    colqd = colqd - cumd * colq
    row1, row2 = row1[:, :H], row2[:, :H]
    row2 = row2 + cumd * row1
    wk = w * kk
    wkd = wd * kk + w * kdot
    dc = row1 - delta * colq + e * g - wk
    dcd = row2 - (deltad * colq + delta * colqd) + ed * g + e * gdot - wkd
    el, edl = e[L - 1 :, :], ed[L - 1 :, :]
    extra = el * kap + jnp.sum(wk, axis=0, keepdims=True)
    extrad = edl * kap + el * kapd + jnp.sum(wkd, axis=0, keepdims=True)
    ddelta = colq + f * kk - rate * (cumulate(dc, True) + extra)
    ddeltad = colqd + fd * kk + f * kdot - rate * (cumulate(dcd, True) + extrad)
    sq = ft["sq"]
    dq = scale * (sq * ddelta)
    dqd = scale * (sq * (1.0 - sq) * ft["qd"] * ddelta + sq * ddeltad)
    return dz, dzd, dq, dqd


def place():
    x = lax.axis_index("dp")
    s = lax.axis_index("seq")
    chip = s // 2
    return x, chip // NZ, lax.rem(chip, NZ), lax.rem(s, 2), chip


def device(x, y, z, k):
    return (x, (y * NZ + z) * 2 + k)


def remote(src, dst, send_sem, recv_sem, dev):
    return pltpu.make_async_remote_copy(
        src_ref=src, dst_ref=dst, send_sem=send_sem, recv_sem=recv_sem,
        device_id=dev, device_id_type=MESH,
    )


def over(first, last, fn):
    def step(d, carry):
        fn(d)
        return carry

    lax.fori_loop(first, last, step, 0)


def enter():
    x, y, z, k, chip = place()
    s = 2 * chip + k
    seq = CHIPS * 2
    partners = [device(x, y, z, 1 - k)]
    partners += [device(lax.rem(x + d, NX), y, z, k) for d in range(1, NX)]
    partners += [device(x, lax.rem(y + d, NY), z, k) for d in range(1, NY)]
    partners += [device(x, y, lax.rem(z + d, NZ), k) for d in range(1, NZ)]
    partners += [(x, lax.rem(s + 1, seq)), (x, lax.rem(s + seq - 1, seq))]
    barrier = pltpu.get_barrier_semaphore()
    for dev in partners:
        pl.semaphore_signal(barrier, inc=1, device_id=dev, device_id_type=MESH)
    pl.semaphore_wait(barrier, len(partners))


def gather(shard, pair, wbuf, ext, ext_t, proj, tok_ref, s_send, s_pair, s_halo, s_z, s_slab, s_swap, landed):
    x, y, z, k, chip = place()
    s = 2 * chip + k
    mate = device(x, y, z, 1 - k)
    to_mate = remote(shard, pair, s_send.at[0], s_pair, mate)
    to_mate.start()
    halo = remote(
        tok_ref.at[pl.ds(L - HALO, HALO)], ext.at[pl.ds(L, HALO)], s_send.at[1], s_halo,
        (x, lax.rem(s + 1, 2 * CHIPS)),
    )
    halo.start()
    ext[L + HALO :, :] = jnp.zeros((ext.shape[0] - L - HALO, ext.shape[1]), BF16)
    to_mate.wait_recv()
    first = k == 0
    mine, other = shard[...], pair[...]
    block = jnp.concatenate([jnp.where(first, mine, other), jnp.where(first, other, mine)], 0)
    half = z // 2
    source = lax.rem(z, 2) == k

    @pl.when(source)
    def _():
        wbuf[x, y, half, k] = block.astype(BF16)

    def z_copy(d):
        return remote(
            wbuf.at[x, y, half, k], wbuf.at[x, y, half, k], s_send.at[1 + d], s_z.at[half],
            device(x, y, lax.rem(z + d, NZ), k),
        )

    @pl.when(source)
    def _():
        for d in range(1, NZ):
            z_copy(d).start()

    for i in range(NZ // 2):

        @pl.when(2 * i + k != z)
        def _(i=i):
            remote(
                wbuf.at[x, y, i, k], wbuf.at[x, y, i, k], s_send.at[0], s_z.at[i], mate
            ).wait_recv()

    sent = []

    def slab_copy(sx, sy, tx, ty, sem):
        ref = wbuf.at[sx, sy, :, k]
        return remote(ref, ref, s_send.at[sem], s_slab.at[sx * NY + sy], device(tx, ty, z, k))

    def swap(sx, sy, kk, sem):
        ref = wbuf.at[sx, sy, :, kk]
        return remote(ref, ref, s_send.at[24 + sem], s_swap.at[sx * NY + sy], mate)

    def start(copy):
        copy.start()
        sent.append(copy)

    def near(d):
        return lax.rem(x + d * k, NX), lax.rem(y + d * (1 - k), NY)

    def far(d):
        return lax.rem(x + d * (1 - k), NX), lax.rem(y + d * k, NY)

    for d in range(1, 4):
        tx, ty = near(d)
        start(slab_copy(x, y, tx, ty, 8 + d))
    for d in range(1, 4):
        tx, ty = far(d)
        start(slab_copy(x, y, tx, ty, 11 + d))
    start(swap(x, y, k, 0))
    n = 0
    for d in range(1, 4):
        sx, sy = near(d)
        slab_copy(sx, sy, x, y, 0).wait_recv()
        for t in range(1, 4):
            tx, ty = far(t)
            start(slab_copy(sx, sy, tx, ty, 15 + n))
            n += 1
        start(swap(sx, sy, k, d))
    landed()
    halo.wait_recv()

    @pl.when(s == 0)
    def _():
        ext[L : L + HALO, :] = jnp.zeros((HALO, ext.shape[1]), BF16)

    ext_t[...] = ext[...].T
    proj[...] = jnp.zeros(proj.shape, F32)

    def project(sx, sy):
        swap(sx, sy, 1 - k, 0).wait_recv()
        depth = NZ * 2 * shard.shape[0]
        at = pl.multiple_of((sx * NY + sy) * depth, depth)
        piece = dg(ext[0 : L + HALO, pl.ds(at, depth)], wbuf[sx, sy].reshape(depth, WIDE), 1, 0)
        proj[HALO:, :] += piece[0:L]
        proj[0:HALO, :] += piece[L:]

    n = 4
    for e in range(4):
        for d in range(1, 4):
            fx, fy = far(d)
            sx = lax.rem(fx + e * k, NX)
            sy = lax.rem(fy + e * (1 - k), NY)
            slab_copy(sx, sy, x, y, 0).wait_recv()
            start(swap(sx, sy, k, n))
            n += 1
        if e == 0:
            project(x, y)
            for d in range(1, 4):
                project(lax.rem(x + d, NX), y)
                project(x, lax.rem(y + d, NY))
    for e in range(1, 4):
        for d in range(1, 4):
            project(lax.rem(x + d, NX), lax.rem(y + e, NY))

    def drain():
        to_mate.wait_send()
        halo.wait_send()
        for copy in sent:
            copy.wait_send()

        @pl.when(source)
        def _():
            for d in range(1, NZ):
                z_copy(d).wait_send()

    return drain


class Half:
    def __init__(self, loc, part, snd, rcv, snd2, rcv2, other, st, rows, s_send, s_mate, s_one, s_two):
        self.loc, self.part, self.snd, self.rcv, self.snd2, self.rcv2 = loc, part, snd, rcv, snd2, rcv2
        self.other, self.st, self.rows = other, st, rows
        self.s_send, self.s_mate, self.s_one, self.s_two = s_send, s_mate, s_one, s_two
        self.x, self.y, self.z, self.k, self.chip = place()
        self.mate = device(self.x, self.y, self.z, 1 - self.k)
        self.first = self.k == 0

    def peer(self, d):
        c = lax.rem(self.chip + d, CHIPS)
        return c, (self.x, 2 * c + self.k)

    def to_mate(self):
        return remote(self.loc.at[1 - self.k], self.part, self.s_send.at[0], self.s_mate.at[0], self.mate)

    def one(self, d):
        c, dev = self.peer(d)
        piece = pl.ds(0, self.rows)
        return remote(self.snd.at[c, piece], self.rcv.at[self.chip, piece], self.s_send.at[d], self.s_one.at[self.chip], dev)

    def one_in(self, d):
        c, dev = self.peer(d)
        piece = pl.ds(0, self.rows)
        return remote(self.snd.at[c, piece], self.rcv.at[c, piece], self.s_send.at[d], self.s_one.at[c], dev)

    def two(self, d):
        c, dev = self.peer(d)
        return remote(self.snd2.at[c], self.rcv2.at[self.chip], self.s_send.at[CHIPS + d], self.s_two.at[self.chip], dev)

    def two_in(self, d):
        c, dev = self.peer(d)
        return remote(self.snd2.at[c], self.rcv2.at[c], self.s_send.at[CHIPS + d], self.s_two.at[c], dev)

    def back(self):
        return remote(self.other, self.st.at[self.k], self.s_send.at[2 * CHIPS], self.s_mate.at[1], self.mate)

    def back_in(self):
        return remote(self.other, self.st.at[1 - self.k], self.s_send.at[2 * CHIPS], self.s_mate.at[1], self.mate)

    def cores(self):
        own, other = self.loc[self.k], self.part[...]
        return jnp.where(self.first, own, other), jnp.where(self.first, other, own)

    def start_one(self):
        over(1, CHIPS, lambda d: self.one(d).start())
        self.rcv[self.chip] = self.snd[self.chip]

    def start_two(self):
        over(1, CHIPS, lambda d: self.two(d).start())
        self.rcv2[self.chip] = self.snd2[self.chip]

    def wait_one(self):
        over(1, CHIPS, lambda d: self.one_in(d).wait_recv())

    def wait_two(self):
        over(1, CHIPS, lambda d: self.two_in(d).wait_recv())

    def slices(self, s, t, rest):
        for j in range(CHIPS):
            rows = slice(8 * (j // 4), 8 * (j // 4) + 8)
            lanes = slice(128 * (j % 4), 128 * (j % 4) + 128)
            self.snd[j, 0:8] = s[rows, lanes]
            self.snd[j, 8:16] = t[rows, lanes]
            for i, row in enumerate(rest):
                self.snd[j, 16 + i : 17 + i] = row[:, lanes]

    def prefix(self, order, decays):
        s = t = jnp.zeros((8, 128), F32)
        for c in order:
            self.snd2[c, 0:8] = s
            self.snd2[c, 8:16] = t
            a, ad = decays[c, 16:17, :], decays[c, 17:18, :]
            s, t = a * s + self.rcv[c, 0:8], a * t + (ad * s + self.rcv[c, 8:16])

    def assemble(self, a, ad, base, base_first):
        for j in range(CHIPS):
            row = 8 * (j // 4)
            lanes = slice(128 * (j % 4), 128 * (j % 4) + 128)
            self.place_slice(row, lanes, j)
        s, t = self.other[0:64, :], self.other[64:128, :]
        next_s = a * s + base[0:64]
        next_t = a * t + ad * s + base[64:128]
        mine_is_base = self.first if base_first else jnp.logical_not(self.first)
        self.st[self.k, 0:64, :] = jnp.where(mine_is_base, s, next_s)
        self.st[self.k, 64:128, :] = jnp.where(mine_is_base, t, next_t)
        self.other[0:64, :] = jnp.where(mine_is_base, next_s, s)
        self.other[64:128, :] = jnp.where(mine_is_base, next_t, t)
        self.back().start()

    def place_slice(self, row, lanes, j):
        self.other[row : row + 8, lanes] = self.rcv2[j, 0:8]
        self.other[64 + row : 72 + row, lanes] = self.rcv2[j, 8:16]

    def drain(self):
        self.to_mate().wait_send()
        over(1, CHIPS, lambda d: self.one(d).wait_send())
        over(1, CHIPS, lambda d: self.two(d).wait_send())
        self.back().wait_send()


def reduce(dp, ext_t, full, g2, m01, m2, a0, a1, a2, r0, r1, r2, b0, b1, b2, q0, q1, q2, c0, c1, c2, p0, p1, p2,
           e2, f2, s_send, s_mate, s_a, s_b, s_c, s_e, out_ref):
    x, y, z, k, chip = place()
    mate = device(x, y, z, 1 - k)
    holder = lax.rem(z, 2) == k

    def x_to(d):
        return device(lax.rem(x + d, NX), y, z, k)

    def y_to(d):
        return device(x, lax.rem(y + d, NY), z, k)

    def z_to(d):
        return device(x, y, lax.rem(z + d, NZ), k)

    high, low = split(dp)
    low_half = iota((8, 128), 1) < 64
    block_rows = NY * NZ * 16
    used = [0]

    def copy(src, dst, recv_sem, dev):
        used[0] += 1
        return remote(src, dst, s_send.at[used[0] - 1], recv_sem, dev)

    everything = []
    mates, first0, first1 = [], [], []

    def settle(i):
        xb = lax.rem(x + 1 + i, NX)
        for c in mates[3 * i : 3 * i + 3]:
            c.wait_recv()
        a0[xb] = full[0, xb, :, :, k] + m01[0, xb]
        if i < NX - 1:
            first0.append(copy(a0.at[xb], r0.at[i], s_a.at[i], x_to(1 + i)))
            first0[-1].start()
        a1[xb] = full[1, xb, :, :, k] + m01[1, xb]
        for d in range(1, NY):
            first1.append(copy(a1.at[xb, lax.rem(y + d, NY)], r1.at[d - 1, xb], s_a.at[3 + 3 * i + d - 1], y_to(d)))
            first1[-1].start()
        a2[xb] = g2[k, xb] + m2[xb]

    for i in range(NX):
        xb = lax.rem(x + 1 + i, NX)
        rows = ext_t[pl.ds(pl.multiple_of(xb * block_rows, block_rows), block_rows), :]
        part = dg(rows, high, 1, 0) + dg(rows, low, 1, 0)
        full[0, xb] = part[:, 0:128].reshape(NY, NZ, 2, 8, 128)
        full[1, xb] = part[:, 128:256].reshape(NY, NZ, 2, 8, 128)
        steps = part[:, 256:384].reshape(NY, NZ // 2, 2, 2, 8, 128)
        for zp in range(2):
            g2[zp, xb] = jnp.where(low_half, steps[:, :, zp, 0], steps[:, :, zp, 1])
        for tile in range(2):
            mates.append(copy(full.at[tile, xb, :, :, 1 - k], m01.at[tile, xb], s_mate.at[3 * i + tile], mate))
            mates[-1].start()
        mates.append(copy(g2.at[1 - k, xb], m2.at[xb], s_mate.at[3 * i + 2], mate))
        mates[-1].start()
        if i > 0:
            settle(i - 1)
    settle(NX - 1)

    def z_block(i, slot):
        used[0] += 1
        return remote(a2.at[:, :, i], r2.at[slot], s_send.at[used[0] - 1], s_a.at[16 + slot], device(x, y, 2 * i + k, k))

    zsend = []
    for i in range(NZ // 2):
        gap = lax.rem(z - (2 * i + k) + NZ, NZ)
        zsend.append((2 * i + k != z, z_block(i, gap)))
        pl.when(zsend[-1][0])(zsend[-1][1].start)

    for c in first0:
        c.wait_recv()
    b0[...] = (a0[x] + r0[0]) + (r0[1] + r0[2])
    second0 = []
    for d in range(1, NY):
        second0.append(copy(b0.at[lax.rem(y + d, NY)], q0.at[d - 1], s_b.at[d], y_to(d)))
        second0[-1].start()
    for i in range(NX):
        xb = lax.rem(x + 1 + i, NX)
        for c in first1[3 * i : 3 * i + 3]:
            c.wait_recv()
    b1[...] = (a1[:, y] + r1[0]) + (r1[1] + r1[2])
    second1 = []
    for d in range(1, NZ):
        second1.append(copy(b1.at[:, lax.rem(z + d, NZ)], q1.at[d - 1], s_b.at[3 + d], z_to(d)))
        second1[-1].start()
    second2 = [copy(b2.at[lax.rem(x + d, NX)], q2.at[d - 1], s_b.at[10 + d], x_to(d)) for d in range(1, NX)]

    @pl.when(holder)
    def _():
        for gap in range(1, NZ):
            remote(a2.at[:, :, 0], r2.at[gap], s_send.at[0], s_a.at[16 + gap], mate).wait_recv()
        total = a2[:, :, z // 2] + ((r2[1] + r2[2]) + (r2[3] + r2[4]))
        b2[...] = total + ((r2[5] + r2[6]) + r2[7])
        for c in second2:
            c.start()

    for c in second0:
        c.wait_recv()
    c0[...] = (b0[y] + q0[0]) + (q0[1] + q0[2])
    third0, third1 = [], []
    for d in range(1, NZ):
        third0.append(copy(c0.at[lax.rem(z + d, NZ)], p0.at[d - 1], s_c.at[d], z_to(d)))
        third0[-1].start()
    third2 = [copy(c2.at[lax.rem(y + d, NY)], p2.at[d - 1], s_c.at[10 + d], y_to(d)) for d in range(1, NY)]

    @pl.when(holder)
    def _():
        for c in second2:
            c.wait_recv()
        c2[...] = (b2[x] + q2[0]) + (q2[1] + q2[2])
        for c in third2:
            c.start()

    for c in second1:
        c.wait_recv()
    c1[...] = b1[:, z] + ((q1[0] + q1[1]) + (q1[2] + q1[3])) + ((q1[4] + q1[5]) + q1[6])
    for d in range(1, NX):
        third1.append(copy(c1.at[lax.rem(x + d, NX)], p1.at[d - 1], s_c.at[7 + d], x_to(d)))
        third1[-1].start()
    last = copy(e2, f2, s_e, mate)

    @pl.when(holder)
    def _():
        for c in third2:
            c.wait_recv()
        e2[...] = (c2[y] + p2[0]) + (p2[1] + p2[2])
        last.start()

    for c in third0:
        c.wait_recv()
    out_ref[:, 0:128] = c0[z] + ((p0[0] + p0[1]) + (p0[2] + p0[3])) + ((p0[4] + p0[5]) + p0[6])
    for c in third1:
        c.wait_recv()
    out_ref[:, 128:256] = (c1[x] + p1[0]) + (p1[1] + p1[2])

    @pl.when(jnp.logical_not(holder))
    def _():
        last.wait_recv()
        e2[...] = f2[...]

    out_ref[:, 256:384] = jnp.where(k == 0, e2[...], roll64(e2[...]))

    for c in mates + first0 + first1 + second0 + second1 + third0 + third1:
        c.wait_send()
    for used_here, c in zsend:
        pl.when(used_here)(c.wait_send)

    @pl.when(holder)
    def _():
        for c in second2 + third2:
            c.wait_send()
        last.wait_send()


def everything(scale, sw_ref, sd_ref, tw_ref, td_ref, tok_ref, v_hbm, u_hbm, conv_ref, bias_ref, rate_ref,
               out_ref, v_ref, u_ref, shard, pair, wbuf, ext, ext_t, proj,
               forward_scratch, backward_scratch, rows_ref, row1_ref, row2_ref, colq_ref, colqd_ref, zp_ref, reduce_scratch,
               s_in, gather_sems, forward_sems, backward_sems, reduce_sems):
    local = [
        pltpu.make_async_copy(tok_ref, ext.at[pl.ds(0, L)], s_in.at[0]),
        pltpu.make_async_copy(v_hbm, v_ref, s_in.at[1]),
        pltpu.make_async_copy(u_hbm, u_ref, s_in.at[2]),
    ]
    for c in local:
        c.start()
    shard[:, 0:128] = sw_ref[...].astype(F32)
    shard[:, 128:256] = sd_ref[...].astype(F32)
    shard[:, 256 : 256 + H] = tw_ref[...].astype(F32)
    shard[:, 256 + H : 256 + 2 * H] = td_ref[...].astype(F32)
    shard[:, 256 + 2 * H :] = jnp.zeros((shard.shape[0], 128 - 2 * H), F32)
    enter()

    def landed():
        for c in local:
            c.wait()

    drain_gather = gather(shard, pair, wbuf, ext, ext_t, proj, tok_ref, *gather_sems, landed)

    rate = rate_ref[...]
    ft = features(lambda row, lane, lanes: proj[row : row + L, lane : lane + lanes], conv_ref[...], bias_ref[...], rate)
    wts = weights_of(ft)
    pp = pair_parts(ft)
    we, wde, es, eds, eu, edu = streams(wts, v_ref[...], u_ref[...])
    fw = Half(*forward_scratch, 18, *forward_sems)
    bw = Half(*backward_scratch, 16, *backward_sems)
    row = iota((8, HP), 0)
    dec = jnp.where(row == 0, es[L - 1 :, :], jnp.where(row == 1, eds[L - 1 :, :], 0.0))
    states = forward_states(pp, we, wde)
    for half in range(2):
        lanes = slice(HALF * half, HALF * half + HALF)
        fw.loc[half, 0:128, :] = states[:, lanes]
        fw.loc[half, 128:136, :] = dec[:, lanes]
    fw.to_mate().start()
    states = backward_states(pp, eu, edu)
    for half in range(2):
        bw.loc[half] = states[:, HALF * half : HALF * half + HALF]
    bw.to_mate().start()

    fw.to_mate().wait_recv()
    one0, one1 = fw.cores()
    a0, ad0 = one0[128:129], one0[129:130]
    a1, ad1 = one1[128:129], one1[129:130]
    fw.slices(
        a1 * one0[0:64] + one1[0:64],
        a1 * one0[64:128] + ad1 * one0[0:64] + one1[64:128],
        [a0 * a1, ad0 * a1 + a0 * ad1],
    )
    fw.start_one()
    bw.to_mate().wait_recv()
    one0, one1 = bw.cores()
    bw.slices(a0 * one1[0:64] + one0[0:64], a0 * one1[64:128] + ad0 * one1[0:64] + one0[64:128], [])
    bw.start_one()

    def tile(ref):
        return lambda i: ref[:, pl.ds(pl.multiple_of(i * 128, 128), 128)]

    g, gd = intra_setup(ft, pp, rows_ref, row1_ref, row2_ref)
    zero = jnp.zeros((L, L), F32)

    def block_terms(first, last, carry):
        return intra(
            ft, g, gd, tile(v_ref), tile(u_ref), rows_ref, row1_ref, row2_ref, colq_ref, colqd_ref, first, last, carry
        )

    carry = block_terms(0, 6, (zero, zero))
    fw.wait_one()
    fw.prefix(range(CHIPS), fw.rcv)
    fw.start_two()
    carry = block_terms(6, 8, carry)
    bw.wait_one()
    bw.prefix(range(CHIPS - 1, -1, -1), fw.rcv)
    bw.start_two()
    pairs = intra_pairs(pp, *carry)
    fw.wait_two()
    fw.assemble(a0, ad0, fw.cores()[0], True)
    fw.back_in().wait_recv()
    xf = jnp.concatenate([fw.st[0], fw.st[1]], 1)
    from_forward = finish_forward(pp, eu, edu, u_ref[...], xf)
    bw.wait_two()
    bw.assemble(a1, ad1, bw.cores()[1], False)
    bw.back_in().wait_recv()
    xb = jnp.concatenate([bw.st[0], bw.st[1]], 1)
    from_backward = finish_backward(pp, we, wde, v_ref[...], xb)
    dz, dzd, dq, dqd = finish(
        ft, wts, pairs, row1_ref[...], row2_ref[...], colq_ref[...], colqd_ref[...],
        from_forward, from_backward, xf, xb, rate, scale,
    )
    zp_ref[...] = jnp.zeros(zp_ref.shape, F32)
    zp_ref[HALO : HALO + L, 0:128] = dz
    zp_ref[HALO : HALO + L, 128:256] = dzd
    conv = conv_ref[...]

    def spread(first_row, count, lanes):
        total = conv[0:1, :] * zp_ref[first_row + 3 : first_row + 3 + count, lanes]
        for tap in range(1, KCONV):
            total = total + conv[tap : tap + 1, :] * zp_ref[first_row + 3 - tap : first_row + 3 - tap + count, lanes]
        return total

    pad = jnp.zeros((128 - HALO, 128), F32)
    columns = []
    for half in range(2):
        lanes = slice(128 * half, 128 * half + 128)
        columns.append(jnp.concatenate([spread(HALO, L, lanes), spread(0, HALO, lanes), pad], 0))
    both = jnp.concatenate([dq, dqd, dq, dqd], 1)
    columns.append(jnp.concatenate([both, jnp.zeros((128, 128), F32)], 0))
    dp = jnp.concatenate(columns, 1)
    reduce(dp, ext_t, *reduce_scratch, *reduce_sems, out_ref)
    drain_gather()
    fw.drain()
    bw.drain()


def split_outputs(sums_ref, o_sel, o_step, o_selh, o_steph):
    o_sel[...] = sums_ref[:, 0:128]
    o_selh[...] = sums_ref[:, 128:256]
    o_step[...] = sums_ref[:, 256 : 256 + H]
    o_steph[...] = sums_ref[:, 256 + H : 256 + 2 * H]


def vmem(shape, dtype=F32):
    return pltpu.VMEM(shape, dtype)


def dma(*shape):
    return pltpu.SemaphoreType.DMA(shape)


def body(tokens, values, cotangent, sel_weight, step_weight, sel_dir, step_dir, conv_weight, step_bias, decay_rate):
    own_tokens, v, u = tokens[0], values[0], cotangent[0]
    depth = own_tokens.shape[1]
    rows = sel_weight.shape[0]
    scale = 1.0 / math.sqrt(NX * CHIPS * 2 * L)
    spec = pl.BlockSpec(memory_space=pltpu.VMEM)
    hbm = pl.BlockSpec(memory_space=pl.ANY)
    tiles = NX * NY * NZ
    reduce_scratch = (
        [vmem((2, NX, NY, NZ, 2, 8, 128)), vmem((2, NX, NY, NZ // 2, 8, 128)),
         vmem((2, NX, NY, NZ, 8, 128)), vmem((NX, NY, NZ // 2, 8, 128))]
        + [vmem((NX, NY, NZ, 8, 128))] * 2 + [vmem((NX, NY, NZ // 2, 8, 128))]
        + [vmem((3, NY, NZ, 8, 128)), vmem((3, NX, NZ, 8, 128)), vmem((NZ, NX, NY, 8, 128))]
        + [vmem((NY, NZ, 8, 128)), vmem((NX, NZ, 8, 128)), vmem((NX, NY, 8, 128))]
        + [vmem((3, NZ, 8, 128)), vmem((7, NX, 8, 128)), vmem((3, NY, 8, 128))]
        + [vmem((NZ, 8, 128)), vmem((NX, 8, 128)), vmem((NY, 8, 128))]
        + [vmem((7, 8, 128)), vmem((3, 8, 128)), vmem((3, 8, 128))]
        + [vmem((8, 128)), vmem((8, 128))]
    )

    def scan_scratch(piece):
        return [vmem((CHIPS, piece, 128))] * 2 + [vmem((CHIPS, 16, 128))] * 2 + [vmem((128, HALF)), vmem((2, 128, HALF))]

    scratch = [
        vmem((L, HP), BF16), vmem((L, HP), BF16),
        vmem((rows, WIDE)), vmem((rows, WIDE)), vmem((NX, NY, NZ // 2, 2, 2 * rows, WIDE), BF16),
        vmem((2 * L, depth), BF16), vmem((depth, 2 * L), BF16), vmem((HALO + L, WIDE)),
        [vmem((2, 136, HALF)), vmem((136, HALF))] + scan_scratch(24),
        [vmem((2, 128, HALF)), vmem((128, HALF))] + scan_scratch(16),
        vmem((3 * H, L)), vmem((L, L)), vmem((L, L)), vmem((H, L)), vmem((H, L)), vmem((HALO + L + 8, 256)),
        reduce_scratch,
        dma(3),
        [dma(40), dma(), dma(), dma(NZ // 2), dma(NX * NY), dma(NX * NY)],
        [dma(2 * CHIPS + 1), dma(2), dma(CHIPS), dma(CHIPS)],
        [dma(2 * CHIPS + 1), dma(2), dma(CHIPS), dma(CHIPS)],
        [dma(64), dma(12), dma(24), dma(14), dma(14), dma()],
    ]
    sums = pl.pallas_call(
        functools.partial(everything, scale),
        out_shape=jax.ShapeDtypeStruct((rows, WIDE), F32),
        in_specs=[spec] * 4 + [hbm] * 3 + [spec] * 3,
        out_specs=spec,
        scratch_shapes=scratch,
        compiler_params=pltpu.CompilerParams(
            vmem_limit_bytes=VMEM_LIMIT, collective_id=0, has_side_effects=True
        ),
    )(sel_weight, sel_dir, step_weight, step_dir, own_tokens, v, u, conv_weight, step_bias[None, :], decay_rate[None, :])
    return pl.pallas_call(
        split_outputs,
        out_shape=[
            jax.ShapeDtypeStruct((rows, 128), F32), jax.ShapeDtypeStruct((rows, H), F32),
            jax.ShapeDtypeStruct((rows, 128), F32), jax.ShapeDtypeStruct((rows, H), F32),
        ],
        in_specs=[spec],
        out_specs=[spec] * 4,
    )(sums)


def solution(mesh):
    shards = P(("dp", "seq"), None)
    stream = P("dp", "seq", None)
    return jax.shard_map(
        body,
        mesh=mesh,
        in_specs=(stream, stream, stream, shards, shards, shards, shards, P(), P(), P()),
        out_specs=(shards, shards, shards, shards),
        check_vma=False,
    )
```

```python
import functools
import math

import jax
import jax.numpy as jnp
from jax import lax
from jax.experimental import pallas as pl
from jax.experimental.pallas import tpu as pltpu
from jax.sharding import PartitionSpec as P

N = 64
P_SIZE = 32
H = 32
KCONV = 4
L = 128
HALO = 16
HP = H * P_SIZE
HALF = HP // 2
WIDE = 384
NX, NY, NZ = 4, 4, 8
CHIPS = NY * NZ
MESH = pl.DeviceIdType.MESH
F32 = jnp.float32
BF16 = jnp.bfloat16
VMEM_LIMIT = 56 * 1024 * 1024


def roll64(x):
    return pltpu.roll(x, 64, 1)


def split(x):
    high = x.astype(BF16)
    low = (x - high.astype(F32)).astype(BF16)
    return high, low


def split3(x):
    high = x.astype(BF16)
    rest = x - high.astype(F32)
    mid = rest.astype(BF16)
    low = (rest - mid.astype(F32)).astype(BF16)
    return high, mid, low


def dg(a, b, ca, cb):
    return lax.dot_general(a, b, (((ca,), (cb,)), ((), ())), preferred_element_type=F32)


def dot_split(a, b, ca, cb):
    ah, al = split(a)
    bh, bl = split(b)
    return dg(ah, bh, ca, cb) + (dg(ah, bl, ca, cb) + dg(al, bh, ca, cb))


def dot_left(a, b, ca, cb):
    ah, al = split(a)
    return dg(ah, b, ca, cb) + dg(al, b, ca, cb)


def iota(shape, dim):
    return lax.broadcasted_iota(jnp.int32, shape, dim)


def low_lanes():
    return iota((L, 128), 1) < 64


def head_spread():
    return (iota((H, HP), 0) == iota((H, HP), 1) // P_SIZE).astype(F32).astype(BF16)


def triangle(reverse):
    row, column = iota((L, L), 0), iota((L, L), 1)
    keep = (column >= row) if reverse else (row >= column)
    return keep.astype(F32).astype(BF16)


def cumulate(x, reverse):
    tri = triangle(reverse)
    a, b, c = split3(x)
    return dg(tri, a, 1, 0) + (dg(tri, b, 1, 0) + dg(tri, c, 1, 0))


def features(proj, conv2, bias, rate):
    z = jnp.zeros((L, 128), F32)
    zd = jnp.zeros((L, 128), F32)
    for k in range(KCONV):
        rows = HALO - (KCONV - 1) + k
        z = z + conv2[k : k + 1, :128] * proj(rows, 0, 128)
        zd = zd + conv2[k : k + 1, :128] * proj(rows, 128, 128)
    sg = jax.nn.sigmoid(z)
    act = z * sg
    first = sg * (1.0 + z * (1.0 - sg))
    second = sg * (1.0 - sg) * (2.0 + z * (1.0 - 2.0 * sg))
    actd = first * zd
    steps = proj(HALO, 256, 128)
    q = steps[:, :H] + bias
    qd = steps[:, H : 2 * H]
    delta = jnp.maximum(q, 0.0) + jnp.log1p(jnp.exp(-jnp.abs(q)))
    sq = jax.nn.sigmoid(q)
    deltad = sq * qd
    cum = cumulate(-(delta * rate), False)
    cumd = cumulate(-(deltad * rate), False)
    return dict(
        zd=zd, act=act, actd=actd, first=first, second=second,
        qd=qd, sq=sq, delta=delta, deltad=deltad, cum=cum, cumd=cumd,
    )


def weights_of(ft):
    cum, cumd = ft["cum"], ft["cumd"]
    last, lastd = cum[L - 1 :, :], cumd[L - 1 :, :]
    e = jnp.exp(cum)
    ed = e * cumd
    f = jnp.exp(last - cum)
    fd = f * (lastd - cumd)
    w = f * ft["delta"]
    wd = fd * ft["delta"] + f * ft["deltad"]
    return e, ed, f, fd, w, wd


def pair_parts(ft):
    act, actd = ft["act"], ft["actd"]
    actr, actdr = roll64(act), roll64(actd)
    m = low_lanes()
    return dict(
        b_bd=jnp.where(m, act, actdr),
        o_b=jnp.where(m, 0.0, actr),
        c_cd=jnp.where(m, actr, actd),
        o_c=jnp.where(m, 0.0, act),
        b_o=jnp.where(m, act, 0.0),
        bd_b=jnp.where(m, actd, actr),
        c_o=jnp.where(m, actr, 0.0),
        cd_c=jnp.where(m, actdr, act),
        b_c=act,
        c_b=actr,
    )


def spread_rows(rows):
    return dot_left(rows, head_spread(), 1, 0)


def streams(wts, values, cotangent):
    e, ed, _, _, w, wd = wts
    v = values.astype(F32)
    u = cotangent.astype(F32)
    we = spread_rows(w) * v
    wde = spread_rows(wd) * v
    es = spread_rows(e)
    eds = spread_rows(ed)
    return we, wde, es, eds, es * u, eds * u


def forward_states(pp, we, wde):
    left = jnp.concatenate([pp["b_bd"], pp["o_b"]], 0)
    return dot_split(left, jnp.concatenate([we, wde], 0), 0, 0)


def backward_states(pp, eu, edu):
    left = jnp.concatenate([pp["c_cd"], pp["o_c"]], 0)
    return dot_split(left, jnp.concatenate([eu, edu], 0), 0, 0)


def intra_setup(ft, pp, rows_ref, row1_ref, row2_ref):
    g = dot_split(pp["c_o"], pp["b_c"], 1, 1)
    gd = dot_split(pp["cd_c"], pp["b_bd"], 1, 1)
    eta = ft["deltad"] - ft["delta"] * ft["cumd"]
    rows_ref[0:H, :] = ft["cum"].T
    rows_ref[H : 2 * H, :] = ft["delta"].T
    rows_ref[2 * H : 3 * H, :] = eta.T
    row1_ref[...] = jnp.zeros((L, L), F32)
    row2_ref[...] = jnp.zeros((L, L), F32)
    return g, gd


def intra(ft, g, gd, v_of, u_of, rows_ref, row1_ref, row2_ref, colq_ref, colqd_ref, first, last, carry):
    parts = split3(ft["cum"])
    partsd = split(ft["cumd"])
    row, lane = iota((L, L), 0), iota((L, L), 1)
    causal = row >= lane

    def one(i, carry):
        dgm, dgd = carry
        pick = (iota((H, 512), 0) == (4 * i + iota((H, 512), 1) // 128)).astype(F32).astype(BF16)
        ct4 = dg(parts[0], pick, 1, 0) + (dg(parts[1], pick, 1, 0) + dg(parts[2], pick, 1, 0))
        cd4 = dg(partsd[0], pick, 1, 0) + dg(partsd[1], pick, 1, 0)
        v_tile, u_tile = v_of(i), u_of(i)
        row1, row2 = row1_ref[...], row2_ref[...]
        for j in range(4):
            h = 4 * i + j
            mask = (iota((L, 128), 1) // P_SIZE == j).astype(F32)
            w = dg((u_tile.astype(F32) * mask).astype(BF16), v_tile, 1, 1)
            ct = ct4[:, 128 * j : 128 * j + 128]
            cd = cd4[:, 128 * j : 128 * j + 128]
            cs = rows_ref[pl.ds(h, 1), :]
            ds = rows_ref[pl.ds(H + h, 1), :]
            et = rows_ref[pl.ds(2 * H + h, 1), :]
            x = jnp.exp(jnp.where(causal, ct - cs, -1e30)) * w
            xd = x * ds
            dgm = dgm + xd
            dgd = dgd + (x * et + cd * xd)
            q = x * g
            xgd = x * gd
            colq_ref[pl.ds(h, 1), :] = jnp.sum(q, axis=0, keepdims=True)
            colqd_ref[pl.ds(h, 1), :] = jnp.sum(xgd + q * cd, axis=0, keepdims=True)
            r1 = jnp.sum(q * ds, axis=1, keepdims=True)
            r2 = jnp.sum(xgd * ds + q * et, axis=1, keepdims=True)
            here = lane == h
            row1 = jnp.where(here, r1, row1)
            row2 = jnp.where(here, r2, row2)
        row1_ref[...] = row1
        row2_ref[...] = row2
        return dgm, dgd

    return lax.fori_loop(first, last, one, carry)


def intra_pairs(pp, dgm, dgd):
    return (
        dot_split(dgm, pp["b_bd"], 1, 0),
        dot_split(dgd, pp["b_c"], 1, 0),
        dot_split(dgm, pp["c_cd"], 0, 0),
        dot_split(dgd, pp["c_b"], 0, 0),
    )


def head_sums(x):
    return dot_left(x, head_spread(), 1, 1)


def finish_forward(pp, eu, edu, cotangent, xf):
    u = cotangent.astype(F32)
    zz = dot_split(jnp.concatenate([pp["c_o"], pp["cd_c"]], 0), xf, 1, 0)
    return head_sums(zz[:L] * u), head_sums(zz[L:] * u), dot_split(jnp.concatenate([eu, edu], 0), xf, 1, 1)


def finish_backward(pp, we, wde, values, xb):
    v = values.astype(F32)
    yy = dot_split(jnp.concatenate([pp["b_o"], pp["bd_b"]], 0), xb, 1, 0)
    return head_sums(yy[:L] * v), head_sums(yy[L:] * v), dot_split(jnp.concatenate([we, wde], 0), xb, 1, 1)


def finish(ft, wts, pairs, row1, row2, colq, colqd, from_forward, from_backward, xf, xb, rate, scale):
    e, ed, f, fd, w, wd = wts
    g, gdot, pc = from_forward
    kk, kdot, pb = from_backward
    kap = jnp.sum(xb[:64] * xf[:64], axis=0, keepdims=True)
    kapd = jnp.sum(xb[64:] * xf[:64] + xb[:64] * xf[64:], axis=0, keepdims=True)
    both = head_sums(jnp.concatenate([jnp.broadcast_to(kap, (8, HP)), jnp.broadcast_to(kapd, (8, HP))], 0))
    kap, kapd = both[0:1], both[8:9]

    m = low_lanes()
    t1, t2, t3, t4 = pairs
    pair_c = t1 + pc[:L] + jnp.where(m, 0.0, roll64(t2 + pc[L:]))
    pair_b = t3 + pb[:L] + jnp.where(m, 0.0, roll64(t4 + pb[L:]))
    dact = jnp.where(m, pair_b, roll64(pair_c))
    dactd = jnp.where(m, roll64(pair_b), pair_c)
    dz = scale * (ft["first"] * dact)
    dzd = scale * (ft["second"] * ft["zd"] * dact + ft["first"] * dactd)

    delta, deltad, cum, cumd = ft["delta"], ft["deltad"], ft["cum"], ft["cumd"]
    colq, colqd = colq.T, colqd.T
    colqd = colqd - cumd * colq
    row1, row2 = row1[:, :H], row2[:, :H]
    row2 = row2 + cumd * row1
    wk = w * kk
    wkd = wd * kk + w * kdot
    dc = row1 - delta * colq + e * g - wk
    dcd = row2 - (deltad * colq + delta * colqd) + ed * g + e * gdot - wkd
    el, edl = e[L - 1 :, :], ed[L - 1 :, :]
    extra = el * kap + jnp.sum(wk, axis=0, keepdims=True)
    extrad = edl * kap + el * kapd + jnp.sum(wkd, axis=0, keepdims=True)
    ddelta = colq + f * kk - rate * (cumulate(dc, True) + extra)
    ddeltad = colqd + fd * kk + f * kdot - rate * (cumulate(dcd, True) + extrad)
    sq = ft["sq"]
    dq = scale * (sq * ddelta)
    dqd = scale * (sq * (1.0 - sq) * ft["qd"] * ddelta + sq * ddeltad)
    return dz, dzd, dq, dqd


def place():
    x = lax.axis_index("dp")
    s = lax.axis_index("seq")
    chip = s // 2
    return x, chip // NZ, lax.rem(chip, NZ), lax.rem(s, 2), chip


def device(x, y, z, k):
    return (x, (y * NZ + z) * 2 + k)


def remote(src, dst, send_sem, recv_sem, dev):
    return pltpu.make_async_remote_copy(
        src_ref=src, dst_ref=dst, send_sem=send_sem, recv_sem=recv_sem,
        device_id=dev, device_id_type=MESH,
    )


def arrived(dst, sem, dev):
    remote(dst, dst, sem, sem, dev).wait_recv()


def sent(src, sem, dev):
    remote(src, src, sem, sem, dev).wait_send()


def enter():
    x, y, z, k, chip = place()
    s = 2 * chip + k
    seq = CHIPS * 2
    partners = [device(x, y, z, 1 - k)]
    partners += [device(lax.rem(x + d, NX), y, z, k) for d in range(1, NX)]
    partners += [device(x, lax.rem(y + d, NY), z, k) for d in range(1, NY)]
    partners += [device(x, y, lax.rem(z + d, NZ), k) for d in range(1, NZ)]
    partners += [(x, lax.rem(s + 1, seq)), (x, lax.rem(s + seq - 1, seq))]
    barrier = pltpu.get_barrier_semaphore()
    for dev in partners:
        pl.semaphore_signal(barrier, inc=1, device_id=dev, device_id_type=MESH)
    return lambda: pl.semaphore_wait(barrier, len(partners))


def gather(wbuf, ext, ext_t, proj, tok_ref, s_send, s_halo, s_z, s_slab, s_swap):
    x, y, z, k, chip = place()
    s = 2 * chip + k
    mate = device(x, y, z, 1 - k)
    own = wbuf.at[x, y, z, k]
    for d in range(1, NZ):
        remote(own, own, s_send.at[0], s_z, device(x, y, lax.rem(z + d, NZ), k)).start()
    halo = remote(
        tok_ref.at[pl.ds(L - HALO, HALO)], ext.at[pl.ds(L, HALO)], s_send.at[4], s_halo,
        (x, lax.rem(s + 1, 2 * CHIPS)),
    )
    halo.start()
    arrived(wbuf.at[x, y, pl.ds(0, NZ - 1), k], s_z, mate)

    def slab_copy(sx, sy, tx, ty, sem):
        ref = wbuf.at[sx, sy, :, k]
        return remote(ref, ref, s_send.at[sem], s_slab.at[sx * NY + sy], device(tx, ty, z, k))

    def swap(sx, sy, kk):
        ref = wbuf.at[sx, sy, :, kk]
        return remote(ref, ref, s_send.at[3], s_swap.at[sx * NY + sy], mate)

    def near(d):
        return lax.rem(x + d * k, NX), lax.rem(y + d * (1 - k), NY)

    def far(d):
        return lax.rem(x + d * (1 - k), NX), lax.rem(y + d * k, NY)

    for d in range(1, 4):
        slab_copy(x, y, *near(d), 1).start()
    for d in range(1, 4):
        slab_copy(x, y, *far(d), 2).start()
    swap(x, y, k).start()
    for d in range(1, 4):
        sx, sy = near(d)
        slab_copy(sx, sy, x, y, 1).wait_recv()
        for t in range(1, 4):
            slab_copy(sx, sy, *far(t), 2).start()
        swap(sx, sy, k).start()
    halo.wait_recv()

    @pl.when(s == 0)
    def _():
        ext[L : L + HALO, :] = jnp.zeros((HALO, ext.shape[1]), BF16)

    ext_t[:, L:] = ext[L:, :].T
    for e in range(4):
        for d in range(1, 4):
            fx, fy = far(d)
            sx = lax.rem(fx + e * k, NX)
            sy = lax.rem(fy + e * (1 - k), NY)
            slab_copy(sx, sy, x, y, 2).wait_recv()
            swap(sx, sy, k).start()
    depth = ext.shape[1] // NX
    total = jnp.zeros((L + HALO, WIDE), F32)
    for d in range(NX):
        sx = lax.rem(x + d, NX)
        for sy in range(NY):
            swap(sx, sy, 1 - k).wait_recv()
        at = pl.multiple_of(sx * depth, depth)
        weights = wbuf[sx].astype(F32).reshape(depth, WIDE).astype(BF16)
        total = total + dg(ext[0 : L + HALO, pl.ds(at, depth)], weights, 1, 0)
    proj[HALO:, :] = total[0:L]
    proj[0:HALO, :] = total[L:]

    def drain():
        sent(wbuf.at[0, 0, pl.ds(0, NZ - 1), 0], s_send.at[0], mate)
        sent(wbuf.at[0, pl.ds(0, NY - 1), :, 0], s_send.at[1], mate)
        sent(wbuf.at[pl.ds(0, NX - 1), :, :, 0], s_send.at[2], mate)
        sent(wbuf.at[:, :, :, 0], s_send.at[3], mate)
        halo.wait_send()

    return drain


class Half:
    def __init__(self, loc, part, snd, rcv, snd2, rcv2, other, st, rows, s_send, s_mate, s_one, s_two):
        self.loc, self.part, self.snd, self.rcv, self.snd2, self.rcv2 = loc, part, snd, rcv, snd2, rcv2
        self.other, self.st, self.rows = other, st, rows
        self.s_send, self.s_mate, self.s_one, self.s_two = s_send, s_mate, s_one, s_two
        self.x, self.y, self.z, self.k, self.chip = place()
        self.mate = device(self.x, self.y, self.z, 1 - self.k)
        self.first = self.k == 0

    def peer(self, d):
        c = lax.rem(self.chip + d, CHIPS)
        return c, (self.x, 2 * c + self.k)

    def to_mate(self):
        return remote(self.loc.at[1 - self.k], self.part, self.s_send.at[0], self.s_mate.at[0], self.mate)

    def start_one(self):
        piece = pl.ds(0, self.rows)
        for d in range(1, CHIPS):
            c, dev = self.peer(d)
            remote(self.snd.at[c, piece], self.rcv.at[self.chip, piece], self.s_send.at[1], self.s_one, dev).start()
        self.rcv[self.chip] = self.snd[self.chip]

    def start_two(self):
        for d in range(1, CHIPS):
            c, dev = self.peer(d)
            remote(self.snd2.at[c], self.rcv2.at[self.chip], self.s_send.at[2], self.s_two, dev).start()
        self.rcv2[self.chip] = self.snd2[self.chip]

    def wait_one(self):
        arrived(self.rcv.at[pl.ds(0, CHIPS - 1), pl.ds(0, self.rows)], self.s_one, self.mate)

    def wait_two(self):
        arrived(self.rcv2.at[pl.ds(0, CHIPS - 1)], self.s_two, self.mate)

    def back(self):
        return remote(self.other, self.st.at[self.k], self.s_send.at[3], self.s_mate.at[1], self.mate)

    def back_in(self):
        return remote(self.other, self.st.at[1 - self.k], self.s_send.at[3], self.s_mate.at[1], self.mate)

    def cores(self):
        own, other = self.loc[self.k], self.part[...]
        return jnp.where(self.first, own, other), jnp.where(self.first, other, own)

    def slices(self, s, t, rest):
        for j in range(CHIPS):
            rows = slice(8 * (j // 4), 8 * (j // 4) + 8)
            lanes = slice(128 * (j % 4), 128 * (j % 4) + 128)
            self.snd[j, 0:8] = s[rows, lanes]
            self.snd[j, 8:16] = t[rows, lanes]
            for i, row in enumerate(rest):
                self.snd[j, 16 + i : 17 + i] = row[:, lanes]

    def prefix(self, order, decays):
        s = t = jnp.zeros((8, 128), F32)
        for c in order:
            self.snd2[c, 0:8] = s
            self.snd2[c, 8:16] = t
            a, ad = decays[c, 16:17, :], decays[c, 17:18, :]
            s, t = a * s + self.rcv[c, 0:8], a * t + (ad * s + self.rcv[c, 8:16])

    def assemble(self, a, ad, base, base_first):
        for j in range(CHIPS):
            row = 8 * (j // 4)
            lanes = slice(128 * (j % 4), 128 * (j % 4) + 128)
            self.place_slice(row, lanes, j)
        s, t = self.other[0:64, :], self.other[64:128, :]
        next_s = a * s + base[0:64]
        next_t = a * t + ad * s + base[64:128]
        mine_is_base = self.first if base_first else jnp.logical_not(self.first)
        self.st[self.k, 0:64, :] = jnp.where(mine_is_base, s, next_s)
        self.st[self.k, 64:128, :] = jnp.where(mine_is_base, t, next_t)
        self.other[0:64, :] = jnp.where(mine_is_base, next_s, s)
        self.other[64:128, :] = jnp.where(mine_is_base, next_t, t)
        self.back().start()

    def place_slice(self, row, lanes, j):
        self.other[row : row + 8, lanes] = self.rcv2[j, 0:8]
        self.other[64 + row : 72 + row, lanes] = self.rcv2[j, 8:16]

    def drain(self):
        self.to_mate().wait_send()
        sent(self.snd.at[pl.ds(0, CHIPS - 1), pl.ds(0, self.rows)], self.s_send.at[1], self.mate)
        sent(self.snd2.at[pl.ds(0, CHIPS - 1)], self.s_send.at[2], self.mate)
        self.back().wait_send()


def reduce(dp, ext_t, full, g2, m01, m2, a0, a1, a2, r0, r1, r2, b0, b1, b2, q0, q1, q2, c0, c1, c2, p0, p1, p2,
           e2, f2, s_send, s_mate, s_a, s_b, s_c, s_e, out_ref):
    x, y, z, k, chip = place()
    mate = device(x, y, z, 1 - k)
    holder = lax.rem(z, 2) == k

    def x_to(d):
        return device(lax.rem(x + d, NX), y, z, k)

    def y_to(d):
        return device(x, lax.rem(y + d, NY), z, k)

    def z_to(d):
        return device(x, y, lax.rem(z + d, NZ), k)

    high, low = split(dp)
    low_half = iota((8, 128), 1) < 64
    block_rows = NY * NZ * 16

    def settle(i):
        xb = lax.rem(x + 1 + i, NX)
        arrived(m01.at[:, xb], s_mate.at[i], mate)
        a0[xb] = full[0, xb, :, :, k] + m01[0, xb]
        if i < NX - 1:
            remote(a0.at[xb], r0.at[i], s_send.at[2], s_a.at[0], x_to(1 + i)).start()
        a1[xb] = full[1, xb, :, :, k] + m01[1, xb]
        for d in range(1, NY):
            remote(a1.at[xb, lax.rem(y + d, NY)], r1.at[d - 1, xb], s_send.at[3], s_a.at[1], y_to(d)).start()
        arrived(m2.at[xb], s_mate.at[NX + i], mate)
        a2[xb] = g2[k, xb] + m2[xb]

    for i in range(NX):
        xb = lax.rem(x + 1 + i, NX)
        rows = ext_t[pl.ds(pl.multiple_of(xb * block_rows, block_rows), block_rows), :]
        part = dg(rows, high, 1, 0) + dg(rows, low, 1, 0)
        full[0, xb] = part[:, 0:128].reshape(NY, NZ, 2, 8, 128)
        full[1, xb] = part[:, 128:256].reshape(NY, NZ, 2, 8, 128)
        steps = part[:, 256:384].reshape(NY, NZ // 2, 2, 2, 8, 128)
        for zp in range(2):
            g2[zp, xb] = jnp.where(low_half, steps[:, :, zp, 0], steps[:, :, zp, 1])
        for tile in range(2):
            remote(full.at[tile, xb, :, :, 1 - k], m01.at[tile, xb], s_send.at[0], s_mate.at[i], mate).start()
        remote(g2.at[1 - k, xb], m2.at[xb], s_send.at[1], s_mate.at[NX + i], mate).start()
        if i > 0:
            settle(i - 1)
    settle(NX - 1)

    zsend = []
    for i in range(NZ // 2):
        target = 2 * i + k
        gap = lax.rem(z - target + NZ, NZ)
        zsend.append((target != z, remote(a2.at[:, :, i], r2.at[gap], s_send.at[4 + i], s_a.at[2], device(x, y, target, k))))
        pl.when(zsend[-1][0])(zsend[-1][1].start)

    arrived(r0, s_a.at[0], mate)
    b0[...] = (a0[x] + r0[0]) + (r0[1] + r0[2])
    for d in range(1, NY):
        remote(b0.at[lax.rem(y + d, NY)], q0.at[d - 1], s_send.at[8], s_b.at[0], y_to(d)).start()
    arrived(r1, s_a.at[1], mate)
    b1[...] = (a1[:, y] + r1[0]) + (r1[1] + r1[2])
    for d in range(1, NZ):
        remote(b1.at[:, lax.rem(z + d, NZ)], q1.at[d - 1], s_send.at[9], s_b.at[1], z_to(d)).start()

    @pl.when(holder)
    def _():
        arrived(r2.at[pl.ds(1, NZ - 1)], s_a.at[2], mate)
        total = a2[:, :, z // 2] + ((r2[1] + r2[2]) + (r2[3] + r2[4]))
        b2[...] = total + ((r2[5] + r2[6]) + r2[7])
        for d in range(1, NX):
            remote(b2.at[lax.rem(x + d, NX)], q2.at[d - 1], s_send.at[10], s_b.at[2], x_to(d)).start()

    arrived(q0, s_b.at[0], mate)
    c0[...] = (b0[y] + q0[0]) + (q0[1] + q0[2])
    for d in range(1, NZ):
        remote(c0.at[lax.rem(z + d, NZ)], p0.at[d - 1], s_send.at[11], s_c.at[0], z_to(d)).start()

    @pl.when(holder)
    def _():
        arrived(q2, s_b.at[2], mate)
        c2[...] = (b2[x] + q2[0]) + (q2[1] + q2[2])
        for d in range(1, NY):
            remote(c2.at[lax.rem(y + d, NY)], p2.at[d - 1], s_send.at[12], s_c.at[2], y_to(d)).start()

    arrived(q1, s_b.at[1], mate)
    c1[...] = b1[:, z] + ((q1[0] + q1[1]) + (q1[2] + q1[3])) + ((q1[4] + q1[5]) + q1[6])
    for d in range(1, NX):
        remote(c1.at[lax.rem(x + d, NX)], p1.at[d - 1], s_send.at[13], s_c.at[1], x_to(d)).start()
    last = remote(e2, f2, s_send.at[14], s_e, mate)

    @pl.when(holder)
    def _():
        arrived(p2, s_c.at[2], mate)
        e2[...] = (c2[y] + p2[0]) + (p2[1] + p2[2])
        last.start()

    sent(m01, s_send.at[0], mate)
    sent(m2, s_send.at[1], mate)
    sent(r0, s_send.at[2], mate)
    sent(r1, s_send.at[3], mate)
    for used, copy in zsend:
        pl.when(used)(copy.wait_send)
    sent(q0, s_send.at[8], mate)
    sent(q1, s_send.at[9], mate)
    arrived(p0, s_c.at[0], mate)
    out_ref[:, 0:128] = c0[z] + ((p0[0] + p0[1]) + (p0[2] + p0[3])) + ((p0[4] + p0[5]) + p0[6])
    arrived(p1, s_c.at[1], mate)
    out_ref[:, 128:256] = (c1[x] + p1[0]) + (p1[1] + p1[2])

    @pl.when(jnp.logical_not(holder))
    def _():
        last.wait_recv()
        e2[...] = f2[...]

    out_ref[:, 256:384] = jnp.where(k == 0, e2[...], roll64(e2[...]))
    sent(p0, s_send.at[11], mate)
    sent(p1, s_send.at[13], mate)

    @pl.when(holder)
    def _():
        sent(q2, s_send.at[10], mate)
        sent(p2, s_send.at[12], mate)
        last.wait_send()


def everything(scale, sw_hbm, sd_hbm, tw_hbm, td_hbm, tok_ref, v_hbm, u_hbm, conv_hbm, bias_hbm, rate_hbm,
               out_ref, v_ref, u_ref, sw_ref, sd_ref, tw_ref, td_ref, conv_ref, bias_ref, rate_ref, wbuf, ext, ext_t, proj,
               forward_scratch, backward_scratch, rows_ref, row1_ref, row2_ref, colq_ref, colqd_ref, zp_ref, reduce_scratch,
               s_in, gather_sems, forward_sems, backward_sems, reduce_sems):
    entered = enter()
    pairs = [
        (sw_hbm, sw_ref), (sd_hbm, sd_ref), (tw_hbm, tw_ref), (td_hbm, td_ref), (tok_ref, ext.at[pl.ds(0, L)]),
        (v_hbm, v_ref), (u_hbm, u_ref), (conv_hbm, conv_ref), (bias_hbm, bias_ref), (rate_hbm, rate_ref),
    ]
    local = [pltpu.make_async_copy(src, dst, s_in.at[i]) for i, (src, dst) in enumerate(pairs)]
    for c in local:
        c.start()
    x, y, z, k, _ = place()
    ext[L + HALO :, :] = jnp.zeros((ext.shape[0] - L - HALO, ext.shape[1]), BF16)
    for c in local[0:4]:
        c.wait()
    wbuf[x, y, z, k, :, 0:128] = sw_ref[...]
    wbuf[x, y, z, k, :, 128:256] = sd_ref[...]
    rows = sw_ref.shape[0]
    wbuf[x, y, z, k, :, 256:384] = jnp.concatenate(
        [tw_ref[...].astype(F32), td_ref[...].astype(F32), jnp.zeros((rows, 128 - 2 * H), F32)], 1
    ).astype(BF16)
    local[4].wait()
    ext_t[:, 0:L] = ext[0:L, :].T
    for c in local[5:]:
        c.wait()
    entered()
    drain_gather = gather(wbuf, ext, ext_t, proj, tok_ref, *gather_sems)

    rate = rate_ref[...]
    ft = features(lambda row, lane, lanes: proj[row : row + L, lane : lane + lanes], conv_ref[...], bias_ref[...], rate)
    wts = weights_of(ft)
    pp = pair_parts(ft)
    we, wde, es, eds, eu, edu = streams(wts, v_ref[...], u_ref[...])
    fw = Half(*forward_scratch, 18, *forward_sems)
    bw = Half(*backward_scratch, 16, *backward_sems)
    row = iota((8, HP), 0)
    dec = jnp.where(row == 0, es[L - 1 :, :], jnp.where(row == 1, eds[L - 1 :, :], 0.0))
    states = forward_states(pp, we, wde)
    for half in range(2):
        lanes = slice(HALF * half, HALF * half + HALF)
        fw.loc[half, 0:128, :] = states[:, lanes]
        fw.loc[half, 128:136, :] = dec[:, lanes]
    fw.to_mate().start()
    states = backward_states(pp, eu, edu)
    for half in range(2):
        bw.loc[half] = states[:, HALF * half : HALF * half + HALF]
    bw.to_mate().start()

    fw.to_mate().wait_recv()
    one0, one1 = fw.cores()
    a0, ad0 = one0[128:129], one0[129:130]
    a1, ad1 = one1[128:129], one1[129:130]
    fw.slices(
        a1 * one0[0:64] + one1[0:64],
        a1 * one0[64:128] + ad1 * one0[0:64] + one1[64:128],
        [a0 * a1, ad0 * a1 + a0 * ad1],
    )
    fw.start_one()
    bw.to_mate().wait_recv()
    one0, one1 = bw.cores()
    bw.slices(a0 * one1[0:64] + one0[0:64], a0 * one1[64:128] + ad0 * one1[0:64] + one0[64:128], [])
    bw.start_one()

    def tile(ref):
        return lambda i: ref[:, pl.ds(pl.multiple_of(i * 128, 128), 128)]

    g, gd = intra_setup(ft, pp, rows_ref, row1_ref, row2_ref)
    zero = jnp.zeros((L, L), F32)

    def block_terms(first, last, carry):
        return intra(
            ft, g, gd, tile(v_ref), tile(u_ref), rows_ref, row1_ref, row2_ref, colq_ref, colqd_ref, first, last, carry
        )

    carry = block_terms(0, 6, (zero, zero))
    fw.wait_one()
    fw.prefix(range(CHIPS), fw.rcv)
    fw.start_two()
    carry = block_terms(6, 8, carry)
    bw.wait_one()
    bw.prefix(range(CHIPS - 1, -1, -1), fw.rcv)
    bw.start_two()
    pairs = intra_pairs(pp, *carry)
    fw.wait_two()
    fw.assemble(a0, ad0, fw.cores()[0], True)
    fw.back_in().wait_recv()
    xf = jnp.concatenate([fw.st[0], fw.st[1]], 1)
    from_forward = finish_forward(pp, eu, edu, u_ref[...], xf)
    bw.wait_two()
    bw.assemble(a1, ad1, bw.cores()[1], False)
    bw.back_in().wait_recv()
    xb = jnp.concatenate([bw.st[0], bw.st[1]], 1)
    from_backward = finish_backward(pp, we, wde, v_ref[...], xb)
    dz, dzd, dq, dqd = finish(
        ft, wts, pairs, row1_ref[...], row2_ref[...], colq_ref[...], colqd_ref[...],
        from_forward, from_backward, xf, xb, rate, scale,
    )
    zp_ref[...] = jnp.zeros(zp_ref.shape, F32)
    zp_ref[HALO : HALO + L, 0:128] = dz
    zp_ref[HALO : HALO + L, 128:256] = dzd
    conv = conv_ref[...]

    def spread(first_row, count, lanes):
        total = conv[0:1, :] * zp_ref[first_row + 3 : first_row + 3 + count, lanes]
        for tap in range(1, KCONV):
            total = total + conv[tap : tap + 1, :] * zp_ref[first_row + 3 - tap : first_row + 3 - tap + count, lanes]
        return total

    pad = jnp.zeros((128 - HALO, 128), F32)
    columns = []
    for half in range(2):
        lanes = slice(128 * half, 128 * half + 128)
        columns.append(jnp.concatenate([spread(HALO, L, lanes), spread(0, HALO, lanes), pad], 0))
    both = jnp.concatenate([dq, dqd, dq, dqd], 1)
    columns.append(jnp.concatenate([both, jnp.zeros((128, 128), F32)], 0))
    dp = jnp.concatenate(columns, 1)
    drain_gather()
    fw.drain()
    bw.drain()
    reduce(dp, ext_t, *reduce_scratch, *reduce_sems, out_ref)


def split_outputs(sums_ref, o_sel, o_step, o_selh, o_steph):
    o_sel[...] = sums_ref[:, 0:128]
    o_selh[...] = sums_ref[:, 128:256]
    o_step[...] = sums_ref[:, 256 : 256 + H]
    o_steph[...] = sums_ref[:, 256 + H : 256 + 2 * H]


def vmem(shape, dtype=F32):
    return pltpu.VMEM(shape, dtype)


def dma(*shape):
    return pltpu.SemaphoreType.DMA(shape)


def body(tokens, values, cotangent, sel_weight, step_weight, sel_dir, step_dir, conv_weight, step_bias, decay_rate):
    own_tokens, v, u = tokens[0], values[0], cotangent[0]
    depth = own_tokens.shape[1]
    rows = sel_weight.shape[0]
    scale = 1.0 / math.sqrt(NX * CHIPS * 2 * L)
    spec = pl.BlockSpec(memory_space=pltpu.VMEM)
    hbm = pl.BlockSpec(memory_space=pl.ANY)
    tiles = NX * NY * NZ
    reduce_scratch = (
        [vmem((2, NX, NY, NZ, 2, 8, 128)), vmem((2, NX, NY, NZ // 2, 8, 128)),
         vmem((2, NX, NY, NZ, 8, 128)), vmem((NX, NY, NZ // 2, 8, 128))]
        + [vmem((NX, NY, NZ, 8, 128))] * 2 + [vmem((NX, NY, NZ // 2, 8, 128))]
        + [vmem((3, NY, NZ, 8, 128)), vmem((3, NX, NZ, 8, 128)), vmem((NZ, NX, NY, 8, 128))]
        + [vmem((NY, NZ, 8, 128)), vmem((NX, NZ, 8, 128)), vmem((NX, NY, 8, 128))]
        + [vmem((3, NZ, 8, 128)), vmem((7, NX, 8, 128)), vmem((3, NY, 8, 128))]
        + [vmem((NZ, 8, 128)), vmem((NX, 8, 128)), vmem((NY, 8, 128))]
        + [vmem((7, 8, 128)), vmem((3, 8, 128)), vmem((3, 8, 128))]
        + [vmem((8, 128)), vmem((8, 128))]
    )

    def scan_scratch(piece):
        return [vmem((CHIPS, piece, 128))] * 2 + [vmem((CHIPS, 16, 128))] * 2 + [vmem((128, HALF)), vmem((2, 128, HALF))]

    scratch = [
        vmem((L, HP), BF16), vmem((L, HP), BF16),
        vmem((rows, 128), BF16), vmem((rows, 128), BF16), vmem((rows, H), BF16), vmem((rows, H), BF16),
        vmem((KCONV, 128)), vmem((1, H)), vmem((1, H)),
        vmem((NX, NY, NZ, 2, rows, WIDE), BF16),
        vmem((2 * L, depth), BF16), vmem((depth, 2 * L), BF16), vmem((HALO + L, WIDE)),
        [vmem((2, 136, HALF)), vmem((136, HALF))] + scan_scratch(24),
        [vmem((2, 128, HALF)), vmem((128, HALF))] + scan_scratch(16),
        vmem((3 * H, L)), vmem((L, L)), vmem((L, L)), vmem((H, L)), vmem((H, L)), vmem((HALO + L + 8, 256)),
        reduce_scratch,
        dma(10),
        [dma(5), dma(), dma(), dma(NX * NY), dma(NX * NY)],
        [dma(4), dma(2), dma(), dma()],
        [dma(4), dma(2), dma(), dma()],
        [dma(15), dma(2 * NX), dma(3), dma(3), dma(3), dma()],
    ]
    sums = pl.pallas_call(
        functools.partial(everything, scale),
        out_shape=jax.ShapeDtypeStruct((rows, WIDE), F32),
        in_specs=[hbm] * 10,
        out_specs=spec,
        scratch_shapes=scratch,
        compiler_params=pltpu.CompilerParams(
            vmem_limit_bytes=VMEM_LIMIT, collective_id=0, has_side_effects=True
        ),
    )(sel_weight, sel_dir, step_weight, step_dir, own_tokens, v, u, conv_weight, step_bias[None, :], decay_rate[None, :])
    return pl.pallas_call(
        split_outputs,
        out_shape=[
            jax.ShapeDtypeStruct((rows, 128), F32), jax.ShapeDtypeStruct((rows, H), F32),
            jax.ShapeDtypeStruct((rows, 128), F32), jax.ShapeDtypeStruct((rows, H), F32),
        ],
        in_specs=[spec],
        out_specs=[spec] * 4,
    )(sums)


def solution(mesh):
    shards = P(("dp", "seq"), None)
    stream = P("dp", "seq", None)
    return jax.shard_map(
        body,
        mesh=mesh,
        in_specs=(stream, stream, stream, shards, shards, shards, shards, P(), P(), P()),
        out_specs=(shards, shards, shards, shards),
        check_vma=False,
    )
```

```python
import functools
import math

import jax
import jax.numpy as jnp
from jax import lax
from jax.experimental import pallas as pl
from jax.experimental.pallas import tpu as pltpu
from jax.sharding import PartitionSpec as P

N = 64
P_SIZE = 32
H = 32
KCONV = 4
L = 128
HALO = 16
HP = H * P_SIZE
HALF = HP // 2
WIDE = 384
NX, NY, NZ = 4, 4, 8
CHIPS = NY * NZ
MESH = pl.DeviceIdType.MESH
F32 = jnp.float32
BF16 = jnp.bfloat16
VMEM_LIMIT = 56 * 1024 * 1024


def roll64(x):
    return pltpu.roll(x, 64, 1)


def split(x):
    high = x.astype(BF16)
    low = (x - high.astype(F32)).astype(BF16)
    return high, low


def split3(x):
    high = x.astype(BF16)
    rest = x - high.astype(F32)
    mid = rest.astype(BF16)
    low = (rest - mid.astype(F32)).astype(BF16)
    return high, mid, low


def dg(a, b, ca, cb):
    return lax.dot_general(a, b, (((ca,), (cb,)), ((), ())), preferred_element_type=F32)


def dot_split(a, b, ca, cb):
    ah, al = split(a)
    bh, bl = split(b)
    return dg(ah, bh, ca, cb) + (dg(ah, bl, ca, cb) + dg(al, bh, ca, cb))


def dot_left(a, b, ca, cb):
    ah, al = split(a)
    return dg(ah, b, ca, cb) + dg(al, b, ca, cb)


def iota(shape, dim):
    return lax.broadcasted_iota(jnp.int32, shape, dim)


def low_lanes():
    return iota((L, 128), 1) < 64


def head_spread():
    return (iota((H, HP), 0) == iota((H, HP), 1) // P_SIZE).astype(F32).astype(BF16)


def triangle(reverse):
    row, column = iota((L, L), 0), iota((L, L), 1)
    keep = (column >= row) if reverse else (row >= column)
    return keep.astype(F32).astype(BF16)


def cumulate(x, reverse):
    tri = triangle(reverse)
    a, b, c = split3(x)
    return dg(tri, a, 1, 0) + (dg(tri, b, 1, 0) + dg(tri, c, 1, 0))


def features(proj, conv2, bias, rate):
    z = jnp.zeros((L, 128), F32)
    zd = jnp.zeros((L, 128), F32)
    for k in range(KCONV):
        rows = HALO - (KCONV - 1) + k
        z = z + conv2[k : k + 1, :128] * proj(rows, 0, 128)
        zd = zd + conv2[k : k + 1, :128] * proj(rows, 128, 128)
    sg = jax.nn.sigmoid(z)
    act = z * sg
    first = sg * (1.0 + z * (1.0 - sg))
    second = sg * (1.0 - sg) * (2.0 + z * (1.0 - 2.0 * sg))
    actd = first * zd
    steps = proj(HALO, 256, 128)
    q = steps[:, :H] + bias
    qd = steps[:, H : 2 * H]
    delta = jnp.maximum(q, 0.0) + jnp.log1p(jnp.exp(-jnp.abs(q)))
    sq = jax.nn.sigmoid(q)
    deltad = sq * qd
    cum = cumulate(-(delta * rate), False)
    cumd = cumulate(-(deltad * rate), False)
    return dict(
        zd=zd, act=act, actd=actd, first=first, second=second,
        qd=qd, sq=sq, delta=delta, deltad=deltad, cum=cum, cumd=cumd,
    )


def weights_of(ft):
    cum, cumd = ft["cum"], ft["cumd"]
    last, lastd = cum[L - 1 :, :], cumd[L - 1 :, :]
    e = jnp.exp(cum)
    ed = e * cumd
    f = jnp.exp(last - cum)
    fd = f * (lastd - cumd)
    w = f * ft["delta"]
    wd = fd * ft["delta"] + f * ft["deltad"]
    return e, ed, f, fd, w, wd


def pair_parts(ft):
    act, actd = ft["act"], ft["actd"]
    actr, actdr = roll64(act), roll64(actd)
    m = low_lanes()
    return dict(
        b_bd=jnp.where(m, act, actdr),
        o_b=jnp.where(m, 0.0, actr),
        c_cd=jnp.where(m, actr, actd),
        o_c=jnp.where(m, 0.0, act),
        b_o=jnp.where(m, act, 0.0),
        bd_b=jnp.where(m, actd, actr),
        c_o=jnp.where(m, actr, 0.0),
        cd_c=jnp.where(m, actdr, act),
        b_c=act,
        c_b=actr,
    )


def spread_rows(rows):
    return dot_left(rows, head_spread(), 1, 0)


def streams(wts, values, cotangent):
    e, ed, _, _, w, wd = wts
    v = values.astype(F32)
    u = cotangent.astype(F32)
    we = spread_rows(w) * v
    wde = spread_rows(wd) * v
    es = spread_rows(e)
    eds = spread_rows(ed)
    return we, wde, es, eds, es * u, eds * u


def forward_states(pp, we, wde):
    left = jnp.concatenate([pp["b_bd"], pp["o_b"]], 0)
    return dot_split(left, jnp.concatenate([we, wde], 0), 0, 0)


def backward_states(pp, eu, edu):
    left = jnp.concatenate([pp["c_cd"], pp["o_c"]], 0)
    return dot_split(left, jnp.concatenate([eu, edu], 0), 0, 0)


def intra_setup(ft, pp, rows_ref, row1_ref, row2_ref):
    g = dot_split(pp["c_o"], pp["b_c"], 1, 1)
    gd = dot_split(pp["cd_c"], pp["b_bd"], 1, 1)
    eta = ft["deltad"] - ft["delta"] * ft["cumd"]
    rows_ref[0:H, :] = ft["cum"].T
    rows_ref[H : 2 * H, :] = ft["delta"].T
    rows_ref[2 * H : 3 * H, :] = eta.T
    row1_ref[...] = jnp.zeros((L, L), F32)
    row2_ref[...] = jnp.zeros((L, L), F32)
    return g, gd


def intra(ft, g, gd, v_of, u_of, rows_ref, row1_ref, row2_ref, colq_ref, colqd_ref, first, last, carry):
    parts = split3(ft["cum"])
    partsd = split(ft["cumd"])
    row, lane = iota((L, L), 0), iota((L, L), 1)
    causal = row >= lane

    def one(i, carry):
        dgm, dgd = carry
        pick = (iota((H, 512), 0) == (4 * i + iota((H, 512), 1) // 128)).astype(F32).astype(BF16)
        ct4 = dg(parts[0], pick, 1, 0) + (dg(parts[1], pick, 1, 0) + dg(parts[2], pick, 1, 0))
        cd4 = dg(partsd[0], pick, 1, 0) + dg(partsd[1], pick, 1, 0)
        v_tile, u_tile = v_of(i), u_of(i)
        row1, row2 = row1_ref[...], row2_ref[...]
        for j in range(4):
            h = 4 * i + j
            mask = (iota((L, 128), 1) // P_SIZE == j).astype(F32)
            w = dg((u_tile.astype(F32) * mask).astype(BF16), v_tile, 1, 1)
            ct = ct4[:, 128 * j : 128 * j + 128]
            cd = cd4[:, 128 * j : 128 * j + 128]
            cs = rows_ref[pl.ds(h, 1), :]
            ds = rows_ref[pl.ds(H + h, 1), :]
            et = rows_ref[pl.ds(2 * H + h, 1), :]
            x = jnp.exp(jnp.where(causal, ct - cs, -1e30)) * w
            xd = x * ds
            dgm = dgm + xd
            dgd = dgd + (x * et + cd * xd)
            q = x * g
            xgd = x * gd
            colq_ref[pl.ds(h, 1), :] = jnp.sum(q, axis=0, keepdims=True)
            colqd_ref[pl.ds(h, 1), :] = jnp.sum(xgd + q * cd, axis=0, keepdims=True)
            r1 = jnp.sum(q * ds, axis=1, keepdims=True)
            r2 = jnp.sum(xgd * ds + q * et, axis=1, keepdims=True)
            here = lane == h
            row1 = jnp.where(here, r1, row1)
            row2 = jnp.where(here, r2, row2)
        row1_ref[...] = row1
        row2_ref[...] = row2
        return dgm, dgd

    return lax.fori_loop(first, last, one, carry)


def intra_pairs(pp, dgm, dgd):
    return (
        dot_split(dgm, pp["b_bd"], 1, 0),
        dot_split(dgd, pp["b_c"], 1, 0),
        dot_split(dgm, pp["c_cd"], 0, 0),
        dot_split(dgd, pp["c_b"], 0, 0),
    )


def head_sums(x):
    return dot_left(x, head_spread(), 1, 1)


def finish_forward(pp, eu, edu, cotangent, xf):
    u = cotangent.astype(F32)
    zz = dot_split(jnp.concatenate([pp["c_o"], pp["cd_c"]], 0), xf, 1, 0)
    return head_sums(zz[:L] * u), head_sums(zz[L:] * u), dot_split(jnp.concatenate([eu, edu], 0), xf, 1, 1)


def finish_backward(pp, we, wde, values, xb):
    v = values.astype(F32)
    yy = dot_split(jnp.concatenate([pp["b_o"], pp["bd_b"]], 0), xb, 1, 0)
    return head_sums(yy[:L] * v), head_sums(yy[L:] * v), dot_split(jnp.concatenate([we, wde], 0), xb, 1, 1)


def finish(ft, wts, pairs, row1, row2, colq, colqd, from_forward, from_backward, xf, xb, rate, scale):
    e, ed, f, fd, w, wd = wts
    g, gdot, pc = from_forward
    kk, kdot, pb = from_backward
    kap = jnp.sum(xb[:64] * xf[:64], axis=0, keepdims=True)
    kapd = jnp.sum(xb[64:] * xf[:64] + xb[:64] * xf[64:], axis=0, keepdims=True)
    both = head_sums(jnp.concatenate([jnp.broadcast_to(kap, (8, HP)), jnp.broadcast_to(kapd, (8, HP))], 0))
    kap, kapd = both[0:1], both[8:9]

    m = low_lanes()
    t1, t2, t3, t4 = pairs
    pair_c = t1 + pc[:L] + jnp.where(m, 0.0, roll64(t2 + pc[L:]))
    pair_b = t3 + pb[:L] + jnp.where(m, 0.0, roll64(t4 + pb[L:]))
    dact = jnp.where(m, pair_b, roll64(pair_c))
    dactd = jnp.where(m, roll64(pair_b), pair_c)
    dz = scale * (ft["first"] * dact)
    dzd = scale * (ft["second"] * ft["zd"] * dact + ft["first"] * dactd)

    delta, deltad, cum, cumd = ft["delta"], ft["deltad"], ft["cum"], ft["cumd"]
    colq, colqd = colq.T, colqd.T
    colqd = colqd - cumd * colq
    row1, row2 = row1[:, :H], row2[:, :H]
    row2 = row2 + cumd * row1
    wk = w * kk
    wkd = wd * kk + w * kdot
    dc = row1 - delta * colq + e * g - wk
    dcd = row2 - (deltad * colq + delta * colqd) + ed * g + e * gdot - wkd
    el, edl = e[L - 1 :, :], ed[L - 1 :, :]
    extra = el * kap + jnp.sum(wk, axis=0, keepdims=True)
    extrad = edl * kap + el * kapd + jnp.sum(wkd, axis=0, keepdims=True)
    ddelta = colq + f * kk - rate * (cumulate(dc, True) + extra)
    ddeltad = colqd + fd * kk + f * kdot - rate * (cumulate(dcd, True) + extrad)
    sq = ft["sq"]
    dq = scale * (sq * ddelta)
    dqd = scale * (sq * (1.0 - sq) * ft["qd"] * ddelta + sq * ddeltad)
    return dz, dzd, dq, dqd


def place():
    x = lax.axis_index("dp")
    s = lax.axis_index("seq")
    chip = s // 2
    return x, chip // NZ, lax.rem(chip, NZ), lax.rem(s, 2), chip


def device(x, y, z, k):
    return (x, (y * NZ + z) * 2 + k)


def remote(src, dst, send_sem, recv_sem, dev):
    return pltpu.make_async_remote_copy(
        src_ref=src, dst_ref=dst, send_sem=send_sem, recv_sem=recv_sem,
        device_id=dev, device_id_type=MESH,
    )


def arrived(dst, sem, dev):
    remote(dst, dst, sem, sem, dev).wait_recv()


def sent(src, sem, dev):
    remote(src, src, sem, sem, dev).wait_send()


FAR4 = (2, 1, 3)
FAR8 = (4, 3, 5, 2, 6, 1, 7)


def far_first():
    offsets = [(dy, dz) for dy in range(NY) for dz in range(NZ) if dy or dz]
    return sorted(offsets, key=lambda o: -(min(o[0], NY - o[0]) + min(o[1], NZ - o[1])))


def enter():
    x, y, z, k, chip = place()
    s = 2 * chip + k
    seq = CHIPS * 2
    partners = [device(x, y, lax.rem(z + d, NZ), k) for d in FAR8]
    partners += [device(lax.rem(x + d, NX), y, z, k) for d in FAR4]
    partners += [device(x, lax.rem(y + d, NY), z, k) for d in FAR4]
    partners += [(x, lax.rem(s + 1, seq)), (x, lax.rem(s + seq - 1, seq)), device(x, y, z, 1 - k)]
    barrier = pltpu.get_barrier_semaphore()
    for dev in partners:
        pl.semaphore_signal(barrier, inc=1, device_id=dev, device_id_type=MESH)
    return lambda: pl.semaphore_wait(barrier, len(partners))


def gather(wbuf, ext, ext_t, proj, tok_ref, s_send, s_halo, s_z, s_slab, s_swap):
    x, y, z, k, chip = place()
    s = 2 * chip + k
    mate = device(x, y, z, 1 - k)
    own = wbuf.at[x, y, z, k]
    for d in FAR8:
        remote(own, own, s_send.at[0], s_z, device(x, y, lax.rem(z + d, NZ), k)).start()
    halo = remote(
        tok_ref.at[pl.ds(L - HALO, HALO)], ext.at[pl.ds(L, HALO)], s_send.at[4], s_halo,
        (x, lax.rem(s + 1, 2 * CHIPS)),
    )
    halo.start()
    arrived(wbuf.at[x, y, pl.ds(0, NZ - 1), k], s_z, mate)

    def slab_copy(sx, sy, tx, ty, sem):
        ref = wbuf.at[sx, sy, :, k]
        return remote(ref, ref, s_send.at[sem], s_slab.at[sx * NY + sy], device(tx, ty, z, k))

    def swap(sx, sy, kk):
        ref = wbuf.at[sx, sy, :, kk]
        return remote(ref, ref, s_send.at[3], s_swap.at[sx * NY + sy], mate)

    def near(d):
        return lax.rem(x + d * k, NX), lax.rem(y + d * (1 - k), NY)

    def far(d):
        return lax.rem(x + d * (1 - k), NX), lax.rem(y + d * k, NY)

    for d in FAR4:
        slab_copy(x, y, *near(d), 1).start()
    for d in FAR4:
        slab_copy(x, y, *far(d), 2).start()
    swap(x, y, k).start()
    for d in (1, 3, 2):
        sx, sy = near(d)
        slab_copy(sx, sy, x, y, 1).wait_recv()
        for t in FAR4:
            slab_copy(sx, sy, *far(t), 2).start()
        swap(sx, sy, k).start()
    halo.wait_recv()

    @pl.when(s == 0)
    def _():
        ext[L : L + HALO, :] = jnp.zeros((HALO, ext.shape[1]), BF16)

    ext_t[:, L:] = ext[L:, :].T
    for e in (0, 1, 3, 2):
        for d in (1, 3, 2):
            fx, fy = far(d)
            sx = lax.rem(fx + e * k, NX)
            sy = lax.rem(fy + e * (1 - k), NY)
            slab_copy(sx, sy, x, y, 2).wait_recv()
            swap(sx, sy, k).start()
    depth = ext.shape[1] // NX
    total = jnp.zeros((L + HALO, WIDE), F32)
    for d in range(NX):
        sx = lax.rem(x + d, NX)
        for sy in range(NY):
            swap(sx, sy, 1 - k).wait_recv()
        at = pl.multiple_of(sx * depth, depth)
        weights = wbuf[sx].astype(F32).reshape(depth, WIDE).astype(BF16)
        total = total + dg(ext[0 : L + HALO, pl.ds(at, depth)], weights, 1, 0)
    proj[HALO:, :] = total[0:L]
    proj[0:HALO, :] = total[L:]

    def drain():
        sent(wbuf.at[0, 0, pl.ds(0, NZ - 1), 0], s_send.at[0], mate)
        sent(wbuf.at[0, pl.ds(0, NY - 1), :, 0], s_send.at[1], mate)
        sent(wbuf.at[pl.ds(0, NX - 1), :, :, 0], s_send.at[2], mate)
        sent(wbuf.at[:, :, :, 0], s_send.at[3], mate)
        halo.wait_send()

    return drain


class Half:
    def __init__(self, loc, part, snd, rcv, snd2, rcv2, other, st, rows, s_send, s_mate, s_one, s_two):
        self.loc, self.part, self.snd, self.rcv, self.snd2, self.rcv2 = loc, part, snd, rcv, snd2, rcv2
        self.other, self.st, self.rows = other, st, rows
        self.s_send, self.s_mate, self.s_one, self.s_two = s_send, s_mate, s_one, s_two
        self.x, self.y, self.z, self.k, self.chip = place()
        self.mate = device(self.x, self.y, self.z, 1 - self.k)
        self.first = self.k == 0

    def peer(self, offset):
        c = lax.rem(self.y + offset[0], NY) * NZ + lax.rem(self.z + offset[1], NZ)
        return c, (self.x, 2 * c + self.k)

    def to_mate(self):
        return remote(self.loc.at[1 - self.k], self.part, self.s_send.at[0], self.s_mate.at[0], self.mate)

    def start_one(self):
        piece = pl.ds(0, self.rows)
        for offset in far_first():
            c, dev = self.peer(offset)
            remote(self.snd.at[c, piece], self.rcv.at[self.chip, piece], self.s_send.at[1], self.s_one, dev).start()
        self.rcv[self.chip] = self.snd[self.chip]

    def start_two(self):
        for offset in far_first():
            c, dev = self.peer(offset)
            remote(self.snd2.at[c], self.rcv2.at[self.chip], self.s_send.at[2], self.s_two, dev).start()
        self.rcv2[self.chip] = self.snd2[self.chip]

    def wait_one(self):
        arrived(self.rcv.at[pl.ds(0, CHIPS - 1), pl.ds(0, self.rows)], self.s_one, self.mate)

    def wait_two(self):
        arrived(self.rcv2.at[pl.ds(0, CHIPS - 1)], self.s_two, self.mate)

    def back(self):
        return remote(self.other, self.st.at[self.k], self.s_send.at[3], self.s_mate.at[1], self.mate)

    def back_in(self):
        return remote(self.other, self.st.at[1 - self.k], self.s_send.at[3], self.s_mate.at[1], self.mate)

    def cores(self):
        own, other = self.loc[self.k], self.part[...]
        return jnp.where(self.first, own, other), jnp.where(self.first, other, own)

    def slices(self, s, t, rest):
        for j in range(CHIPS):
            rows = slice(8 * (j // 4), 8 * (j // 4) + 8)
            lanes = slice(128 * (j % 4), 128 * (j % 4) + 128)
            self.snd[j, 0:8] = s[rows, lanes]
            self.snd[j, 8:16] = t[rows, lanes]
            for i, row in enumerate(rest):
                self.snd[j, 16 + i : 17 + i] = row[:, lanes]

    def prefix(self, order, decays):
        s = t = jnp.zeros((8, 128), F32)
        for c in order:
            self.snd2[c, 0:8] = s
            self.snd2[c, 8:16] = t
            a, ad = decays[c, 16:17, :], decays[c, 17:18, :]
            s, t = a * s + self.rcv[c, 0:8], a * t + (ad * s + self.rcv[c, 8:16])

    def assemble(self, a, ad, base, base_first):
        for j in range(CHIPS):
            row = 8 * (j // 4)
            lanes = slice(128 * (j % 4), 128 * (j % 4) + 128)
            self.place_slice(row, lanes, j)
        s, t = self.other[0:64, :], self.other[64:128, :]
        next_s = a * s + base[0:64]
        next_t = a * t + ad * s + base[64:128]
        mine_is_base = self.first if base_first else jnp.logical_not(self.first)
        self.st[self.k, 0:64, :] = jnp.where(mine_is_base, s, next_s)
        self.st[self.k, 64:128, :] = jnp.where(mine_is_base, t, next_t)
        self.other[0:64, :] = jnp.where(mine_is_base, next_s, s)
        self.other[64:128, :] = jnp.where(mine_is_base, next_t, t)
        self.back().start()

    def place_slice(self, row, lanes, j):
        self.other[row : row + 8, lanes] = self.rcv2[j, 0:8]
        self.other[64 + row : 72 + row, lanes] = self.rcv2[j, 8:16]

    def drain(self):
        self.to_mate().wait_send()
        sent(self.snd.at[pl.ds(0, CHIPS - 1), pl.ds(0, self.rows)], self.s_send.at[1], self.mate)
        sent(self.snd2.at[pl.ds(0, CHIPS - 1)], self.s_send.at[2], self.mate)
        self.back().wait_send()


def reduce(dp, ext_t, full, g2, m01, m2, a0, a1, a2, r0, r1, r2, b0, b1, b2, q0, q1, q2, c0, c1, c2, p0, p1, p2,
           e2, f2, s_send, s_mate, s_a, s_b, s_c, s_e, out_ref):
    x, y, z, k, chip = place()
    mate = device(x, y, z, 1 - k)
    holder = lax.rem(z, 2) == k

    def x_to(d):
        return device(lax.rem(x + d, NX), y, z, k)

    def y_to(d):
        return device(x, lax.rem(y + d, NY), z, k)

    def z_to(d):
        return device(x, y, lax.rem(z + d, NZ), k)

    high, low = split(dp)
    low_half = iota((8, 128), 1) < 64
    block_rows = NY * NZ * 16

    order = FAR4 + (0,)

    def settle(i):
        xb = lax.rem(x + order[i], NX)
        arrived(m01.at[:, xb], s_mate.at[i], mate)
        a0[xb] = full[0, xb, :, :, k] + m01[0, xb]
        if i < NX - 1:
            remote(a0.at[xb], r0.at[i], s_send.at[2], s_a.at[0], x_to(order[i])).start()
        a1[xb] = full[1, xb, :, :, k] + m01[1, xb]
        for d in FAR4:
            remote(a1.at[xb, lax.rem(y + d, NY)], r1.at[d - 1, xb], s_send.at[3], s_a.at[1], y_to(d)).start()
        arrived(m2.at[xb], s_mate.at[NX + i], mate)
        a2[xb] = g2[k, xb] + m2[xb]

    for i in range(NX):
        xb = lax.rem(x + order[i], NX)
        rows = ext_t[pl.ds(pl.multiple_of(xb * block_rows, block_rows), block_rows), :]
        part = dg(rows, high, 1, 0) + dg(rows, low, 1, 0)
        full[0, xb] = part[:, 0:128].reshape(NY, NZ, 2, 8, 128)
        full[1, xb] = part[:, 128:256].reshape(NY, NZ, 2, 8, 128)
        steps = part[:, 256:384].reshape(NY, NZ // 2, 2, 2, 8, 128)
        for zp in range(2):
            g2[zp, xb] = jnp.where(low_half, steps[:, :, zp, 0], steps[:, :, zp, 1])
        for tile in range(2):
            remote(full.at[tile, xb, :, :, 1 - k], m01.at[tile, xb], s_send.at[0], s_mate.at[i], mate).start()
        remote(g2.at[1 - k, xb], m2.at[xb], s_send.at[1], s_mate.at[NX + i], mate).start()
        if i > 0:
            settle(i - 1)
    settle(NX - 1)

    zsend = []
    for i in range(NZ // 2):
        target = 2 * i + k
        gap = lax.rem(z - target + NZ, NZ)
        zsend.append((target != z, remote(a2.at[:, :, i], r2.at[gap], s_send.at[4 + i], s_a.at[2], device(x, y, target, k))))
        pl.when(zsend[-1][0])(zsend[-1][1].start)

    arrived(r0, s_a.at[0], mate)
    b0[...] = (a0[x] + r0[0]) + (r0[1] + r0[2])
    for d in FAR4:
        remote(b0.at[lax.rem(y + d, NY)], q0.at[d - 1], s_send.at[8], s_b.at[0], y_to(d)).start()
    arrived(r1, s_a.at[1], mate)
    b1[...] = (a1[:, y] + r1[0]) + (r1[1] + r1[2])
    for d in FAR8:
        remote(b1.at[:, lax.rem(z + d, NZ)], q1.at[d - 1], s_send.at[9], s_b.at[1], z_to(d)).start()

    @pl.when(holder)
    def _():
        arrived(r2.at[pl.ds(1, NZ - 1)], s_a.at[2], mate)
        total = a2[:, :, z // 2] + ((r2[1] + r2[2]) + (r2[3] + r2[4]))
        b2[...] = total + ((r2[5] + r2[6]) + r2[7])
        for d in FAR4:
            remote(b2.at[lax.rem(x + d, NX)], q2.at[d - 1], s_send.at[10], s_b.at[2], x_to(d)).start()

    arrived(q0, s_b.at[0], mate)
    c0[...] = (b0[y] + q0[0]) + (q0[1] + q0[2])
    for d in FAR8:
        remote(c0.at[lax.rem(z + d, NZ)], p0.at[d - 1], s_send.at[11], s_c.at[0], z_to(d)).start()

    @pl.when(holder)
    def _():
        arrived(q2, s_b.at[2], mate)
        c2[...] = (b2[x] + q2[0]) + (q2[1] + q2[2])
        for d in FAR4:
            remote(c2.at[lax.rem(y + d, NY)], p2.at[d - 1], s_send.at[12], s_c.at[2], y_to(d)).start()

    arrived(q1, s_b.at[1], mate)
    c1[...] = b1[:, z] + ((q1[0] + q1[1]) + (q1[2] + q1[3])) + ((q1[4] + q1[5]) + q1[6])
    for d in FAR4:
        remote(c1.at[lax.rem(x + d, NX)], p1.at[d - 1], s_send.at[13], s_c.at[1], x_to(d)).start()
    last = remote(e2, f2, s_send.at[14], s_e, mate)

    @pl.when(holder)
    def _():
        arrived(p2, s_c.at[2], mate)
        e2[...] = (c2[y] + p2[0]) + (p2[1] + p2[2])
        last.start()

    sent(m01, s_send.at[0], mate)
    sent(m2, s_send.at[1], mate)
    sent(r0, s_send.at[2], mate)
    sent(r1, s_send.at[3], mate)
    for used, copy in zsend:
        pl.when(used)(copy.wait_send)
    sent(q0, s_send.at[8], mate)
    sent(q1, s_send.at[9], mate)
    arrived(p0, s_c.at[0], mate)
    out_ref[:, 0:128] = c0[z] + ((p0[0] + p0[1]) + (p0[2] + p0[3])) + ((p0[4] + p0[5]) + p0[6])
    arrived(p1, s_c.at[1], mate)
    out_ref[:, 128:256] = (c1[x] + p1[0]) + (p1[1] + p1[2])

    @pl.when(jnp.logical_not(holder))
    def _():
        last.wait_recv()
        e2[...] = f2[...]

    out_ref[:, 256:384] = jnp.where(k == 0, e2[...], roll64(e2[...]))
    sent(p0, s_send.at[11], mate)
    sent(p1, s_send.at[13], mate)

    @pl.when(holder)
    def _():
        sent(q2, s_send.at[10], mate)
        sent(p2, s_send.at[12], mate)
        last.wait_send()


def everything(scale, sw_hbm, sd_hbm, tw_hbm, td_hbm, tok_ref, v_hbm, u_hbm, conv_hbm, bias_hbm, rate_hbm,
               out_ref, v_ref, u_ref, sw_ref, sd_ref, tw_ref, td_ref, conv_ref, bias_ref, rate_ref, wbuf, ext, ext_t, proj,
               forward_scratch, backward_scratch, rows_ref, row1_ref, row2_ref, colq_ref, colqd_ref, zp_ref, reduce_scratch,
               s_in, gather_sems, forward_sems, backward_sems, reduce_sems):
    entered = enter()
    pairs = [
        (sw_hbm, sw_ref), (sd_hbm, sd_ref), (tw_hbm, tw_ref), (td_hbm, td_ref), (tok_ref, ext.at[pl.ds(0, L)]),
        (v_hbm, v_ref), (u_hbm, u_ref), (conv_hbm, conv_ref), (bias_hbm, bias_ref), (rate_hbm, rate_ref),
    ]
    local = [pltpu.make_async_copy(src, dst, s_in.at[i]) for i, (src, dst) in enumerate(pairs)]
    for c in local:
        c.start()
    x, y, z, k, _ = place()
    ext[L + HALO :, :] = jnp.zeros((ext.shape[0] - L - HALO, ext.shape[1]), BF16)
    for c in local[0:4]:
        c.wait()
    wbuf[x, y, z, k, :, 0:128] = sw_ref[...]
    wbuf[x, y, z, k, :, 128:256] = sd_ref[...]
    rows = sw_ref.shape[0]
    wbuf[x, y, z, k, :, 256:384] = jnp.concatenate(
        [tw_ref[...].astype(F32), td_ref[...].astype(F32), jnp.zeros((rows, 128 - 2 * H), F32)], 1
    ).astype(BF16)
    local[4].wait()
    ext_t[:, 0:L] = ext[0:L, :].T
    for c in local[5:]:
        c.wait()
    entered()
    drain_gather = gather(wbuf, ext, ext_t, proj, tok_ref, *gather_sems)

    rate = rate_ref[...]
    ft = features(lambda row, lane, lanes: proj[row : row + L, lane : lane + lanes], conv_ref[...], bias_ref[...], rate)
    wts = weights_of(ft)
    pp = pair_parts(ft)
    we, wde, es, eds, eu, edu = streams(wts, v_ref[...], u_ref[...])
    fw = Half(*forward_scratch, 18, *forward_sems)
    bw = Half(*backward_scratch, 16, *backward_sems)
    row = iota((8, HP), 0)
    dec = jnp.where(row == 0, es[L - 1 :, :], jnp.where(row == 1, eds[L - 1 :, :], 0.0))
    states = forward_states(pp, we, wde)
    for half in range(2):
        lanes = slice(HALF * half, HALF * half + HALF)
        fw.loc[half, 0:128, :] = states[:, lanes]
        fw.loc[half, 128:136, :] = dec[:, lanes]
    fw.to_mate().start()
    states = backward_states(pp, eu, edu)
    for half in range(2):
        bw.loc[half] = states[:, HALF * half : HALF * half + HALF]
    bw.to_mate().start()

    fw.to_mate().wait_recv()
    one0, one1 = fw.cores()
    a0, ad0 = one0[128:129], one0[129:130]
    a1, ad1 = one1[128:129], one1[129:130]
    fw.slices(
        a1 * one0[0:64] + one1[0:64],
        a1 * one0[64:128] + ad1 * one0[0:64] + one1[64:128],
        [a0 * a1, ad0 * a1 + a0 * ad1],
    )
    fw.start_one()
    bw.to_mate().wait_recv()
    one0, one1 = bw.cores()
    bw.slices(a0 * one1[0:64] + one0[0:64], a0 * one1[64:128] + ad0 * one1[0:64] + one0[64:128], [])
    bw.start_one()

    def tile(ref):
        return lambda i: ref[:, pl.ds(pl.multiple_of(i * 128, 128), 128)]

    g, gd = intra_setup(ft, pp, rows_ref, row1_ref, row2_ref)
    zero = jnp.zeros((L, L), F32)

    def block_terms(first, last, carry):
        return intra(
            ft, g, gd, tile(v_ref), tile(u_ref), rows_ref, row1_ref, row2_ref, colq_ref, colqd_ref, first, last, carry
        )

    carry = block_terms(0, 6, (zero, zero))
    fw.wait_one()
    fw.prefix(range(CHIPS), fw.rcv)
    fw.start_two()
    carry = block_terms(6, 8, carry)
    bw.wait_one()
    bw.prefix(range(CHIPS - 1, -1, -1), fw.rcv)
    bw.start_two()
    pairs = intra_pairs(pp, *carry)
    fw.wait_two()
    fw.assemble(a0, ad0, fw.cores()[0], True)
    fw.back_in().wait_recv()
    xf = jnp.concatenate([fw.st[0], fw.st[1]], 1)
    from_forward = finish_forward(pp, eu, edu, u_ref[...], xf)
    bw.wait_two()
    bw.assemble(a1, ad1, bw.cores()[1], False)
    bw.back_in().wait_recv()
    xb = jnp.concatenate([bw.st[0], bw.st[1]], 1)
    from_backward = finish_backward(pp, we, wde, v_ref[...], xb)
    dz, dzd, dq, dqd = finish(
        ft, wts, pairs, row1_ref[...], row2_ref[...], colq_ref[...], colqd_ref[...],
        from_forward, from_backward, xf, xb, rate, scale,
    )
    zp_ref[...] = jnp.zeros(zp_ref.shape, F32)
    zp_ref[HALO : HALO + L, 0:128] = dz
    zp_ref[HALO : HALO + L, 128:256] = dzd
    conv = conv_ref[...]

    def spread(first_row, count, lanes):
        total = conv[0:1, :] * zp_ref[first_row + 3 : first_row + 3 + count, lanes]
        for tap in range(1, KCONV):
            total = total + conv[tap : tap + 1, :] * zp_ref[first_row + 3 - tap : first_row + 3 - tap + count, lanes]
        return total

    pad = jnp.zeros((128 - HALO, 128), F32)
    columns = []
    for half in range(2):
        lanes = slice(128 * half, 128 * half + 128)
        columns.append(jnp.concatenate([spread(HALO, L, lanes), spread(0, HALO, lanes), pad], 0))
    both = jnp.concatenate([dq, dqd, dq, dqd], 1)
    columns.append(jnp.concatenate([both, jnp.zeros((128, 128), F32)], 0))
    dp = jnp.concatenate(columns, 1)
    drain_gather()
    fw.drain()
    bw.drain()
    reduce(dp, ext_t, *reduce_scratch, *reduce_sems, out_ref)


def split_outputs(sums_ref, o_sel, o_step, o_selh, o_steph):
    o_sel[...] = sums_ref[:, 0:128]
    o_selh[...] = sums_ref[:, 128:256]
    o_step[...] = sums_ref[:, 256 : 256 + H]
    o_steph[...] = sums_ref[:, 256 + H : 256 + 2 * H]


def vmem(shape, dtype=F32):
    return pltpu.VMEM(shape, dtype)


def dma(*shape):
    return pltpu.SemaphoreType.DMA(shape)


def body(tokens, values, cotangent, sel_weight, step_weight, sel_dir, step_dir, conv_weight, step_bias, decay_rate):
    own_tokens, v, u = tokens[0], values[0], cotangent[0]
    depth = own_tokens.shape[1]
    rows = sel_weight.shape[0]
    scale = 1.0 / math.sqrt(NX * CHIPS * 2 * L)
    spec = pl.BlockSpec(memory_space=pltpu.VMEM)
    hbm = pl.BlockSpec(memory_space=pl.ANY)
    tiles = NX * NY * NZ
    reduce_scratch = (
        [vmem((2, NX, NY, NZ, 2, 8, 128)), vmem((2, NX, NY, NZ // 2, 8, 128)),
         vmem((2, NX, NY, NZ, 8, 128)), vmem((NX, NY, NZ // 2, 8, 128))]
        + [vmem((NX, NY, NZ, 8, 128))] * 2 + [vmem((NX, NY, NZ // 2, 8, 128))]
        + [vmem((3, NY, NZ, 8, 128)), vmem((3, NX, NZ, 8, 128)), vmem((NZ, NX, NY, 8, 128))]
        + [vmem((NY, NZ, 8, 128)), vmem((NX, NZ, 8, 128)), vmem((NX, NY, 8, 128))]
        + [vmem((3, NZ, 8, 128)), vmem((7, NX, 8, 128)), vmem((3, NY, 8, 128))]
        + [vmem((NZ, 8, 128)), vmem((NX, 8, 128)), vmem((NY, 8, 128))]
        + [vmem((7, 8, 128)), vmem((3, 8, 128)), vmem((3, 8, 128))]
        + [vmem((8, 128)), vmem((8, 128))]
    )

    def scan_scratch(piece):
        return [vmem((CHIPS, piece, 128))] * 2 + [vmem((CHIPS, 16, 128))] * 2 + [vmem((128, HALF)), vmem((2, 128, HALF))]

    scratch = [
        vmem((L, HP), BF16), vmem((L, HP), BF16),
        vmem((rows, 128), BF16), vmem((rows, 128), BF16), vmem((rows, H), BF16), vmem((rows, H), BF16),
        vmem((KCONV, 128)), vmem((1, H)), vmem((1, H)),
        vmem((NX, NY, NZ, 2, rows, WIDE), BF16),
        vmem((2 * L, depth), BF16), vmem((depth, 2 * L), BF16), vmem((HALO + L, WIDE)),
        [vmem((2, 136, HALF)), vmem((136, HALF))] + scan_scratch(24),
        [vmem((2, 128, HALF)), vmem((128, HALF))] + scan_scratch(16),
        vmem((3 * H, L)), vmem((L, L)), vmem((L, L)), vmem((H, L)), vmem((H, L)), vmem((HALO + L + 8, 256)),
        reduce_scratch,
        dma(10),
        [dma(5), dma(), dma(), dma(NX * NY), dma(NX * NY)],
        [dma(4), dma(2), dma(), dma()],
        [dma(4), dma(2), dma(), dma()],
        [dma(15), dma(2 * NX), dma(3), dma(3), dma(3), dma()],
    ]
    sums = pl.pallas_call(
        functools.partial(everything, scale),
        out_shape=jax.ShapeDtypeStruct((rows, WIDE), F32),
        in_specs=[hbm] * 10,
        out_specs=spec,
        scratch_shapes=scratch,
        compiler_params=pltpu.CompilerParams(
            vmem_limit_bytes=VMEM_LIMIT, collective_id=0, has_side_effects=True
        ),
    )(sel_weight, sel_dir, step_weight, step_dir, own_tokens, v, u, conv_weight, step_bias[None, :], decay_rate[None, :])
    return pl.pallas_call(
        split_outputs,
        out_shape=[
            jax.ShapeDtypeStruct((rows, 128), F32), jax.ShapeDtypeStruct((rows, H), F32),
            jax.ShapeDtypeStruct((rows, 128), F32), jax.ShapeDtypeStruct((rows, H), F32),
        ],
        in_specs=[spec],
        out_specs=[spec] * 4,
    )(sums)


def solution(mesh):
    shards = P(("dp", "seq"), None)
    stream = P("dp", "seq", None)
    return jax.shard_map(
        body,
        mesh=mesh,
        in_specs=(stream, stream, stream, shards, shards, shards, shards, P(), P(), P()),
        out_specs=(shards, shards, shards, shards),
        check_vma=False,
    )
```

```python
import functools
import math

import jax
import jax.numpy as jnp
from jax import lax
from jax.experimental import pallas as pl
from jax.experimental.pallas import tpu as pltpu
from jax.sharding import PartitionSpec as P

N = 64
P_SIZE = 32
H = 32
KCONV = 4
L = 128
HALO = 16
HP = H * P_SIZE
HALF = HP // 2
WIDE = 384
NX, NY, NZ = 4, 4, 8
CHIPS = NY * NZ
MESH = pl.DeviceIdType.MESH
F32 = jnp.float32
BF16 = jnp.bfloat16
VMEM_LIMIT = 56 * 1024 * 1024


def roll64(x):
    return pltpu.roll(x, 64, 1)


def split(x):
    high = x.astype(BF16)
    low = (x - high.astype(F32)).astype(BF16)
    return high, low


def split3(x):
    high = x.astype(BF16)
    rest = x - high.astype(F32)
    mid = rest.astype(BF16)
    low = (rest - mid.astype(F32)).astype(BF16)
    return high, mid, low


def dg(a, b, ca, cb):
    return lax.dot_general(a, b, (((ca,), (cb,)), ((), ())), preferred_element_type=F32)


def dot_split(a, b, ca, cb):
    ah, al = split(a)
    bh, bl = split(b)
    return dg(ah, bh, ca, cb) + (dg(ah, bl, ca, cb) + dg(al, bh, ca, cb))


def dot_left(a, b, ca, cb):
    ah, al = split(a)
    return dg(ah, b, ca, cb) + dg(al, b, ca, cb)


def iota(shape, dim):
    return lax.broadcasted_iota(jnp.int32, shape, dim)


def low_lanes():
    return iota((L, 128), 1) < 64


def head_spread():
    return (iota((H, HP), 0) == iota((H, HP), 1) // P_SIZE).astype(F32).astype(BF16)


def triangle(reverse):
    row, column = iota((L, L), 0), iota((L, L), 1)
    keep = (column >= row) if reverse else (row >= column)
    return keep.astype(F32).astype(BF16)


def cumulate(x, reverse):
    tri = triangle(reverse)
    a, b, c = split3(x)
    return dg(tri, a, 1, 0) + (dg(tri, b, 1, 0) + dg(tri, c, 1, 0))


def features(proj, conv2, bias, rate):
    z = jnp.zeros((L, 128), F32)
    zd = jnp.zeros((L, 128), F32)
    for k in range(KCONV):
        rows = HALO - (KCONV - 1) + k
        z = z + conv2[k : k + 1, :128] * proj(rows, 0, 128)
        zd = zd + conv2[k : k + 1, :128] * proj(rows, 128, 128)
    sg = jax.nn.sigmoid(z)
    act = z * sg
    first = sg * (1.0 + z * (1.0 - sg))
    second = sg * (1.0 - sg) * (2.0 + z * (1.0 - 2.0 * sg))
    actd = first * zd
    steps = proj(HALO, 256, 128)
    q = steps[:, :H] + bias
    qd = steps[:, H : 2 * H]
    delta = jnp.maximum(q, 0.0) + jnp.log1p(jnp.exp(-jnp.abs(q)))
    sq = jax.nn.sigmoid(q)
    deltad = sq * qd
    cum = cumulate(-(delta * rate), False)
    cumd = cumulate(-(deltad * rate), False)
    return dict(
        zd=zd, act=act, actd=actd, first=first, second=second,
        qd=qd, sq=sq, delta=delta, deltad=deltad, cum=cum, cumd=cumd,
    )


def weights_of(ft):
    cum, cumd = ft["cum"], ft["cumd"]
    last, lastd = cum[L - 1 :, :], cumd[L - 1 :, :]
    e = jnp.exp(cum)
    ed = e * cumd
    f = jnp.exp(last - cum)
    fd = f * (lastd - cumd)
    w = f * ft["delta"]
    wd = fd * ft["delta"] + f * ft["deltad"]
    return e, ed, f, fd, w, wd


def pair_parts(ft):
    act, actd = ft["act"], ft["actd"]
    actr, actdr = roll64(act), roll64(actd)
    m = low_lanes()
    return dict(
        b_bd=jnp.where(m, act, actdr),
        o_b=jnp.where(m, 0.0, actr),
        c_cd=jnp.where(m, actr, actd),
        o_c=jnp.where(m, 0.0, act),
        b_o=jnp.where(m, act, 0.0),
        bd_b=jnp.where(m, actd, actr),
        c_o=jnp.where(m, actr, 0.0),
        cd_c=jnp.where(m, actdr, act),
        b_c=act,
        c_b=actr,
    )


def spread_rows(rows):
    return dot_left(rows, head_spread(), 1, 0)


def streams(wts, values, cotangent):
    e, ed, _, _, w, wd = wts
    v = values.astype(F32)
    u = cotangent.astype(F32)
    we = spread_rows(w) * v
    wde = spread_rows(wd) * v
    es = spread_rows(e)
    eds = spread_rows(ed)
    return we, wde, es, eds, es * u, eds * u


def forward_states(pp, we, wde):
    left = jnp.concatenate([pp["b_bd"], pp["o_b"]], 0)
    return dot_split(left, jnp.concatenate([we, wde], 0), 0, 0)


def backward_states(pp, eu, edu):
    left = jnp.concatenate([pp["c_cd"], pp["o_c"]], 0)
    return dot_split(left, jnp.concatenate([eu, edu], 0), 0, 0)


def intra_setup(ft, pp, rows_ref, row1_ref, row2_ref):
    g = dot_split(pp["c_o"], pp["b_c"], 1, 1)
    gd = dot_split(pp["cd_c"], pp["b_bd"], 1, 1)
    eta = ft["deltad"] - ft["delta"] * ft["cumd"]
    rows_ref[0:H, :] = ft["cum"].T
    rows_ref[H : 2 * H, :] = ft["delta"].T
    rows_ref[2 * H : 3 * H, :] = eta.T
    row1_ref[...] = jnp.zeros((L, L), F32)
    row2_ref[...] = jnp.zeros((L, L), F32)
    return g, gd


def intra(ft, g, gd, v_of, u_of, rows_ref, row1_ref, row2_ref, colq_ref, colqd_ref, first, last, carry):
    parts = split3(ft["cum"])
    partsd = split(ft["cumd"])
    row, lane = iota((L, L), 0), iota((L, L), 1)
    causal = row >= lane

    def one(i, carry):
        dgm, dgd = carry
        pick = (iota((H, 512), 0) == (4 * i + iota((H, 512), 1) // 128)).astype(F32).astype(BF16)
        ct4 = dg(parts[0], pick, 1, 0) + (dg(parts[1], pick, 1, 0) + dg(parts[2], pick, 1, 0))
        cd4 = dg(partsd[0], pick, 1, 0) + dg(partsd[1], pick, 1, 0)
        v_tile, u_tile = v_of(i), u_of(i)
        row1, row2 = row1_ref[...], row2_ref[...]
        for j in range(4):
            h = 4 * i + j
            mask = (iota((L, 128), 1) // P_SIZE == j).astype(F32)
            w = dg((u_tile.astype(F32) * mask).astype(BF16), v_tile, 1, 1)
            ct = ct4[:, 128 * j : 128 * j + 128]
            cd = cd4[:, 128 * j : 128 * j + 128]
            cs = rows_ref[pl.ds(h, 1), :]
            ds = rows_ref[pl.ds(H + h, 1), :]
            et = rows_ref[pl.ds(2 * H + h, 1), :]
            x = jnp.exp(jnp.where(causal, ct - cs, -1e30)) * w
            xd = x * ds
            dgm = dgm + xd
            dgd = dgd + (x * et + cd * xd)
            q = x * g
            xgd = x * gd
            colq_ref[pl.ds(h, 1), :] = jnp.sum(q, axis=0, keepdims=True)
            colqd_ref[pl.ds(h, 1), :] = jnp.sum(xgd + q * cd, axis=0, keepdims=True)
            r1 = jnp.sum(q * ds, axis=1, keepdims=True)
            r2 = jnp.sum(xgd * ds + q * et, axis=1, keepdims=True)
            here = lane == h
            row1 = jnp.where(here, r1, row1)
            row2 = jnp.where(here, r2, row2)
        row1_ref[...] = row1
        row2_ref[...] = row2
        return dgm, dgd

    return lax.fori_loop(first, last, one, carry)


def intra_pairs(pp, dgm, dgd):
    return (
        dot_split(dgm, pp["b_bd"], 1, 0),
        dot_split(dgd, pp["b_c"], 1, 0),
        dot_split(dgm, pp["c_cd"], 0, 0),
        dot_split(dgd, pp["c_b"], 0, 0),
    )


def head_sums(x):
    return dot_left(x, head_spread(), 1, 1)


def finish_forward(pp, eu, edu, cotangent, xf):
    u = cotangent.astype(F32)
    zz = dot_split(jnp.concatenate([pp["c_o"], pp["cd_c"]], 0), xf, 1, 0)
    return head_sums(zz[:L] * u), head_sums(zz[L:] * u), dot_split(jnp.concatenate([eu, edu], 0), xf, 1, 1)


def finish_backward(pp, we, wde, values, xb):
    v = values.astype(F32)
    yy = dot_split(jnp.concatenate([pp["b_o"], pp["bd_b"]], 0), xb, 1, 0)
    return head_sums(yy[:L] * v), head_sums(yy[L:] * v), dot_split(jnp.concatenate([we, wde], 0), xb, 1, 1)


def finish(ft, wts, pairs, row1, row2, colq, colqd, from_forward, from_backward, xf, xb, rate, scale):
    e, ed, f, fd, w, wd = wts
    g, gdot, pc = from_forward
    kk, kdot, pb = from_backward
    kap = jnp.sum(xb[:64] * xf[:64], axis=0, keepdims=True)
    kapd = jnp.sum(xb[64:] * xf[:64] + xb[:64] * xf[64:], axis=0, keepdims=True)
    both = head_sums(jnp.concatenate([jnp.broadcast_to(kap, (8, HP)), jnp.broadcast_to(kapd, (8, HP))], 0))
    kap, kapd = both[0:1], both[8:9]

    m = low_lanes()
    t1, t2, t3, t4 = pairs
    pair_c = t1 + pc[:L] + jnp.where(m, 0.0, roll64(t2 + pc[L:]))
    pair_b = t3 + pb[:L] + jnp.where(m, 0.0, roll64(t4 + pb[L:]))
    dact = jnp.where(m, pair_b, roll64(pair_c))
    dactd = jnp.where(m, roll64(pair_b), pair_c)
    dz = scale * (ft["first"] * dact)
    dzd = scale * (ft["second"] * ft["zd"] * dact + ft["first"] * dactd)

    delta, deltad, cum, cumd = ft["delta"], ft["deltad"], ft["cum"], ft["cumd"]
    colq, colqd = colq.T, colqd.T
    colqd = colqd - cumd * colq
    row1, row2 = row1[:, :H], row2[:, :H]
    row2 = row2 + cumd * row1
    wk = w * kk
    wkd = wd * kk + w * kdot
    dc = row1 - delta * colq + e * g - wk
    dcd = row2 - (deltad * colq + delta * colqd) + ed * g + e * gdot - wkd
    el, edl = e[L - 1 :, :], ed[L - 1 :, :]
    extra = el * kap + jnp.sum(wk, axis=0, keepdims=True)
    extrad = edl * kap + el * kapd + jnp.sum(wkd, axis=0, keepdims=True)
    ddelta = colq + f * kk - rate * (cumulate(dc, True) + extra)
    ddeltad = colqd + fd * kk + f * kdot - rate * (cumulate(dcd, True) + extrad)
    sq = ft["sq"]
    dq = scale * (sq * ddelta)
    dqd = scale * (sq * (1.0 - sq) * ft["qd"] * ddelta + sq * ddeltad)
    return dz, dzd, dq, dqd


def place():
    x = lax.axis_index("dp")
    s = lax.axis_index("seq")
    chip = s // 2
    return x, chip // NZ, lax.rem(chip, NZ), lax.rem(s, 2), chip


def device(x, y, z, k):
    return (x, (y * NZ + z) * 2 + k)


def remote(src, dst, send_sem, recv_sem, dev):
    return pltpu.make_async_remote_copy(
        src_ref=src, dst_ref=dst, send_sem=send_sem, recv_sem=recv_sem,
        device_id=dev, device_id_type=MESH,
    )


def arrived(dst, sem, dev):
    remote(dst, dst, sem, sem, dev).wait_recv()


def sent(src, sem, dev):
    remote(src, src, sem, sem, dev).wait_send()


FAR4 = (2, 1, 3)
LANES = HALF // 128
FAR8 = (4, 3, 5, 2, 6, 1, 7)


def enter():
    x, y, z, k, chip = place()
    s = 2 * chip + k
    seq = CHIPS * 2
    partners = [device(x, y, lax.rem(z + d, NZ), k) for d in FAR8]
    partners += [device(lax.rem(x + d, NX), y, z, k) for d in FAR4]
    partners += [device(x, lax.rem(y + d, NY), z, k) for d in FAR4]
    partners += [(x, lax.rem(s + 1, seq)), (x, lax.rem(s + seq - 1, seq)), device(x, y, z, 1 - k)]
    barrier = pltpu.get_barrier_semaphore()
    for dev in partners:
        pl.semaphore_signal(barrier, inc=1, device_id=dev, device_id_type=MESH)
    return lambda: pl.semaphore_wait(barrier, len(partners))


def gather(wbuf, ext, ext_t, proj, tok_ref, s_send, s_halo, s_z, s_slab, s_swap):
    x, y, z, k, chip = place()
    s = 2 * chip + k
    mate = device(x, y, z, 1 - k)
    own = wbuf.at[x, y, z, k]
    for d in FAR8:
        remote(own, own, s_send.at[0], s_z, device(x, y, lax.rem(z + d, NZ), k)).start()
    halo = remote(
        tok_ref.at[pl.ds(L - HALO, HALO)], ext.at[pl.ds(L, HALO)], s_send.at[4], s_halo,
        (x, lax.rem(s + 1, 2 * CHIPS)),
    )
    halo.start()
    arrived(wbuf.at[x, y, pl.ds(0, NZ - 1), k], s_z, mate)

    def slab_copy(sx, sy, tx, ty, sem):
        ref = wbuf.at[sx, sy, :, k]
        return remote(ref, ref, s_send.at[sem], s_slab.at[sx * NY + sy], device(tx, ty, z, k))

    def swap(sx, sy, kk):
        ref = wbuf.at[sx, sy, :, kk]
        return remote(ref, ref, s_send.at[3], s_swap.at[sx * NY + sy], mate)

    def near(d):
        return lax.rem(x + d * k, NX), lax.rem(y + d * (1 - k), NY)

    def far(d):
        return lax.rem(x + d * (1 - k), NX), lax.rem(y + d * k, NY)

    for d in FAR4:
        slab_copy(x, y, *near(d), 1).start()
    for d in FAR4:
        slab_copy(x, y, *far(d), 2).start()
    swap(x, y, k).start()
    for d in (1, 3, 2):
        sx, sy = near(d)
        slab_copy(sx, sy, x, y, 1).wait_recv()
        for t in FAR4:
            slab_copy(sx, sy, *far(t), 2).start()
        swap(sx, sy, k).start()
    halo.wait_recv()

    @pl.when(s == 0)
    def _():
        ext[L : L + HALO, :] = jnp.zeros((HALO, ext.shape[1]), BF16)

    ext_t[:, L:] = ext[L:, :].T
    for e in (0, 1, 3, 2):
        for d in (1, 3, 2):
            fx, fy = far(d)
            sx = lax.rem(fx + e * k, NX)
            sy = lax.rem(fy + e * (1 - k), NY)
            slab_copy(sx, sy, x, y, 2).wait_recv()
            swap(sx, sy, k).start()
    depth = ext.shape[1] // NX
    total = jnp.zeros((L + HALO, WIDE), F32)
    for d in range(NX):
        sx = lax.rem(x + d, NX)
        for sy in range(NY):
            swap(sx, sy, 1 - k).wait_recv()
        at = pl.multiple_of(sx * depth, depth)
        weights = wbuf[sx].astype(F32).reshape(depth, WIDE).astype(BF16)
        total = total + dg(ext[0 : L + HALO, pl.ds(at, depth)], weights, 1, 0)
    proj[HALO:, :] = total[0:L]
    proj[0:HALO, :] = total[L:]

    def drain():
        sent(wbuf.at[0, 0, pl.ds(0, NZ - 1), 0], s_send.at[0], mate)
        sent(wbuf.at[0, pl.ds(0, NY - 1), :, 0], s_send.at[1], mate)
        sent(wbuf.at[pl.ds(0, NX - 1), :, :, 0], s_send.at[2], mate)
        sent(wbuf.at[:, :, :, 0], s_send.at[3], mate)
        halo.wait_send()

    return drain


class Half:
    def __init__(self, loc, part, snd, rcv, tot, tots, snd2, rcv2, other, st, decays, s_send, s_mate, s_one, s_row, s_two):
        self.loc, self.part, self.snd, self.rcv, self.tot, self.tots = loc, part, snd, rcv, tot, tots
        self.snd2, self.rcv2, self.other, self.st = snd2, rcv2, other, st
        self.reverse = decays is not None
        self.decays = decays if self.reverse else self
        self.rows = pl.ds(0, 16 if self.reverse else 18)
        self.s_send, self.s_mate, self.s_one, self.s_row, self.s_two = s_send, s_mate, s_one, s_row, s_two
        self.x, self.y, self.z, self.k, self.chip = place()
        self.mate = device(self.x, self.y, self.z, 1 - self.k)
        self.first = self.k == 0

    def to_mate(self):
        return remote(self.loc.at[1 - self.k], self.part, self.s_send.at[0], self.s_mate.at[0], self.mate)

    def back(self):
        return remote(self.other, self.st.at[self.k], self.s_send.at[4], self.s_mate.at[1], self.mate)

    def back_in(self):
        return remote(self.other, self.st.at[1 - self.k], self.s_send.at[4], self.s_mate.at[1], self.mate)

    def cores(self):
        own, other = self.loc[self.k], self.part[...]
        return jnp.where(self.first, own, other), jnp.where(self.first, other, own)

    def start_one(self, s, t, a, ad):
        for j in range(NZ):
            rows = slice(8 * j, 8 * j + 8)
            for i in range(LANES):
                lanes = slice(128 * i, 128 * i + 128)
                self.snd[j, i, 0:8] = s[rows, lanes]
                self.snd[j, i, 8:16] = t[rows, lanes]
                if not self.reverse:
                    self.snd[j, i, 16:17] = a[:, lanes]
                    self.snd[j, i, 17:18] = ad[:, lanes]
        for d in FAR8:
            c = lax.rem(self.z + d, NZ)
            dev = device(self.x, self.y, c, self.k)
            remote(self.snd.at[c, :, self.rows], self.rcv.at[self.z, :, self.rows], self.s_send.at[1], self.s_one, dev).start()
        self.rcv[self.z] = self.snd[self.z]

    def wait_one(self):
        arrived(self.rcv.at[pl.ds(0, NZ - 1), :, self.rows], self.s_one, self.mate)

    @staticmethod
    def step(carry, ref, decays, c):
        s, t = carry
        a, ad = decays[c, :, 16:17, :], decays[c, :, 17:18, :]
        return a * s + ref[c, :, 0:8, :], a * t + (ad * s + ref[c, :, 8:16, :])

    def order(self, count):
        return range(count - 1, -1, -1) if self.reverse else range(count)

    def row_total(self):
        carry = (jnp.zeros((LANES, 8, 128), F32),) * 2
        for c in self.order(NZ):
            carry = self.step(carry, self.rcv, self.decays.rcv, c)
        self.tot[:, 0:8, :], self.tot[:, 8:16, :] = carry
        if not self.reverse:
            a, ad = self.rcv[0, :, 16:17, :], self.rcv[0, :, 17:18, :]
            for c in range(1, NZ):
                b, bd = self.rcv[c, :, 16:17, :], self.rcv[c, :, 17:18, :]
                a, ad = a * b, ad * b + a * bd
            self.tot[:, 16:17, :], self.tot[:, 17:18, :] = a, ad
        for d in FAR4:
            dev = device(self.x, lax.rem(self.y + d, NY), self.z, self.k)
            remote(self.tot.at[:, self.rows], self.tots.at[self.y, :, self.rows], self.s_send.at[2], self.s_row, dev).start()
        self.tots[self.y] = self.tot[...]

    def start_two(self):
        arrived(self.tots.at[pl.ds(0, NY - 1), :, self.rows], self.s_row, self.mate)
        carry = (jnp.zeros((LANES, 8, 128), F32),) * 2
        for row in self.order(NY):
            after = self.step(carry, self.tots, self.decays.tots, row)
            ahead = (row > self.y) if self.reverse else (row < self.y)
            carry = tuple(jnp.where(ahead, new, old) for new, old in zip(after, carry))
        for c in self.order(NZ):
            self.snd2[c, :, 0:8, :], self.snd2[c, :, 8:16, :] = carry
            carry = self.step(carry, self.rcv, self.decays.rcv, c)
        for d in FAR8:
            c = lax.rem(self.z + d, NZ)
            dev = device(self.x, self.y, c, self.k)
            remote(self.snd2.at[c], self.rcv2.at[self.z], self.s_send.at[3], self.s_two, dev).start()
        self.rcv2[self.z] = self.snd2[self.z]

    def wait_two(self):
        arrived(self.rcv2.at[pl.ds(0, NZ - 1)], self.s_two, self.mate)

    def assemble(self, a, ad, base, base_first):
        s, t = (
            jnp.concatenate(
                [jnp.concatenate([self.rcv2[j, i, rows] for j in range(NZ)], 0) for i in range(LANES)], 1
            )
            for rows in (slice(0, 8), slice(8, 16))
        )
        next_s = a * s + base[0:64]
        next_t = a * t + ad * s + base[64:128]
        mine_is_base = self.first if base_first else jnp.logical_not(self.first)
        self.other[0:64, :] = jnp.where(mine_is_base, next_s, s)
        self.other[64:128, :] = jnp.where(mine_is_base, next_t, t)
        self.back().start()
        self.st[self.k, 0:64, :] = jnp.where(mine_is_base, s, next_s)
        self.st[self.k, 64:128, :] = jnp.where(mine_is_base, t, next_t)

    def drain(self):
        self.to_mate().wait_send()
        sent(self.snd.at[pl.ds(0, NZ - 1), :, self.rows], self.s_send.at[1], self.mate)
        sent(self.tots.at[pl.ds(0, NY - 1), :, self.rows], self.s_send.at[2], self.mate)
        sent(self.snd2.at[pl.ds(0, NZ - 1)], self.s_send.at[3], self.mate)
        self.back().wait_send()


def reduce(dp, ext_t, full, g2, m01, m2, a0, a1, a2, r0, r1, r2, b0, b1, b2, q0, q1, q2, c0, c1, c2, p0, p1, p2,
           e2, f2, s_send, s_mate, s_a, s_b, s_c, s_e, out_ref):
    x, y, z, k, chip = place()
    mate = device(x, y, z, 1 - k)
    holder = lax.rem(z, 2) == k

    def x_to(d):
        return device(lax.rem(x + d, NX), y, z, k)

    def y_to(d):
        return device(x, lax.rem(y + d, NY), z, k)

    def z_to(d):
        return device(x, y, lax.rem(z + d, NZ), k)

    high, low = split(dp)
    low_half = iota((8, 128), 1) < 64
    block_rows = NY * NZ * 16

    order = FAR4 + (0,)

    def settle(i):
        xb = lax.rem(x + order[i], NX)
        arrived(m01.at[:, xb], s_mate.at[i], mate)
        a0[xb] = full[0, xb, :, :, k] + m01[0, xb]
        if i < NX - 1:
            remote(a0.at[xb], r0.at[i], s_send.at[2], s_a.at[0], x_to(order[i])).start()
        a1[xb] = full[1, xb, :, :, k] + m01[1, xb]
        for d in FAR4:
            remote(a1.at[xb, lax.rem(y + d, NY)], r1.at[d - 1, xb], s_send.at[3], s_a.at[1], y_to(d)).start()
        arrived(m2.at[xb], s_mate.at[NX + i], mate)
        a2[xb] = g2[k, xb] + m2[xb]

    for i in range(NX):
        xb = lax.rem(x + order[i], NX)
        rows = ext_t[pl.ds(pl.multiple_of(xb * block_rows, block_rows), block_rows), :]
        part = dg(rows, high, 1, 0) + dg(rows, low, 1, 0)
        full[0, xb] = part[:, 0:128].reshape(NY, NZ, 2, 8, 128)
        full[1, xb] = part[:, 128:256].reshape(NY, NZ, 2, 8, 128)
        steps = part[:, 256:384].reshape(NY, NZ // 2, 2, 2, 8, 128)
        for zp in range(2):
            g2[zp, xb] = jnp.where(low_half, steps[:, :, zp, 0], steps[:, :, zp, 1])
        for tile in range(2):
            remote(full.at[tile, xb, :, :, 1 - k], m01.at[tile, xb], s_send.at[0], s_mate.at[i], mate).start()
        remote(g2.at[1 - k, xb], m2.at[xb], s_send.at[1], s_mate.at[NX + i], mate).start()
        if i > 0:
            settle(i - 1)
    settle(NX - 1)

    zsend = []
    for i in range(NZ // 2):
        target = 2 * i + k
        gap = lax.rem(z - target + NZ, NZ)
        zsend.append((target != z, remote(a2.at[:, :, i], r2.at[gap], s_send.at[4 + i], s_a.at[2], device(x, y, target, k))))
        pl.when(zsend[-1][0])(zsend[-1][1].start)

    arrived(r0, s_a.at[0], mate)
    b0[...] = (a0[x] + r0[0]) + (r0[1] + r0[2])
    for d in FAR4:
        remote(b0.at[lax.rem(y + d, NY)], q0.at[d - 1], s_send.at[8], s_b.at[0], y_to(d)).start()
    arrived(r1, s_a.at[1], mate)
    b1[...] = (a1[:, y] + r1[0]) + (r1[1] + r1[2])
    for d in FAR8:
        remote(b1.at[:, lax.rem(z + d, NZ)], q1.at[d - 1], s_send.at[9], s_b.at[1], z_to(d)).start()

    @pl.when(holder)
    def _():
        arrived(r2.at[pl.ds(1, NZ - 1)], s_a.at[2], mate)
        total = a2[:, :, z // 2] + ((r2[1] + r2[2]) + (r2[3] + r2[4]))
        b2[...] = total + ((r2[5] + r2[6]) + r2[7])
        for d in FAR4:
            remote(b2.at[lax.rem(x + d, NX)], q2.at[d - 1], s_send.at[10], s_b.at[2], x_to(d)).start()

    arrived(q0, s_b.at[0], mate)
    c0[...] = (b0[y] + q0[0]) + (q0[1] + q0[2])
    for d in FAR8:
        remote(c0.at[lax.rem(z + d, NZ)], p0.at[d - 1], s_send.at[11], s_c.at[0], z_to(d)).start()

    @pl.when(holder)
    def _():
        arrived(q2, s_b.at[2], mate)
        c2[...] = (b2[x] + q2[0]) + (q2[1] + q2[2])
        for d in FAR4:
            remote(c2.at[lax.rem(y + d, NY)], p2.at[d - 1], s_send.at[12], s_c.at[2], y_to(d)).start()

    arrived(q1, s_b.at[1], mate)
    c1[...] = b1[:, z] + ((q1[0] + q1[1]) + (q1[2] + q1[3])) + ((q1[4] + q1[5]) + q1[6])
    for d in FAR4:
        remote(c1.at[lax.rem(x + d, NX)], p1.at[d - 1], s_send.at[13], s_c.at[1], x_to(d)).start()
    last = remote(e2, f2, s_send.at[14], s_e, mate)

    @pl.when(holder)
    def _():
        arrived(p2, s_c.at[2], mate)
        e2[...] = (c2[y] + p2[0]) + (p2[1] + p2[2])
        last.start()

    sent(m01, s_send.at[0], mate)
    sent(m2, s_send.at[1], mate)
    sent(r0, s_send.at[2], mate)
    sent(r1, s_send.at[3], mate)
    for used, copy in zsend:
        pl.when(used)(copy.wait_send)
    sent(q0, s_send.at[8], mate)
    sent(q1, s_send.at[9], mate)
    arrived(p0, s_c.at[0], mate)
    out_ref[:, 0:128] = c0[z] + ((p0[0] + p0[1]) + (p0[2] + p0[3])) + ((p0[4] + p0[5]) + p0[6])
    arrived(p1, s_c.at[1], mate)
    out_ref[:, 128:256] = (c1[x] + p1[0]) + (p1[1] + p1[2])

    @pl.when(jnp.logical_not(holder))
    def _():
        last.wait_recv()
        e2[...] = f2[...]

    out_ref[:, 256:384] = jnp.where(k == 0, e2[...], roll64(e2[...]))
    sent(p0, s_send.at[11], mate)
    sent(p1, s_send.at[13], mate)

    @pl.when(holder)
    def _():
        sent(q2, s_send.at[10], mate)
        sent(p2, s_send.at[12], mate)
        last.wait_send()


def everything(scale, sw_hbm, sd_hbm, tw_hbm, td_hbm, tok_ref, v_hbm, u_hbm, conv_hbm, bias_hbm, rate_hbm,
               out_ref, v_ref, u_ref, sw_ref, sd_ref, tw_ref, td_ref, conv_ref, bias_ref, rate_ref, wbuf, ext, ext_t, proj,
               forward_scratch, backward_scratch, rows_ref, row1_ref, row2_ref, colq_ref, colqd_ref, zp_ref, reduce_scratch,
               s_in, gather_sems, forward_sems, backward_sems, reduce_sems):
    entered = enter()
    pairs = [
        (sw_hbm, sw_ref), (sd_hbm, sd_ref), (tw_hbm, tw_ref), (td_hbm, td_ref), (tok_ref, ext.at[pl.ds(0, L)]),
        (v_hbm, v_ref), (u_hbm, u_ref), (conv_hbm, conv_ref), (bias_hbm, bias_ref), (rate_hbm, rate_ref),
    ]
    local = [pltpu.make_async_copy(src, dst, s_in.at[i]) for i, (src, dst) in enumerate(pairs)]
    for c in local:
        c.start()
    x, y, z, k, _ = place()
    ext[L + HALO :, :] = jnp.zeros((ext.shape[0] - L - HALO, ext.shape[1]), BF16)
    for c in local[0:4]:
        c.wait()
    wbuf[x, y, z, k, :, 0:128] = sw_ref[...]
    wbuf[x, y, z, k, :, 128:256] = sd_ref[...]
    rows = sw_ref.shape[0]
    wbuf[x, y, z, k, :, 256:384] = jnp.concatenate(
        [tw_ref[...].astype(F32), td_ref[...].astype(F32), jnp.zeros((rows, 128 - 2 * H), F32)], 1
    ).astype(BF16)
    local[4].wait()
    ext_t[:, 0:L] = ext[0:L, :].T
    for c in local[5:]:
        c.wait()
    entered()
    drain_gather = gather(wbuf, ext, ext_t, proj, tok_ref, *gather_sems)

    rate = rate_ref[...]
    ft = features(lambda row, lane, lanes: proj[row : row + L, lane : lane + lanes], conv_ref[...], bias_ref[...], rate)
    wts = weights_of(ft)
    pp = pair_parts(ft)
    we, wde, es, eds, eu, edu = streams(wts, v_ref[...], u_ref[...])
    fw = Half(*forward_scratch, None, *forward_sems)
    bw = Half(*backward_scratch, fw, *backward_sems)
    row = iota((8, HP), 0)
    dec = jnp.where(row == 0, es[L - 1 :, :], jnp.where(row == 1, eds[L - 1 :, :], 0.0))
    states = forward_states(pp, we, wde)
    for half in range(2):
        lanes = slice(HALF * half, HALF * half + HALF)
        fw.loc[half, 0:128, :] = states[:, lanes]
        fw.loc[half, 128:136, :] = dec[:, lanes]
    fw.to_mate().start()
    states = backward_states(pp, eu, edu)
    for half in range(2):
        bw.loc[half] = states[:, HALF * half : HALF * half + HALF]
    bw.to_mate().start()

    fw.to_mate().wait_recv()
    one0, one1 = fw.cores()
    a0, ad0 = one0[128:129], one0[129:130]
    a1, ad1 = one1[128:129], one1[129:130]
    a, ad = a0 * a1, ad0 * a1 + a0 * ad1
    fw.start_one(
        a1 * one0[0:64] + one1[0:64], a1 * one0[64:128] + ad1 * one0[0:64] + one1[64:128], a, ad
    )
    bw.to_mate().wait_recv()
    one0, one1 = bw.cores()
    bw.start_one(
        a0 * one1[0:64] + one0[0:64], a0 * one1[64:128] + ad0 * one1[0:64] + one0[64:128], a, ad
    )

    def tile(ref):
        return lambda i: ref[:, pl.ds(pl.multiple_of(i * 128, 128), 128)]

    g, gd = intra_setup(ft, pp, rows_ref, row1_ref, row2_ref)
    zero = jnp.zeros((L, L), F32)

    def block_terms(first, last, carry):
        return intra(
            ft, g, gd, tile(v_ref), tile(u_ref), rows_ref, row1_ref, row2_ref, colq_ref, colqd_ref, first, last, carry
        )

    carry = block_terms(0, 4, (zero, zero))
    fw.wait_one()
    fw.row_total()
    carry = block_terms(4, 6, carry)
    bw.wait_one()
    bw.row_total()
    fw.start_two()
    carry = block_terms(6, 8, carry)
    bw.start_two()
    pairs = intra_pairs(pp, *carry)
    fw.wait_two()
    fw.assemble(a0, ad0, fw.cores()[0], True)
    fw.back_in().wait_recv()
    xf = jnp.concatenate([fw.st[0], fw.st[1]], 1)
    from_forward = finish_forward(pp, eu, edu, u_ref[...], xf)
    bw.wait_two()
    bw.assemble(a1, ad1, bw.cores()[1], False)
    bw.back_in().wait_recv()
    xb = jnp.concatenate([bw.st[0], bw.st[1]], 1)
    from_backward = finish_backward(pp, we, wde, v_ref[...], xb)
    dz, dzd, dq, dqd = finish(
        ft, wts, pairs, row1_ref[...], row2_ref[...], colq_ref[...], colqd_ref[...],
        from_forward, from_backward, xf, xb, rate, scale,
    )
    zp_ref[...] = jnp.zeros(zp_ref.shape, F32)
    zp_ref[HALO : HALO + L, 0:128] = dz
    zp_ref[HALO : HALO + L, 128:256] = dzd
    conv = conv_ref[...]

    def spread(first_row, count, lanes):
        total = conv[0:1, :] * zp_ref[first_row + 3 : first_row + 3 + count, lanes]
        for tap in range(1, KCONV):
            total = total + conv[tap : tap + 1, :] * zp_ref[first_row + 3 - tap : first_row + 3 - tap + count, lanes]
        return total

    pad = jnp.zeros((128 - HALO, 128), F32)
    columns = []
    for half in range(2):
        lanes = slice(128 * half, 128 * half + 128)
        columns.append(jnp.concatenate([spread(HALO, L, lanes), spread(0, HALO, lanes), pad], 0))
    both = jnp.concatenate([dq, dqd, dq, dqd], 1)
    columns.append(jnp.concatenate([both, jnp.zeros((128, 128), F32)], 0))
    dp = jnp.concatenate(columns, 1)
    drain_gather()
    fw.drain()
    bw.drain()
    reduce(dp, ext_t, *reduce_scratch, *reduce_sems, out_ref)


def split_outputs(sums_ref, o_sel, o_step, o_selh, o_steph):
    o_sel[...] = sums_ref[:, 0:128]
    o_selh[...] = sums_ref[:, 128:256]
    o_step[...] = sums_ref[:, 256 : 256 + H]
    o_steph[...] = sums_ref[:, 256 + H : 256 + 2 * H]


def vmem(shape, dtype=F32):
    return pltpu.VMEM(shape, dtype)


def dma(*shape):
    return pltpu.SemaphoreType.DMA(shape)


def body(tokens, values, cotangent, sel_weight, step_weight, sel_dir, step_dir, conv_weight, step_bias, decay_rate):
    own_tokens, v, u = tokens[0], values[0], cotangent[0]
    depth = own_tokens.shape[1]
    rows = sel_weight.shape[0]
    scale = 1.0 / math.sqrt(NX * CHIPS * 2 * L)
    spec = pl.BlockSpec(memory_space=pltpu.VMEM)
    hbm = pl.BlockSpec(memory_space=pl.ANY)
    tiles = NX * NY * NZ
    reduce_scratch = (
        [vmem((2, NX, NY, NZ, 2, 8, 128)), vmem((2, NX, NY, NZ // 2, 8, 128)),
         vmem((2, NX, NY, NZ, 8, 128)), vmem((NX, NY, NZ // 2, 8, 128))]
        + [vmem((NX, NY, NZ, 8, 128))] * 2 + [vmem((NX, NY, NZ // 2, 8, 128))]
        + [vmem((3, NY, NZ, 8, 128)), vmem((3, NX, NZ, 8, 128)), vmem((NZ, NX, NY, 8, 128))]
        + [vmem((NY, NZ, 8, 128)), vmem((NX, NZ, 8, 128)), vmem((NX, NY, 8, 128))]
        + [vmem((3, NZ, 8, 128)), vmem((7, NX, 8, 128)), vmem((3, NY, 8, 128))]
        + [vmem((NZ, 8, 128)), vmem((NX, 8, 128)), vmem((NY, 8, 128))]
        + [vmem((7, 8, 128)), vmem((3, 8, 128)), vmem((3, 8, 128))]
        + [vmem((8, 128)), vmem((8, 128))]
    )

    def scan_scratch():
        return (
            [vmem((NZ, LANES, 24, 128))] * 2 + [vmem((LANES, 24, 128)), vmem((NY, LANES, 24, 128))]
            + [vmem((NZ, LANES, 16, 128))] * 2 + [vmem((128, HALF)), vmem((2, 128, HALF))]
        )

    scratch = [
        vmem((L, HP), BF16), vmem((L, HP), BF16),
        vmem((rows, 128), BF16), vmem((rows, 128), BF16), vmem((rows, H), BF16), vmem((rows, H), BF16),
        vmem((KCONV, 128)), vmem((1, H)), vmem((1, H)),
        vmem((NX, NY, NZ, 2, rows, WIDE), BF16),
        vmem((2 * L, depth), BF16), vmem((depth, 2 * L), BF16), vmem((HALO + L, WIDE)),
        [vmem((2, 136, HALF)), vmem((136, HALF))] + scan_scratch(),
        [vmem((2, 128, HALF)), vmem((128, HALF))] + scan_scratch(),
        vmem((3 * H, L)), vmem((L, L)), vmem((L, L)), vmem((H, L)), vmem((H, L)), vmem((HALO + L + 8, 256)),
        reduce_scratch,
        dma(10),
        [dma(5), dma(), dma(), dma(NX * NY), dma(NX * NY)],
        [dma(5), dma(2), dma(), dma(), dma()],
        [dma(5), dma(2), dma(), dma(), dma()],
        [dma(15), dma(2 * NX), dma(3), dma(3), dma(3), dma()],
    ]
    sums = pl.pallas_call(
        functools.partial(everything, scale),
        out_shape=jax.ShapeDtypeStruct((rows, WIDE), F32),
        in_specs=[hbm] * 10,
        out_specs=spec,
        scratch_shapes=scratch,
        compiler_params=pltpu.CompilerParams(
            vmem_limit_bytes=VMEM_LIMIT, collective_id=0, has_side_effects=True
        ),
    )(sel_weight, sel_dir, step_weight, step_dir, own_tokens, v, u, conv_weight, step_bias[None, :], decay_rate[None, :])
    return pl.pallas_call(
        split_outputs,
        out_shape=[
            jax.ShapeDtypeStruct((rows, 128), F32), jax.ShapeDtypeStruct((rows, H), F32),
            jax.ShapeDtypeStruct((rows, 128), F32), jax.ShapeDtypeStruct((rows, H), F32),
        ],
        in_specs=[spec],
        out_specs=[spec] * 4,
    )(sums)


def solution(mesh):
    shards = P(("dp", "seq"), None)
    stream = P("dp", "seq", None)
    return jax.shard_map(
        body,
        mesh=mesh,
        in_specs=(stream, stream, stream, shards, shards, shards, shards, P(), P(), P()),
        out_specs=(shards, shards, shards, shards),
        check_vma=False,
    )
```

```python
import functools
import math

import jax
import jax.numpy as jnp
from jax import lax
from jax.experimental import pallas as pl
from jax.experimental.pallas import tpu as pltpu
from jax.sharding import PartitionSpec as P

N = 64
P_SIZE = 32
H = 32
KCONV = 4
L = 128
HALO = 16
HP = H * P_SIZE
HALF = HP // 2
WIDE = 384
NX, NY, NZ = 4, 4, 8
CHIPS = NY * NZ
MESH = pl.DeviceIdType.MESH
F32 = jnp.float32
BF16 = jnp.bfloat16
VMEM_LIMIT = 56 * 1024 * 1024


def roll64(x):
    return pltpu.roll(x, 64, 1)


def split(x):
    high = x.astype(BF16)
    low = (x - high.astype(F32)).astype(BF16)
    return high, low


def split3(x):
    high = x.astype(BF16)
    rest = x - high.astype(F32)
    mid = rest.astype(BF16)
    low = (rest - mid.astype(F32)).astype(BF16)
    return high, mid, low


def dg(a, b, ca, cb):
    return lax.dot_general(a, b, (((ca,), (cb,)), ((), ())), preferred_element_type=F32)


def dot_split(a, b, ca, cb):
    return dot_parts(split(a), split(b), ca, cb)


def dot_parts(a, b, ca, cb):
    (ah, al), (bh, bl) = a, b
    return dg(ah, bh, ca, cb) + (dg(ah, bl, ca, cb) + dg(al, bh, ca, cb))


def dot_left(a, b, ca, cb):
    ah, al = split(a)
    return dg(ah, b, ca, cb) + dg(al, b, ca, cb)


def iota(shape, dim):
    return lax.broadcasted_iota(jnp.int32, shape, dim)


def low_lanes():
    return iota((L, 128), 1) < 64


def head_spread():
    return (iota((H, HP), 0) == iota((H, HP), 1) // P_SIZE).astype(F32).astype(BF16)


def triangle(reverse):
    row, column = iota((L, L), 0), iota((L, L), 1)
    keep = (column >= row) if reverse else (row >= column)
    return keep.astype(F32).astype(BF16)


def cumulate(x, reverse):
    tri = triangle(reverse)
    a, b, c = split3(x)
    return dg(tri, a, 1, 0) + (dg(tri, b, 1, 0) + dg(tri, c, 1, 0))


def features(proj, conv2, bias, rate):
    z = jnp.zeros((L, 128), F32)
    zd = jnp.zeros((L, 128), F32)
    for k in range(KCONV):
        rows = HALO - (KCONV - 1) + k
        z = z + conv2[k : k + 1, :128] * proj(rows, 0, 128)
        zd = zd + conv2[k : k + 1, :128] * proj(rows, 128, 128)
    sg = jax.nn.sigmoid(z)
    act = z * sg
    first = sg * (1.0 + z * (1.0 - sg))
    second = sg * (1.0 - sg) * (2.0 + z * (1.0 - 2.0 * sg))
    actd = first * zd
    steps = proj(HALO, 256, 128)
    q = steps[:, :H] + bias
    qd = steps[:, H : 2 * H]
    delta = jnp.maximum(q, 0.0) + jnp.log1p(jnp.exp(-jnp.abs(q)))
    sq = jax.nn.sigmoid(q)
    deltad = sq * qd
    cum = cumulate(-(delta * rate), False)
    cumd = cumulate(-(deltad * rate), False)
    return dict(
        zd=zd, act=act, actd=actd, first=first, second=second,
        qd=qd, sq=sq, delta=delta, deltad=deltad, cum=cum, cumd=cumd,
    )


def weights_of(ft):
    cum, cumd = ft["cum"], ft["cumd"]
    last, lastd = cum[L - 1 :, :], cumd[L - 1 :, :]
    e = jnp.exp(cum)
    ed = e * cumd
    f = jnp.exp(last - cum)
    fd = f * (lastd - cumd)
    w = f * ft["delta"]
    wd = fd * ft["delta"] + f * ft["deltad"]
    return e, ed, f, fd, w, wd


def pair_parts(ft):
    act, actd = ft["act"], ft["actd"]
    actr, actdr = roll64(act), roll64(actd)
    m = low_lanes()
    return dict(
        b_bd=jnp.where(m, act, actdr),
        o_b=jnp.where(m, 0.0, actr),
        c_cd=jnp.where(m, actr, actd),
        o_c=jnp.where(m, 0.0, act),
        b_o=jnp.where(m, act, 0.0),
        bd_b=jnp.where(m, actd, actr),
        c_o=jnp.where(m, actr, 0.0),
        cd_c=jnp.where(m, actdr, act),
        b_c=act,
        c_b=actr,
    )


def spread_rows(rows):
    return dot_left(rows, head_spread(), 1, 0)


def streams(wts, values, cotangent):
    e, ed, _, _, w, wd = wts
    v = values.astype(F32)
    u = cotangent.astype(F32)
    we = spread_rows(w) * v
    wde = spread_rows(wd) * v
    es = spread_rows(e)
    eds = spread_rows(ed)
    return we, wde, es, eds, es * u, eds * u


def forward_states(pp, we, wde):
    left = jnp.concatenate([pp["b_bd"], pp["o_b"]], 0)
    return dot_split(left, jnp.concatenate([we, wde], 0), 0, 0)


def backward_states(pp, eu, edu):
    left = jnp.concatenate([pp["c_cd"], pp["o_c"]], 0)
    return dot_split(left, jnp.concatenate([eu, edu], 0), 0, 0)


def intra_setup(ft, pp, rows_ref, row1_ref, row2_ref):
    g = dot_split(pp["c_o"], pp["b_c"], 1, 1)
    gd = dot_split(pp["cd_c"], pp["b_bd"], 1, 1)
    eta = ft["deltad"] - ft["delta"] * ft["cumd"]
    rows_ref[0:H, :] = ft["cum"].T
    rows_ref[H : 2 * H, :] = ft["delta"].T
    rows_ref[2 * H : 3 * H, :] = eta.T
    row1_ref[...] = jnp.zeros((L, L), F32)
    row2_ref[...] = jnp.zeros((L, L), F32)
    return g, gd


def intra(ft, g, gd, v_of, u_of, rows_ref, row1_ref, row2_ref, colq_ref, colqd_ref, first, last, carry):
    parts = split3(ft["cum"])
    partsd = split(ft["cumd"])
    row, lane = iota((L, L), 0), iota((L, L), 1)
    causal = row >= lane

    def one(i, carry):
        dgm, dgd = carry
        pick = (iota((H, 512), 0) == (4 * i + iota((H, 512), 1) // 128)).astype(F32).astype(BF16)
        ct4 = dg(parts[0], pick, 1, 0) + (dg(parts[1], pick, 1, 0) + dg(parts[2], pick, 1, 0))
        cd4 = dg(partsd[0], pick, 1, 0) + dg(partsd[1], pick, 1, 0)
        v_tile, u_tile = v_of(i), u_of(i)
        row1, row2 = row1_ref[...], row2_ref[...]
        for j in range(4):
            h = 4 * i + j
            mask = (iota((L, 128), 1) // P_SIZE == j).astype(F32)
            w = dg((u_tile.astype(F32) * mask).astype(BF16), v_tile, 1, 1)
            ct = ct4[:, 128 * j : 128 * j + 128]
            cd = cd4[:, 128 * j : 128 * j + 128]
            cs = rows_ref[pl.ds(h, 1), :]
            ds = rows_ref[pl.ds(H + h, 1), :]
            et = rows_ref[pl.ds(2 * H + h, 1), :]
            x = jnp.exp(jnp.where(causal, ct - cs, -1e30)) * w
            xd = x * ds
            dgm = dgm + xd
            dgd = dgd + (x * et + cd * xd)
            q = x * g
            xgd = x * gd
            colq_ref[pl.ds(h, 1), :] = jnp.sum(q, axis=0, keepdims=True)
            colqd_ref[pl.ds(h, 1), :] = jnp.sum(xgd + q * cd, axis=0, keepdims=True)
            r1 = jnp.sum(q * ds, axis=1, keepdims=True)
            r2 = jnp.sum(xgd * ds + q * et, axis=1, keepdims=True)
            here = lane == h
            row1 = jnp.where(here, r1, row1)
            row2 = jnp.where(here, r2, row2)
        row1_ref[...] = row1
        row2_ref[...] = row2
        return dgm, dgd

    return lax.fori_loop(first, last, one, carry)


def intra_pairs(pp, dgm, dgd):
    return (
        dot_split(dgm, pp["b_bd"], 1, 0),
        dot_split(dgd, pp["b_c"], 1, 0),
        dot_split(dgm, pp["c_cd"], 0, 0),
        dot_split(dgd, pp["c_b"], 0, 0),
    )


def head_sums(x):
    return dot_left(x, head_spread(), 1, 1)


def finish_forward(pp, e_split, cotangent, xf):
    u = cotangent.astype(F32)
    x_split = split(xf)
    zz = dot_parts(split(jnp.concatenate([pp["c_o"], pp["cd_c"]], 0)), x_split, 1, 0)
    return head_sums(zz[:L] * u), head_sums(zz[L:] * u), dot_parts(e_split, x_split, 1, 1)


def finish_backward(pp, w_split, values, xb):
    v = values.astype(F32)
    x_split = split(xb)
    yy = dot_parts(split(jnp.concatenate([pp["b_o"], pp["bd_b"]], 0)), x_split, 1, 0)
    return head_sums(yy[:L] * v), head_sums(yy[L:] * v), dot_parts(w_split, x_split, 1, 1)


def finish(ft, wts, pairs, row1, row2, colq, colqd, from_forward, from_backward, xf, xb, rate, scale):
    e, ed, f, fd, w, wd = wts
    g, gdot, pc = from_forward
    kk, kdot, pb = from_backward
    kap = jnp.sum(xb[:64] * xf[:64], axis=0, keepdims=True)
    kapd = jnp.sum(xb[64:] * xf[:64] + xb[:64] * xf[64:], axis=0, keepdims=True)
    both = head_sums(jnp.concatenate([jnp.broadcast_to(kap, (8, HP)), jnp.broadcast_to(kapd, (8, HP))], 0))
    kap, kapd = both[0:1], both[8:9]

    m = low_lanes()
    t1, t2, t3, t4 = pairs
    pair_c = t1 + pc[:L] + jnp.where(m, 0.0, roll64(t2 + pc[L:]))
    pair_b = t3 + pb[:L] + jnp.where(m, 0.0, roll64(t4 + pb[L:]))
    dact = jnp.where(m, pair_b, roll64(pair_c))
    dactd = jnp.where(m, roll64(pair_b), pair_c)
    dz = scale * (ft["first"] * dact)
    dzd = scale * (ft["second"] * ft["zd"] * dact + ft["first"] * dactd)

    delta, deltad, cum, cumd = ft["delta"], ft["deltad"], ft["cum"], ft["cumd"]
    colq, colqd = colq.T, colqd.T
    colqd = colqd - cumd * colq
    row1, row2 = row1[:, :H], row2[:, :H]
    row2 = row2 + cumd * row1
    wk = w * kk
    wkd = wd * kk + w * kdot
    dc = row1 - delta * colq + e * g - wk
    dcd = row2 - (deltad * colq + delta * colqd) + ed * g + e * gdot - wkd
    el, edl = e[L - 1 :, :], ed[L - 1 :, :]
    extra = el * kap + jnp.sum(wk, axis=0, keepdims=True)
    extrad = edl * kap + el * kapd + jnp.sum(wkd, axis=0, keepdims=True)
    ddelta = colq + f * kk - rate * (cumulate(dc, True) + extra)
    ddeltad = colqd + fd * kk + f * kdot - rate * (cumulate(dcd, True) + extrad)
    sq = ft["sq"]
    dq = scale * (sq * ddelta)
    dqd = scale * (sq * (1.0 - sq) * ft["qd"] * ddelta + sq * ddeltad)
    return dz, dzd, dq, dqd


def place():
    x = lax.axis_index("dp")
    s = lax.axis_index("seq")
    chip = s // 2
    return x, chip // NZ, lax.rem(chip, NZ), lax.rem(s, 2), chip


def device(x, y, z, k):
    return (x, (y * NZ + z) * 2 + k)


def remote(src, dst, send_sem, recv_sem, dev):
    return pltpu.make_async_remote_copy(
        src_ref=src, dst_ref=dst, send_sem=send_sem, recv_sem=recv_sem,
        device_id=dev, device_id_type=MESH,
    )


def arrived(dst, sem, dev):
    remote(dst, dst, sem, sem, dev).wait_recv()


def sent(src, sem, dev):
    remote(src, src, sem, sem, dev).wait_send()


FAR4 = (2, 1, 3)
LANES = HALF // 256
FAR8 = (4, 3, 5, 2, 6, 1, 7)


def enter():
    x, y, z, k, chip = place()
    s = 2 * chip + k
    seq = CHIPS * 2
    partners = [device(x, y, lax.rem(z + d, NZ), k) for d in FAR8]
    partners += [
        device(lax.rem(x + dx, NX), lax.rem(y + dy, NY), z, k) for dx in range(NX) for dy in range(NY) if dx or dy
    ]
    partners += [(x, lax.rem(s + 1, seq)), (x, lax.rem(s + seq - 1, seq)), device(x, y, z, 1 - k)]
    barrier = pltpu.get_barrier_semaphore()
    for dev in partners:
        pl.semaphore_signal(barrier, inc=1, device_id=dev, device_id_type=MESH)
    return lambda: pl.semaphore_wait(barrier, len(partners))


def gather(wbuf, ext, ext_t, proj, tok_ref, s_send, s_halo, s_z, s_slab, s_swap):
    x, y, z, k, chip = place()
    s = 2 * chip + k
    mate = device(x, y, z, 1 - k)
    own = wbuf.at[x, y, z, k]
    for d in FAR8:
        remote(own, own, s_send.at[0], s_z, device(x, y, lax.rem(z + d, NZ), k)).start()
    halo = remote(
        tok_ref.at[pl.ds(L - HALO, HALO)], ext.at[pl.ds(L, HALO)], s_send.at[4], s_halo,
        (x, lax.rem(s + 1, 2 * CHIPS)),
    )
    halo.start()
    arrived(wbuf.at[x, y, pl.ds(0, NZ - 1), k], s_z, mate)

    def slab_copy(sx, sy, tx, ty):
        ref = wbuf.at[sx, sy, :, k]
        return remote(ref, ref, s_send.at[1], s_slab.at[sx * NY + sy], device(tx, ty, z, k))

    def swap(sx, sy, kk):
        ref = wbuf.at[sx, sy, :, kk]
        return remote(ref, ref, s_send.at[3], s_swap.at[sx * NY + sy], mate)

    def hops(offset):
        return sum(min(d, 4 - d) for d in offset)

    offsets = sorted([(dx, dy) for dx in range(NX) for dy in range(NY) if dx or dy], key=hops)
    for dx, dy in offsets[::-1]:
        slab_copy(x, y, lax.rem(x + dx, NX), lax.rem(y + dy, NY)).start()
    swap(x, y, k).start()
    halo.wait_recv()

    @pl.when(s == 0)
    def _():
        ext[L : L + HALO, :] = jnp.zeros((HALO, ext.shape[1]), BF16)

    ext_t[:, L:] = ext[L:, :].T
    for dx, dy in offsets:
        sx, sy = lax.rem(x + dx, NX), lax.rem(y + dy, NY)
        slab_copy(sx, sy, x, y).wait_recv()
        swap(sx, sy, k).start()
    depth = ext.shape[1] // NX
    total = jnp.zeros((L + HALO, WIDE), F32)
    for d in range(NX):
        sx = lax.rem(x + d, NX)
        for sy in range(NY):
            swap(sx, sy, 1 - k).wait_recv()
        at = pl.multiple_of(sx * depth, depth)
        weights = wbuf[sx].astype(F32).reshape(depth, WIDE).astype(BF16)
        total = total + dg(ext[0 : L + HALO, pl.ds(at, depth)], weights, 1, 0)
    proj[HALO:, :] = total[0:L]
    proj[0:HALO, :] = total[L:]

    def drain():
        sent(wbuf.at[0, 0, pl.ds(0, NZ - 1), 0], s_send.at[0], mate)
        sent(wbuf.at[pl.ds(0, 3), :, pl.ds(0, 5)], s_send.at[1], mate)
        sent(wbuf.at[:, :, :, 0], s_send.at[3], mate)
        halo.wait_send()

    return drain


class Half:
    def __init__(self, loc, part, snd, rcv, tot, tots, snd2, rcv2, other, st, decays, s_send, s_mate, s_one, s_row, s_two):
        self.loc, self.part, self.snd, self.rcv, self.tot, self.tots = loc, part, snd, rcv, tot, tots
        self.snd2, self.rcv2, self.other, self.st = snd2, rcv2, other, st
        self.reverse = decays is not None
        self.decays = decays if self.reverse else self
        self.rows = pl.ds(0, 16 if self.reverse else 18)
        self.s_send, self.s_mate, self.s_one, self.s_row, self.s_two = s_send, s_mate, s_one, s_row, s_two
        self.x, self.y, self.z, self.k, self.chip = place()
        self.mate = device(self.x, self.y, self.z, 1 - self.k)
        self.first = self.k == 0

    def to_mate(self):
        return remote(self.loc.at[1 - self.k], self.part, self.s_send.at[0], self.s_mate.at[0], self.mate)

    def back(self):
        return remote(self.other, self.st.at[self.k], self.s_send.at[4], self.s_mate.at[1], self.mate)

    def back_in(self):
        return remote(self.other, self.st.at[1 - self.k], self.s_send.at[4], self.s_mate.at[1], self.mate)

    def cores(self):
        own, other = self.loc[self.k], self.part[...]
        return jnp.where(self.first, own, other), jnp.where(self.first, other, own)

    def start_one(self, s, t, a, ad):
        for h in range(2):
            for j in range(NZ):
                rows = slice(8 * j, 8 * j + 8)
                for i in range(LANES):
                    at = 128 * (LANES * h + i)
                    lanes = slice(at, at + 128)
                    self.snd[h, j, i, 0:8] = s[rows, lanes]
                    self.snd[h, j, i, 8:16] = t[rows, lanes]
                    if not self.reverse:
                        self.snd[h, j, i, 16:17] = a[:, lanes]
                        self.snd[h, j, i, 17:18] = ad[:, lanes]
            for d in FAR8:
                c = lax.rem(self.z + d, NZ)
                dev = device(self.x, self.y, c, self.k)
                remote(
                    self.snd.at[h, c, :, self.rows], self.rcv.at[h, self.z, :, self.rows],
                    self.s_send.at[1], self.s_one.at[h], dev,
                ).start()
            self.rcv[h, self.z] = self.snd[h, self.z]

    @staticmethod
    def step(carry, ref, decays, c):
        s, t = carry
        a, ad = decays[*c, :, 16:17, :], decays[*c, :, 17:18, :]
        return a * s + ref[*c, :, 0:8, :], a * t + (ad * s + ref[*c, :, 8:16, :])

    def order(self, count):
        return range(count - 1, -1, -1) if self.reverse else range(count)

    def row_total(self, h):
        arrived(self.rcv.at[h, pl.ds(0, NZ - 1), :, self.rows], self.s_one.at[h], self.mate)
        carry = (jnp.zeros((LANES, 8, 128), F32),) * 2
        for c in self.order(NZ):
            carry = self.step(carry, self.rcv, self.decays.rcv, (h, c))
        self.tot[h, :, 0:8, :], self.tot[h, :, 8:16, :] = carry
        if not self.reverse:
            a, ad = self.rcv[h, 0, :, 16:17, :], self.rcv[h, 0, :, 17:18, :]
            for c in range(1, NZ):
                b, bd = self.rcv[h, c, :, 16:17, :], self.rcv[h, c, :, 17:18, :]
                a, ad = a * b, ad * b + a * bd
            self.tot[h, :, 16:17, :], self.tot[h, :, 17:18, :] = a, ad
        for d in FAR4:
            dev = device(self.x, lax.rem(self.y + d, NY), self.z, self.k)
            remote(
                self.tot.at[h, :, self.rows], self.tots.at[h, self.y, :, self.rows],
                self.s_send.at[2], self.s_row.at[h], dev,
            ).start()
        self.tots[h, self.y] = self.tot[h]

    def start_two(self, h):
        arrived(self.tots.at[h, pl.ds(0, NY - 1), :, self.rows], self.s_row.at[h], self.mate)
        carry = (jnp.zeros((LANES, 8, 128), F32),) * 2
        for row in self.order(NY):
            after = self.step(carry, self.tots, self.decays.tots, (h, row))
            ahead = (row > self.y) if self.reverse else (row < self.y)
            carry = tuple(jnp.where(ahead, new, old) for new, old in zip(after, carry))
        for c in self.order(NZ):
            self.snd2[h, c, :, 0:8, :], self.snd2[h, c, :, 8:16, :] = carry
            carry = self.step(carry, self.rcv, self.decays.rcv, (h, c))
        for d in FAR8:
            c = lax.rem(self.z + d, NZ)
            dev = device(self.x, self.y, c, self.k)
            remote(self.snd2.at[h, c], self.rcv2.at[h, self.z], self.s_send.at[3], self.s_two.at[h], dev).start()
        self.rcv2[h, self.z] = self.snd2[h, self.z]

    def wait_two(self, h):
        arrived(self.rcv2.at[h, pl.ds(0, NZ - 1)], self.s_two.at[h], self.mate)

    def assemble(self, a, ad, base, base_first):
        s, t = (
            jnp.concatenate(
                [jnp.concatenate([self.rcv2[i // LANES, j, i % LANES, rows] for j in range(NZ)], 0) for i in range(2 * LANES)], 1
            )
            for rows in (slice(0, 8), slice(8, 16))
        )
        next_s = a * s + base[0:64]
        next_t = a * t + ad * s + base[64:128]
        mine_is_base = self.first if base_first else jnp.logical_not(self.first)
        self.other[0:64, :] = jnp.where(mine_is_base, next_s, s)
        self.other[64:128, :] = jnp.where(mine_is_base, next_t, t)
        self.back().start()
        self.st[self.k, 0:64, :] = jnp.where(mine_is_base, s, next_s)
        self.st[self.k, 64:128, :] = jnp.where(mine_is_base, t, next_t)

    def drain(self):
        self.to_mate().wait_send()
        sent(self.snd.at[:, pl.ds(0, NZ - 1), :, self.rows], self.s_send.at[1], self.mate)
        sent(self.tots.at[:, pl.ds(0, NY - 1), :, self.rows], self.s_send.at[2], self.mate)
        sent(self.snd2.at[:, pl.ds(0, NZ - 1)], self.s_send.at[3], self.mate)
        self.back().wait_send()


def reduce(dp, ext_t, full, g2, m01, m2, a0, a1, a2, r0, r1, r2, b0, b1, b2, q0, q1, q2, c0, c1, c2, p0, p1, p2,
           e2, f2, s_send, s_mate, s_a, s_b, s_c, s_e, out_ref):
    x, y, z, k, chip = place()
    mate = device(x, y, z, 1 - k)
    holder = lax.rem(z, 2) == k

    def x_to(d):
        return device(lax.rem(x + d, NX), y, z, k)

    def y_to(d):
        return device(x, lax.rem(y + d, NY), z, k)

    def z_to(d):
        return device(x, y, lax.rem(z + d, NZ), k)

    high, low = split(dp)
    low_half = iota((8, 128), 1) < 64
    block_rows = NY * NZ * 16

    order = FAR4 + (0,)

    def settle(i):
        xb = lax.rem(x + order[i], NX)
        arrived(m01.at[:, xb], s_mate.at[i], mate)
        a0[xb] = full[0, xb, :, :, k] + m01[0, xb]
        if i < NX - 1:
            remote(a0.at[xb], r0.at[i], s_send.at[2], s_a.at[0], x_to(order[i])).start()
        a1[xb] = full[1, xb, :, :, k] + m01[1, xb]
        for d in FAR4:
            remote(a1.at[xb, lax.rem(y + d, NY)], r1.at[d - 1, xb], s_send.at[3], s_a.at[1], y_to(d)).start()
        arrived(m2.at[xb], s_mate.at[NX + i], mate)
        a2[xb] = g2[k, xb] + m2[xb]

    for i in range(NX):
        xb = lax.rem(x + order[i], NX)
        rows = ext_t[pl.ds(pl.multiple_of(xb * block_rows, block_rows), block_rows), :]
        part = dg(rows, high, 1, 0) + dg(rows, low, 1, 0)
        full[0, xb] = part[:, 0:128].reshape(NY, NZ, 2, 8, 128)
        full[1, xb] = part[:, 128:256].reshape(NY, NZ, 2, 8, 128)
        steps = part[:, 256:384].reshape(NY, NZ // 2, 2, 2, 8, 128)
        for zp in range(2):
            g2[zp, xb] = jnp.where(low_half, steps[:, :, zp, 0], steps[:, :, zp, 1])
        for tile in range(2):
            remote(full.at[tile, xb, :, :, 1 - k], m01.at[tile, xb], s_send.at[0], s_mate.at[i], mate).start()
        remote(g2.at[1 - k, xb], m2.at[xb], s_send.at[1], s_mate.at[NX + i], mate).start()
        if i > 0:
            settle(i - 1)
    settle(NX - 1)

    zsend = []
    for i in range(NZ // 2):
        target = 2 * i + k
        gap = lax.rem(z - target + NZ, NZ)
        zsend.append((target != z, remote(a2.at[:, :, i], r2.at[gap], s_send.at[4 + i], s_a.at[2], device(x, y, target, k))))
        pl.when(zsend[-1][0])(zsend[-1][1].start)

    arrived(r0, s_a.at[0], mate)
    b0[...] = (a0[x] + r0[0]) + (r0[1] + r0[2])
    for d in FAR4:
        remote(b0.at[lax.rem(y + d, NY)], q0.at[d - 1], s_send.at[8], s_b.at[0], y_to(d)).start()
    arrived(r1, s_a.at[1], mate)
    b1[...] = (a1[:, y] + r1[0]) + (r1[1] + r1[2])
    for d in FAR8:
        remote(b1.at[:, lax.rem(z + d, NZ)], q1.at[d - 1], s_send.at[9], s_b.at[1], z_to(d)).start()

    @pl.when(holder)
    def _():
        arrived(r2.at[pl.ds(1, NZ - 1)], s_a.at[2], mate)
        total = a2[:, :, z // 2] + ((r2[1] + r2[2]) + (r2[3] + r2[4]))
        b2[...] = total + ((r2[5] + r2[6]) + r2[7])
        for d in FAR4:
            remote(b2.at[lax.rem(x + d, NX)], q2.at[d - 1], s_send.at[10], s_b.at[2], x_to(d)).start()

    arrived(q0, s_b.at[0], mate)
    c0[...] = (b0[y] + q0[0]) + (q0[1] + q0[2])
    for d in FAR8:
        remote(c0.at[lax.rem(z + d, NZ)], p0.at[d - 1], s_send.at[11], s_c.at[0], z_to(d)).start()

    @pl.when(holder)
    def _():
        arrived(q2, s_b.at[2], mate)
        c2[...] = (b2[x] + q2[0]) + (q2[1] + q2[2])
        for d in FAR4:
            remote(c2.at[lax.rem(y + d, NY)], p2.at[d - 1], s_send.at[12], s_c.at[2], y_to(d)).start()

    arrived(q1, s_b.at[1], mate)
    c1[...] = b1[:, z] + ((q1[0] + q1[1]) + (q1[2] + q1[3])) + ((q1[4] + q1[5]) + q1[6])
    for d in FAR4:
        remote(c1.at[lax.rem(x + d, NX)], p1.at[d - 1], s_send.at[13], s_c.at[1], x_to(d)).start()
    last = remote(e2, f2, s_send.at[14], s_e, mate)

    @pl.when(holder)
    def _():
        arrived(p2, s_c.at[2], mate)
        e2[...] = (c2[y] + p2[0]) + (p2[1] + p2[2])
        last.start()

    sent(m01, s_send.at[0], mate)
    sent(m2, s_send.at[1], mate)
    sent(r0, s_send.at[2], mate)
    sent(r1, s_send.at[3], mate)
    for used, copy in zsend:
        pl.when(used)(copy.wait_send)
    sent(q0, s_send.at[8], mate)
    sent(q1, s_send.at[9], mate)
    arrived(p0, s_c.at[0], mate)
    out_ref[:, 0:128] = c0[z] + ((p0[0] + p0[1]) + (p0[2] + p0[3])) + ((p0[4] + p0[5]) + p0[6])
    arrived(p1, s_c.at[1], mate)
    out_ref[:, 128:256] = (c1[x] + p1[0]) + (p1[1] + p1[2])

    @pl.when(jnp.logical_not(holder))
    def _():
        last.wait_recv()
        e2[...] = f2[...]

    out_ref[:, 256:384] = jnp.where(k == 0, e2[...], roll64(e2[...]))
    sent(p0, s_send.at[11], mate)
    sent(p1, s_send.at[13], mate)

    @pl.when(holder)
    def _():
        sent(q2, s_send.at[10], mate)
        sent(p2, s_send.at[12], mate)
        last.wait_send()


def everything(scale, sw_hbm, sd_hbm, tw_hbm, td_hbm, tok_ref, v_hbm, u_hbm, conv_hbm, bias_hbm, rate_hbm,
               out_ref, v_ref, u_ref, sw_ref, sd_ref, tw_ref, td_ref, conv_ref, bias_ref, rate_ref, wbuf, ext, ext_t, proj,
               forward_scratch, backward_scratch, rows_ref, row1_ref, row2_ref, colq_ref, colqd_ref, zp_ref, reduce_scratch,
               s_in, gather_sems, forward_sems, backward_sems, reduce_sems):
    entered = enter()
    pairs = [
        (sw_hbm, sw_ref), (sd_hbm, sd_ref), (tw_hbm, tw_ref), (td_hbm, td_ref), (tok_ref, ext.at[pl.ds(0, L)]),
        (v_hbm, v_ref), (u_hbm, u_ref), (conv_hbm, conv_ref), (bias_hbm, bias_ref), (rate_hbm, rate_ref),
    ]
    local = [pltpu.make_async_copy(src, dst, s_in.at[i]) for i, (src, dst) in enumerate(pairs)]
    for c in local:
        c.start()
    x, y, z, k, _ = place()
    ext[L + HALO :, :] = jnp.zeros((ext.shape[0] - L - HALO, ext.shape[1]), BF16)
    for c in local[0:4]:
        c.wait()
    wbuf[x, y, z, k, :, 0:128] = sw_ref[...]
    wbuf[x, y, z, k, :, 128:256] = sd_ref[...]
    rows = sw_ref.shape[0]
    wbuf[x, y, z, k, :, 256:384] = jnp.concatenate(
        [tw_ref[...].astype(F32), td_ref[...].astype(F32), jnp.zeros((rows, 128 - 2 * H), F32)], 1
    ).astype(BF16)
    local[4].wait()
    ext_t[:, 0:L] = ext[0:L, :].T
    for c in local[5:]:
        c.wait()
    entered()
    drain_gather = gather(wbuf, ext, ext_t, proj, tok_ref, *gather_sems)

    rate = rate_ref[...]
    ft = features(lambda row, lane, lanes: proj[row : row + L, lane : lane + lanes], conv_ref[...], bias_ref[...], rate)
    wts = weights_of(ft)
    pp = pair_parts(ft)
    we, wde, es, eds, eu, edu = streams(wts, v_ref[...], u_ref[...])
    fw = Half(*forward_scratch, None, *forward_sems)
    bw = Half(*backward_scratch, fw, *backward_sems)
    row = iota((8, HP), 0)
    dec = jnp.where(row == 0, es[L - 1 :, :], jnp.where(row == 1, eds[L - 1 :, :], 0.0))
    states = forward_states(pp, we, wde)
    for half in range(2):
        lanes = slice(HALF * half, HALF * half + HALF)
        fw.loc[half, 0:128, :] = states[:, lanes]
        fw.loc[half, 128:136, :] = dec[:, lanes]
    fw.to_mate().start()
    states = backward_states(pp, eu, edu)
    for half in range(2):
        bw.loc[half] = states[:, HALF * half : HALF * half + HALF]
    bw.to_mate().start()

    fw.to_mate().wait_recv()
    one0, one1 = fw.cores()
    a0, ad0 = one0[128:129], one0[129:130]
    a1, ad1 = one1[128:129], one1[129:130]
    a, ad = a0 * a1, ad0 * a1 + a0 * ad1
    fw.start_one(
        a1 * one0[0:64] + one1[0:64], a1 * one0[64:128] + ad1 * one0[0:64] + one1[64:128], a, ad
    )
    bw.to_mate().wait_recv()
    one0, one1 = bw.cores()
    bw.start_one(
        a0 * one1[0:64] + one0[0:64], a0 * one1[64:128] + ad0 * one1[0:64] + one0[64:128], a, ad
    )

    def tile(ref):
        return lambda i: ref[:, pl.ds(pl.multiple_of(i * 128, 128), 128)]

    g, gd = intra_setup(ft, pp, rows_ref, row1_ref, row2_ref)
    zero = jnp.zeros((L, L), F32)

    def block_terms(first, last, carry):
        return intra(
            ft, g, gd, tile(v_ref), tile(u_ref), rows_ref, row1_ref, row2_ref, colq_ref, colqd_ref, first, last, carry
        )

    carry = block_terms(0, 7, (zero, zero))
    fw.row_total(0)
    carry = block_terms(7, 8, carry)
    fw.row_total(1)
    fw.start_two(0)
    bw.row_total(0)
    fw.start_two(1)
    bw.row_total(1)
    bw.start_two(0)
    pairs = intra_pairs(pp, *carry)
    bw.start_two(1)
    e_split = split(jnp.concatenate([eu, edu], 0))
    w_split = split(jnp.concatenate([we, wde], 0))
    fw.wait_two(0)
    fw.wait_two(1)
    fw.assemble(a0, ad0, fw.cores()[0], True)
    fw.back_in().wait_recv()
    xf = jnp.concatenate([fw.st[0], fw.st[1]], 1)
    from_forward = finish_forward(pp, e_split, u_ref[...], xf)
    bw.wait_two(0)
    bw.wait_two(1)
    bw.assemble(a1, ad1, bw.cores()[1], False)
    bw.back_in().wait_recv()
    xb = jnp.concatenate([bw.st[0], bw.st[1]], 1)
    from_backward = finish_backward(pp, w_split, v_ref[...], xb)
    dz, dzd, dq, dqd = finish(
        ft, wts, pairs, row1_ref[...], row2_ref[...], colq_ref[...], colqd_ref[...],
        from_forward, from_backward, xf, xb, rate, scale,
    )
    zp_ref[...] = jnp.zeros(zp_ref.shape, F32)
    zp_ref[HALO : HALO + L, 0:128] = dz
    zp_ref[HALO : HALO + L, 128:256] = dzd
    conv = conv_ref[...]

    def spread(first_row, count, lanes):
        total = conv[0:1, :] * zp_ref[first_row + 3 : first_row + 3 + count, lanes]
        for tap in range(1, KCONV):
            total = total + conv[tap : tap + 1, :] * zp_ref[first_row + 3 - tap : first_row + 3 - tap + count, lanes]
        return total

    pad = jnp.zeros((128 - HALO, 128), F32)
    columns = []
    for half in range(2):
        lanes = slice(128 * half, 128 * half + 128)
        columns.append(jnp.concatenate([spread(HALO, L, lanes), spread(0, HALO, lanes), pad], 0))
    both = jnp.concatenate([dq, dqd, dq, dqd], 1)
    columns.append(jnp.concatenate([both, jnp.zeros((128, 128), F32)], 0))
    dp = jnp.concatenate(columns, 1)
    drain_gather()
    fw.drain()
    bw.drain()
    reduce(dp, ext_t, *reduce_scratch, *reduce_sems, out_ref)


def split_outputs(sums_ref, o_sel, o_step, o_selh, o_steph):
    o_sel[...] = sums_ref[:, 0:128]
    o_selh[...] = sums_ref[:, 128:256]
    o_step[...] = sums_ref[:, 256 : 256 + H]
    o_steph[...] = sums_ref[:, 256 + H : 256 + 2 * H]


def vmem(shape, dtype=F32):
    return pltpu.VMEM(shape, dtype)


def dma(*shape):
    return pltpu.SemaphoreType.DMA(shape)


def body(tokens, values, cotangent, sel_weight, step_weight, sel_dir, step_dir, conv_weight, step_bias, decay_rate):
    own_tokens, v, u = tokens[0], values[0], cotangent[0]
    depth = own_tokens.shape[1]
    rows = sel_weight.shape[0]
    scale = 1.0 / math.sqrt(NX * CHIPS * 2 * L)
    spec = pl.BlockSpec(memory_space=pltpu.VMEM)
    hbm = pl.BlockSpec(memory_space=pl.ANY)
    tiles = NX * NY * NZ
    reduce_scratch = (
        [vmem((2, NX, NY, NZ, 2, 8, 128)), vmem((2, NX, NY, NZ // 2, 8, 128)),
         vmem((2, NX, NY, NZ, 8, 128)), vmem((NX, NY, NZ // 2, 8, 128))]
        + [vmem((NX, NY, NZ, 8, 128))] * 2 + [vmem((NX, NY, NZ // 2, 8, 128))]
        + [vmem((3, NY, NZ, 8, 128)), vmem((3, NX, NZ, 8, 128)), vmem((NZ, NX, NY, 8, 128))]
        + [vmem((NY, NZ, 8, 128)), vmem((NX, NZ, 8, 128)), vmem((NX, NY, 8, 128))]
        + [vmem((3, NZ, 8, 128)), vmem((7, NX, 8, 128)), vmem((3, NY, 8, 128))]
        + [vmem((NZ, 8, 128)), vmem((NX, 8, 128)), vmem((NY, 8, 128))]
        + [vmem((7, 8, 128)), vmem((3, 8, 128)), vmem((3, 8, 128))]
        + [vmem((8, 128)), vmem((8, 128))]
    )

    def scan_scratch():
        return (
            [vmem((2, NZ, LANES, 24, 128))] * 2 + [vmem((2, LANES, 24, 128)), vmem((2, NY, LANES, 24, 128))]
            + [vmem((2, NZ, LANES, 16, 128))] * 2 + [vmem((128, HALF)), vmem((2, 128, HALF))]
        )

    scratch = [
        vmem((L, HP), BF16), vmem((L, HP), BF16),
        vmem((rows, 128), BF16), vmem((rows, 128), BF16), vmem((rows, H), BF16), vmem((rows, H), BF16),
        vmem((KCONV, 128)), vmem((1, H)), vmem((1, H)),
        vmem((NX, NY, NZ, 2, rows, WIDE), BF16),
        vmem((2 * L, depth), BF16), vmem((depth, 2 * L), BF16), vmem((HALO + L, WIDE)),
        [vmem((2, 136, HALF)), vmem((136, HALF))] + scan_scratch(),
        [vmem((2, 128, HALF)), vmem((128, HALF))] + scan_scratch(),
        vmem((3 * H, L)), vmem((L, L)), vmem((L, L)), vmem((H, L)), vmem((H, L)), vmem((HALO + L + 8, 256)),
        reduce_scratch,
        dma(10),
        [dma(5), dma(), dma(), dma(NX * NY), dma(NX * NY)],
        [dma(5), dma(2), dma(2), dma(2), dma(2)],
        [dma(5), dma(2), dma(2), dma(2), dma(2)],
        [dma(15), dma(2 * NX), dma(3), dma(3), dma(3), dma()],
    ]
    sums = pl.pallas_call(
        functools.partial(everything, scale),
        out_shape=jax.ShapeDtypeStruct((rows, WIDE), F32),
        in_specs=[hbm] * 10,
        out_specs=spec,
        scratch_shapes=scratch,
        compiler_params=pltpu.CompilerParams(
            vmem_limit_bytes=VMEM_LIMIT, collective_id=0, has_side_effects=True
        ),
    )(sel_weight, sel_dir, step_weight, step_dir, own_tokens, v, u, conv_weight, step_bias[None, :], decay_rate[None, :])
    return pl.pallas_call(
        split_outputs,
        out_shape=[
            jax.ShapeDtypeStruct((rows, 128), F32), jax.ShapeDtypeStruct((rows, H), F32),
            jax.ShapeDtypeStruct((rows, 128), F32), jax.ShapeDtypeStruct((rows, H), F32),
        ],
        in_specs=[spec],
        out_specs=[spec] * 4,
    )(sums)


def solution(mesh):
    shards = P(("dp", "seq"), None)
    stream = P("dp", "seq", None)
    return jax.shard_map(
        body,
        mesh=mesh,
        in_specs=(stream, stream, stream, shards, shards, shards, shards, P(), P(), P()),
        out_specs=(shards, shards, shards, shards),
        check_vma=False,
    )
```

```python
import functools
import math

import jax
import jax.numpy as jnp
from jax import lax
from jax.experimental import pallas as pl
from jax.experimental.pallas import tpu as pltpu
from jax.sharding import PartitionSpec as P

N = 64
P_SIZE = 32
H = 32
KCONV = 4
L = 128
HALO = 16
HP = H * P_SIZE
HALF = HP // 2
WIDE = 384
NX, NY, NZ = 4, 4, 8
CHIPS = NY * NZ
MESH = pl.DeviceIdType.MESH
F32 = jnp.float32
BF16 = jnp.bfloat16
VMEM_LIMIT = 56 * 1024 * 1024


def roll64(x):
    return pltpu.roll(x, 64, 1)


def split(x):
    high = x.astype(BF16)
    low = (x - high.astype(F32)).astype(BF16)
    return high, low


def split3(x):
    high = x.astype(BF16)
    rest = x - high.astype(F32)
    mid = rest.astype(BF16)
    low = (rest - mid.astype(F32)).astype(BF16)
    return high, mid, low


def dg(a, b, ca, cb):
    return lax.dot_general(a, b, (((ca,), (cb,)), ((), ())), preferred_element_type=F32)


def dot_split(a, b, ca, cb):
    return dot_parts(split(a), split(b), ca, cb)


def dot_parts(a, b, ca, cb):
    (ah, al), (bh, bl) = a, b
    return dg(ah, bh, ca, cb) + (dg(ah, bl, ca, cb) + dg(al, bh, ca, cb))


def dot_left(a, b, ca, cb):
    ah, al = split(a)
    return dg(ah, b, ca, cb) + dg(al, b, ca, cb)


def iota(shape, dim):
    return lax.broadcasted_iota(jnp.int32, shape, dim)


def low_lanes():
    return iota((L, 128), 1) < 64


def head_spread():
    return (iota((H, HP), 0) == iota((H, HP), 1) // P_SIZE).astype(F32).astype(BF16)


def triangle(reverse):
    row, column = iota((L, L), 0), iota((L, L), 1)
    keep = (column >= row) if reverse else (row >= column)
    return keep.astype(F32).astype(BF16)


def cumulate(x, reverse):
    tri = triangle(reverse)
    a, b, c = split3(x)
    return dg(tri, a, 1, 0) + (dg(tri, b, 1, 0) + dg(tri, c, 1, 0))


def features(proj, conv2, bias, rate):
    z = jnp.zeros((L, 128), F32)
    zd = jnp.zeros((L, 128), F32)
    for k in range(KCONV):
        rows = HALO - (KCONV - 1) + k
        z = z + conv2[k : k + 1, :128] * proj(rows, 0, 128)
        zd = zd + conv2[k : k + 1, :128] * proj(rows, 128, 128)
    sg = jax.nn.sigmoid(z)
    act = z * sg
    first = sg * (1.0 + z * (1.0 - sg))
    second = sg * (1.0 - sg) * (2.0 + z * (1.0 - 2.0 * sg))
    actd = first * zd
    steps = proj(HALO, 256, 128)
    q = steps[:, :H] + bias
    qd = steps[:, H : 2 * H]
    delta = jnp.maximum(q, 0.0) + jnp.log1p(jnp.exp(-jnp.abs(q)))
    sq = jax.nn.sigmoid(q)
    deltad = sq * qd
    cum = cumulate(-(delta * rate), False)
    cumd = cumulate(-(deltad * rate), False)
    return dict(
        zd=zd, act=act, actd=actd, first=first, second=second,
        qd=qd, sq=sq, delta=delta, deltad=deltad, cum=cum, cumd=cumd,
    )


def weights_of(ft):
    cum, cumd = ft["cum"], ft["cumd"]
    last, lastd = cum[L - 1 :, :], cumd[L - 1 :, :]
    e = jnp.exp(cum)
    ed = e * cumd
    f = jnp.exp(last - cum)
    fd = f * (lastd - cumd)
    w = f * ft["delta"]
    wd = fd * ft["delta"] + f * ft["deltad"]
    return e, ed, f, fd, w, wd


def pair_parts(ft):
    act, actd = ft["act"], ft["actd"]
    actr, actdr = roll64(act), roll64(actd)
    m = low_lanes()
    return dict(
        b_bd=jnp.where(m, act, actdr),
        o_b=jnp.where(m, 0.0, actr),
        c_cd=jnp.where(m, actr, actd),
        o_c=jnp.where(m, 0.0, act),
        b_o=jnp.where(m, act, 0.0),
        bd_b=jnp.where(m, actd, actr),
        c_o=jnp.where(m, actr, 0.0),
        cd_c=jnp.where(m, actdr, act),
        b_c=act,
        c_b=actr,
    )


def spread_rows(rows):
    return dot_left(rows, head_spread(), 1, 0)


def streams(wts, values, cotangent):
    e, ed, _, _, w, wd = wts
    v = values.astype(F32)
    u = cotangent.astype(F32)
    we = spread_rows(w) * v
    wde = spread_rows(wd) * v
    es = spread_rows(e)
    eds = spread_rows(ed)
    return we, wde, es, eds, es * u, eds * u


def forward_states(pp, we, wde):
    left = jnp.concatenate([pp["b_bd"], pp["o_b"]], 0)
    return dot_split(left, jnp.concatenate([we, wde], 0), 0, 0)


def backward_states(pp, eu, edu):
    left = jnp.concatenate([pp["c_cd"], pp["o_c"]], 0)
    return dot_split(left, jnp.concatenate([eu, edu], 0), 0, 0)


def intra_setup(ft, pp, rows_ref, row1_ref, row2_ref):
    g = dot_split(pp["c_o"], pp["b_c"], 1, 1)
    gd = dot_split(pp["cd_c"], pp["b_bd"], 1, 1)
    eta = ft["deltad"] - ft["delta"] * ft["cumd"]
    rows_ref[0:H, :] = ft["cum"].T
    rows_ref[H : 2 * H, :] = ft["delta"].T
    rows_ref[2 * H : 3 * H, :] = eta.T
    row1_ref[...] = jnp.zeros((L, L), F32)
    row2_ref[...] = jnp.zeros((L, L), F32)
    return g, gd


def intra(ft, g, gd, v_of, u_of, rows_ref, row1_ref, row2_ref, colq_ref, colqd_ref, first, last, carry):
    parts = split3(ft["cum"])
    partsd = split(ft["cumd"])
    row, lane = iota((L, L), 0), iota((L, L), 1)
    causal = row >= lane

    def one(i, carry):
        dgm, dgd = carry
        pick = (iota((H, 512), 0) == (4 * i + iota((H, 512), 1) // 128)).astype(F32).astype(BF16)
        ct4 = dg(parts[0], pick, 1, 0) + (dg(parts[1], pick, 1, 0) + dg(parts[2], pick, 1, 0))
        cd4 = dg(partsd[0], pick, 1, 0) + dg(partsd[1], pick, 1, 0)
        v_tile, u_tile = v_of(i), u_of(i)
        row1, row2 = row1_ref[...], row2_ref[...]
        for j in range(4):
            h = 4 * i + j
            mask = (iota((L, 128), 1) // P_SIZE == j).astype(F32)
            w = dg((u_tile.astype(F32) * mask).astype(BF16), v_tile, 1, 1)
            ct = ct4[:, 128 * j : 128 * j + 128]
            cd = cd4[:, 128 * j : 128 * j + 128]
            cs = rows_ref[pl.ds(h, 1), :]
            ds = rows_ref[pl.ds(H + h, 1), :]
            et = rows_ref[pl.ds(2 * H + h, 1), :]
            x = jnp.exp(jnp.where(causal, ct - cs, -1e30)) * w
            xd = x * ds
            dgm = dgm + xd
            dgd = dgd + (x * et + cd * xd)
            q = x * g
            xgd = x * gd
            colq_ref[pl.ds(h, 1), :] = jnp.sum(q, axis=0, keepdims=True)
            colqd_ref[pl.ds(h, 1), :] = jnp.sum(xgd + q * cd, axis=0, keepdims=True)
            r1 = jnp.sum(q * ds, axis=1, keepdims=True)
            r2 = jnp.sum(xgd * ds + q * et, axis=1, keepdims=True)
            here = lane == h
            row1 = jnp.where(here, r1, row1)
            row2 = jnp.where(here, r2, row2)
        row1_ref[...] = row1
        row2_ref[...] = row2
        return dgm, dgd

    return lax.fori_loop(first, last, one, carry)


def intra_pairs(pp, dgm, dgd):
    return (
        dot_split(dgm, pp["b_bd"], 1, 0),
        dot_split(dgd, pp["b_c"], 1, 0),
        dot_split(dgm, pp["c_cd"], 0, 0),
        dot_split(dgd, pp["c_b"], 0, 0),
    )


def head_sums(x):
    return dot_left(x, head_spread(), 1, 1)


def finish_forward(pp, e_split, cotangent, xf):
    u = cotangent.astype(F32)
    x_split = split(xf)
    zz = dot_parts(split(jnp.concatenate([pp["c_o"], pp["cd_c"]], 0)), x_split, 1, 0)
    return head_sums(zz[:L] * u), head_sums(zz[L:] * u), dot_parts(e_split, x_split, 1, 1)


def finish_backward(pp, w_split, values, xb):
    v = values.astype(F32)
    x_split = split(xb)
    yy = dot_parts(split(jnp.concatenate([pp["b_o"], pp["bd_b"]], 0)), x_split, 1, 0)
    return head_sums(yy[:L] * v), head_sums(yy[L:] * v), dot_parts(w_split, x_split, 1, 1)


def finish(ft, wts, pairs, row1, row2, colq, colqd, from_forward, from_backward, xf, xb, rate, scale):
    e, ed, f, fd, w, wd = wts
    g, gdot, pc = from_forward
    kk, kdot, pb = from_backward
    kap = jnp.sum(xb[:64] * xf[:64], axis=0, keepdims=True)
    kapd = jnp.sum(xb[64:] * xf[:64] + xb[:64] * xf[64:], axis=0, keepdims=True)
    both = head_sums(jnp.concatenate([jnp.broadcast_to(kap, (8, HP)), jnp.broadcast_to(kapd, (8, HP))], 0))
    kap, kapd = both[0:1], both[8:9]

    m = low_lanes()
    t1, t2, t3, t4 = pairs
    pair_c = t1 + pc[:L] + jnp.where(m, 0.0, roll64(t2 + pc[L:]))
    pair_b = t3 + pb[:L] + jnp.where(m, 0.0, roll64(t4 + pb[L:]))
    dact = jnp.where(m, pair_b, roll64(pair_c))
    dactd = jnp.where(m, roll64(pair_b), pair_c)
    dz = scale * (ft["first"] * dact)
    dzd = scale * (ft["second"] * ft["zd"] * dact + ft["first"] * dactd)

    delta, deltad, cum, cumd = ft["delta"], ft["deltad"], ft["cum"], ft["cumd"]
    colq, colqd = colq.T, colqd.T
    colqd = colqd - cumd * colq
    row1, row2 = row1[:, :H], row2[:, :H]
    row2 = row2 + cumd * row1
    wk = w * kk
    wkd = wd * kk + w * kdot
    dc = row1 - delta * colq + e * g - wk
    dcd = row2 - (deltad * colq + delta * colqd) + ed * g + e * gdot - wkd
    el, edl = e[L - 1 :, :], ed[L - 1 :, :]
    extra = el * kap + jnp.sum(wk, axis=0, keepdims=True)
    extrad = edl * kap + el * kapd + jnp.sum(wkd, axis=0, keepdims=True)
    ddelta = colq + f * kk - rate * (cumulate(dc, True) + extra)
    ddeltad = colqd + fd * kk + f * kdot - rate * (cumulate(dcd, True) + extrad)
    sq = ft["sq"]
    dq = scale * (sq * ddelta)
    dqd = scale * (sq * (1.0 - sq) * ft["qd"] * ddelta + sq * ddeltad)
    return dz, dzd, dq, dqd


def place():
    x = lax.axis_index("dp")
    s = lax.axis_index("seq")
    chip = s // 2
    return x, chip // NZ, lax.rem(chip, NZ), lax.rem(s, 2), chip


def device(x, y, z, k):
    return (x, (y * NZ + z) * 2 + k)


def remote(src, dst, send_sem, recv_sem, dev):
    return pltpu.make_async_remote_copy(
        src_ref=src, dst_ref=dst, send_sem=send_sem, recv_sem=recv_sem,
        device_id=dev, device_id_type=MESH,
    )


def arrived(dst, sem, dev):
    remote(dst, dst, sem, sem, dev).wait_recv()


def sent(src, sem, dev):
    remote(src, src, sem, sem, dev).wait_send()


FAR4 = (2, 1, 3)
LANES = HALF // 256
FAR8 = (4, 3, 5, 2, 6, 1, 7)


def enter():
    x, y, z, k, chip = place()
    s = 2 * chip + k
    seq = CHIPS * 2
    partners = [device(x, y, lax.rem(z + d, NZ), k) for d in FAR8]
    partners += [device(lax.rem(x + d, NX), y, z, k) for d in FAR4]
    partners += [device(x, lax.rem(y + d, NY), z, k) for d in FAR4]
    partners += [(x, lax.rem(s + 1, seq)), (x, lax.rem(s + seq - 1, seq)), device(x, y, z, 1 - k)]
    barrier = pltpu.get_barrier_semaphore()
    for dev in partners:
        pl.semaphore_signal(barrier, inc=1, device_id=dev, device_id_type=MESH)
    return lambda: pl.semaphore_wait(barrier, len(partners))


def gather(wbuf, ext, ext_t, proj, tok_ref, s_send, s_halo, s_z, s_slab, s_swap):
    x, y, z, k, chip = place()
    s = 2 * chip + k
    mate = device(x, y, z, 1 - k)
    own = wbuf.at[x, y, z, k]
    for d in FAR8:
        remote(own, own, s_send.at[0], s_z, device(x, y, lax.rem(z + d, NZ), k)).start()
    halo = remote(
        tok_ref.at[pl.ds(L - HALO, HALO)], ext.at[pl.ds(L, HALO)], s_send.at[4], s_halo,
        (x, lax.rem(s + 1, 2 * CHIPS)),
    )
    halo.start()
    arrived(wbuf.at[x, y, pl.ds(0, NZ - 1), k], s_z, mate)

    def slab_copy(sx, sy, tx, ty, sem):
        ref = wbuf.at[sx, sy, :, k]
        return remote(ref, ref, s_send.at[sem], s_slab.at[sx * NY + sy], device(tx, ty, z, k))

    def swap(sx, sy, kk):
        ref = wbuf.at[sx, sy, :, kk]
        return remote(ref, ref, s_send.at[3], s_swap.at[sx * NY + sy], mate)

    def near(d):
        return lax.rem(x + d * k, NX), lax.rem(y + d * (1 - k), NY)

    def far(d):
        return lax.rem(x + d * (1 - k), NX), lax.rem(y + d * k, NY)

    for d in FAR4:
        slab_copy(x, y, *near(d), 1).start()
    for d in FAR4:
        slab_copy(x, y, *far(d), 2).start()
    swap(x, y, k).start()
    for d in (1, 3, 2):
        sx, sy = near(d)
        slab_copy(sx, sy, x, y, 1).wait_recv()
        for t in FAR4:
            slab_copy(sx, sy, *far(t), 2).start()
        swap(sx, sy, k).start()
    halo.wait_recv()

    @pl.when(s == 0)
    def _():
        ext[L : L + HALO, :] = jnp.zeros((HALO, ext.shape[1]), BF16)

    ext_t[:, L:] = ext[L:, :].T
    for e in (0, 1, 3, 2):
        for d in (1, 3, 2):
            fx, fy = far(d)
            sx = lax.rem(fx + e * k, NX)
            sy = lax.rem(fy + e * (1 - k), NY)
            slab_copy(sx, sy, x, y, 2).wait_recv()
            swap(sx, sy, k).start()
    depth = ext.shape[1] // NX
    total = jnp.zeros((L + HALO, WIDE), F32)
    for d in range(NX):
        sx = lax.rem(x + d, NX)
        for sy in range(NY):
            swap(sx, sy, 1 - k).wait_recv()
        at = pl.multiple_of(sx * depth, depth)
        weights = wbuf[sx].astype(F32).reshape(depth, WIDE).astype(BF16)
        total = total + dg(ext[0 : L + HALO, pl.ds(at, depth)], weights, 1, 0)
    proj[HALO:, :] = total[0:L]
    proj[0:HALO, :] = total[L:]

    def drain():
        sent(wbuf.at[0, 0, pl.ds(0, NZ - 1), 0], s_send.at[0], mate)
        sent(wbuf.at[0, pl.ds(0, NY - 1), :, 0], s_send.at[1], mate)
        sent(wbuf.at[pl.ds(0, NX - 1), :, :, 0], s_send.at[2], mate)
        sent(wbuf.at[:, :, :, 0], s_send.at[3], mate)
        halo.wait_send()

    return drain


class Half:
    def __init__(self, loc, part, snd, rcv, tot, tots, snd2, rcv2, other, st, decays, s_send, s_mate, s_one, s_row, s_two):
        self.loc, self.part, self.snd, self.rcv, self.tot, self.tots = loc, part, snd, rcv, tot, tots
        self.snd2, self.rcv2, self.other, self.st = snd2, rcv2, other, st
        self.reverse = decays is not None
        self.decays = decays if self.reverse else self
        self.rows = pl.ds(0, 16 if self.reverse else 18)
        self.s_send, self.s_mate, self.s_one, self.s_row, self.s_two = s_send, s_mate, s_one, s_row, s_two
        self.x, self.y, self.z, self.k, self.chip = place()
        self.mate = device(self.x, self.y, self.z, 1 - self.k)
        self.first = self.k == 0

    def to_mate(self):
        return remote(self.loc.at[1 - self.k], self.part, self.s_send.at[0], self.s_mate.at[0], self.mate)

    def back(self):
        return remote(self.other, self.st.at[self.k], self.s_send.at[4], self.s_mate.at[1], self.mate)

    def back_in(self):
        return remote(self.other, self.st.at[1 - self.k], self.s_send.at[4], self.s_mate.at[1], self.mate)

    def cores(self):
        own, other = self.loc[self.k], self.part[...]
        return jnp.where(self.first, own, other), jnp.where(self.first, other, own)

    def start_one(self, s, t, a, ad):
        for h in range(2):
            for j in range(NZ):
                rows = slice(8 * j, 8 * j + 8)
                for i in range(LANES):
                    at = 128 * (LANES * h + i)
                    lanes = slice(at, at + 128)
                    self.snd[h, j, i, 0:8] = s[rows, lanes]
                    self.snd[h, j, i, 8:16] = t[rows, lanes]
                    if not self.reverse:
                        self.snd[h, j, i, 16:17] = a[:, lanes]
                        self.snd[h, j, i, 17:18] = ad[:, lanes]
            for d in FAR8:
                c = lax.rem(self.z + d, NZ)
                dev = device(self.x, self.y, c, self.k)
                remote(
                    self.snd.at[h, c, :, self.rows], self.rcv.at[h, self.z, :, self.rows],
                    self.s_send.at[1], self.s_one.at[h], dev,
                ).start()
            self.rcv[h, self.z] = self.snd[h, self.z]

    @staticmethod
    def step(carry, ref, decays, c):
        s, t = carry
        a, ad = decays[*c, :, 16:17, :], decays[*c, :, 17:18, :]
        return a * s + ref[*c, :, 0:8, :], a * t + (ad * s + ref[*c, :, 8:16, :])

    def order(self, count):
        return range(count - 1, -1, -1) if self.reverse else range(count)

    def row_total(self, h):
        arrived(self.rcv.at[h, pl.ds(0, NZ - 1), :, self.rows], self.s_one.at[h], self.mate)
        carry = (jnp.zeros((LANES, 8, 128), F32),) * 2
        for c in self.order(NZ):
            carry = self.step(carry, self.rcv, self.decays.rcv, (h, c))
        self.tot[h, :, 0:8, :], self.tot[h, :, 8:16, :] = carry
        if not self.reverse:
            a, ad = self.rcv[h, 0, :, 16:17, :], self.rcv[h, 0, :, 17:18, :]
            for c in range(1, NZ):
                b, bd = self.rcv[h, c, :, 16:17, :], self.rcv[h, c, :, 17:18, :]
                a, ad = a * b, ad * b + a * bd
            self.tot[h, :, 16:17, :], self.tot[h, :, 17:18, :] = a, ad
        for d in FAR4:
            dev = device(self.x, lax.rem(self.y + d, NY), self.z, self.k)
            remote(
                self.tot.at[h, :, self.rows], self.tots.at[h, self.y, :, self.rows],
                self.s_send.at[2], self.s_row.at[h], dev,
            ).start()
        self.tots[h, self.y] = self.tot[h]

    def start_two(self, h):
        arrived(self.tots.at[h, pl.ds(0, NY - 1), :, self.rows], self.s_row.at[h], self.mate)
        carry = (jnp.zeros((LANES, 8, 128), F32),) * 2
        for row in self.order(NY):
            after = self.step(carry, self.tots, self.decays.tots, (h, row))
            ahead = (row > self.y) if self.reverse else (row < self.y)
            carry = tuple(jnp.where(ahead, new, old) for new, old in zip(after, carry))
        for c in self.order(NZ):
            self.snd2[h, c, :, 0:8, :], self.snd2[h, c, :, 8:16, :] = carry
            carry = self.step(carry, self.rcv, self.decays.rcv, (h, c))
        for d in FAR8:
            c = lax.rem(self.z + d, NZ)
            dev = device(self.x, self.y, c, self.k)
            remote(self.snd2.at[h, c], self.rcv2.at[h, self.z], self.s_send.at[3], self.s_two.at[h], dev).start()
        self.rcv2[h, self.z] = self.snd2[h, self.z]

    def wait_two(self, h):
        arrived(self.rcv2.at[h, pl.ds(0, NZ - 1)], self.s_two.at[h], self.mate)

    def assemble(self, a, ad, base, base_first):
        s, t = (
            jnp.concatenate(
                [jnp.concatenate([self.rcv2[i // LANES, j, i % LANES, rows] for j in range(NZ)], 0) for i in range(2 * LANES)], 1
            )
            for rows in (slice(0, 8), slice(8, 16))
        )
        next_s = a * s + base[0:64]
        next_t = a * t + ad * s + base[64:128]
        mine_is_base = self.first if base_first else jnp.logical_not(self.first)
        self.other[0:64, :] = jnp.where(mine_is_base, next_s, s)
        self.other[64:128, :] = jnp.where(mine_is_base, next_t, t)
        self.back().start()
        self.st[self.k, 0:64, :] = jnp.where(mine_is_base, s, next_s)
        self.st[self.k, 64:128, :] = jnp.where(mine_is_base, t, next_t)

    def drain(self):
        self.to_mate().wait_send()
        sent(self.snd.at[:, pl.ds(0, NZ - 1), :, self.rows], self.s_send.at[1], self.mate)
        sent(self.tots.at[:, pl.ds(0, NY - 1), :, self.rows], self.s_send.at[2], self.mate)
        sent(self.snd2.at[:, pl.ds(0, NZ - 1)], self.s_send.at[3], self.mate)
        self.back().wait_send()


def reduce(dp, ext_t, full, g2, m01, m2, a0, a1, a2, r0, r1, r2, b0, b1, b2, q0, q1, q2, c0, c1, c2, p0, p1, p2,
           e2, s_send, s_mate, s_a, s_b, s_c, s_e, out_ref):
    x, y, z, k, chip = place()
    mate = device(x, y, z, 1 - k)
    holder = lax.rem(z, 2) == k

    def x_to(d):
        return device(lax.rem(x + d, NX), y, z, k)

    def y_to(d):
        return device(x, lax.rem(y + d, NY), z, k)

    def z_to(d):
        return device(x, y, lax.rem(z + d, NZ), k)

    both = jnp.concatenate(split(dp), 1)
    low_half = iota((8, 128), 1) < 64
    block_rows = NY * NZ * 16

    order = FAR4 + (0,)

    def settle(i):
        xb = lax.rem(x + order[i], NX)
        arrived(m01.at[:, xb], s_mate.at[i], mate)
        a0[xb] = full[0, xb, :, :, k] + m01[0, xb]
        if i < NX - 1:
            remote(a0.at[xb], r0.at[i], s_send.at[2], s_a.at[0], x_to(order[i])).start()
        a1[xb] = full[1, xb, :, :, k] + m01[1, xb]
        for d in FAR4:
            remote(a1.at[xb, lax.rem(y + d, NY)], r1.at[d - 1, xb], s_send.at[3], s_a.at[1], y_to(d)).start()
        arrived(m2.at[xb], s_mate.at[NX + i], mate)
        a2[xb] = g2[k, xb] + m2[xb]

    for i in range(NX):
        xb = lax.rem(x + order[i], NX)
        rows = ext_t[pl.ds(pl.multiple_of(xb * block_rows, block_rows), block_rows), :]
        part = dg(rows, both, 1, 0)
        part = part[:, :WIDE] + part[:, WIDE:]
        full[0, xb] = part[:, 0:128].reshape(NY, NZ, 2, 8, 128)
        full[1, xb] = part[:, 128:256].reshape(NY, NZ, 2, 8, 128)
        steps = part[:, 256:384].reshape(NY, NZ // 2, 2, 2, 8, 128)
        for zp in range(2):
            g2[zp, xb] = jnp.where(low_half, steps[:, :, zp, 0], steps[:, :, zp, 1])
        for tile in range(2):
            remote(full.at[tile, xb, :, :, 1 - k], m01.at[tile, xb], s_send.at[0], s_mate.at[i], mate).start()
        remote(g2.at[1 - k, xb], m2.at[xb], s_send.at[1], s_mate.at[NX + i], mate).start()
        if i > 0:
            settle(i - 1)
    settle(NX - 1)

    zsend = []
    for i in range(NZ // 2):
        target = 2 * i + k
        gap = lax.rem(z - target + NZ, NZ)
        zsend.append((target != z, remote(a2.at[:, :, i], r2.at[gap], s_send.at[4 + i], s_a.at[2], device(x, y, target, k))))
        pl.when(zsend[-1][0])(zsend[-1][1].start)

    arrived(r0, s_a.at[0], mate)
    b0[...] = (a0[x] + r0[0]) + (r0[1] + r0[2])
    for d in FAR4:
        remote(b0.at[lax.rem(y + d, NY)], q0.at[d - 1], s_send.at[8], s_b.at[0], y_to(d)).start()
    arrived(r1, s_a.at[1], mate)
    b1[...] = (a1[:, y] + r1[0]) + (r1[1] + r1[2])
    for d in FAR4:
        remote(b1.at[lax.rem(x + d, NX)], q1.at[d - 1], s_send.at[9], s_b.at[1], x_to(d)).start()

    @pl.when(holder)
    def _():
        arrived(r2.at[pl.ds(1, NZ - 1)], s_a.at[2], mate)
        total = a2[:, :, z // 2] + ((r2[1] + r2[2]) + (r2[3] + r2[4]))
        b2[...] = total + ((r2[5] + r2[6]) + r2[7])
        for d in FAR4:
            remote(b2.at[lax.rem(x + d, NX)], q2.at[d - 1], s_send.at[10], s_b.at[2], x_to(d)).start()

    arrived(q0, s_b.at[0], mate)
    c0[...] = (b0[y] + q0[0]) + (q0[1] + q0[2])
    for d in FAR8:
        remote(c0.at[lax.rem(z + d, NZ)], p0.at[d - 1], s_send.at[11], s_c.at[0], z_to(d)).start()

    arrived(q1, s_b.at[1], mate)
    c1[...] = (b1[x] + q1[0]) + (q1[1] + q1[2])
    for d in FAR8:
        remote(c1.at[lax.rem(z + d, NZ)], p1.at[d - 1], s_send.at[13], s_c.at[1], z_to(d)).start()
    last = remote(c2.at[y], e2, s_send.at[14], s_e, mate)

    @pl.when(holder)
    def _():
        arrived(q2, s_b.at[2], mate)
        c2[...] = (b2[x] + q2[0]) + (q2[1] + q2[2])
        for d in FAR4:
            for core in range(2):
                row = lax.rem(y + d, NY)
                remote(c2.at[row], p2.at[d - 1], s_send.at[12], s_c.at[2], device(x, row, z, core)).start()
        last.start()
        e2[...] = c2[y]

    sent(m01, s_send.at[0], mate)
    sent(m2, s_send.at[1], mate)
    sent(r0, s_send.at[2], mate)
    sent(r1, s_send.at[3], mate)
    for used, copy in zsend:
        pl.when(used)(copy.wait_send)
    sent(q0, s_send.at[8], mate)
    sent(q1, s_send.at[9], mate)
    arrived(p0, s_c.at[0], mate)
    out_ref[:, 0:128] = c0[z] + ((p0[0] + p0[1]) + (p0[2] + p0[3])) + ((p0[4] + p0[5]) + p0[6])
    arrived(p1, s_c.at[1], mate)
    out_ref[:, 128:256] = c1[z] + ((p1[0] + p1[1]) + (p1[2] + p1[3])) + ((p1[4] + p1[5]) + p1[6])
    arrived(p2, s_c.at[2], mate)

    @pl.when(jnp.logical_not(holder))
    def _():
        remote(c2.at[y], e2, s_send.at[14], s_e, mate).wait_recv()

    steps = (e2[...] + p2[0]) + (p2[1] + p2[2])
    out_ref[:, 256:384] = jnp.where(k == 0, steps, roll64(steps))
    sent(p0, s_send.at[11], mate)
    sent(p1, s_send.at[13], mate)

    @pl.when(holder)
    def _():
        sent(q2, s_send.at[10], mate)
        sent(p1.at[pl.ds(0, 6)], s_send.at[12], mate)
        last.wait_send()


def everything(scale, sw_hbm, sd_hbm, tw_hbm, td_hbm, tok_ref, v_hbm, u_hbm, conv_hbm, bias_hbm, rate_hbm,
               out_ref, v_ref, u_ref, sw_ref, sd_ref, tw_ref, td_ref, conv_ref, bias_ref, rate_ref, wbuf, ext, ext_t, proj,
               forward_scratch, backward_scratch, rows_ref, row1_ref, row2_ref, colq_ref, colqd_ref, zp_ref, reduce_scratch,
               s_in, gather_sems, forward_sems, backward_sems, reduce_sems):
    entered = enter()
    pairs = [
        (sw_hbm, sw_ref), (sd_hbm, sd_ref), (tw_hbm, tw_ref), (td_hbm, td_ref), (tok_ref, ext.at[pl.ds(0, L)]),
        (v_hbm, v_ref), (u_hbm, u_ref), (conv_hbm, conv_ref), (bias_hbm, bias_ref), (rate_hbm, rate_ref),
    ]
    local = [pltpu.make_async_copy(src, dst, s_in.at[i]) for i, (src, dst) in enumerate(pairs)]
    for c in local:
        c.start()
    x, y, z, k, _ = place()
    ext[L + HALO :, :] = jnp.zeros((ext.shape[0] - L - HALO, ext.shape[1]), BF16)
    for c in local[0:4]:
        c.wait()
    wbuf[x, y, z, k, :, 0:128] = sw_ref[...]
    wbuf[x, y, z, k, :, 128:256] = sd_ref[...]
    rows = sw_ref.shape[0]
    wbuf[x, y, z, k, :, 256:384] = jnp.concatenate(
        [tw_ref[...].astype(F32), td_ref[...].astype(F32), jnp.zeros((rows, 128 - 2 * H), F32)], 1
    ).astype(BF16)
    local[4].wait()
    ext_t[:, 0:L] = ext[0:L, :].T
    for c in local[5:]:
        c.wait()
    entered()
    drain_gather = gather(wbuf, ext, ext_t, proj, tok_ref, *gather_sems)

    rate = rate_ref[...]
    ft = features(lambda row, lane, lanes: proj[row : row + L, lane : lane + lanes], conv_ref[...], bias_ref[...], rate)
    wts = weights_of(ft)
    pp = pair_parts(ft)
    we, wde, es, eds, eu, edu = streams(wts, v_ref[...], u_ref[...])
    fw = Half(*forward_scratch, None, *forward_sems)
    bw = Half(*backward_scratch, fw, *backward_sems)
    row = iota((8, HP), 0)
    dec = jnp.where(row == 0, es[L - 1 :, :], jnp.where(row == 1, eds[L - 1 :, :], 0.0))
    states = forward_states(pp, we, wde)
    for half in range(2):
        lanes = slice(HALF * half, HALF * half + HALF)
        fw.loc[half, 0:128, :] = states[:, lanes]
        fw.loc[half, 128:136, :] = dec[:, lanes]
    fw.to_mate().start()
    states = backward_states(pp, eu, edu)
    for half in range(2):
        bw.loc[half] = states[:, HALF * half : HALF * half + HALF]
    bw.to_mate().start()

    fw.to_mate().wait_recv()
    one0, one1 = fw.cores()
    a0, ad0 = one0[128:129], one0[129:130]
    a1, ad1 = one1[128:129], one1[129:130]
    a, ad = a0 * a1, ad0 * a1 + a0 * ad1
    fw.start_one(
        a1 * one0[0:64] + one1[0:64], a1 * one0[64:128] + ad1 * one0[0:64] + one1[64:128], a, ad
    )
    bw.to_mate().wait_recv()
    one0, one1 = bw.cores()
    bw.start_one(
        a0 * one1[0:64] + one0[0:64], a0 * one1[64:128] + ad0 * one1[0:64] + one0[64:128], a, ad
    )

    def tile(ref):
        return lambda i: ref[:, pl.ds(pl.multiple_of(i * 128, 128), 128)]

    g, gd = intra_setup(ft, pp, rows_ref, row1_ref, row2_ref)
    zero = jnp.zeros((L, L), F32)

    def block_terms(first, last, carry):
        return intra(
            ft, g, gd, tile(v_ref), tile(u_ref), rows_ref, row1_ref, row2_ref, colq_ref, colqd_ref, first, last, carry
        )

    carry = block_terms(0, 7, (zero, zero))
    fw.row_total(0)
    carry = block_terms(7, 8, carry)
    fw.row_total(1)
    fw.start_two(0)
    bw.row_total(0)
    fw.start_two(1)
    bw.row_total(1)
    bw.start_two(0)
    pairs = intra_pairs(pp, *carry)
    bw.start_two(1)
    e_split = split(jnp.concatenate([eu, edu], 0))
    w_split = split(jnp.concatenate([we, wde], 0))
    fw.wait_two(0)
    fw.wait_two(1)
    fw.assemble(a0, ad0, fw.cores()[0], True)
    fw.back_in().wait_recv()
    xf = jnp.concatenate([fw.st[0], fw.st[1]], 1)
    from_forward = finish_forward(pp, e_split, u_ref[...], xf)
    bw.wait_two(0)
    bw.wait_two(1)
    bw.assemble(a1, ad1, bw.cores()[1], False)
    bw.back_in().wait_recv()
    xb = jnp.concatenate([bw.st[0], bw.st[1]], 1)
    from_backward = finish_backward(pp, w_split, v_ref[...], xb)
    dz, dzd, dq, dqd = finish(
        ft, wts, pairs, row1_ref[...], row2_ref[...], colq_ref[...], colqd_ref[...],
        from_forward, from_backward, xf, xb, rate, scale,
    )
    zp_ref[...] = jnp.zeros(zp_ref.shape, F32)
    zp_ref[HALO : HALO + L, 0:128] = dz
    zp_ref[HALO : HALO + L, 128:256] = dzd
    conv = conv_ref[...]

    def spread(first_row, count, lanes):
        total = conv[0:1, :] * zp_ref[first_row + 3 : first_row + 3 + count, lanes]
        for tap in range(1, KCONV):
            total = total + conv[tap : tap + 1, :] * zp_ref[first_row + 3 - tap : first_row + 3 - tap + count, lanes]
        return total

    pad = jnp.zeros((128 - HALO, 128), F32)
    columns = []
    for half in range(2):
        lanes = slice(128 * half, 128 * half + 128)
        columns.append(jnp.concatenate([spread(HALO, L, lanes), spread(0, HALO, lanes), pad], 0))
    both = jnp.concatenate([dq, dqd, dq, dqd], 1)
    columns.append(jnp.concatenate([both, jnp.zeros((128, 128), F32)], 0))
    dp = jnp.concatenate(columns, 1)
    drain_gather()
    fw.drain()
    bw.drain()
    reduce(dp, ext_t, *reduce_scratch, *reduce_sems, out_ref)


def split_outputs(sums_ref, o_sel, o_step, o_selh, o_steph):
    o_sel[...] = sums_ref[:, 0:128]
    o_selh[...] = sums_ref[:, 128:256]
    o_step[...] = sums_ref[:, 256 : 256 + H]
    o_steph[...] = sums_ref[:, 256 + H : 256 + 2 * H]


def vmem(shape, dtype=F32):
    return pltpu.VMEM(shape, dtype)


def dma(*shape):
    return pltpu.SemaphoreType.DMA(shape)


def body(tokens, values, cotangent, sel_weight, step_weight, sel_dir, step_dir, conv_weight, step_bias, decay_rate):
    own_tokens, v, u = tokens[0], values[0], cotangent[0]
    depth = own_tokens.shape[1]
    rows = sel_weight.shape[0]
    scale = 1.0 / math.sqrt(NX * CHIPS * 2 * L)
    spec = pl.BlockSpec(memory_space=pltpu.VMEM)
    hbm = pl.BlockSpec(memory_space=pl.ANY)
    tiles = NX * NY * NZ
    reduce_scratch = (
        [vmem((2, NX, NY, NZ, 2, 8, 128)), vmem((2, NX, NY, NZ // 2, 8, 128)),
         vmem((2, NX, NY, NZ, 8, 128)), vmem((NX, NY, NZ // 2, 8, 128))]
        + [vmem((NX, NY, NZ, 8, 128))] * 2 + [vmem((NX, NY, NZ // 2, 8, 128))]
        + [vmem((3, NY, NZ, 8, 128)), vmem((3, NX, NZ, 8, 128)), vmem((NZ, NX, NY, 8, 128))]
        + [vmem((NY, NZ, 8, 128)), vmem((NX, NZ, 8, 128)), vmem((NX, NY, 8, 128))]
        + [vmem((3, NZ, 8, 128)), vmem((3, NZ, 8, 128)), vmem((3, NY, 8, 128))]
        + [vmem((NZ, 8, 128)), vmem((NZ, 8, 128)), vmem((NY, 8, 128))]
        + [vmem((7, 8, 128)), vmem((7, 8, 128)), vmem((3, 8, 128))]
        + [vmem((8, 128))]
    )

    def scan_scratch():
        return (
            [vmem((2, NZ, LANES, 24, 128))] * 2 + [vmem((2, LANES, 24, 128)), vmem((2, NY, LANES, 24, 128))]
            + [vmem((2, NZ, LANES, 16, 128))] * 2 + [vmem((128, HALF)), vmem((2, 128, HALF))]
        )

    scratch = [
        vmem((L, HP), BF16), vmem((L, HP), BF16),
        vmem((rows, 128), BF16), vmem((rows, 128), BF16), vmem((rows, H), BF16), vmem((rows, H), BF16),
        vmem((KCONV, 128)), vmem((1, H)), vmem((1, H)),
        vmem((NX, NY, NZ, 2, rows, WIDE), BF16),
        vmem((2 * L, depth), BF16), vmem((depth, 2 * L), BF16), vmem((HALO + L, WIDE)),
        [vmem((2, 136, HALF)), vmem((136, HALF))] + scan_scratch(),
        [vmem((2, 128, HALF)), vmem((128, HALF))] + scan_scratch(),
        vmem((3 * H, L)), vmem((L, L)), vmem((L, L)), vmem((H, L)), vmem((H, L)), vmem((HALO + L + 8, 256)),
        reduce_scratch,
        dma(10),
        [dma(5), dma(), dma(), dma(NX * NY), dma(NX * NY)],
        [dma(5), dma(2), dma(2), dma(2), dma(2)],
        [dma(5), dma(2), dma(2), dma(2), dma(2)],
        [dma(15), dma(2 * NX), dma(3), dma(3), dma(3), dma()],
    ]
    sums = pl.pallas_call(
        functools.partial(everything, scale),
        out_shape=jax.ShapeDtypeStruct((rows, WIDE), F32),
        in_specs=[hbm] * 10,
        out_specs=spec,
        scratch_shapes=scratch,
        compiler_params=pltpu.CompilerParams(
            vmem_limit_bytes=VMEM_LIMIT, collective_id=0, has_side_effects=True
        ),
    )(sel_weight, sel_dir, step_weight, step_dir, own_tokens, v, u, conv_weight, step_bias[None, :], decay_rate[None, :])
    return pl.pallas_call(
        split_outputs,
        out_shape=[
            jax.ShapeDtypeStruct((rows, 128), F32), jax.ShapeDtypeStruct((rows, H), F32),
            jax.ShapeDtypeStruct((rows, 128), F32), jax.ShapeDtypeStruct((rows, H), F32),
        ],
        in_specs=[spec],
        out_specs=[spec] * 4,
    )(sums)


def solution(mesh):
    shards = P(("dp", "seq"), None)
    stream = P("dp", "seq", None)
    return jax.shard_map(
        body,
        mesh=mesh,
        in_specs=(stream, stream, stream, shards, shards, shards, shards, P(), P(), P()),
        out_specs=(shards, shards, shards, shards),
        check_vma=False,
    )
```

```python
import functools
import math

import jax
import jax.numpy as jnp
from jax import lax
from jax.experimental import pallas as pl
from jax.experimental.pallas import tpu as pltpu
from jax.sharding import PartitionSpec as P

N = 64
P_SIZE = 32
H = 32
KCONV = 4
L = 128
HALO = 16
HP = H * P_SIZE
HALF = HP // 2
WIDE = 384
NX, NY, NZ = 4, 4, 8
CHIPS = NY * NZ
MESH = pl.DeviceIdType.MESH
F32 = jnp.float32
BF16 = jnp.bfloat16
VMEM_LIMIT = 56 * 1024 * 1024


def roll64(x):
    return pltpu.roll(x, 64, 1)


def split(x):
    high = x.astype(BF16)
    low = (x - high.astype(F32)).astype(BF16)
    return high, low


def split3(x):
    high = x.astype(BF16)
    rest = x - high.astype(F32)
    mid = rest.astype(BF16)
    low = (rest - mid.astype(F32)).astype(BF16)
    return high, mid, low


def dg(a, b, ca, cb):
    return lax.dot_general(a, b, (((ca,), (cb,)), ((), ())), preferred_element_type=F32)


def dot_split(a, b, ca, cb):
    return dot_parts(split(a), split(b), ca, cb)


def dot_parts(a, b, ca, cb):
    (ah, al), (bh, bl) = a, b
    return dg(ah, bh, ca, cb) + (dg(ah, bl, ca, cb) + dg(al, bh, ca, cb))


def dot_left(a, b, ca, cb):
    ah, al = split(a)
    return dg(ah, b, ca, cb) + dg(al, b, ca, cb)


def iota(shape, dim):
    return lax.broadcasted_iota(jnp.int32, shape, dim)


def low_lanes():
    return iota((L, 128), 1) < 64


def head_spread():
    return (iota((H, HP), 0) == iota((H, HP), 1) // P_SIZE).astype(F32).astype(BF16)


def triangle(reverse):
    row, column = iota((L, L), 0), iota((L, L), 1)
    keep = (column >= row) if reverse else (row >= column)
    return keep.astype(F32).astype(BF16)


def cumulate(x, reverse):
    tri = triangle(reverse)
    a, b, c = split3(x)
    return dg(tri, a, 1, 0) + (dg(tri, b, 1, 0) + dg(tri, c, 1, 0))


def features(proj, conv2, bias, rate):
    z = jnp.zeros((L, 128), F32)
    zd = jnp.zeros((L, 128), F32)
    for k in range(KCONV):
        rows = HALO - (KCONV - 1) + k
        z = z + conv2[k : k + 1, :128] * proj(rows, 0, 128)
        zd = zd + conv2[k : k + 1, :128] * proj(rows, 128, 128)
    sg = jax.nn.sigmoid(z)
    act = z * sg
    first = sg * (1.0 + z * (1.0 - sg))
    second = sg * (1.0 - sg) * (2.0 + z * (1.0 - 2.0 * sg))
    actd = first * zd
    steps = proj(HALO, 256, 128)
    q = steps[:, :H] + bias
    qd = steps[:, H : 2 * H]
    delta = jnp.maximum(q, 0.0) + jnp.log1p(jnp.exp(-jnp.abs(q)))
    sq = jax.nn.sigmoid(q)
    deltad = sq * qd
    cum = cumulate(-(delta * rate), False)
    cumd = cumulate(-(deltad * rate), False)
    return dict(
        zd=zd, act=act, actd=actd, first=first, second=second,
        qd=qd, sq=sq, delta=delta, deltad=deltad, cum=cum, cumd=cumd,
    )


def weights_of(ft):
    cum, cumd = ft["cum"], ft["cumd"]
    last, lastd = cum[L - 1 :, :], cumd[L - 1 :, :]
    e = jnp.exp(cum)
    ed = e * cumd
    f = jnp.exp(last - cum)
    fd = f * (lastd - cumd)
    w = f * ft["delta"]
    wd = fd * ft["delta"] + f * ft["deltad"]
    return e, ed, f, fd, w, wd


def pair_parts(ft):
    act, actd = ft["act"], ft["actd"]
    actr, actdr = roll64(act), roll64(actd)
    m = low_lanes()
    return dict(
        b_bd=jnp.where(m, act, actdr),
        o_b=jnp.where(m, 0.0, actr),
        c_cd=jnp.where(m, actr, actd),
        o_c=jnp.where(m, 0.0, act),
        b_o=jnp.where(m, act, 0.0),
        bd_b=jnp.where(m, actd, actr),
        c_o=jnp.where(m, actr, 0.0),
        cd_c=jnp.where(m, actdr, act),
        b_c=act,
        c_b=actr,
    )


def spread_rows(rows):
    return dot_left(rows, head_spread(), 1, 0)


def streams(wts, values, cotangent):
    e, ed, _, _, w, wd = wts
    v = values.astype(F32)
    u = cotangent.astype(F32)
    we = spread_rows(w) * v
    wde = spread_rows(wd) * v
    es = spread_rows(e)
    eds = spread_rows(ed)
    return we, wde, es, eds, es * u, eds * u


def forward_states(pp, we, wde):
    left = jnp.concatenate([pp["b_bd"], pp["o_b"]], 0)
    return dot_split(left, jnp.concatenate([we, wde], 0), 0, 0)


def backward_states(pp, eu, edu):
    left = jnp.concatenate([pp["c_cd"], pp["o_c"]], 0)
    return dot_split(left, jnp.concatenate([eu, edu], 0), 0, 0)


def intra_setup(ft, pp, rows_ref, row1_ref, row2_ref):
    g = dot_split(pp["c_o"], pp["b_c"], 1, 1)
    gd = dot_split(pp["cd_c"], pp["b_bd"], 1, 1)
    eta = ft["deltad"] - ft["delta"] * ft["cumd"]
    rows_ref[0:H, :] = ft["cum"].T
    rows_ref[H : 2 * H, :] = ft["delta"].T
    rows_ref[2 * H : 3 * H, :] = eta.T
    row1_ref[...] = jnp.zeros((L, L), F32)
    row2_ref[...] = jnp.zeros((L, L), F32)
    return g, gd


def intra(ft, g, gd, v_of, u_of, rows_ref, row1_ref, row2_ref, colq_ref, colqd_ref, first, last, carry):
    parts = split3(ft["cum"])
    partsd = split(ft["cumd"])
    row, lane = iota((L, L), 0), iota((L, L), 1)
    causal = row >= lane

    def one(i, carry):
        dgm, dgd = carry
        pick = (iota((H, 512), 0) == (4 * i + iota((H, 512), 1) // 128)).astype(F32).astype(BF16)
        ct4 = dg(parts[0], pick, 1, 0) + (dg(parts[1], pick, 1, 0) + dg(parts[2], pick, 1, 0))
        cd4 = dg(partsd[0], pick, 1, 0) + dg(partsd[1], pick, 1, 0)
        v_tile, u_tile = v_of(i), u_of(i)
        row1, row2 = row1_ref[...], row2_ref[...]
        for j in range(4):
            h = 4 * i + j
            mask = (iota((L, 128), 1) // P_SIZE == j).astype(F32)
            w = dg((u_tile.astype(F32) * mask).astype(BF16), v_tile, 1, 1)
            ct = ct4[:, 128 * j : 128 * j + 128]
            cd = cd4[:, 128 * j : 128 * j + 128]
            cs = rows_ref[pl.ds(h, 1), :]
            ds = rows_ref[pl.ds(H + h, 1), :]
            et = rows_ref[pl.ds(2 * H + h, 1), :]
            x = jnp.exp(jnp.where(causal, ct - cs, -1e30)) * w
            xd = x * ds
            dgm = dgm + xd
            dgd = dgd + (x * et + cd * xd)
            q = x * g
            xgd = x * gd
            colq_ref[pl.ds(h, 1), :] = jnp.sum(q, axis=0, keepdims=True)
            colqd_ref[pl.ds(h, 1), :] = jnp.sum(xgd + q * cd, axis=0, keepdims=True)
            r1 = jnp.sum(q * ds, axis=1, keepdims=True)
            r2 = jnp.sum(xgd * ds + q * et, axis=1, keepdims=True)
            here = lane == h
            row1 = jnp.where(here, r1, row1)
            row2 = jnp.where(here, r2, row2)
        row1_ref[...] = row1
        row2_ref[...] = row2
        return dgm, dgd

    return lax.fori_loop(first, last, one, carry)


def intra_pairs(pp, dgm, dgd):
    return (
        dot_split(dgm, pp["b_bd"], 1, 0),
        dot_split(dgd, pp["b_c"], 1, 0),
        dot_split(dgm, pp["c_cd"], 0, 0),
        dot_split(dgd, pp["c_b"], 0, 0),
    )


def head_sums(x):
    return dot_left(x, head_spread(), 1, 1)


def finish_forward(pp, e_split, cotangent, xf):
    u = cotangent.astype(F32)
    x_split = split(xf)
    zz = dot_parts(split(jnp.concatenate([pp["c_o"], pp["cd_c"]], 0)), x_split, 1, 0)
    return head_sums(zz[:L] * u), head_sums(zz[L:] * u), dot_parts(e_split, x_split, 1, 1)


def finish_backward(pp, w_split, values, xb):
    v = values.astype(F32)
    x_split = split(xb)
    yy = dot_parts(split(jnp.concatenate([pp["b_o"], pp["bd_b"]], 0)), x_split, 1, 0)
    return head_sums(yy[:L] * v), head_sums(yy[L:] * v), dot_parts(w_split, x_split, 1, 1)


def finish(ft, wts, pairs, row1, row2, colq, colqd, from_forward, from_backward, xf, xb, rate, scale):
    e, ed, f, fd, w, wd = wts
    g, gdot, pc = from_forward
    kk, kdot, pb = from_backward
    kap = jnp.sum(xb[:64] * xf[:64], axis=0, keepdims=True)
    kapd = jnp.sum(xb[64:] * xf[:64] + xb[:64] * xf[64:], axis=0, keepdims=True)
    both = head_sums(jnp.concatenate([jnp.broadcast_to(kap, (8, HP)), jnp.broadcast_to(kapd, (8, HP))], 0))
    kap, kapd = both[0:1], both[8:9]

    m = low_lanes()
    t1, t2, t3, t4 = pairs
    pair_c = t1 + pc[:L] + jnp.where(m, 0.0, roll64(t2 + pc[L:]))
    pair_b = t3 + pb[:L] + jnp.where(m, 0.0, roll64(t4 + pb[L:]))
    dact = jnp.where(m, pair_b, roll64(pair_c))
    dactd = jnp.where(m, roll64(pair_b), pair_c)
    dz = scale * (ft["first"] * dact)
    dzd = scale * (ft["second"] * ft["zd"] * dact + ft["first"] * dactd)

    delta, deltad, cum, cumd = ft["delta"], ft["deltad"], ft["cum"], ft["cumd"]
    colq, colqd = colq.T, colqd.T
    colqd = colqd - cumd * colq
    row1, row2 = row1[:, :H], row2[:, :H]
    row2 = row2 + cumd * row1
    wk = w * kk
    wkd = wd * kk + w * kdot
    dc = row1 - delta * colq + e * g - wk
    dcd = row2 - (deltad * colq + delta * colqd) + ed * g + e * gdot - wkd
    el, edl = e[L - 1 :, :], ed[L - 1 :, :]
    extra = el * kap + jnp.sum(wk, axis=0, keepdims=True)
    extrad = edl * kap + el * kapd + jnp.sum(wkd, axis=0, keepdims=True)
    ddelta = colq + f * kk - rate * (cumulate(dc, True) + extra)
    ddeltad = colqd + fd * kk + f * kdot - rate * (cumulate(dcd, True) + extrad)
    sq = ft["sq"]
    dq = scale * (sq * ddelta)
    dqd = scale * (sq * (1.0 - sq) * ft["qd"] * ddelta + sq * ddeltad)
    return dz, dzd, dq, dqd


def place():
    x = lax.axis_index("dp")
    s = lax.axis_index("seq")
    chip = s // 2
    return x, chip // NZ, lax.rem(chip, NZ), lax.rem(s, 2), chip


def device(x, y, z, k):
    return (x, (y * NZ + z) * 2 + k)


def remote(src, dst, send_sem, recv_sem, dev):
    return pltpu.make_async_remote_copy(
        src_ref=src, dst_ref=dst, send_sem=send_sem, recv_sem=recv_sem,
        device_id=dev, device_id_type=MESH,
    )


def arrived(dst, sem, dev):
    remote(dst, dst, sem, sem, dev).wait_recv()


def sent(src, sem, dev):
    remote(src, src, sem, sem, dev).wait_send()


FAR4 = (2, 1, 3)
LANES = HALF // 256
FAR8 = (4, 3, 5, 2, 6, 1, 7)


def enter():
    x, y, z, k, chip = place()
    s = 2 * chip + k
    seq = CHIPS * 2
    partners = [device(x, y, lax.rem(z + d, NZ), k) for d in FAR8]
    partners += [device(lax.rem(x + d, NX), y, z, k) for d in FAR4]
    partners += [device(x, lax.rem(y + d, NY), z, k) for d in FAR4]
    partners += [(x, lax.rem(s + 1, seq)), (x, lax.rem(s + seq - 1, seq)), device(x, y, z, 1 - k)]
    barrier = pltpu.get_barrier_semaphore()
    for dev in partners:
        pl.semaphore_signal(barrier, inc=1, device_id=dev, device_id_type=MESH)
    return lambda: pl.semaphore_wait(barrier, len(partners))


def gather(wbuf, ext, ext_t, proj, tok_ref, s_send, s_halo, s_z, s_slab, s_swap):
    x, y, z, k, chip = place()
    s = 2 * chip + k
    mate = device(x, y, z, 1 - k)
    own = wbuf.at[x, y, z, k]
    for d in FAR8:
        remote(own, own, s_send.at[0], s_z, device(x, y, lax.rem(z + d, NZ), k)).start()
    halo = remote(
        tok_ref.at[pl.ds(L - HALO, HALO)], ext.at[pl.ds(L, HALO)], s_send.at[4], s_halo,
        (x, lax.rem(s + 1, 2 * CHIPS)),
    )
    halo.start()
    arrived(wbuf.at[x, y, pl.ds(0, NZ - 1), k], s_z, mate)

    def slab_copy(sx, sy, tx, ty, sem):
        ref = wbuf.at[sx, sy, :, k]
        return remote(ref, ref, s_send.at[sem], s_slab.at[sx * NY + sy], device(tx, ty, z, k))

    def swap(sx, sy, kk):
        ref = wbuf.at[sx, sy, :, kk]
        return remote(ref, ref, s_send.at[3], s_swap.at[sx * NY + sy], mate)

    def near(d):
        return lax.rem(x + d * k, NX), lax.rem(y + d * (1 - k), NY)

    def far(d):
        return lax.rem(x + d * (1 - k), NX), lax.rem(y + d * k, NY)

    for d in FAR4:
        slab_copy(x, y, *near(d), 1).start()
    for d in FAR4:
        slab_copy(x, y, *far(d), 2).start()
    swap(x, y, k).start()
    for d in (1, 3, 2):
        sx, sy = near(d)
        slab_copy(sx, sy, x, y, 1).wait_recv()
        for t in FAR4:
            slab_copy(sx, sy, *far(t), 2).start()
        swap(sx, sy, k).start()
    halo.wait_recv()

    @pl.when(s == 0)
    def _():
        ext[L : L + HALO, :] = jnp.zeros((HALO, ext.shape[1]), BF16)

    ext_t[:, L:] = ext[L:, :].T
    for e in (0, 1, 3, 2):
        for d in (1, 3, 2):
            fx, fy = far(d)
            sx = lax.rem(fx + e * k, NX)
            sy = lax.rem(fy + e * (1 - k), NY)
            slab_copy(sx, sy, x, y, 2).wait_recv()
            swap(sx, sy, k).start()
    depth = ext.shape[1] // NX
    total = jnp.zeros((L + HALO, WIDE), F32)
    for d in range(NX):
        sx = lax.rem(x + d, NX)
        for sy in range(NY):
            swap(sx, sy, 1 - k).wait_recv()
        at = pl.multiple_of(sx * depth, depth)
        weights = wbuf[sx].astype(F32).reshape(depth, WIDE).astype(BF16)
        total = total + dg(ext[0 : L + HALO, pl.ds(at, depth)], weights, 1, 0)
    proj[HALO:, :] = total[0:L]
    proj[0:HALO, :] = total[L:]

    def drain():
        sent(wbuf.at[0, 0, pl.ds(0, NZ - 1), 0], s_send.at[0], mate)
        sent(wbuf.at[0, pl.ds(0, NY - 1), :, 0], s_send.at[1], mate)
        sent(wbuf.at[pl.ds(0, NX - 1), :, :, 0], s_send.at[2], mate)
        sent(wbuf.at[:, :, :, 0], s_send.at[3], mate)
        halo.wait_send()

    return drain


class Half:
    def __init__(self, loc, part, snd, rcv, tot, tots, snd2, rcv2, other, st, decays, s_send, s_mate, s_one, s_row, s_two):
        self.loc, self.part, self.snd, self.rcv, self.tot, self.tots = loc, part, snd, rcv, tot, tots
        self.snd2, self.rcv2, self.other, self.st = snd2, rcv2, other, st
        self.reverse = decays is not None
        self.decays = decays if self.reverse else self
        self.rows = pl.ds(0, 16 if self.reverse else 18)
        self.s_send, self.s_mate, self.s_one, self.s_row, self.s_two = s_send, s_mate, s_one, s_row, s_two
        self.x, self.y, self.z, self.k, self.chip = place()
        self.mate = device(self.x, self.y, self.z, 1 - self.k)
        self.first = self.k == 0

    def to_mate(self):
        return remote(self.loc.at[1 - self.k], self.part, self.s_send.at[0], self.s_mate.at[0], self.mate)

    def back(self):
        return remote(self.other, self.st.at[self.k], self.s_send.at[4], self.s_mate.at[1], self.mate)

    def back_in(self):
        return remote(self.other, self.st.at[1 - self.k], self.s_send.at[4], self.s_mate.at[1], self.mate)

    def cores(self):
        own, other = self.loc[self.k], self.part[...]
        return jnp.where(self.first, own, other), jnp.where(self.first, other, own)

    def start_one(self, s, t, a, ad):
        for h in range(2):
            for j in range(NZ):
                rows = slice(8 * j, 8 * j + 8)
                for i in range(LANES):
                    at = 128 * (LANES * h + i)
                    lanes = slice(at, at + 128)
                    self.snd[h, j, i, 0:8] = s[rows, lanes]
                    self.snd[h, j, i, 8:16] = t[rows, lanes]
                    if not self.reverse:
                        self.snd[h, j, i, 16:17] = a[:, lanes]
                        self.snd[h, j, i, 17:18] = ad[:, lanes]
            for d in FAR8:
                c = lax.rem(self.z + d, NZ)
                dev = device(self.x, self.y, c, self.k)
                remote(
                    self.snd.at[h, c, :, self.rows], self.rcv.at[h, self.z, :, self.rows],
                    self.s_send.at[1], self.s_one.at[h], dev,
                ).start()
            self.rcv[h, self.z] = self.snd[h, self.z]

    @staticmethod
    def step(carry, ref, decays, c):
        s, t = carry
        a, ad = decays[*c, :, 16:17, :], decays[*c, :, 17:18, :]
        return a * s + ref[*c, :, 0:8, :], a * t + (ad * s + ref[*c, :, 8:16, :])

    def order(self, count):
        return range(count - 1, -1, -1) if self.reverse else range(count)

    def row_total(self, h):
        arrived(self.rcv.at[h, pl.ds(0, NZ - 1), :, self.rows], self.s_one.at[h], self.mate)
        carry = (jnp.zeros((LANES, 8, 128), F32),) * 2
        for c in self.order(NZ):
            carry = self.step(carry, self.rcv, self.decays.rcv, (h, c))
        self.tot[h, :, 0:8, :], self.tot[h, :, 8:16, :] = carry
        if not self.reverse:
            a, ad = self.rcv[h, 0, :, 16:17, :], self.rcv[h, 0, :, 17:18, :]
            for c in range(1, NZ):
                b, bd = self.rcv[h, c, :, 16:17, :], self.rcv[h, c, :, 17:18, :]
                a, ad = a * b, ad * b + a * bd
            self.tot[h, :, 16:17, :], self.tot[h, :, 17:18, :] = a, ad
        for d in FAR4:
            dev = device(self.x, lax.rem(self.y + d, NY), self.z, self.k)
            remote(
                self.tot.at[h, :, self.rows], self.tots.at[h, self.y, :, self.rows],
                self.s_send.at[2], self.s_row.at[h], dev,
            ).start()
        self.tots[h, self.y] = self.tot[h]

    def start_two(self, h):
        arrived(self.tots.at[h, pl.ds(0, NY - 1), :, self.rows], self.s_row.at[h], self.mate)
        carry = (jnp.zeros((LANES, 8, 128), F32),) * 2
        for row in self.order(NY):
            after = self.step(carry, self.tots, self.decays.tots, (h, row))
            ahead = (row > self.y) if self.reverse else (row < self.y)
            carry = tuple(jnp.where(ahead, new, old) for new, old in zip(after, carry))
        for c in self.order(NZ):
            self.snd2[h, c, :, 0:8, :], self.snd2[h, c, :, 8:16, :] = carry
            carry = self.step(carry, self.rcv, self.decays.rcv, (h, c))
        for d in FAR8:
            c = lax.rem(self.z + d, NZ)
            dev = device(self.x, self.y, c, self.k)
            remote(self.snd2.at[h, c], self.rcv2.at[h, self.z], self.s_send.at[3], self.s_two.at[h], dev).start()
        self.rcv2[h, self.z] = self.snd2[h, self.z]

    def wait_two(self, h):
        arrived(self.rcv2.at[h, pl.ds(0, NZ - 1)], self.s_two.at[h], self.mate)

    def assemble(self, a, ad, base, base_first):
        s, t = (
            jnp.concatenate(
                [jnp.concatenate([self.rcv2[i // LANES, j, i % LANES, rows] for j in range(NZ)], 0) for i in range(2 * LANES)], 1
            )
            for rows in (slice(0, 8), slice(8, 16))
        )
        next_s = a * s + base[0:64]
        next_t = a * t + ad * s + base[64:128]
        mine_is_base = self.first if base_first else jnp.logical_not(self.first)
        self.other[0:64, :] = jnp.where(mine_is_base, next_s, s)
        self.other[64:128, :] = jnp.where(mine_is_base, next_t, t)
        self.back().start()
        self.st[self.k, 0:64, :] = jnp.where(mine_is_base, s, next_s)
        self.st[self.k, 64:128, :] = jnp.where(mine_is_base, t, next_t)

    def drain(self):
        self.to_mate().wait_send()
        sent(self.snd.at[:, pl.ds(0, NZ - 1), :, self.rows], self.s_send.at[1], self.mate)
        sent(self.tots.at[:, pl.ds(0, NY - 1), :, self.rows], self.s_send.at[2], self.mate)
        sent(self.snd2.at[:, pl.ds(0, NZ - 1)], self.s_send.at[3], self.mate)
        self.back().wait_send()


def reduce(dp, ext_t, full, g2, m01, m2, a0, a1, a2, r0, r1, r2, b0, b1, b2, q0, q1, q2, c0, c1, c2, p0, p1, p2,
           e2, s_send, s_mate, s_a, s_b, s_c, s_e, out_sel, out_selh, out_step, out_steph):
    x, y, z, k, chip = place()
    mate = device(x, y, z, 1 - k)
    holder = lax.rem(z, 2) == k

    def x_to(d):
        return device(lax.rem(x + d, NX), y, z, k)

    def y_to(d):
        return device(x, lax.rem(y + d, NY), z, k)

    def z_to(d):
        return device(x, y, lax.rem(z + d, NZ), k)

    both = jnp.concatenate(split(dp), 1)
    low_half = iota((8, 128), 1) < 64
    block_rows = NY * NZ * 16

    order = FAR4 + (0,)

    def settle(i):
        xb = lax.rem(x + order[i], NX)
        arrived(m01.at[:, xb], s_mate.at[i], mate)
        a0[xb] = full[0, xb, :, :, k] + m01[0, xb]
        if i < NX - 1:
            remote(a0.at[xb], r0.at[i], s_send.at[2], s_a.at[0], x_to(order[i])).start()
        a1[xb] = full[1, xb, :, :, k] + m01[1, xb]
        for d in FAR4:
            remote(a1.at[xb, lax.rem(y + d, NY)], r1.at[d - 1, xb], s_send.at[3], s_a.at[1], y_to(d)).start()
        arrived(m2.at[xb], s_mate.at[NX + i], mate)
        a2[xb] = g2[k, xb] + m2[xb]

    for i in range(NX):
        xb = lax.rem(x + order[i], NX)
        rows = ext_t[pl.ds(pl.multiple_of(xb * block_rows, block_rows), block_rows), :]
        part = dg(rows, both, 1, 0)
        part = part[:, :WIDE] + part[:, WIDE:]
        full[0, xb] = part[:, 0:128].reshape(NY, NZ, 2, 8, 128)
        full[1, xb] = part[:, 128:256].reshape(NY, NZ, 2, 8, 128)
        steps = part[:, 256:384].reshape(NY, NZ // 2, 2, 2, 8, 128)
        for zp in range(2):
            g2[zp, xb] = jnp.where(low_half, steps[:, :, zp, 0], steps[:, :, zp, 1])
        for tile in range(2):
            remote(full.at[tile, xb, :, :, 1 - k], m01.at[tile, xb], s_send.at[0], s_mate.at[i], mate).start()
        remote(g2.at[1 - k, xb], m2.at[xb], s_send.at[1], s_mate.at[NX + i], mate).start()
        if i > 1:
            settle(i - 2)
    settle(NX - 2)
    settle(NX - 1)

    zsend = []
    for i in range(NZ // 2):
        target = 2 * i + k
        gap = lax.rem(z - target + NZ, NZ)
        zsend.append((target != z, remote(a2.at[:, :, i], r2.at[gap], s_send.at[4 + i], s_a.at[2], device(x, y, target, k))))
        pl.when(zsend[-1][0])(zsend[-1][1].start)

    arrived(r0, s_a.at[0], mate)
    b0[...] = (a0[x] + r0[0]) + (r0[1] + r0[2])
    for d in FAR4:
        remote(b0.at[lax.rem(y + d, NY)], q0.at[d - 1], s_send.at[8], s_b.at[0], y_to(d)).start()
    arrived(r1, s_a.at[1], mate)
    b1[...] = (a1[:, y] + r1[0]) + (r1[1] + r1[2])
    for d in FAR4:
        remote(b1.at[lax.rem(x + d, NX)], q1.at[d - 1], s_send.at[9], s_b.at[1], x_to(d)).start()

    @pl.when(holder)
    def _():
        arrived(r2.at[pl.ds(1, NZ - 1)], s_a.at[2], mate)
        total = a2[:, :, z // 2] + ((r2[1] + r2[2]) + (r2[3] + r2[4]))
        b2[...] = total + ((r2[5] + r2[6]) + r2[7])
        for d in FAR4:
            remote(b2.at[lax.rem(x + d, NX)], q2.at[d - 1], s_send.at[10], s_b.at[2], x_to(d)).start()

    arrived(q0, s_b.at[0], mate)
    c0[...] = (b0[y] + q0[0]) + (q0[1] + q0[2])
    for d in FAR8:
        remote(c0.at[lax.rem(z + d, NZ)], p0.at[d - 1], s_send.at[11], s_c.at[0], z_to(d)).start()

    arrived(q1, s_b.at[1], mate)
    c1[...] = (b1[x] + q1[0]) + (q1[1] + q1[2])
    for d in FAR8:
        remote(c1.at[lax.rem(z + d, NZ)], p1.at[d - 1], s_send.at[13], s_c.at[1], z_to(d)).start()
    last = remote(c2.at[y], e2, s_send.at[14], s_e, mate)

    @pl.when(holder)
    def _():
        arrived(q2, s_b.at[2], mate)
        c2[...] = (b2[x] + q2[0]) + (q2[1] + q2[2])
        for d in FAR4:
            for core in range(2):
                row = lax.rem(y + d, NY)
                remote(c2.at[row], p2.at[d - 1], s_send.at[12], s_c.at[2], device(x, row, z, core)).start()
        last.start()
        e2[...] = c2[y]

    sent(m01, s_send.at[0], mate)
    sent(m2, s_send.at[1], mate)
    sent(r0, s_send.at[2], mate)
    sent(r1, s_send.at[3], mate)
    for used, copy in zsend:
        pl.when(used)(copy.wait_send)
    sent(q0, s_send.at[8], mate)
    sent(q1, s_send.at[9], mate)
    arrived(p0, s_c.at[0], mate)
    out_sel[...] = c0[z] + ((p0[0] + p0[1]) + (p0[2] + p0[3])) + ((p0[4] + p0[5]) + p0[6])
    arrived(p1, s_c.at[1], mate)
    out_selh[...] = c1[z] + ((p1[0] + p1[1]) + (p1[2] + p1[3])) + ((p1[4] + p1[5]) + p1[6])
    arrived(p2, s_c.at[2], mate)

    @pl.when(jnp.logical_not(holder))
    def _():
        remote(c2.at[y], e2, s_send.at[14], s_e, mate).wait_recv()

    steps = (e2[...] + p2[0]) + (p2[1] + p2[2])
    steps = jnp.where(k == 0, steps, roll64(steps))
    out_step[...] = steps[:, 0:H]
    out_steph[...] = steps[:, H : 2 * H]
    sent(p0, s_send.at[11], mate)
    sent(p1, s_send.at[13], mate)

    @pl.when(holder)
    def _():
        sent(q2, s_send.at[10], mate)
        sent(p1.at[pl.ds(0, 6)], s_send.at[12], mate)
        last.wait_send()


def everything(scale, sw_hbm, sd_hbm, tw_hbm, td_hbm, tok_ref, v_hbm, u_hbm, conv_hbm, bias_hbm, rate_hbm,
               out_sel, out_selh, out_step, out_steph, v_ref, u_ref, sw_ref, sd_ref, tw_ref, td_ref, conv_ref, bias_ref, rate_ref, wbuf, ext, ext_t, proj,
               forward_scratch, backward_scratch, rows_ref, row1_ref, row2_ref, colq_ref, colqd_ref, zp_ref, reduce_scratch,
               s_in, gather_sems, forward_sems, backward_sems, reduce_sems):
    entered = enter()
    pairs = [
        (sw_hbm, sw_ref), (sd_hbm, sd_ref), (tw_hbm, tw_ref), (td_hbm, td_ref), (tok_ref, ext.at[pl.ds(0, L)]),
        (v_hbm, v_ref), (u_hbm, u_ref), (conv_hbm, conv_ref), (bias_hbm, bias_ref), (rate_hbm, rate_ref),
    ]
    local = [pltpu.make_async_copy(src, dst, s_in.at[i]) for i, (src, dst) in enumerate(pairs)]
    for c in local:
        c.start()
    x, y, z, k, _ = place()
    ext[L + HALO :, :] = jnp.zeros((ext.shape[0] - L - HALO, ext.shape[1]), BF16)
    for c in local[0:4]:
        c.wait()
    wbuf[x, y, z, k, :, 0:128] = sw_ref[...]
    wbuf[x, y, z, k, :, 128:256] = sd_ref[...]
    rows = sw_ref.shape[0]
    wbuf[x, y, z, k, :, 256:384] = jnp.concatenate(
        [tw_ref[...].astype(F32), td_ref[...].astype(F32), jnp.zeros((rows, 128 - 2 * H), F32)], 1
    ).astype(BF16)
    local[4].wait()
    ext_t[:, 0:L] = ext[0:L, :].T
    for c in local[5:]:
        c.wait()
    entered()
    drain_gather = gather(wbuf, ext, ext_t, proj, tok_ref, *gather_sems)

    rate = rate_ref[...]
    ft = features(lambda row, lane, lanes: proj[row : row + L, lane : lane + lanes], conv_ref[...], bias_ref[...], rate)
    wts = weights_of(ft)
    pp = pair_parts(ft)
    we, wde, es, eds, eu, edu = streams(wts, v_ref[...], u_ref[...])
    fw = Half(*forward_scratch, None, *forward_sems)
    bw = Half(*backward_scratch, fw, *backward_sems)
    row = iota((8, HP), 0)
    dec = jnp.where(row == 0, es[L - 1 :, :], jnp.where(row == 1, eds[L - 1 :, :], 0.0))
    states = forward_states(pp, we, wde)
    for half in range(2):
        lanes = slice(HALF * half, HALF * half + HALF)
        fw.loc[half, 0:128, :] = states[:, lanes]
        fw.loc[half, 128:136, :] = dec[:, lanes]
    fw.to_mate().start()
    states = backward_states(pp, eu, edu)
    for half in range(2):
        bw.loc[half] = states[:, HALF * half : HALF * half + HALF]
    bw.to_mate().start()

    fw.to_mate().wait_recv()
    one0, one1 = fw.cores()
    a0, ad0 = one0[128:129], one0[129:130]
    a1, ad1 = one1[128:129], one1[129:130]
    a, ad = a0 * a1, ad0 * a1 + a0 * ad1
    fw.start_one(
        a1 * one0[0:64] + one1[0:64], a1 * one0[64:128] + ad1 * one0[0:64] + one1[64:128], a, ad
    )
    bw.to_mate().wait_recv()
    one0, one1 = bw.cores()
    bw.start_one(
        a0 * one1[0:64] + one0[0:64], a0 * one1[64:128] + ad0 * one1[0:64] + one0[64:128], a, ad
    )

    def tile(ref):
        return lambda i: ref[:, pl.ds(pl.multiple_of(i * 128, 128), 128)]

    g, gd = intra_setup(ft, pp, rows_ref, row1_ref, row2_ref)
    zero = jnp.zeros((L, L), F32)

    def block_terms(first, last, carry):
        return intra(
            ft, g, gd, tile(v_ref), tile(u_ref), rows_ref, row1_ref, row2_ref, colq_ref, colqd_ref, first, last, carry
        )

    carry = block_terms(0, 7, (zero, zero))
    fw.row_total(0)
    carry = block_terms(7, 8, carry)
    fw.row_total(1)
    fw.start_two(0)
    bw.row_total(0)
    fw.start_two(1)
    bw.row_total(1)
    bw.start_two(0)
    pairs = intra_pairs(pp, *carry)
    bw.start_two(1)
    e_split = split(jnp.concatenate([eu, edu], 0))
    w_split = split(jnp.concatenate([we, wde], 0))
    fw.wait_two(0)
    fw.wait_two(1)
    fw.assemble(a0, ad0, fw.cores()[0], True)
    fw.back_in().wait_recv()
    xf = jnp.concatenate([fw.st[0], fw.st[1]], 1)
    from_forward = finish_forward(pp, e_split, u_ref[...], xf)
    bw.wait_two(0)
    bw.wait_two(1)
    bw.assemble(a1, ad1, bw.cores()[1], False)
    bw.back_in().wait_recv()
    xb = jnp.concatenate([bw.st[0], bw.st[1]], 1)
    from_backward = finish_backward(pp, w_split, v_ref[...], xb)
    dz, dzd, dq, dqd = finish(
        ft, wts, pairs, row1_ref[...], row2_ref[...], colq_ref[...], colqd_ref[...],
        from_forward, from_backward, xf, xb, rate, scale,
    )
    zp_ref[...] = jnp.zeros(zp_ref.shape, F32)
    zp_ref[HALO : HALO + L, 0:128] = dz
    zp_ref[HALO : HALO + L, 128:256] = dzd
    conv = conv_ref[...]

    def spread(first_row, count, lanes):
        total = conv[0:1, :] * zp_ref[first_row + 3 : first_row + 3 + count, lanes]
        for tap in range(1, KCONV):
            total = total + conv[tap : tap + 1, :] * zp_ref[first_row + 3 - tap : first_row + 3 - tap + count, lanes]
        return total

    pad = jnp.zeros((128 - HALO, 128), F32)
    columns = []
    for half in range(2):
        lanes = slice(128 * half, 128 * half + 128)
        columns.append(jnp.concatenate([spread(HALO, L, lanes), spread(0, HALO, lanes), pad], 0))
    both = jnp.concatenate([dq, dqd, dq, dqd], 1)
    columns.append(jnp.concatenate([both, jnp.zeros((128, 128), F32)], 0))
    dp = jnp.concatenate(columns, 1)
    drain_gather()
    fw.drain()
    bw.drain()
    reduce(dp, ext_t, *reduce_scratch, *reduce_sems, out_sel, out_selh, out_step, out_steph)


def hand_on(*refs):
    sources, results, sem = refs[0:4], refs[4:8], refs[8]
    copies = [pltpu.make_async_copy(src, dst, sem.at[i]) for i, (src, dst) in enumerate(zip(sources, results))]
    for copy in copies:
        copy.start()
    for copy in copies:
        copy.wait()


def vmem(shape, dtype=F32):
    return pltpu.VMEM(shape, dtype)


def dma(*shape):
    return pltpu.SemaphoreType.DMA(shape)


def body(tokens, values, cotangent, sel_weight, step_weight, sel_dir, step_dir, conv_weight, step_bias, decay_rate):
    own_tokens, v, u = tokens[0], values[0], cotangent[0]
    depth = own_tokens.shape[1]
    rows = sel_weight.shape[0]
    scale = 1.0 / math.sqrt(NX * CHIPS * 2 * L)
    spec = pl.BlockSpec(memory_space=pltpu.VMEM)
    hbm = pl.BlockSpec(memory_space=pl.ANY)
    tiles = NX * NY * NZ
    reduce_scratch = (
        [vmem((2, NX, NY, NZ, 2, 8, 128)), vmem((2, NX, NY, NZ // 2, 8, 128)),
         vmem((2, NX, NY, NZ, 8, 128)), vmem((NX, NY, NZ // 2, 8, 128))]
        + [vmem((NX, NY, NZ, 8, 128))] * 2 + [vmem((NX, NY, NZ // 2, 8, 128))]
        + [vmem((3, NY, NZ, 8, 128)), vmem((3, NX, NZ, 8, 128)), vmem((NZ, NX, NY, 8, 128))]
        + [vmem((NY, NZ, 8, 128)), vmem((NX, NZ, 8, 128)), vmem((NX, NY, 8, 128))]
        + [vmem((3, NZ, 8, 128)), vmem((3, NZ, 8, 128)), vmem((3, NY, 8, 128))]
        + [vmem((NZ, 8, 128)), vmem((NZ, 8, 128)), vmem((NY, 8, 128))]
        + [vmem((7, 8, 128)), vmem((7, 8, 128)), vmem((3, 8, 128))]
        + [vmem((8, 128))]
    )

    def scan_scratch():
        return (
            [vmem((2, NZ, LANES, 24, 128))] * 2 + [vmem((2, LANES, 24, 128)), vmem((2, NY, LANES, 24, 128))]
            + [vmem((2, NZ, LANES, 16, 128))] * 2 + [vmem((128, HALF)), vmem((2, 128, HALF))]
        )

    scratch = [
        vmem((L, HP), BF16), vmem((L, HP), BF16),
        vmem((rows, 128), BF16), vmem((rows, 128), BF16), vmem((rows, H), BF16), vmem((rows, H), BF16),
        vmem((KCONV, 128)), vmem((1, H)), vmem((1, H)),
        vmem((NX, NY, NZ, 2, rows, WIDE), BF16),
        vmem((2 * L, depth), BF16), vmem((depth, 2 * L), BF16), vmem((HALO + L, WIDE)),
        [vmem((2, 136, HALF)), vmem((136, HALF))] + scan_scratch(),
        [vmem((2, 128, HALF)), vmem((128, HALF))] + scan_scratch(),
        vmem((3 * H, L)), vmem((L, L)), vmem((L, L)), vmem((H, L)), vmem((H, L)), vmem((HALO + L + 8, 256)),
        reduce_scratch,
        dma(10),
        [dma(5), dma(), dma(), dma(NX * NY), dma(NX * NY)],
        [dma(5), dma(2), dma(2), dma(2), dma(2)],
        [dma(5), dma(2), dma(2), dma(2), dma(2)],
        [dma(15), dma(2 * NX), dma(3), dma(3), dma(3), dma()],
    ]
    shapes = [jax.ShapeDtypeStruct((rows, columns), F32) for columns in (128, 128, H, H)]
    sums = pl.pallas_call(
        functools.partial(everything, scale),
        out_shape=shapes,
        in_specs=[hbm] * 10,
        out_specs=[spec] * 4,
        scratch_shapes=scratch,
        compiler_params=pltpu.CompilerParams(
            vmem_limit_bytes=VMEM_LIMIT, collective_id=0, has_side_effects=True
        ),
    )(sel_weight, sel_dir, step_weight, step_dir, own_tokens, v, u, conv_weight, step_bias[None, :], decay_rate[None, :])
    sel, selh, step, steph = pl.pallas_call(
        hand_on, out_shape=shapes, in_specs=[hbm] * 4, out_specs=[hbm] * 4, scratch_shapes=[dma(4)],
    )(*sums)
    return sel, step, selh, steph


def solution(mesh):
    shards = P(("dp", "seq"), None)
    stream = P("dp", "seq", None)
    return jax.shard_map(
        body,
        mesh=mesh,
        in_specs=(stream, stream, stream, shards, shards, shards, shards, P(), P(), P()),
        out_specs=(shards, shards, shards, shards),
        check_vma=False,
    )
```

```python
import functools
import math

import jax
import jax.numpy as jnp
from jax import lax
from jax.experimental import pallas as pl
from jax.experimental.pallas import tpu as pltpu
from jax.sharding import PartitionSpec as P

N = 64
P_SIZE = 32
H = 32
KCONV = 4
L = 128
HALO = 16
HP = H * P_SIZE
HALF = HP // 2
WIDE = 384
NX, NY, NZ = 4, 4, 8
CHIPS = NY * NZ
MESH = pl.DeviceIdType.MESH
F32 = jnp.float32
BF16 = jnp.bfloat16
VMEM_LIMIT = 56 * 1024 * 1024


def roll64(x):
    return pltpu.roll(x, 64, 1)


def split(x):
    high = x.astype(BF16)
    low = (x - high.astype(F32)).astype(BF16)
    return high, low


def split3(x):
    high = x.astype(BF16)
    rest = x - high.astype(F32)
    mid = rest.astype(BF16)
    low = (rest - mid.astype(F32)).astype(BF16)
    return high, mid, low


def dg(a, b, ca, cb):
    return lax.dot_general(a, b, (((ca,), (cb,)), ((), ())), preferred_element_type=F32)


def dot_split(a, b, ca, cb):
    return dot_parts(split(a), split(b), ca, cb)


def dot_parts(a, b, ca, cb):
    (ah, al), (bh, bl) = a, b
    return dg(ah, bh, ca, cb) + (dg(ah, bl, ca, cb) + dg(al, bh, ca, cb))


def dot_left(a, b, ca, cb):
    ah, al = split(a)
    return dg(ah, b, ca, cb) + dg(al, b, ca, cb)


def iota(shape, dim):
    return lax.broadcasted_iota(jnp.int32, shape, dim)


def low_lanes():
    return iota((L, 128), 1) < 64


def head_spread():
    return (iota((H, HP), 0) == iota((H, HP), 1) // P_SIZE).astype(F32).astype(BF16)


def triangle(reverse):
    row, column = iota((L, L), 0), iota((L, L), 1)
    keep = (column >= row) if reverse else (row >= column)
    return keep.astype(F32).astype(BF16)


def cumulate(x, reverse):
    tri = triangle(reverse)
    a, b, c = split3(x)
    return dg(tri, a, 1, 0) + (dg(tri, b, 1, 0) + dg(tri, c, 1, 0))


def features(proj, conv2, bias, rate):
    z = jnp.zeros((L, 128), F32)
    zd = jnp.zeros((L, 128), F32)
    for k in range(KCONV):
        rows = HALO - (KCONV - 1) + k
        z = z + conv2[k : k + 1, :128] * proj(rows, 0, 128)
        zd = zd + conv2[k : k + 1, :128] * proj(rows, 128, 128)
    sg = jax.nn.sigmoid(z)
    act = z * sg
    first = sg * (1.0 + z * (1.0 - sg))
    second = sg * (1.0 - sg) * (2.0 + z * (1.0 - 2.0 * sg))
    actd = first * zd
    steps = proj(HALO, 256, 128)
    q = steps[:, :H] + bias
    qd = steps[:, H : 2 * H]
    delta = jnp.maximum(q, 0.0) + jnp.log1p(jnp.exp(-jnp.abs(q)))
    sq = jax.nn.sigmoid(q)
    deltad = sq * qd
    cum = cumulate(-(delta * rate), False)
    cumd = cumulate(-(deltad * rate), False)
    return dict(
        zd=zd, act=act, actd=actd, first=first, second=second,
        qd=qd, sq=sq, delta=delta, deltad=deltad, cum=cum, cumd=cumd,
    )


def weights_of(ft):
    cum, cumd = ft["cum"], ft["cumd"]
    last, lastd = cum[L - 1 :, :], cumd[L - 1 :, :]
    e = jnp.exp(cum)
    ed = e * cumd
    f = jnp.exp(last - cum)
    fd = f * (lastd - cumd)
    w = f * ft["delta"]
    wd = fd * ft["delta"] + f * ft["deltad"]
    return e, ed, f, fd, w, wd


def pair_parts(ft):
    act, actd = ft["act"], ft["actd"]
    actr, actdr = roll64(act), roll64(actd)
    m = low_lanes()
    return dict(
        b_bd=jnp.where(m, act, actdr),
        o_b=jnp.where(m, 0.0, actr),
        c_cd=jnp.where(m, actr, actd),
        o_c=jnp.where(m, 0.0, act),
        b_o=jnp.where(m, act, 0.0),
        bd_b=jnp.where(m, actd, actr),
        c_o=jnp.where(m, actr, 0.0),
        cd_c=jnp.where(m, actdr, act),
        b_c=act,
        c_b=actr,
    )


def spread_rows(rows):
    return dot_left(rows, head_spread(), 1, 0)


def streams(wts, values, cotangent):
    e, ed, _, _, w, wd = wts
    v = values.astype(F32)
    u = cotangent.astype(F32)
    we = spread_rows(w) * v
    wde = spread_rows(wd) * v
    es = spread_rows(e)
    eds = spread_rows(ed)
    return we, wde, es, eds, es * u, eds * u


def forward_states(pp, we, wde):
    left = jnp.concatenate([pp["b_bd"], pp["o_b"]], 0)
    return dot_split(left, jnp.concatenate([we, wde], 0), 0, 0)


def backward_states(pp, eu, edu):
    left = jnp.concatenate([pp["c_cd"], pp["o_c"]], 0)
    return dot_split(left, jnp.concatenate([eu, edu], 0), 0, 0)


def intra_setup(ft, pp, rows_ref, row1_ref, row2_ref):
    g = dot_split(pp["c_o"], pp["b_c"], 1, 1)
    gd = dot_split(pp["cd_c"], pp["b_bd"], 1, 1)
    eta = ft["deltad"] - ft["delta"] * ft["cumd"]
    rows_ref[0:H, :] = ft["cum"].T
    rows_ref[H : 2 * H, :] = ft["delta"].T
    rows_ref[2 * H : 3 * H, :] = eta.T
    row1_ref[...] = jnp.zeros((L, L), F32)
    row2_ref[...] = jnp.zeros((L, L), F32)
    return g, gd


def intra(ft, g, gd, v_of, u_of, rows_ref, row1_ref, row2_ref, colq_ref, colqd_ref, first, last, carry):
    parts = split3(ft["cum"])
    partsd = split(ft["cumd"])
    row, lane = iota((L, L), 0), iota((L, L), 1)
    causal = row >= lane

    def one(i, carry):
        dgm, dgd = carry
        pick = (iota((H, 512), 0) == (4 * i + iota((H, 512), 1) // 128)).astype(F32).astype(BF16)
        ct4 = dg(parts[0], pick, 1, 0) + (dg(parts[1], pick, 1, 0) + dg(parts[2], pick, 1, 0))
        cd4 = dg(partsd[0], pick, 1, 0) + dg(partsd[1], pick, 1, 0)
        v_tile, u_tile = v_of(i), u_of(i)
        row1, row2 = row1_ref[...], row2_ref[...]
        for j in range(4):
            h = 4 * i + j
            mask = (iota((L, 128), 1) // P_SIZE == j).astype(F32)
            w = dg((u_tile.astype(F32) * mask).astype(BF16), v_tile, 1, 1)
            ct = ct4[:, 128 * j : 128 * j + 128]
            cd = cd4[:, 128 * j : 128 * j + 128]
            cs = rows_ref[pl.ds(h, 1), :]
            ds = rows_ref[pl.ds(H + h, 1), :]
            et = rows_ref[pl.ds(2 * H + h, 1), :]
            x = jnp.exp(jnp.where(causal, ct - cs, -1e30)) * w
            xd = x * ds
            dgm = dgm + xd
            dgd = dgd + (x * et + cd * xd)
            q = x * g
            xgd = x * gd
            colq_ref[pl.ds(h, 1), :] = jnp.sum(q, axis=0, keepdims=True)
            colqd_ref[pl.ds(h, 1), :] = jnp.sum(xgd + q * cd, axis=0, keepdims=True)
            r1 = jnp.sum(q * ds, axis=1, keepdims=True)
            r2 = jnp.sum(xgd * ds + q * et, axis=1, keepdims=True)
            here = lane == h
            row1 = jnp.where(here, r1, row1)
            row2 = jnp.where(here, r2, row2)
        row1_ref[...] = row1
        row2_ref[...] = row2
        return dgm, dgd

    return lax.fori_loop(first, last, one, carry)


def intra_pairs(pp, dgm, dgd):
    return (
        dot_split(dgm, pp["b_bd"], 1, 0),
        dot_split(dgd, pp["b_c"], 1, 0),
        dot_split(dgm, pp["c_cd"], 0, 0),
        dot_split(dgd, pp["c_b"], 0, 0),
    )


def head_sums(x):
    return dot_left(x, head_spread(), 1, 1)


def finish_forward(pp, e_split, cotangent, xf):
    u = cotangent.astype(F32)
    x_split = split(xf)
    zz = dot_parts(split(jnp.concatenate([pp["c_o"], pp["cd_c"]], 0)), x_split, 1, 0)
    return head_sums(zz[:L] * u), head_sums(zz[L:] * u), dot_parts(e_split, x_split, 1, 1)


def finish_backward(pp, w_split, values, xb):
    v = values.astype(F32)
    x_split = split(xb)
    yy = dot_parts(split(jnp.concatenate([pp["b_o"], pp["bd_b"]], 0)), x_split, 1, 0)
    return head_sums(yy[:L] * v), head_sums(yy[L:] * v), dot_parts(w_split, x_split, 1, 1)


def sel_terms(ft, dact, dactd, scale):
    dz = scale * (ft["first"] * dact)
    return dz, scale * (ft["second"] * ft["zd"] * dact + ft["first"] * dactd)


def finish_c(ft, pairs, pc, scale):
    m = low_lanes()
    pair = pairs[0] + pc[:L] + jnp.where(m, 0.0, roll64(pairs[1] + pc[L:]))
    dz, dzd = sel_terms(ft, roll64(pair), pair, scale)
    return jnp.where(m, roll64(dz), dzd)


def finish(ft, wts, pairs, row1, row2, colq, colqd, from_forward, from_backward, xf, xb, rate, scale):
    e, ed, f, fd, w, wd = wts
    g, gdot, _ = from_forward
    kk, kdot, pb = from_backward
    kap = jnp.sum(xb[:64] * xf[:64], axis=0, keepdims=True)
    kapd = jnp.sum(xb[64:] * xf[:64] + xb[:64] * xf[64:], axis=0, keepdims=True)
    both = head_sums(jnp.concatenate([jnp.broadcast_to(kap, (8, HP)), jnp.broadcast_to(kapd, (8, HP))], 0))
    kap, kapd = both[0:1], both[8:9]

    m = low_lanes()
    pair = pairs[2] + pb[:L] + jnp.where(m, 0.0, roll64(pairs[3] + pb[L:]))
    dz, dzd = sel_terms(ft, pair, roll64(pair), scale)
    tile_b = jnp.where(m, dz, roll64(dzd))

    delta, deltad, cum, cumd = ft["delta"], ft["deltad"], ft["cum"], ft["cumd"]
    colq, colqd = colq.T, colqd.T
    colqd = colqd - cumd * colq
    row1, row2 = row1[:, :H], row2[:, :H]
    row2 = row2 + cumd * row1
    wk = w * kk
    wkd = wd * kk + w * kdot
    dc = row1 - delta * colq + e * g - wk
    dcd = row2 - (deltad * colq + delta * colqd) + ed * g + e * gdot - wkd
    el, edl = e[L - 1 :, :], ed[L - 1 :, :]
    extra = el * kap + jnp.sum(wk, axis=0, keepdims=True)
    extrad = edl * kap + el * kapd + jnp.sum(wkd, axis=0, keepdims=True)
    ddelta = colq + f * kk - rate * (cumulate(dc, True) + extra)
    ddeltad = colqd + fd * kk + f * kdot - rate * (cumulate(dcd, True) + extrad)
    sq = ft["sq"]
    dq = scale * (sq * ddelta)
    dqd = scale * (sq * (1.0 - sq) * ft["qd"] * ddelta + sq * ddeltad)
    return tile_b, dq, dqd


def place():
    x = lax.axis_index("dp")
    s = lax.axis_index("seq")
    chip = s // 2
    return x, chip // NZ, lax.rem(chip, NZ), lax.rem(s, 2), chip


def device(x, y, z, k):
    return (x, (y * NZ + z) * 2 + k)


def remote(src, dst, send_sem, recv_sem, dev):
    return pltpu.make_async_remote_copy(
        src_ref=src, dst_ref=dst, send_sem=send_sem, recv_sem=recv_sem,
        device_id=dev, device_id_type=MESH,
    )


def arrived(dst, sem, dev):
    remote(dst, dst, sem, sem, dev).wait_recv()


def sent(src, sem, dev):
    remote(src, src, sem, sem, dev).wait_send()


FAR4 = (2, 1, 3)
LANES = HALF // 256
FAR8 = (4, 3, 5, 2, 6, 1, 7)


def enter():
    x, y, z, k, chip = place()
    s = 2 * chip + k
    seq = CHIPS * 2
    partners = [device(x, y, lax.rem(z + d, NZ), k) for d in FAR8]
    partners += [device(lax.rem(x + d, NX), y, z, k) for d in FAR4]
    partners += [device(x, lax.rem(y + d, NY), z, k) for d in FAR4]
    partners += [(x, lax.rem(s + 1, seq)), (x, lax.rem(s + seq - 1, seq)), device(x, y, z, 1 - k)]
    barrier = pltpu.get_barrier_semaphore()
    for dev in partners:
        pl.semaphore_signal(barrier, inc=1, device_id=dev, device_id_type=MESH)
    return lambda: pl.semaphore_wait(barrier, len(partners))


def gather(wbuf, ext, ext_t, proj, tok_ref, s_send, s_halo, s_z, s_slab, s_swap):
    x, y, z, k, chip = place()
    s = 2 * chip + k
    mate = device(x, y, z, 1 - k)
    own = wbuf.at[x, y, z, k]
    for d in FAR8:
        remote(own, own, s_send.at[0], s_z, device(x, y, lax.rem(z + d, NZ), k)).start()
    halo = remote(
        tok_ref.at[pl.ds(L - HALO, HALO)], ext.at[pl.ds(L, HALO)], s_send.at[4], s_halo,
        (x, lax.rem(s + 1, 2 * CHIPS)),
    )
    halo.start()
    arrived(wbuf.at[x, y, pl.ds(0, NZ - 1), k], s_z, mate)

    def slab_copy(sx, sy, tx, ty, sem):
        ref = wbuf.at[sx, sy, :, k]
        return remote(ref, ref, s_send.at[sem], s_slab.at[sx * NY + sy], device(tx, ty, z, k))

    def swap(sx, sy, kk):
        ref = wbuf.at[sx, sy, :, kk]
        return remote(ref, ref, s_send.at[3], s_swap.at[sx * NY + sy], mate)

    def near(d):
        return lax.rem(x + d * k, NX), lax.rem(y + d * (1 - k), NY)

    def far(d):
        return lax.rem(x + d * (1 - k), NX), lax.rem(y + d * k, NY)

    for d in FAR4:
        slab_copy(x, y, *near(d), 1).start()
    for d in FAR4:
        slab_copy(x, y, *far(d), 2).start()
    swap(x, y, k).start()
    for d in (1, 3, 2):
        sx, sy = near(d)
        slab_copy(sx, sy, x, y, 1).wait_recv()
        for t in FAR4:
            slab_copy(sx, sy, *far(t), 2).start()
        swap(sx, sy, k).start()
    halo.wait_recv()

    @pl.when(s == 0)
    def _():
        ext[L : L + HALO, :] = jnp.zeros((HALO, ext.shape[1]), BF16)

    ext_t[:, L:] = ext[L:, :].T
    for e in (0, 1, 3, 2):
        for d in (1, 3, 2):
            fx, fy = far(d)
            sx = lax.rem(fx + e * k, NX)
            sy = lax.rem(fy + e * (1 - k), NY)
            slab_copy(sx, sy, x, y, 2).wait_recv()
            swap(sx, sy, k).start()
    depth = ext.shape[1] // NX
    total = jnp.zeros((L + HALO, WIDE), F32)
    for d in range(NX):
        sx = lax.rem(x + d, NX)
        for sy in range(NY):
            swap(sx, sy, 1 - k).wait_recv()
        at = pl.multiple_of(sx * depth, depth)
        weights = wbuf[sx].astype(F32).reshape(depth, WIDE).astype(BF16)
        total = total + dg(ext[0 : L + HALO, pl.ds(at, depth)], weights, 1, 0)
    proj[HALO:, :] = total[0:L]
    proj[0:HALO, :] = total[L:]

    def drain():
        sent(wbuf.at[0, 0, pl.ds(0, NZ - 1), 0], s_send.at[0], mate)
        sent(wbuf.at[0, pl.ds(0, NY - 1), :, 0], s_send.at[1], mate)
        sent(wbuf.at[pl.ds(0, NX - 1), :, :, 0], s_send.at[2], mate)
        sent(wbuf.at[:, :, :, 0], s_send.at[3], mate)
        halo.wait_send()

    return drain


class Half:
    def __init__(self, loc, part, snd, rcv, tot, tots, snd2, rcv2, other, st, decays, s_send, s_mate, s_one, s_row, s_two):
        self.loc, self.part, self.snd, self.rcv, self.tot, self.tots = loc, part, snd, rcv, tot, tots
        self.snd2, self.rcv2, self.other, self.st = snd2, rcv2, other, st
        self.reverse = decays is not None
        self.decays = decays if self.reverse else self
        self.rows = pl.ds(0, 16 if self.reverse else 18)
        self.s_send, self.s_mate, self.s_one, self.s_row, self.s_two = s_send, s_mate, s_one, s_row, s_two
        self.x, self.y, self.z, self.k, self.chip = place()
        self.mate = device(self.x, self.y, self.z, 1 - self.k)
        self.first = self.k == 0

    def to_mate(self):
        return remote(self.loc.at[1 - self.k], self.part, self.s_send.at[0], self.s_mate.at[0], self.mate)

    def back(self):
        return remote(self.other, self.st.at[self.k], self.s_send.at[4], self.s_mate.at[1], self.mate)

    def back_in(self):
        return remote(self.other, self.st.at[1 - self.k], self.s_send.at[4], self.s_mate.at[1], self.mate)

    def cores(self):
        own, other = self.loc[self.k], self.part[...]
        return jnp.where(self.first, own, other), jnp.where(self.first, other, own)

    def start_one(self, s, t, a, ad):
        for h in range(2):
            for j in range(NZ):
                rows = slice(8 * j, 8 * j + 8)
                for i in range(LANES):
                    at = 128 * (LANES * h + i)
                    lanes = slice(at, at + 128)
                    self.snd[h, j, i, 0:8] = s[rows, lanes]
                    self.snd[h, j, i, 8:16] = t[rows, lanes]
                    if not self.reverse:
                        self.snd[h, j, i, 16:17] = a[:, lanes]
                        self.snd[h, j, i, 17:18] = ad[:, lanes]
            for d in FAR8:
                c = lax.rem(self.z + d, NZ)
                dev = device(self.x, self.y, c, self.k)
                remote(
                    self.snd.at[h, c, :, self.rows], self.rcv.at[h, self.z, :, self.rows],
                    self.s_send.at[1], self.s_one.at[h], dev,
                ).start()
            self.rcv[h, self.z] = self.snd[h, self.z]

    @staticmethod
    def step(carry, ref, decays, c):
        s, t = carry
        a, ad = decays[*c, :, 16:17, :], decays[*c, :, 17:18, :]
        return a * s + ref[*c, :, 0:8, :], a * t + (ad * s + ref[*c, :, 8:16, :])

    def order(self, count):
        return range(count - 1, -1, -1) if self.reverse else range(count)

    def row_total(self, h):
        arrived(self.rcv.at[h, pl.ds(0, NZ - 1), :, self.rows], self.s_one.at[h], self.mate)
        carry = (jnp.zeros((LANES, 8, 128), F32),) * 2
        for c in self.order(NZ):
            carry = self.step(carry, self.rcv, self.decays.rcv, (h, c))
        self.tot[h, :, 0:8, :], self.tot[h, :, 8:16, :] = carry
        if not self.reverse:
            a, ad = self.rcv[h, 0, :, 16:17, :], self.rcv[h, 0, :, 17:18, :]
            for c in range(1, NZ):
                b, bd = self.rcv[h, c, :, 16:17, :], self.rcv[h, c, :, 17:18, :]
                a, ad = a * b, ad * b + a * bd
            self.tot[h, :, 16:17, :], self.tot[h, :, 17:18, :] = a, ad
        for d in FAR4:
            dev = device(self.x, lax.rem(self.y + d, NY), self.z, self.k)
            remote(
                self.tot.at[h, :, self.rows], self.tots.at[h, self.y, :, self.rows],
                self.s_send.at[2], self.s_row.at[h], dev,
            ).start()
        self.tots[h, self.y] = self.tot[h]

    def start_two(self, h):
        arrived(self.tots.at[h, pl.ds(0, NY - 1), :, self.rows], self.s_row.at[h], self.mate)
        carry = (jnp.zeros((LANES, 8, 128), F32),) * 2
        for row in self.order(NY):
            after = self.step(carry, self.tots, self.decays.tots, (h, row))
            ahead = (row > self.y) if self.reverse else (row < self.y)
            carry = tuple(jnp.where(ahead, new, old) for new, old in zip(after, carry))
        for c in self.order(NZ):
            self.snd2[h, c, :, 0:8, :], self.snd2[h, c, :, 8:16, :] = carry
            carry = self.step(carry, self.rcv, self.decays.rcv, (h, c))
        for d in FAR8:
            c = lax.rem(self.z + d, NZ)
            dev = device(self.x, self.y, c, self.k)
            remote(self.snd2.at[h, c], self.rcv2.at[h, self.z], self.s_send.at[3], self.s_two.at[h], dev).start()
        self.rcv2[h, self.z] = self.snd2[h, self.z]

    def wait_two(self, h):
        arrived(self.rcv2.at[h, pl.ds(0, NZ - 1)], self.s_two.at[h], self.mate)

    def assemble(self, a, ad, base, base_first):
        s, t = (
            jnp.concatenate(
                [jnp.concatenate([self.rcv2[i // LANES, j, i % LANES, rows] for j in range(NZ)], 0) for i in range(2 * LANES)], 1
            )
            for rows in (slice(0, 8), slice(8, 16))
        )
        next_s = a * s + base[0:64]
        next_t = a * t + ad * s + base[64:128]
        mine_is_base = self.first if base_first else jnp.logical_not(self.first)
        self.other[0:64, :] = jnp.where(mine_is_base, next_s, s)
        self.other[64:128, :] = jnp.where(mine_is_base, next_t, t)
        self.back().start()
        self.st[self.k, 0:64, :] = jnp.where(mine_is_base, s, next_s)
        self.st[self.k, 64:128, :] = jnp.where(mine_is_base, t, next_t)

    def drain(self):
        self.to_mate().wait_send()
        sent(self.snd.at[:, pl.ds(0, NZ - 1), :, self.rows], self.s_send.at[1], self.mate)
        sent(self.tots.at[:, pl.ds(0, NY - 1), :, self.rows], self.s_send.at[2], self.mate)
        sent(self.snd2.at[:, pl.ds(0, NZ - 1)], self.s_send.at[3], self.mate)
        self.back().wait_send()


class Sums:
    def __init__(self, ext_t, scratch, sems):
        self.ext_t, self.sc, self.sb, self.ss = ext_t, scratch[0], scratch[1], scratch[2]
        self.s_send, self.s_mate, self.s_in = sems
        self.x, self.y, self.z, self.k, self.chip = place()
        self.mate = device(self.x, self.y, self.z, 1 - self.k)
        self.holder = lax.rem(self.z, 2) == self.k
        self.order = FAR4 + (0,)

    def x_to(self, d):
        return device(lax.rem(self.x + d, NX), self.y, self.z, self.k)

    def y_to(self, d):
        return device(self.x, lax.rem(self.y + d, NY), self.z, self.k)

    def z_to(self, d):
        return device(self.x, self.y, lax.rem(self.z + d, NZ), self.k)

    def block(self, i):
        xb = lax.rem(self.x + self.order[i], NX)
        count = NY * NZ * 16
        return xb, self.ext_t[pl.ds(pl.multiple_of(xb * count, count), count), :]

    def product_c(self, dp):
        full, m = self.sc[0], self.sc[1]
        both = jnp.concatenate(split(dp), 1)
        for i in range(NX):
            xb, rows = self.block(i)
            part = dg(rows, both, 1, 0)
            full[xb] = (part[:, 0:128] + part[:, 128:256]).reshape(NY, NZ, 2, 8, 128)
            remote(full.at[xb, :, :, 1 - self.k], m.at[xb], self.s_send.at[0], self.s_mate.at[i], self.mate).start()

    def settle_c(self):
        full, m, a, r = self.sc[0:4]
        for i in range(NX):
            xb = lax.rem(self.x + self.order[i], NX)
            arrived(m.at[xb], self.s_mate.at[i], self.mate)
            a[xb] = full[xb, :, :, self.k] + m[xb]
            if i < NX - 1:
                remote(a.at[xb], r.at[i], self.s_send.at[1], self.s_in.at[0], self.x_to(self.order[i])).start()

    def second_c(self):
        a, r, b, q = self.sc[2:6]
        arrived(r, self.s_in.at[0], self.mate)
        b[...] = (a[self.x] + r[0]) + (r[1] + r[2])
        for d in FAR4:
            remote(b.at[lax.rem(self.y + d, NY)], q.at[d - 1], self.s_send.at[2], self.s_in.at[1], self.y_to(d)).start()

    def third(self, c, p, send, land):
        for d in FAR8:
            remote(c.at[lax.rem(self.z + d, NZ)], p.at[d - 1], self.s_send.at[send], self.s_in.at[land], self.z_to(d)).start()

    def third_c(self):
        b, q, c, p = self.sc[4:8]
        arrived(q, self.s_in.at[1], self.mate)
        c[...] = (b[self.y] + q[0]) + (q[1] + q[2])
        self.third(c, p, 3, 2)

    def product(self, dpb, dps):
        full, m, a, ry, rx, by, bx, qy, qx, c, p = self.sb
        g2, m2, a2, r2, b2, q2, c2, p2, e2 = self.ss
        x, y, z, k = self.x, self.y, self.z, self.k
        both = jnp.concatenate(split(dpb) + split(dps), 1)
        low_half = iota((8, 128), 1) < 64

        def settle(i):
            xb = lax.rem(x + self.order[i], NX)
            arrived(m.at[xb], self.s_mate.at[NX + i], self.mate)
            a[xb] = full[xb, :, :, k] + m[xb]
            if i < NX - 1:
                remote(
                    a.at[xb, :, pl.ds(4, 4)], rx.at[i], self.s_send.at[6], self.s_in.at[4], self.x_to(self.order[i])
                ).start()
            for d in FAR4:
                remote(
                    a.at[xb, lax.rem(y + d, NY), pl.ds(0, 4)], ry.at[d - 1, xb],
                    self.s_send.at[7], self.s_in.at[5], self.y_to(d),
                ).start()
            arrived(m2.at[xb], self.s_mate.at[2 * NX + i], self.mate)
            a2[xb] = g2[k, xb] + m2[xb]

        for i in range(NX):
            xb, rows = self.block(i)
            part = dg(rows, both, 1, 0)
            full[xb] = (part[:, 0:128] + part[:, 128:256]).reshape(NY, NZ, 2, 8, 128)
            remote(full.at[xb, :, :, 1 - k], m.at[xb], self.s_send.at[4], self.s_mate.at[NX + i], self.mate).start()
            steps = (part[:, 256:384] + part[:, 384:512]).reshape(NY, NZ // 2, 2, 2, 8, 128)
            for zp in range(2):
                g2[zp, xb] = jnp.where(low_half, steps[:, :, zp, 0], steps[:, :, zp, 1])
            remote(g2.at[1 - k, xb], m2.at[xb], self.s_send.at[5], self.s_mate.at[2 * NX + i], self.mate).start()
            if i > 1:
                settle(i - 2)
        settle(NX - 2)
        settle(NX - 1)

    def rest(self, out_ref):
        full, m, a, ry, rx, by, bx, qy, qx, c, p = self.sb
        g2, m2, a2, r2, b2, q2, c2, p2, e2 = self.ss
        x, y, z, k, mate, holder = self.x, self.y, self.z, self.k, self.mate, self.holder
        s_send, s_in = self.s_send, self.s_in
        zsend = []
        for i in range(NZ // 2):
            target = 2 * i + k
            gap = lax.rem(z - target + NZ, NZ)
            copy = remote(a2.at[:, :, i], r2.at[gap], s_send.at[8 + i], s_in.at[6], device(x, y, target, k))
            zsend.append((target != z, copy))
            pl.when(target != z)(copy.start)
        self.third_c()

        arrived(rx, s_in.at[4], mate)
        bx[...] = (a[x, :, 4:8] + rx[0]) + (rx[1] + rx[2])
        for d in FAR4:
            remote(bx.at[lax.rem(y + d, NY)], qx.at[d - 1], s_send.at[12], s_in.at[7], self.y_to(d)).start()
        arrived(ry, s_in.at[5], mate)
        by[...] = (a[:, y, 0:4] + ry[0]) + (ry[1] + ry[2])
        for d in FAR4:
            remote(by.at[lax.rem(x + d, NX)], qy.at[d - 1], s_send.at[13], s_in.at[8], self.x_to(d)).start()

        @pl.when(holder)
        def _():
            arrived(r2.at[pl.ds(1, NZ - 1)], s_in.at[6], mate)
            total = a2[:, :, z // 2] + ((r2[1] + r2[2]) + (r2[3] + r2[4]))
            b2[...] = total + ((r2[5] + r2[6]) + r2[7])
            for d in FAR4:
                remote(b2.at[lax.rem(x + d, NX)], q2.at[d - 1], s_send.at[14], s_in.at[9], self.x_to(d)).start()

        arrived(qx, s_in.at[7], mate)
        c[4:8] = (bx[y] + qx[0]) + (qx[1] + qx[2])
        arrived(qy, s_in.at[8], mate)
        c[0:4] = (by[x] + qy[0]) + (qy[1] + qy[2])
        self.third(c, p, 15, 10)
        last = remote(c2.at[y], e2, s_send.at[16], s_in.at[12], mate)

        @pl.when(holder)
        def _():
            arrived(q2, s_in.at[9], mate)
            c2[...] = (b2[x] + q2[0]) + (q2[1] + q2[2])
            for d in FAR4:
                for core in range(2):
                    row = lax.rem(y + d, NY)
                    remote(c2.at[row], p2.at[d - 1], s_send.at[17], s_in.at[11], device(x, row, z, core)).start()
            last.start()
            e2[...] = c2[y]

        cm, cr, cq, cc, cp = self.sc[1], self.sc[3], self.sc[5], self.sc[6], self.sc[7]
        for sem, ref in ((0, cm), (1, cr), (2, cq), (4, m), (5, m2), (6, rx), (7, ry), (12, qx), (13, qy)):
            sent(ref, s_send.at[sem], mate)
        for used, copy in zsend:
            pl.when(used)(copy.wait_send)

        def total(c, p):
            return c[z] + ((p[0] + p[1]) + (p[2] + p[3])) + ((p[4] + p[5]) + p[6])

        arrived(cp, s_in.at[2], mate)
        tile_c = total(cc, cp)
        arrived(p, s_in.at[10], mate)
        tile_b = total(c, p)
        m8 = iota((8, 128), 1) < 64
        out_ref[:, 0:128] = jnp.where(m8, tile_b, roll64(tile_c))
        out_ref[:, 128:256] = jnp.where(m8, roll64(tile_b), tile_c)
        arrived(p2, s_in.at[11], mate)

        @pl.when(jnp.logical_not(holder))
        def _():
            remote(c2.at[y], e2, s_send.at[16], s_in.at[12], mate).wait_recv()

        steps = (e2[...] + p2[0]) + (p2[1] + p2[2])
        out_ref[:, 256:384] = jnp.where(k == 0, steps, roll64(steps))
        sent(cp, s_send.at[3], mate)
        sent(p, s_send.at[15], mate)

        @pl.when(holder)
        def _():
            sent(q2, s_send.at[14], mate)
            sent(p.at[pl.ds(0, 6)], s_send.at[17], mate)
            last.wait_send()


def everything(scale, sw_hbm, sd_hbm, tw_hbm, td_hbm, tok_ref, v_hbm, u_hbm, conv_hbm, bias_hbm, rate_hbm,
               out_ref, v_ref, u_ref, sw_ref, sd_ref, tw_ref, td_ref, conv_ref, bias_ref, rate_ref, wbuf, ext, ext_t, proj,
               forward_scratch, backward_scratch, rows_ref, row1_ref, row2_ref, colq_ref, colqd_ref, zp_ref, reduce_scratch,
               s_in, gather_sems, forward_sems, backward_sems, reduce_sems):
    entered = enter()
    pairs = [
        (sw_hbm, sw_ref), (sd_hbm, sd_ref), (tw_hbm, tw_ref), (td_hbm, td_ref), (tok_ref, ext.at[pl.ds(0, L)]),
        (v_hbm, v_ref), (u_hbm, u_ref), (conv_hbm, conv_ref), (bias_hbm, bias_ref), (rate_hbm, rate_ref),
    ]
    local = [pltpu.make_async_copy(src, dst, s_in.at[i]) for i, (src, dst) in enumerate(pairs)]
    for c in local:
        c.start()
    x, y, z, k, _ = place()
    ext[L + HALO :, :] = jnp.zeros((ext.shape[0] - L - HALO, ext.shape[1]), BF16)
    for c in local[0:4]:
        c.wait()
    wbuf[x, y, z, k, :, 0:128] = sw_ref[...]
    wbuf[x, y, z, k, :, 128:256] = sd_ref[...]
    rows = sw_ref.shape[0]
    wbuf[x, y, z, k, :, 256:384] = jnp.concatenate(
        [tw_ref[...].astype(F32), td_ref[...].astype(F32), jnp.zeros((rows, 128 - 2 * H), F32)], 1
    ).astype(BF16)
    local[4].wait()
    ext_t[:, 0:L] = ext[0:L, :].T
    for c in local[5:]:
        c.wait()
    entered()
    drain_gather = gather(wbuf, ext, ext_t, proj, tok_ref, *gather_sems)

    rate = rate_ref[...]
    ft = features(lambda row, lane, lanes: proj[row : row + L, lane : lane + lanes], conv_ref[...], bias_ref[...], rate)
    wts = weights_of(ft)
    pp = pair_parts(ft)
    we, wde, es, eds, eu, edu = streams(wts, v_ref[...], u_ref[...])
    fw = Half(*forward_scratch, None, *forward_sems)
    bw = Half(*backward_scratch, fw, *backward_sems)
    row = iota((8, HP), 0)
    dec = jnp.where(row == 0, es[L - 1 :, :], jnp.where(row == 1, eds[L - 1 :, :], 0.0))
    states = forward_states(pp, we, wde)
    for half in range(2):
        lanes = slice(HALF * half, HALF * half + HALF)
        fw.loc[half, 0:128, :] = states[:, lanes]
        fw.loc[half, 128:136, :] = dec[:, lanes]
    fw.to_mate().start()
    states = backward_states(pp, eu, edu)
    for half in range(2):
        bw.loc[half] = states[:, HALF * half : HALF * half + HALF]
    bw.to_mate().start()

    fw.to_mate().wait_recv()
    one0, one1 = fw.cores()
    a0, ad0 = one0[128:129], one0[129:130]
    a1, ad1 = one1[128:129], one1[129:130]
    a, ad = a0 * a1, ad0 * a1 + a0 * ad1
    fw.start_one(
        a1 * one0[0:64] + one1[0:64], a1 * one0[64:128] + ad1 * one0[0:64] + one1[64:128], a, ad
    )
    bw.to_mate().wait_recv()
    one0, one1 = bw.cores()
    bw.start_one(
        a0 * one1[0:64] + one0[0:64], a0 * one1[64:128] + ad0 * one1[0:64] + one0[64:128], a, ad
    )

    def tile(ref):
        return lambda i: ref[:, pl.ds(pl.multiple_of(i * 128, 128), 128)]

    g, gd = intra_setup(ft, pp, rows_ref, row1_ref, row2_ref)
    zero = jnp.zeros((L, L), F32)

    def block_terms(first, last, carry):
        return intra(
            ft, g, gd, tile(v_ref), tile(u_ref), rows_ref, row1_ref, row2_ref, colq_ref, colqd_ref, first, last, carry
        )

    carry = block_terms(0, 7, (zero, zero))
    fw.row_total(0)
    carry = block_terms(7, 8, carry)
    fw.row_total(1)
    fw.start_two(0)
    bw.row_total(0)
    fw.start_two(1)
    bw.row_total(1)
    bw.start_two(0)
    pairs = intra_pairs(pp, *carry)
    bw.start_two(1)
    e_split = split(jnp.concatenate([eu, edu], 0))
    w_split = split(jnp.concatenate([we, wde], 0))
    fw.wait_two(0)
    fw.wait_two(1)
    fw.assemble(a0, ad0, fw.cores()[0], True)
    fw.back_in().wait_recv()
    xf = jnp.concatenate([fw.st[0], fw.st[1]], 1)
    from_forward = finish_forward(pp, e_split, u_ref[...], xf)

    conv = conv_ref[...]
    conv_roll = roll64(jnp.concatenate([conv, conv], 0))[0:KCONV]
    low = iota((KCONV, 128), 1) < 64

    def to_tokens(tile, taps, lanes):
        zp_ref[0:HALO, lanes] = jnp.zeros((HALO, 128), F32)
        zp_ref[HALO + L :, lanes] = jnp.zeros((zp_ref.shape[0] - HALO - L, 128), F32)
        zp_ref[HALO : HALO + L, lanes] = tile

        def spread(first_row, count):
            total = taps[0:1, :] * zp_ref[first_row + 3 : first_row + 3 + count, lanes]
            for tap in range(1, KCONV):
                total = total + taps[tap : tap + 1, :] * zp_ref[first_row + 3 - tap : first_row + 3 - tap + count, lanes]
            return total

        return jnp.concatenate([spread(HALO, L), spread(0, HALO), jnp.zeros((128 - HALO, 128), F32)], 0)

    sums = Sums(ext_t, reduce_scratch, reduce_sems)
    tile_c = finish_c(ft, pairs, from_forward[2], scale)
    sums.product_c(to_tokens(tile_c, jnp.where(low, conv_roll, conv), slice(0, 128)))
    bw.wait_two(0)
    bw.wait_two(1)
    bw.assemble(a1, ad1, bw.cores()[1], False)
    sums.settle_c()
    bw.back_in().wait_recv()
    xb = jnp.concatenate([bw.st[0], bw.st[1]], 1)
    from_backward = finish_backward(pp, w_split, v_ref[...], xb)
    tile_b, dq, dqd = finish(
        ft, wts, pairs, row1_ref[...], row2_ref[...], colq_ref[...], colqd_ref[...],
        from_forward, from_backward, xf, xb, rate, scale,
    )
    dpb = to_tokens(tile_b, jnp.where(low, conv, conv_roll), slice(128, 256))
    dps = jnp.concatenate([jnp.concatenate([dq, dqd, dq, dqd], 1), jnp.zeros((128, 128), F32)], 0)
    sums.second_c()
    sums.product(dpb, dps)
    sums.rest(out_ref)
    drain_gather()
    fw.drain()
    bw.drain()


def split_outputs(sums_ref, o_sel, o_step, o_selh, o_steph):
    o_sel[...] = sums_ref[:, 0:128]
    o_selh[...] = sums_ref[:, 128:256]
    o_step[...] = sums_ref[:, 256 : 256 + H]
    o_steph[...] = sums_ref[:, 256 + H : 256 + 2 * H]


def vmem(shape, dtype=F32):
    return pltpu.VMEM(shape, dtype)


def dma(*shape):
    return pltpu.SemaphoreType.DMA(shape)


def body(tokens, values, cotangent, sel_weight, step_weight, sel_dir, step_dir, conv_weight, step_bias, decay_rate):
    own_tokens, v, u = tokens[0], values[0], cotangent[0]
    depth = own_tokens.shape[1]
    rows = sel_weight.shape[0]
    scale = 1.0 / math.sqrt(NX * CHIPS * 2 * L)
    spec = pl.BlockSpec(memory_space=pltpu.VMEM)
    hbm = pl.BlockSpec(memory_space=pl.ANY)
    tile = (8, 128)
    grid = (NX, NY, NZ)
    reduce_scratch = [
        [vmem(shape + tile) for shape in (
            grid + (2,), grid, grid, (3, NY, NZ), (NY, NZ), (3, NZ), (NZ,), (7,),
        )],
        [vmem(shape + tile) for shape in (
            grid + (2,), grid, grid, (3, NX, 4), (3, NY, 4), (NX, 4), (NY, 4), (3, 4), (3, 4), (NZ,), (7,),
        )],
        [vmem(shape + tile) for shape in (
            (2, NX, NY, NZ // 2), (NX, NY, NZ // 2), (NX, NY, NZ // 2), (NZ, NX, NY), (NX, NY), (3, NY), (NY,), (3,), (),
        )],
    ]

    def scan_scratch():
        return (
            [vmem((2, NZ, LANES, 24, 128))] * 2 + [vmem((2, LANES, 24, 128)), vmem((2, NY, LANES, 24, 128))]
            + [vmem((2, NZ, LANES, 16, 128))] * 2 + [vmem((128, HALF)), vmem((2, 128, HALF))]
        )

    scratch = [
        vmem((L, HP), BF16), vmem((L, HP), BF16),
        vmem((rows, 128), BF16), vmem((rows, 128), BF16), vmem((rows, H), BF16), vmem((rows, H), BF16),
        vmem((KCONV, 128)), vmem((1, H)), vmem((1, H)),
        vmem((NX, NY, NZ, 2, rows, WIDE), BF16),
        vmem((2 * L, depth), BF16), vmem((depth, 2 * L), BF16), vmem((HALO + L, WIDE)),
        [vmem((2, 136, HALF)), vmem((136, HALF))] + scan_scratch(),
        [vmem((2, 128, HALF)), vmem((128, HALF))] + scan_scratch(),
        vmem((3 * H, L)), vmem((L, L)), vmem((L, L)), vmem((H, L)), vmem((H, L)), vmem((HALO + L + 8, 256)),
        reduce_scratch,
        dma(10),
        [dma(5), dma(), dma(), dma(NX * NY), dma(NX * NY)],
        [dma(5), dma(2), dma(2), dma(2), dma(2)],
        [dma(5), dma(2), dma(2), dma(2), dma(2)],
        [dma(18), dma(3 * NX), dma(13)],
    ]
    sums = pl.pallas_call(
        functools.partial(everything, scale),
        out_shape=jax.ShapeDtypeStruct((rows, WIDE), F32),
        in_specs=[hbm] * 10,
        out_specs=spec,
        scratch_shapes=scratch,
        compiler_params=pltpu.CompilerParams(
            vmem_limit_bytes=VMEM_LIMIT, collective_id=0, has_side_effects=True
        ),
    )(sel_weight, sel_dir, step_weight, step_dir, own_tokens, v, u, conv_weight, step_bias[None, :], decay_rate[None, :])
    return pl.pallas_call(
        split_outputs,
        out_shape=[
            jax.ShapeDtypeStruct((rows, 128), F32), jax.ShapeDtypeStruct((rows, H), F32),
            jax.ShapeDtypeStruct((rows, 128), F32), jax.ShapeDtypeStruct((rows, H), F32),
        ],
        in_specs=[spec],
        out_specs=[spec] * 4,
    )(sums)


def solution(mesh):
    shards = P(("dp", "seq"), None)
    stream = P("dp", "seq", None)
    return jax.shard_map(
        body,
        mesh=mesh,
        in_specs=(stream, stream, stream, shards, shards, shards, shards, P(), P(), P()),
        out_specs=(shards, shards, shards, shards),
        check_vma=False,
    )
```

```python
import functools
import math

import jax
import jax.numpy as jnp
from jax import lax
from jax.experimental import pallas as pl
from jax.experimental.pallas import tpu as pltpu
from jax.sharding import PartitionSpec as P

N = 64
P_SIZE = 32
H = 32
KCONV = 4
L = 128
HALO = 16
HP = H * P_SIZE
HALF = HP // 2
WIDE = 384
NX, NY, NZ = 4, 4, 8
CHIPS = NY * NZ
MESH = pl.DeviceIdType.MESH
F32 = jnp.float32
BF16 = jnp.bfloat16
VMEM_LIMIT = 56 * 1024 * 1024


def roll64(x):
    return pltpu.roll(x, 64, 1)


def split(x):
    high = x.astype(BF16)
    low = (x - high.astype(F32)).astype(BF16)
    return high, low


def split3(x):
    high = x.astype(BF16)
    rest = x - high.astype(F32)
    mid = rest.astype(BF16)
    low = (rest - mid.astype(F32)).astype(BF16)
    return high, mid, low


def dg(a, b, ca, cb):
    return lax.dot_general(a, b, (((ca,), (cb,)), ((), ())), preferred_element_type=F32)


def dot_split(a, b, ca, cb):
    return dot_parts(split(a), split(b), ca, cb)


def dot_parts(a, b, ca, cb):
    (ah, al), (bh, bl) = a, b
    return dg(ah, bh, ca, cb) + (dg(ah, bl, ca, cb) + dg(al, bh, ca, cb))


def dot_left(a, b, ca, cb):
    ah, al = split(a)
    return dg(ah, b, ca, cb) + dg(al, b, ca, cb)


def iota(shape, dim):
    return lax.broadcasted_iota(jnp.int32, shape, dim)


def low_lanes():
    return iota((L, 128), 1) < 64


def head_spread():
    return (iota((H, HP), 0) == iota((H, HP), 1) // P_SIZE).astype(F32).astype(BF16)


def triangle(reverse):
    row, column = iota((L, L), 0), iota((L, L), 1)
    keep = (column >= row) if reverse else (row >= column)
    return keep.astype(F32).astype(BF16)


def cumulate(x, reverse):
    tri = triangle(reverse)
    a, b, c = split3(x)
    return dg(tri, a, 1, 0) + (dg(tri, b, 1, 0) + dg(tri, c, 1, 0))


def features(proj, conv2, bias, rate):
    z = jnp.zeros((L, 128), F32)
    zd = jnp.zeros((L, 128), F32)
    for k in range(KCONV):
        rows = HALO - (KCONV - 1) + k
        z = z + conv2[k : k + 1, :128] * proj(rows, 0, 128)
        zd = zd + conv2[k : k + 1, :128] * proj(rows, 128, 128)
    sg = jax.nn.sigmoid(z)
    act = z * sg
    first = sg * (1.0 + z * (1.0 - sg))
    second = sg * (1.0 - sg) * (2.0 + z * (1.0 - 2.0 * sg))
    actd = first * zd
    steps = proj(HALO, 256, 128)
    q = steps[:, :H] + bias
    qd = steps[:, H : 2 * H]
    delta = jnp.maximum(q, 0.0) + jnp.log1p(jnp.exp(-jnp.abs(q)))
    sq = jax.nn.sigmoid(q)
    deltad = sq * qd
    cum = cumulate(-(delta * rate), False)
    cumd = cumulate(-(deltad * rate), False)
    return dict(
        zd=zd, act=act, actd=actd, first=first, second=second,
        qd=qd, sq=sq, delta=delta, deltad=deltad, cum=cum, cumd=cumd,
    )


def weights_of(ft):
    cum, cumd = ft["cum"], ft["cumd"]
    last, lastd = cum[L - 1 :, :], cumd[L - 1 :, :]
    e = jnp.exp(cum)
    ed = e * cumd
    f = jnp.exp(last - cum)
    fd = f * (lastd - cumd)
    w = f * ft["delta"]
    wd = fd * ft["delta"] + f * ft["deltad"]
    return e, ed, f, fd, w, wd


def pair_parts(ft):
    act, actd = ft["act"], ft["actd"]
    actr, actdr = roll64(act), roll64(actd)
    m = low_lanes()
    return dict(
        b_bd=jnp.where(m, act, actdr),
        o_b=jnp.where(m, 0.0, actr),
        c_cd=jnp.where(m, actr, actd),
        o_c=jnp.where(m, 0.0, act),
        b_o=jnp.where(m, act, 0.0),
        bd_b=jnp.where(m, actd, actr),
        c_o=jnp.where(m, actr, 0.0),
        cd_c=jnp.where(m, actdr, act),
        b_c=act,
        c_b=actr,
    )


def spread_rows(rows):
    return dot_left(rows, head_spread(), 1, 0)


def streams(wts, values, cotangent):
    e, ed, _, _, w, wd = wts
    v = values.astype(F32)
    u = cotangent.astype(F32)
    we = spread_rows(w) * v
    wde = spread_rows(wd) * v
    es = spread_rows(e)
    eds = spread_rows(ed)
    return we, wde, es, eds, es * u, eds * u


def forward_states(pp, we, wde):
    left = jnp.concatenate([pp["b_bd"], pp["o_b"]], 0)
    return dot_split(left, jnp.concatenate([we, wde], 0), 0, 0)


def backward_states(pp, eu, edu):
    left = jnp.concatenate([pp["c_cd"], pp["o_c"]], 0)
    return dot_split(left, jnp.concatenate([eu, edu], 0), 0, 0)


def intra_setup(ft, pp, rows_ref, row1_ref, row2_ref):
    g = dot_split(pp["c_o"], pp["b_c"], 1, 1)
    gd = dot_split(pp["cd_c"], pp["b_bd"], 1, 1)
    eta = ft["deltad"] - ft["delta"] * ft["cumd"]
    rows_ref[0:H, :] = ft["cum"].T
    rows_ref[H : 2 * H, :] = ft["delta"].T
    rows_ref[2 * H : 3 * H, :] = eta.T
    row1_ref[...] = jnp.zeros((L, L), F32)
    row2_ref[...] = jnp.zeros((L, L), F32)
    return g, gd


def intra(ft, g, gd, v_of, u_of, rows_ref, row1_ref, row2_ref, colq_ref, colqd_ref, first, last, carry):
    parts = split3(ft["cum"])
    partsd = split(ft["cumd"])
    row, lane = iota((L, L), 0), iota((L, L), 1)
    causal = row >= lane

    def one(i, carry):
        dgm, dgd = carry
        pick = (iota((H, 512), 0) == (4 * i + iota((H, 512), 1) // 128)).astype(F32).astype(BF16)
        ct4 = dg(parts[0], pick, 1, 0) + (dg(parts[1], pick, 1, 0) + dg(parts[2], pick, 1, 0))
        cd4 = dg(partsd[0], pick, 1, 0) + dg(partsd[1], pick, 1, 0)
        v_tile, u_tile = v_of(i), u_of(i)
        row1, row2 = row1_ref[...], row2_ref[...]
        for j in range(4):
            h = 4 * i + j
            mask = (iota((L, 128), 1) // P_SIZE == j).astype(F32)
            w = dg((u_tile.astype(F32) * mask).astype(BF16), v_tile, 1, 1)
            ct = ct4[:, 128 * j : 128 * j + 128]
            cd = cd4[:, 128 * j : 128 * j + 128]
            cs = rows_ref[pl.ds(h, 1), :]
            ds = rows_ref[pl.ds(H + h, 1), :]
            et = rows_ref[pl.ds(2 * H + h, 1), :]
            x = jnp.exp(jnp.where(causal, ct - cs, -1e30)) * w
            xd = x * ds
            dgm = dgm + xd
            dgd = dgd + (x * et + cd * xd)
            q = x * g
            xgd = x * gd
            colq_ref[pl.ds(h, 1), :] = jnp.sum(q, axis=0, keepdims=True)
            colqd_ref[pl.ds(h, 1), :] = jnp.sum(xgd + q * cd, axis=0, keepdims=True)
            r1 = jnp.sum(q * ds, axis=1, keepdims=True)
            r2 = jnp.sum(xgd * ds + q * et, axis=1, keepdims=True)
            here = lane == h
            row1 = jnp.where(here, r1, row1)
            row2 = jnp.where(here, r2, row2)
        row1_ref[...] = row1
        row2_ref[...] = row2
        return dgm, dgd

    return lax.fori_loop(first, last, one, carry)


def intra_pairs(pp, dgm, dgd):
    return (
        dot_split(dgm, pp["b_bd"], 1, 0),
        dot_split(dgd, pp["b_c"], 1, 0),
        dot_split(dgm, pp["c_cd"], 0, 0),
        dot_split(dgd, pp["c_b"], 0, 0),
    )


def head_sums(x):
    return dot_left(x, head_spread(), 1, 1)


def finish_forward(pp, e_split, cotangent, xf):
    u = cotangent.astype(F32)
    x_split = split(xf)
    zz = dot_parts(split(jnp.concatenate([pp["c_o"], pp["cd_c"]], 0)), x_split, 1, 0)
    return head_sums(zz[:L] * u), head_sums(zz[L:] * u), dot_parts(e_split, x_split, 1, 1)


def finish_backward(pp, w_split, values, xb):
    v = values.astype(F32)
    x_split = split(xb)
    yy = dot_parts(split(jnp.concatenate([pp["b_o"], pp["bd_b"]], 0)), x_split, 1, 0)
    return head_sums(yy[:L] * v), head_sums(yy[L:] * v), dot_parts(w_split, x_split, 1, 1)


def finish(ft, wts, pairs, row1, row2, colq, colqd, from_forward, from_backward, xf, xb, rate, scale):
    e, ed, f, fd, w, wd = wts
    g, gdot, pc = from_forward
    kk, kdot, pb = from_backward
    kap = jnp.sum(xb[:64] * xf[:64], axis=0, keepdims=True)
    kapd = jnp.sum(xb[64:] * xf[:64] + xb[:64] * xf[64:], axis=0, keepdims=True)
    both = head_sums(jnp.concatenate([jnp.broadcast_to(kap, (8, HP)), jnp.broadcast_to(kapd, (8, HP))], 0))
    kap, kapd = both[0:1], both[8:9]

    m = low_lanes()
    t1, t2, t3, t4 = pairs
    pair_c = t1 + pc[:L] + jnp.where(m, 0.0, roll64(t2 + pc[L:]))
    pair_b = t3 + pb[:L] + jnp.where(m, 0.0, roll64(t4 + pb[L:]))
    dact = jnp.where(m, pair_b, roll64(pair_c))
    dactd = jnp.where(m, roll64(pair_b), pair_c)
    dz = scale * (ft["first"] * dact)
    dzd = scale * (ft["second"] * ft["zd"] * dact + ft["first"] * dactd)

    delta, deltad, cum, cumd = ft["delta"], ft["deltad"], ft["cum"], ft["cumd"]
    colq, colqd = colq.T, colqd.T
    colqd = colqd - cumd * colq
    row1, row2 = row1[:, :H], row2[:, :H]
    row2 = row2 + cumd * row1
    wk = w * kk
    wkd = wd * kk + w * kdot
    dc = row1 - delta * colq + e * g - wk
    dcd = row2 - (deltad * colq + delta * colqd) + ed * g + e * gdot - wkd
    el, edl = e[L - 1 :, :], ed[L - 1 :, :]
    extra = el * kap + jnp.sum(wk, axis=0, keepdims=True)
    extrad = edl * kap + el * kapd + jnp.sum(wkd, axis=0, keepdims=True)
    ddelta = colq + f * kk - rate * (cumulate(dc, True) + extra)
    ddeltad = colqd + fd * kk + f * kdot - rate * (cumulate(dcd, True) + extrad)
    sq = ft["sq"]
    dq = scale * (sq * ddelta)
    dqd = scale * (sq * (1.0 - sq) * ft["qd"] * ddelta + sq * ddeltad)
    return dz, dzd, dq, dqd


def place():
    x = lax.axis_index("dp")
    s = lax.axis_index("seq")
    chip = s // 2
    return x, chip // NZ, lax.rem(chip, NZ), lax.rem(s, 2), chip


def device(x, y, z, k):
    return (x, (y * NZ + z) * 2 + k)


def remote(src, dst, send_sem, recv_sem, dev):
    return pltpu.make_async_remote_copy(
        src_ref=src, dst_ref=dst, send_sem=send_sem, recv_sem=recv_sem,
        device_id=dev, device_id_type=MESH,
    )


def arrived(dst, sem, dev):
    remote(dst, dst, sem, sem, dev).wait_recv()


def sent(src, sem, dev):
    remote(src, src, sem, sem, dev).wait_send()


FAR4 = (2, 1, 3)
LANES = HALF // 256
FAR8 = (4, 3, 5, 2, 6, 1, 7)


def enter():
    x, y, z, k, chip = place()
    s = 2 * chip + k
    seq = CHIPS * 2
    partners = [device(x, y, lax.rem(z + d, NZ), k) for d in FAR8]
    partners += [device(lax.rem(x + d, NX), y, z, k) for d in FAR4]
    partners += [device(x, lax.rem(y + d, NY), z, k) for d in FAR4]
    partners += [(x, lax.rem(s + 1, seq)), (x, lax.rem(s + seq - 1, seq)), device(x, y, z, 1 - k)]
    barrier = pltpu.get_barrier_semaphore()
    for dev in partners:
        pl.semaphore_signal(barrier, inc=1, device_id=dev, device_id_type=MESH)
    return lambda: pl.semaphore_wait(barrier, len(partners))


def gather(wbuf, ext, ext_t, proj, tok_ref, s_send, s_halo, s_z, s_slab, s_swap):
    x, y, z, k, chip = place()
    s = 2 * chip + k
    mate = device(x, y, z, 1 - k)
    own = wbuf.at[x, y, z, k]
    for d in FAR8:
        remote(own, own, s_send.at[0], s_z, device(x, y, lax.rem(z + d, NZ), k)).start()
    halo = remote(
        tok_ref.at[pl.ds(L - HALO, HALO)], ext.at[pl.ds(L, HALO)], s_send.at[4], s_halo,
        (x, lax.rem(s + 1, 2 * CHIPS)),
    )
    halo.start()
    arrived(wbuf.at[x, y, pl.ds(0, NZ - 1), k], s_z, mate)

    def slab_copy(sx, sy, tx, ty, sem):
        ref = wbuf.at[sx, sy, :, k]
        return remote(ref, ref, s_send.at[sem], s_slab.at[sx * NY + sy], device(tx, ty, z, k))

    def swap(sx, sy, kk):
        ref = wbuf.at[sx, sy, :, kk]
        return remote(ref, ref, s_send.at[3], s_swap.at[sx * NY + sy], mate)

    def near(d):
        return lax.rem(x + d * k, NX), lax.rem(y + d * (1 - k), NY)

    def far(d):
        return lax.rem(x + d * (1 - k), NX), lax.rem(y + d * k, NY)

    for d in FAR4:
        slab_copy(x, y, *near(d), 1).start()
    for d in FAR4:
        slab_copy(x, y, *far(d), 2).start()
    swap(x, y, k).start()
    for d in (1, 3, 2):
        sx, sy = near(d)
        slab_copy(sx, sy, x, y, 1).wait_recv()
        for t in FAR4:
            slab_copy(sx, sy, *far(t), 2).start()
        swap(sx, sy, k).start()
    halo.wait_recv()

    @pl.when(s == 0)
    def _():
        ext[L : L + HALO, :] = jnp.zeros((HALO, ext.shape[1]), BF16)

    ext_t[:, L:] = ext[L:, :].T
    for e in (0, 1, 3, 2):
        for d in (1, 3, 2):
            fx, fy = far(d)
            sx = lax.rem(fx + e * k, NX)
            sy = lax.rem(fy + e * (1 - k), NY)
            slab_copy(sx, sy, x, y, 2).wait_recv()
            swap(sx, sy, k).start()
    depth = ext.shape[1] // NX
    total = jnp.zeros((L + HALO, WIDE), F32)
    for d in range(NX):
        sx = lax.rem(x + d, NX)
        for sy in range(NY):
            swap(sx, sy, 1 - k).wait_recv()
        at = pl.multiple_of(sx * depth, depth)
        weights = wbuf[sx].astype(F32).reshape(depth, WIDE).astype(BF16)
        total = total + dg(ext[0 : L + HALO, pl.ds(at, depth)], weights, 1, 0)
    proj[HALO:, :] = total[0:L]
    proj[0:HALO, :] = total[L:]

    def drain():
        sent(wbuf.at[0, 0, pl.ds(0, NZ - 1), 0], s_send.at[0], mate)
        sent(wbuf.at[0, pl.ds(0, NY - 1), :, 0], s_send.at[1], mate)
        sent(wbuf.at[pl.ds(0, NX - 1), :, :, 0], s_send.at[2], mate)
        sent(wbuf.at[:, :, :, 0], s_send.at[3], mate)
        halo.wait_send()

    return drain


class Half:
    def __init__(self, loc, part, snd, rcv, tot, tots, snd2, rcv2, other, st, decays, s_send, s_mate, s_one, s_row, s_two):
        self.loc, self.part, self.snd, self.rcv, self.tot, self.tots = loc, part, snd, rcv, tot, tots
        self.snd2, self.rcv2, self.other, self.st = snd2, rcv2, other, st
        self.reverse = decays is not None
        self.decays = decays if self.reverse else self
        self.rows = pl.ds(0, 16 if self.reverse else 18)
        self.s_send, self.s_mate, self.s_one, self.s_row, self.s_two = s_send, s_mate, s_one, s_row, s_two
        self.x, self.y, self.z, self.k, self.chip = place()
        self.mate = device(self.x, self.y, self.z, 1 - self.k)
        self.first = self.k == 0

    def to_mate(self):
        return remote(self.loc.at[1 - self.k], self.part, self.s_send.at[0], self.s_mate.at[0], self.mate)

    def back(self):
        return remote(self.other, self.st.at[self.k], self.s_send.at[4], self.s_mate.at[1], self.mate)

    def back_in(self):
        return remote(self.other, self.st.at[1 - self.k], self.s_send.at[4], self.s_mate.at[1], self.mate)

    def cores(self):
        own, other = self.loc[self.k], self.part[...]
        return jnp.where(self.first, own, other), jnp.where(self.first, other, own)

    def start_one(self, s, t, a, ad):
        for h in range(2):
            for j in range(NZ):
                rows = slice(8 * j, 8 * j + 8)
                for i in range(LANES):
                    at = 128 * (LANES * h + i)
                    lanes = slice(at, at + 128)
                    self.snd[h, j, i, 0:8] = s[rows, lanes]
                    self.snd[h, j, i, 8:16] = t[rows, lanes]
                    if not self.reverse:
                        self.snd[h, j, i, 16:17] = a[:, lanes]
                        self.snd[h, j, i, 17:18] = ad[:, lanes]
            for d in FAR8:
                c = lax.rem(self.z + d, NZ)
                dev = device(self.x, self.y, c, self.k)
                remote(
                    self.snd.at[h, c, :, self.rows], self.rcv.at[h, self.z, :, self.rows],
                    self.s_send.at[1], self.s_one.at[h], dev,
                ).start()
            self.rcv[h, self.z] = self.snd[h, self.z]

    @staticmethod
    def step(carry, ref, decays, c):
        s, t = carry
        a, ad = decays[*c, :, 16:17, :], decays[*c, :, 17:18, :]
        return a * s + ref[*c, :, 0:8, :], a * t + (ad * s + ref[*c, :, 8:16, :])

    def order(self, count):
        return range(count - 1, -1, -1) if self.reverse else range(count)

    def row_total(self, h):
        arrived(self.rcv.at[h, pl.ds(0, NZ - 1), :, self.rows], self.s_one.at[h], self.mate)
        carry = (jnp.zeros((LANES, 8, 128), F32),) * 2
        for c in self.order(NZ):
            carry = self.step(carry, self.rcv, self.decays.rcv, (h, c))
        self.tot[h, :, 0:8, :], self.tot[h, :, 8:16, :] = carry
        if not self.reverse:
            a, ad = self.rcv[h, 0, :, 16:17, :], self.rcv[h, 0, :, 17:18, :]
            for c in range(1, NZ):
                b, bd = self.rcv[h, c, :, 16:17, :], self.rcv[h, c, :, 17:18, :]
                a, ad = a * b, ad * b + a * bd
            self.tot[h, :, 16:17, :], self.tot[h, :, 17:18, :] = a, ad
        for d in FAR4:
            dev = device(self.x, lax.rem(self.y + d, NY), self.z, self.k)
            remote(
                self.tot.at[h, :, self.rows], self.tots.at[h, self.y, :, self.rows],
                self.s_send.at[2], self.s_row.at[h], dev,
            ).start()
        self.tots[h, self.y] = self.tot[h]

    def start_two(self, h):
        arrived(self.tots.at[h, pl.ds(0, NY - 1), :, self.rows], self.s_row.at[h], self.mate)
        carry = (jnp.zeros((LANES, 8, 128), F32),) * 2
        for row in self.order(NY):
            after = self.step(carry, self.tots, self.decays.tots, (h, row))
            ahead = (row > self.y) if self.reverse else (row < self.y)
            carry = tuple(jnp.where(ahead, new, old) for new, old in zip(after, carry))
        for c in self.order(NZ):
            self.snd2[h, c, :, 0:8, :], self.snd2[h, c, :, 8:16, :] = carry
            carry = self.step(carry, self.rcv, self.decays.rcv, (h, c))
        for d in FAR8:
            c = lax.rem(self.z + d, NZ)
            dev = device(self.x, self.y, c, self.k)
            remote(self.snd2.at[h, c], self.rcv2.at[h, self.z], self.s_send.at[3], self.s_two.at[h], dev).start()
        self.rcv2[h, self.z] = self.snd2[h, self.z]

    def wait_two(self, h):
        arrived(self.rcv2.at[h, pl.ds(0, NZ - 1)], self.s_two.at[h], self.mate)

    def assemble(self, a, ad, base, base_first):
        s, t = (
            jnp.concatenate(
                [jnp.concatenate([self.rcv2[i // LANES, j, i % LANES, rows] for j in range(NZ)], 0) for i in range(2 * LANES)], 1
            )
            for rows in (slice(0, 8), slice(8, 16))
        )
        next_s = a * s + base[0:64]
        next_t = a * t + ad * s + base[64:128]
        mine_is_base = self.first if base_first else jnp.logical_not(self.first)
        self.other[0:64, :] = jnp.where(mine_is_base, next_s, s)
        self.other[64:128, :] = jnp.where(mine_is_base, next_t, t)
        self.back().start()
        self.st[self.k, 0:64, :] = jnp.where(mine_is_base, s, next_s)
        self.st[self.k, 64:128, :] = jnp.where(mine_is_base, t, next_t)

    def drain(self):
        self.to_mate().wait_send()
        sent(self.snd.at[:, pl.ds(0, NZ - 1), :, self.rows], self.s_send.at[1], self.mate)
        sent(self.tots.at[:, pl.ds(0, NY - 1), :, self.rows], self.s_send.at[2], self.mate)
        sent(self.snd2.at[:, pl.ds(0, NZ - 1)], self.s_send.at[3], self.mate)
        self.back().wait_send()


def reduce(dp, ext_t, full, g2, m01, m2, a0, a1, a2, r0, r1, r2, b0, b1, b2, q0, q1, q2, c0, c1, c2, p0, p1, p2,
           e2, s_send, s_mate, s_a, s_b, s_c, s_e, out_ref):
    x, y, z, k, chip = place()
    mate = device(x, y, z, 1 - k)
    holder = lax.rem(z, 2) == k

    def x_to(d):
        return device(lax.rem(x + d, NX), y, z, k)

    def y_to(d):
        return device(x, lax.rem(y + d, NY), z, k)

    def z_to(d):
        return device(x, y, lax.rem(z + d, NZ), k)

    both = jnp.concatenate(split(dp), 1)
    low_half = iota((8, 128), 1) < 64
    block_rows = NY * NZ * 16

    order = FAR4 + (0,)

    def settle(i):
        xb = lax.rem(x + order[i], NX)
        arrived(m01.at[:, xb], s_mate.at[i], mate)
        a0[xb] = full[0, xb, :, :, k] + m01[0, xb]
        if i < NX - 1:
            remote(a0.at[xb], r0.at[i], s_send.at[2], s_a.at[0], x_to(order[i])).start()
        a1[xb] = full[1, xb, :, :, k] + m01[1, xb]
        for d in FAR4:
            remote(a1.at[xb, lax.rem(y + d, NY)], r1.at[d - 1, xb], s_send.at[3], s_a.at[1], y_to(d)).start()
        arrived(m2.at[xb], s_mate.at[NX + i], mate)
        a2[xb] = g2[k, xb] + m2[xb]

    for i in range(NX):
        xb = lax.rem(x + order[i], NX)
        rows = ext_t[pl.ds(pl.multiple_of(xb * block_rows, block_rows), block_rows), :]
        part = dg(rows, both, 1, 0)
        part = part[:, :WIDE] + part[:, WIDE:]
        full[0, xb] = part[:, 0:128].reshape(NY, NZ, 2, 8, 128)
        full[1, xb] = part[:, 128:256].reshape(NY, NZ, 2, 8, 128)
        steps = part[:, 256:384].reshape(NY, NZ // 2, 2, 2, 8, 128)
        for zp in range(2):
            g2[zp, xb] = jnp.where(low_half, steps[:, :, zp, 0], steps[:, :, zp, 1])
        for tile in range(2):
            remote(full.at[tile, xb, :, :, 1 - k], m01.at[tile, xb], s_send.at[0], s_mate.at[i], mate).start()
        remote(g2.at[1 - k, xb], m2.at[xb], s_send.at[1], s_mate.at[NX + i], mate).start()
        if i > 1:
            settle(i - 2)
    settle(NX - 2)
    settle(NX - 1)

    zsend = []
    for i in range(NZ // 2):
        target = 2 * i + k
        gap = lax.rem(z - target + NZ, NZ)
        zsend.append((target != z, remote(a2.at[:, :, i], r2.at[gap], s_send.at[4 + i], s_a.at[2], device(x, y, target, k))))
        pl.when(zsend[-1][0])(zsend[-1][1].start)

    arrived(r0, s_a.at[0], mate)
    b0[...] = (a0[x] + r0[0]) + (r0[1] + r0[2])
    for d in FAR4:
        remote(b0.at[lax.rem(y + d, NY)], q0.at[d - 1], s_send.at[8], s_b.at[0], y_to(d)).start()
    arrived(r1, s_a.at[1], mate)
    b1[...] = (a1[:, y] + r1[0]) + (r1[1] + r1[2])
    for d in FAR4:
        remote(b1.at[lax.rem(x + d, NX)], q1.at[d - 1], s_send.at[9], s_b.at[1], x_to(d)).start()

    @pl.when(holder)
    def _():
        arrived(r2.at[pl.ds(1, NZ - 1)], s_a.at[2], mate)
        total = a2[:, :, z // 2] + ((r2[1] + r2[2]) + (r2[3] + r2[4]))
        b2[...] = total + ((r2[5] + r2[6]) + r2[7])
        for d in FAR4:
            remote(b2.at[lax.rem(x + d, NX)], q2.at[d - 1], s_send.at[10], s_b.at[2], x_to(d)).start()

    arrived(q0, s_b.at[0], mate)
    c0[...] = (b0[y] + q0[0]) + (q0[1] + q0[2])
    for d in FAR8:
        remote(c0.at[lax.rem(z + d, NZ)], p0.at[d - 1], s_send.at[11], s_c.at[0], z_to(d)).start()

    arrived(q1, s_b.at[1], mate)
    c1[...] = (b1[x] + q1[0]) + (q1[1] + q1[2])
    for d in FAR8:
        remote(c1.at[lax.rem(z + d, NZ)], p1.at[d - 1], s_send.at[13], s_c.at[1], z_to(d)).start()
    last = remote(c2.at[y], e2, s_send.at[14], s_e, mate)

    @pl.when(holder)
    def _():
        arrived(q2, s_b.at[2], mate)
        c2[...] = (b2[x] + q2[0]) + (q2[1] + q2[2])
        for d in FAR4:
            for core in range(2):
                row = lax.rem(y + d, NY)
                remote(c2.at[row], p2.at[d - 1], s_send.at[12], s_c.at[2], device(x, row, z, core)).start()
        last.start()
        e2[...] = c2[y]

    sent(m01, s_send.at[0], mate)
    sent(m2, s_send.at[1], mate)
    sent(r0, s_send.at[2], mate)
    sent(r1, s_send.at[3], mate)
    for used, copy in zsend:
        pl.when(used)(copy.wait_send)
    sent(q0, s_send.at[8], mate)
    sent(q1, s_send.at[9], mate)
    arrived(p0, s_c.at[0], mate)
    out_ref[:, 0:128] = c0[z] + ((p0[0] + p0[1]) + (p0[2] + p0[3])) + ((p0[4] + p0[5]) + p0[6])
    arrived(p1, s_c.at[1], mate)
    out_ref[:, 128:256] = c1[z] + ((p1[0] + p1[1]) + (p1[2] + p1[3])) + ((p1[4] + p1[5]) + p1[6])
    arrived(p2, s_c.at[2], mate)

    @pl.when(jnp.logical_not(holder))
    def _():
        remote(c2.at[y], e2, s_send.at[14], s_e, mate).wait_recv()

    steps = (e2[...] + p2[0]) + (p2[1] + p2[2])
    out_ref[:, 256:384] = jnp.where(k == 0, steps, roll64(steps))
    sent(p0, s_send.at[11], mate)
    sent(p1, s_send.at[13], mate)

    @pl.when(holder)
    def _():
        sent(q2, s_send.at[10], mate)
        sent(p1.at[pl.ds(0, 6)], s_send.at[12], mate)
        last.wait_send()


def everything(scale, sw_hbm, sd_hbm, tw_hbm, td_hbm, tok_ref, v_hbm, u_hbm, conv_hbm, bias_hbm, rate_hbm,
               out_ref, v_ref, u_ref, sw_ref, sd_ref, tw_ref, td_ref, conv_ref, bias_ref, rate_ref, wbuf, ext, ext_t, proj,
               forward_scratch, backward_scratch, rows_ref, row1_ref, row2_ref, colq_ref, colqd_ref, zp_ref, reduce_scratch,
               s_in, gather_sems, forward_sems, backward_sems, reduce_sems):
    entered = enter()
    pairs = [
        (sw_hbm, sw_ref), (sd_hbm, sd_ref), (tw_hbm, tw_ref), (td_hbm, td_ref), (tok_ref, ext.at[pl.ds(0, L)]),
        (v_hbm, v_ref), (u_hbm, u_ref), (conv_hbm, conv_ref), (bias_hbm, bias_ref), (rate_hbm, rate_ref),
    ]
    local = [pltpu.make_async_copy(src, dst, s_in.at[i]) for i, (src, dst) in enumerate(pairs)]
    for c in local:
        c.start()
    x, y, z, k, _ = place()
    ext[L + HALO :, :] = jnp.zeros((ext.shape[0] - L - HALO, ext.shape[1]), BF16)
    for c in local[0:4]:
        c.wait()
    wbuf[x, y, z, k, :, 0:128] = sw_ref[...]
    wbuf[x, y, z, k, :, 128:256] = sd_ref[...]
    rows = sw_ref.shape[0]
    wbuf[x, y, z, k, :, 256:384] = jnp.concatenate(
        [tw_ref[...].astype(F32), td_ref[...].astype(F32), jnp.zeros((rows, 128 - 2 * H), F32)], 1
    ).astype(BF16)
    local[4].wait()
    ext_t[:, 0:L] = ext[0:L, :].T
    for c in local[5:]:
        c.wait()
    entered()
    drain_gather = gather(wbuf, ext, ext_t, proj, tok_ref, *gather_sems)

    rate = rate_ref[...]
    ft = features(lambda row, lane, lanes: proj[row : row + L, lane : lane + lanes], conv_ref[...], bias_ref[...], rate)
    wts = weights_of(ft)
    pp = pair_parts(ft)
    we, wde, es, eds, eu, edu = streams(wts, v_ref[...], u_ref[...])
    fw = Half(*forward_scratch, None, *forward_sems)
    bw = Half(*backward_scratch, fw, *backward_sems)
    row = iota((8, HP), 0)
    dec = jnp.where(row == 0, es[L - 1 :, :], jnp.where(row == 1, eds[L - 1 :, :], 0.0))
    states = forward_states(pp, we, wde)
    for half in range(2):
        lanes = slice(HALF * half, HALF * half + HALF)
        fw.loc[half, 0:128, :] = states[:, lanes]
        fw.loc[half, 128:136, :] = dec[:, lanes]
    fw.to_mate().start()
    states = backward_states(pp, eu, edu)
    for half in range(2):
        bw.loc[half] = states[:, HALF * half : HALF * half + HALF]
    bw.to_mate().start()

    fw.to_mate().wait_recv()
    one0, one1 = fw.cores()
    a0, ad0 = one0[128:129], one0[129:130]
    a1, ad1 = one1[128:129], one1[129:130]
    a, ad = a0 * a1, ad0 * a1 + a0 * ad1
    fw.start_one(
        a1 * one0[0:64] + one1[0:64], a1 * one0[64:128] + ad1 * one0[0:64] + one1[64:128], a, ad
    )
    bw.to_mate().wait_recv()
    one0, one1 = bw.cores()
    bw.start_one(
        a0 * one1[0:64] + one0[0:64], a0 * one1[64:128] + ad0 * one1[0:64] + one0[64:128], a, ad
    )

    def tile(ref):
        return lambda i: ref[:, pl.ds(pl.multiple_of(i * 128, 128), 128)]

    g, gd = intra_setup(ft, pp, rows_ref, row1_ref, row2_ref)
    zero = jnp.zeros((L, L), F32)

    def block_terms(first, last, carry):
        return intra(
            ft, g, gd, tile(v_ref), tile(u_ref), rows_ref, row1_ref, row2_ref, colq_ref, colqd_ref, first, last, carry
        )

    carry = block_terms(0, 4, (zero, zero))
    fw.row_total(0)
    carry = block_terms(4, 6, carry)
    fw.row_total(1)
    carry = block_terms(6, 7, carry)
    fw.start_two(0)
    bw.row_total(0)
    fw.start_two(1)
    carry = block_terms(7, 8, carry)
    bw.row_total(1)
    bw.start_two(0)
    pairs = intra_pairs(pp, *carry)
    bw.start_two(1)
    e_split = split(jnp.concatenate([eu, edu], 0))
    w_split = split(jnp.concatenate([we, wde], 0))
    fw.wait_two(0)
    fw.wait_two(1)
    fw.assemble(a0, ad0, fw.cores()[0], True)
    fw.back_in().wait_recv()
    xf = jnp.concatenate([fw.st[0], fw.st[1]], 1)
    from_forward = finish_forward(pp, e_split, u_ref[...], xf)
    bw.wait_two(0)
    bw.wait_two(1)
    bw.assemble(a1, ad1, bw.cores()[1], False)
    bw.back_in().wait_recv()
    xb = jnp.concatenate([bw.st[0], bw.st[1]], 1)
    from_backward = finish_backward(pp, w_split, v_ref[...], xb)
    dz, dzd, dq, dqd = finish(
        ft, wts, pairs, row1_ref[...], row2_ref[...], colq_ref[...], colqd_ref[...],
        from_forward, from_backward, xf, xb, rate, scale,
    )
    zp_ref[...] = jnp.zeros(zp_ref.shape, F32)
    zp_ref[HALO : HALO + L, 0:128] = dz
    zp_ref[HALO : HALO + L, 128:256] = dzd
    conv = conv_ref[...]

    def spread(first_row, count, lanes):
        total = conv[0:1, :] * zp_ref[first_row + 3 : first_row + 3 + count, lanes]
        for tap in range(1, KCONV):
            total = total + conv[tap : tap + 1, :] * zp_ref[first_row + 3 - tap : first_row + 3 - tap + count, lanes]
        return total

    pad = jnp.zeros((128 - HALO, 128), F32)
    columns = []
    for half in range(2):
        lanes = slice(128 * half, 128 * half + 128)
        columns.append(jnp.concatenate([spread(HALO, L, lanes), spread(0, HALO, lanes), pad], 0))
    both = jnp.concatenate([dq, dqd, dq, dqd], 1)
    columns.append(jnp.concatenate([both, jnp.zeros((128, 128), F32)], 0))
    dp = jnp.concatenate(columns, 1)
    drain_gather()
    fw.drain()
    bw.drain()
    reduce(dp, ext_t, *reduce_scratch, *reduce_sems, out_ref)


def split_outputs(sums_ref, o_sel, o_step, o_selh, o_steph):
    o_sel[...] = sums_ref[:, 0:128]
    o_selh[...] = sums_ref[:, 128:256]
    o_step[...] = sums_ref[:, 256 : 256 + H]
    o_steph[...] = sums_ref[:, 256 + H : 256 + 2 * H]


def vmem(shape, dtype=F32):
    return pltpu.VMEM(shape, dtype)


def dma(*shape):
    return pltpu.SemaphoreType.DMA(shape)


def body(tokens, values, cotangent, sel_weight, step_weight, sel_dir, step_dir, conv_weight, step_bias, decay_rate):
    own_tokens, v, u = tokens[0], values[0], cotangent[0]
    depth = own_tokens.shape[1]
    rows = sel_weight.shape[0]
    scale = 1.0 / math.sqrt(NX * CHIPS * 2 * L)
    spec = pl.BlockSpec(memory_space=pltpu.VMEM)
    hbm = pl.BlockSpec(memory_space=pl.ANY)
    tiles = NX * NY * NZ
    reduce_scratch = (
        [vmem((2, NX, NY, NZ, 2, 8, 128)), vmem((2, NX, NY, NZ // 2, 8, 128)),
         vmem((2, NX, NY, NZ, 8, 128)), vmem((NX, NY, NZ // 2, 8, 128))]
        + [vmem((NX, NY, NZ, 8, 128))] * 2 + [vmem((NX, NY, NZ // 2, 8, 128))]
        + [vmem((3, NY, NZ, 8, 128)), vmem((3, NX, NZ, 8, 128)), vmem((NZ, NX, NY, 8, 128))]
        + [vmem((NY, NZ, 8, 128)), vmem((NX, NZ, 8, 128)), vmem((NX, NY, 8, 128))]
        + [vmem((3, NZ, 8, 128)), vmem((3, NZ, 8, 128)), vmem((3, NY, 8, 128))]
        + [vmem((NZ, 8, 128)), vmem((NZ, 8, 128)), vmem((NY, 8, 128))]
        + [vmem((7, 8, 128)), vmem((7, 8, 128)), vmem((3, 8, 128))]
        + [vmem((8, 128))]
    )

    def scan_scratch():
        return (
            [vmem((2, NZ, LANES, 24, 128))] * 2 + [vmem((2, LANES, 24, 128)), vmem((2, NY, LANES, 24, 128))]
            + [vmem((2, NZ, LANES, 16, 128))] * 2 + [vmem((128, HALF)), vmem((2, 128, HALF))]
        )

    scratch = [
        vmem((L, HP), BF16), vmem((L, HP), BF16),
        vmem((rows, 128), BF16), vmem((rows, 128), BF16), vmem((rows, H), BF16), vmem((rows, H), BF16),
        vmem((KCONV, 128)), vmem((1, H)), vmem((1, H)),
        vmem((NX, NY, NZ, 2, rows, WIDE), BF16),
        vmem((2 * L, depth), BF16), vmem((depth, 2 * L), BF16), vmem((HALO + L, WIDE)),
        [vmem((2, 136, HALF)), vmem((136, HALF))] + scan_scratch(),
        [vmem((2, 128, HALF)), vmem((128, HALF))] + scan_scratch(),
        vmem((3 * H, L)), vmem((L, L)), vmem((L, L)), vmem((H, L)), vmem((H, L)), vmem((HALO + L + 8, 256)),
        reduce_scratch,
        dma(10),
        [dma(5), dma(), dma(), dma(NX * NY), dma(NX * NY)],
        [dma(5), dma(2), dma(2), dma(2), dma(2)],
        [dma(5), dma(2), dma(2), dma(2), dma(2)],
        [dma(15), dma(2 * NX), dma(3), dma(3), dma(3), dma()],
    ]
    sums = pl.pallas_call(
        functools.partial(everything, scale),
        out_shape=jax.ShapeDtypeStruct((rows, WIDE), F32),
        in_specs=[hbm] * 10,
        out_specs=spec,
        scratch_shapes=scratch,
        compiler_params=pltpu.CompilerParams(
            vmem_limit_bytes=VMEM_LIMIT, collective_id=0, has_side_effects=True
        ),
    )(sel_weight, sel_dir, step_weight, step_dir, own_tokens, v, u, conv_weight, step_bias[None, :], decay_rate[None, :])
    return pl.pallas_call(
        split_outputs,
        out_shape=[
            jax.ShapeDtypeStruct((rows, 128), F32), jax.ShapeDtypeStruct((rows, H), F32),
            jax.ShapeDtypeStruct((rows, 128), F32), jax.ShapeDtypeStruct((rows, H), F32),
        ],
        in_specs=[spec],
        out_specs=[spec] * 4,
    )(sums)


def solution(mesh):
    shards = P(("dp", "seq"), None)
    stream = P("dp", "seq", None)
    return jax.shard_map(
        body,
        mesh=mesh,
        in_specs=(stream, stream, stream, shards, shards, shards, shards, P(), P(), P()),
        out_specs=(shards, shards, shards, shards),
        check_vma=False,
    )
```

```python
import functools
import math

import jax
import jax.numpy as jnp
from jax import lax
from jax.experimental import pallas as pl
from jax.experimental.pallas import tpu as pltpu
from jax.sharding import PartitionSpec as P

N = 64
P_SIZE = 32
H = 32
KCONV = 4
L = 128
HALO = 16
HP = H * P_SIZE
HALF = HP // 2
WIDE = 384
NX, NY, NZ = 4, 4, 8
CHIPS = NY * NZ
MESH = pl.DeviceIdType.MESH
F32 = jnp.float32
BF16 = jnp.bfloat16
VMEM_LIMIT = 56 * 1024 * 1024


def roll64(x):
    return pltpu.roll(x, 64, 1)


def split(x):
    high = x.astype(BF16)
    low = (x - high.astype(F32)).astype(BF16)
    return high, low


def split3(x):
    high = x.astype(BF16)
    rest = x - high.astype(F32)
    mid = rest.astype(BF16)
    low = (rest - mid.astype(F32)).astype(BF16)
    return high, mid, low


def dg(a, b, ca, cb):
    return lax.dot_general(a, b, (((ca,), (cb,)), ((), ())), preferred_element_type=F32)


def dot_split(a, b, ca, cb):
    return dot_parts(split(a), split(b), ca, cb)


def dot_parts(a, b, ca, cb):
    (ah, al), (bh, bl) = a, b
    return dg(ah, bh, ca, cb) + (dg(ah, bl, ca, cb) + dg(al, bh, ca, cb))


def dot_left(a, b, ca, cb):
    ah, al = split(a)
    return dg(ah, b, ca, cb) + dg(al, b, ca, cb)


def iota(shape, dim):
    return lax.broadcasted_iota(jnp.int32, shape, dim)


def low_lanes():
    return iota((L, 128), 1) < 64


def head_spread():
    return (iota((H, HP), 0) == iota((H, HP), 1) // P_SIZE).astype(F32).astype(BF16)


def triangle(reverse):
    row, column = iota((L, L), 0), iota((L, L), 1)
    keep = (column >= row) if reverse else (row >= column)
    return keep.astype(F32).astype(BF16)


def cumulate(x, reverse):
    tri = triangle(reverse)
    a, b, c = split3(x)
    return dg(tri, a, 1, 0) + (dg(tri, b, 1, 0) + dg(tri, c, 1, 0))


def features(proj, conv2, bias, rate):
    z = jnp.zeros((L, 128), F32)
    zd = jnp.zeros((L, 128), F32)
    for k in range(KCONV):
        rows = HALO - (KCONV - 1) + k
        z = z + conv2[k : k + 1, :128] * proj(rows, 0, 128)
        zd = zd + conv2[k : k + 1, :128] * proj(rows, 128, 128)
    sg = jax.nn.sigmoid(z)
    act = z * sg
    first = sg * (1.0 + z * (1.0 - sg))
    second = sg * (1.0 - sg) * (2.0 + z * (1.0 - 2.0 * sg))
    actd = first * zd
    steps = proj(HALO, 256, 128)
    q = steps[:, :H] + bias
    qd = steps[:, H : 2 * H]
    delta = jnp.maximum(q, 0.0) + jnp.log1p(jnp.exp(-jnp.abs(q)))
    sq = jax.nn.sigmoid(q)
    deltad = sq * qd
    cum = cumulate(-(delta * rate), False)
    cumd = cumulate(-(deltad * rate), False)
    return dict(
        zd=zd, act=act, actd=actd, first=first, second=second,
        qd=qd, sq=sq, delta=delta, deltad=deltad, cum=cum, cumd=cumd,
    )


def weights_of(ft):
    cum, cumd = ft["cum"], ft["cumd"]
    last, lastd = cum[L - 1 :, :], cumd[L - 1 :, :]
    e = jnp.exp(cum)
    ed = e * cumd
    f = jnp.exp(last - cum)
    fd = f * (lastd - cumd)
    w = f * ft["delta"]
    wd = fd * ft["delta"] + f * ft["deltad"]
    return e, ed, f, fd, w, wd


def pair_parts(ft):
    act, actd = ft["act"], ft["actd"]
    actr, actdr = roll64(act), roll64(actd)
    m = low_lanes()
    return dict(
        b_bd=jnp.where(m, act, actdr),
        o_b=jnp.where(m, 0.0, actr),
        c_cd=jnp.where(m, actr, actd),
        o_c=jnp.where(m, 0.0, act),
        b_o=jnp.where(m, act, 0.0),
        bd_b=jnp.where(m, actd, actr),
        c_o=jnp.where(m, actr, 0.0),
        cd_c=jnp.where(m, actdr, act),
        b_c=act,
        c_b=actr,
    )


def spread_rows(rows):
    return dot_left(rows, head_spread(), 1, 0)


def forward_streams(wts, values):
    e, ed, _, _, w, wd = wts
    v = values.astype(F32)
    last = jnp.concatenate([jnp.broadcast_to(row[L - 1 :, :], (8, H)) for row in (e, ed)], 0)
    last = spread_rows(last)
    return spread_rows(w) * v, spread_rows(wd) * v, last[0:8], last[8:16]


def backward_streams(wts, cotangent):
    u = cotangent.astype(F32)
    return spread_rows(wts[0]) * u, spread_rows(wts[1]) * u


def forward_states(pp, we, wde):
    left = jnp.concatenate([pp["b_bd"], pp["o_b"]], 0)
    return dot_split(left, jnp.concatenate([we, wde], 0), 0, 0)


def backward_states(pp, eu, edu):
    left = jnp.concatenate([pp["c_cd"], pp["o_c"]], 0)
    return dot_split(left, jnp.concatenate([eu, edu], 0), 0, 0)


def intra_setup(ft, pp, rows_ref, row1_ref, row2_ref):
    g = dot_split(pp["c_o"], pp["b_c"], 1, 1)
    gd = dot_split(pp["cd_c"], pp["b_bd"], 1, 1)
    eta = ft["deltad"] - ft["delta"] * ft["cumd"]
    rows_ref[0:H, :] = ft["cum"].T
    rows_ref[H : 2 * H, :] = ft["delta"].T
    rows_ref[2 * H : 3 * H, :] = eta.T
    row1_ref[...] = jnp.zeros((L, L), F32)
    row2_ref[...] = jnp.zeros((L, L), F32)
    return g, gd


def intra(ft, g, gd, v_of, u_of, rows_ref, row1_ref, row2_ref, colq_ref, colqd_ref, first, last, carry):
    parts = split3(ft["cum"])
    partsd = split(ft["cumd"])
    row, lane = iota((L, L), 0), iota((L, L), 1)
    causal = row >= lane

    def one(i, carry):
        dgm, dgd = carry
        pick = (iota((H, 512), 0) == (4 * i + iota((H, 512), 1) // 128)).astype(F32).astype(BF16)
        ct4 = dg(parts[0], pick, 1, 0) + (dg(parts[1], pick, 1, 0) + dg(parts[2], pick, 1, 0))
        cd4 = dg(partsd[0], pick, 1, 0) + dg(partsd[1], pick, 1, 0)
        v_tile, u_tile = v_of(i), u_of(i)
        row1, row2 = row1_ref[...], row2_ref[...]
        for j in range(4):
            h = 4 * i + j
            mask = (iota((L, 128), 1) // P_SIZE == j).astype(F32)
            w = dg((u_tile.astype(F32) * mask).astype(BF16), v_tile, 1, 1)
            ct = ct4[:, 128 * j : 128 * j + 128]
            cd = cd4[:, 128 * j : 128 * j + 128]
            cs = rows_ref[pl.ds(h, 1), :]
            ds = rows_ref[pl.ds(H + h, 1), :]
            et = rows_ref[pl.ds(2 * H + h, 1), :]
            x = jnp.exp(jnp.where(causal, ct - cs, -1e30)) * w
            xd = x * ds
            dgm = dgm + xd
            dgd = dgd + (x * et + cd * xd)
            q = x * g
            xgd = x * gd
            colq_ref[pl.ds(h, 1), :] = jnp.sum(q, axis=0, keepdims=True)
            colqd_ref[pl.ds(h, 1), :] = jnp.sum(xgd + q * cd, axis=0, keepdims=True)
            r1 = jnp.sum(q * ds, axis=1, keepdims=True)
            r2 = jnp.sum(xgd * ds + q * et, axis=1, keepdims=True)
            here = lane == h
            row1 = jnp.where(here, r1, row1)
            row2 = jnp.where(here, r2, row2)
        row1_ref[...] = row1
        row2_ref[...] = row2
        return dgm, dgd

    return lax.fori_loop(first, last, one, carry)


def intra_pairs(pp, dgm, dgd):
    return (
        dot_split(dgm, pp["b_bd"], 1, 0),
        dot_split(dgd, pp["b_c"], 1, 0),
        dot_split(dgm, pp["c_cd"], 0, 0),
        dot_split(dgd, pp["c_b"], 0, 0),
    )


def head_sums(x):
    return dot_left(x, head_spread(), 1, 1)


def finish_forward(pp, e_split, cotangent, xf):
    u = cotangent.astype(F32)
    x_split = split(xf)
    zz = dot_parts(split(jnp.concatenate([pp["c_o"], pp["cd_c"]], 0)), x_split, 1, 0)
    return head_sums(zz[:L] * u), head_sums(zz[L:] * u), dot_parts(e_split, x_split, 1, 1)


def finish_backward(pp, w_split, values, xb):
    v = values.astype(F32)
    x_split = split(xb)
    yy = dot_parts(split(jnp.concatenate([pp["b_o"], pp["bd_b"]], 0)), x_split, 1, 0)
    return head_sums(yy[:L] * v), head_sums(yy[L:] * v), dot_parts(w_split, x_split, 1, 1)


def finish(ft, wts, pairs, row1, row2, colq, colqd, from_forward, from_backward, xf, xb, rate, scale):
    e, ed, f, fd, w, wd = wts
    g, gdot, pc = from_forward
    kk, kdot, pb = from_backward
    kap = jnp.sum(xb[:64] * xf[:64], axis=0, keepdims=True)
    kapd = jnp.sum(xb[64:] * xf[:64] + xb[:64] * xf[64:], axis=0, keepdims=True)
    both = head_sums(jnp.concatenate([jnp.broadcast_to(kap, (8, HP)), jnp.broadcast_to(kapd, (8, HP))], 0))
    kap, kapd = both[0:1], both[8:9]

    m = low_lanes()
    t1, t2, t3, t4 = pairs
    pair_c = t1 + pc[:L] + jnp.where(m, 0.0, roll64(t2 + pc[L:]))
    pair_b = t3 + pb[:L] + jnp.where(m, 0.0, roll64(t4 + pb[L:]))
    dact = jnp.where(m, pair_b, roll64(pair_c))
    dactd = jnp.where(m, roll64(pair_b), pair_c)
    dz = scale * (ft["first"] * dact)
    dzd = scale * (ft["second"] * ft["zd"] * dact + ft["first"] * dactd)

    delta, deltad, cum, cumd = ft["delta"], ft["deltad"], ft["cum"], ft["cumd"]
    colqd = colqd - cumd * colq
    row1, row2 = row1[:, :H], row2[:, :H]
    row2 = row2 + cumd * row1
    wk = w * kk
    wkd = wd * kk + w * kdot
    dc = row1 - delta * colq + e * g - wk
    dcd = row2 - (deltad * colq + delta * colqd) + ed * g + e * gdot - wkd
    el, edl = e[L - 1 :, :], ed[L - 1 :, :]
    extra = el * kap + jnp.sum(wk, axis=0, keepdims=True)
    extrad = edl * kap + el * kapd + jnp.sum(wkd, axis=0, keepdims=True)
    ddelta = colq + f * kk - rate * (cumulate(dc, True) + extra)
    ddeltad = colqd + fd * kk + f * kdot - rate * (cumulate(dcd, True) + extrad)
    sq = ft["sq"]
    dq = scale * (sq * ddelta)
    dqd = scale * (sq * (1.0 - sq) * ft["qd"] * ddelta + sq * ddeltad)
    return dz, dzd, dq, dqd


def place():
    x = lax.axis_index("dp")
    s = lax.axis_index("seq")
    chip = s // 2
    return x, chip // NZ, lax.rem(chip, NZ), lax.rem(s, 2), chip


def device(x, y, z, k):
    return (x, (y * NZ + z) * 2 + k)


def remote(src, dst, send_sem, recv_sem, dev):
    return pltpu.make_async_remote_copy(
        src_ref=src, dst_ref=dst, send_sem=send_sem, recv_sem=recv_sem,
        device_id=dev, device_id_type=MESH,
    )


def arrived(dst, sem, dev):
    remote(dst, dst, sem, sem, dev).wait_recv()


def sent(src, sem, dev):
    remote(src, src, sem, sem, dev).wait_send()


FAR4 = (2, 1, 3)
LANES = HALF // 256
FAR8 = (4, 3, 5, 2, 6, 1, 7)


def enter():
    x, y, z, k, chip = place()
    s = 2 * chip + k
    seq = CHIPS * 2
    partners = [device(x, y, lax.rem(z + d, NZ), k) for d in FAR8]
    partners += [device(lax.rem(x + d, NX), y, z, k) for d in FAR4]
    partners += [device(x, lax.rem(y + d, NY), z, k) for d in FAR4]
    partners += [(x, lax.rem(s + 1, seq)), (x, lax.rem(s + seq - 1, seq)), device(x, y, z, 1 - k)]
    barrier = pltpu.get_barrier_semaphore()
    for dev in partners:
        pl.semaphore_signal(barrier, inc=1, device_id=dev, device_id_type=MESH)
    return lambda: pl.semaphore_wait(barrier, len(partners))


def gather(wbuf, ext, ext_t, proj, tok_ref, s_send, s_halo, s_z, s_slab, s_swap):
    x, y, z, k, chip = place()
    s = 2 * chip + k
    mate = device(x, y, z, 1 - k)
    own = wbuf.at[x, y, z, k]
    for d in FAR8:
        remote(own, own, s_send.at[0], s_z, device(x, y, lax.rem(z + d, NZ), k)).start()
    halo = remote(
        tok_ref.at[pl.ds(L - HALO, HALO)], ext.at[pl.ds(L, HALO)], s_send.at[4], s_halo,
        (x, lax.rem(s + 1, 2 * CHIPS)),
    )
    halo.start()
    arrived(wbuf.at[x, y, pl.ds(0, NZ - 1), k], s_z, mate)

    def slab_copy(sx, sy, tx, ty, sem):
        ref = wbuf.at[sx, sy, :, k]
        return remote(ref, ref, s_send.at[sem], s_slab.at[sx * NY + sy], device(tx, ty, z, k))

    def swap(sx, sy, kk):
        ref = wbuf.at[sx, sy, :, kk]
        return remote(ref, ref, s_send.at[3], s_swap.at[sx * NY + sy], mate)

    def near(d):
        return lax.rem(x + d * k, NX), lax.rem(y + d * (1 - k), NY)

    def far(d):
        return lax.rem(x + d * (1 - k), NX), lax.rem(y + d * k, NY)

    for d in FAR4:
        slab_copy(x, y, *near(d), 1).start()
    for d in FAR4:
        slab_copy(x, y, *far(d), 2).start()
    swap(x, y, k).start()
    for d in (1, 3, 2):
        sx, sy = near(d)
        slab_copy(sx, sy, x, y, 1).wait_recv()
        for t in FAR4:
            slab_copy(sx, sy, *far(t), 2).start()
        swap(sx, sy, k).start()
    halo.wait_recv()

    @pl.when(s == 0)
    def _():
        ext[L : L + HALO, :] = jnp.zeros((HALO, ext.shape[1]), BF16)

    ext_t[:, L : L + HALO] = ext[L:, :].T
    for e in (0, 1, 3, 2):
        for d in (1, 3, 2):
            fx, fy = far(d)
            sx = lax.rem(fx + e * k, NX)
            sy = lax.rem(fy + e * (1 - k), NY)
            slab_copy(sx, sy, x, y, 2).wait_recv()
            swap(sx, sy, k).start()
    depth = ext.shape[1] // NX
    total = jnp.zeros((L + HALO, WIDE), F32)
    for d in range(NX):
        sx = lax.rem(x + d, NX)
        for sy in range(NY):
            swap(sx, sy, 1 - k).wait_recv()
        at = pl.multiple_of(sx * depth, depth)
        weights = wbuf[sx].astype(F32).reshape(depth, WIDE).astype(BF16)
        total = total + dg(ext[0 : L + HALO, pl.ds(at, depth)], weights, 1, 0)
    proj[HALO:, :] = total[0:L]
    proj[0:HALO, :] = total[L:]

    def drain():
        sent(wbuf.at[0, 0, pl.ds(0, NZ - 1), 0], s_send.at[0], mate)
        sent(wbuf.at[0, pl.ds(0, NY - 1), :, 0], s_send.at[1], mate)
        sent(wbuf.at[pl.ds(0, NX - 1), :, :, 0], s_send.at[2], mate)
        sent(wbuf.at[:, :, :, 0], s_send.at[3], mate)
        halo.wait_send()

    return drain


class Half:
    def __init__(self, loc, part, snd, rcv, tot, tots, snd2, rcv2, other, st, decays, s_send, s_mate, s_one, s_row, s_two):
        self.loc, self.part, self.snd, self.rcv, self.tot, self.tots = loc, part, snd, rcv, tot, tots
        self.snd2, self.rcv2, self.other, self.st = snd2, rcv2, other, st
        self.reverse = decays is not None
        self.decays = decays if self.reverse else self
        self.rows = pl.ds(0, 16 if self.reverse else 18)
        self.s_send, self.s_mate, self.s_one, self.s_row, self.s_two = s_send, s_mate, s_one, s_row, s_two
        self.x, self.y, self.z, self.k, self.chip = place()
        self.mate = device(self.x, self.y, self.z, 1 - self.k)
        self.first = self.k == 0

    def to_mate(self):
        return remote(self.loc.at[1 - self.k], self.part, self.s_send.at[0], self.s_mate.at[0], self.mate)

    def back(self):
        return remote(self.other, self.st.at[self.k], self.s_send.at[4], self.s_mate.at[1], self.mate)

    def back_in(self):
        return remote(self.other, self.st.at[1 - self.k], self.s_send.at[4], self.s_mate.at[1], self.mate)

    def cores(self):
        own, other = self.loc[self.k], self.part[...]
        return jnp.where(self.first, own, other), jnp.where(self.first, other, own)

    def start_one(self, s, t, a, ad):
        for h in range(2):
            for j in range(NZ):
                rows = slice(8 * j, 8 * j + 8)
                for i in range(LANES):
                    at = 128 * (LANES * h + i)
                    lanes = slice(at, at + 128)
                    self.snd[h, j, i, 0:8] = s[rows, lanes]
                    self.snd[h, j, i, 8:16] = t[rows, lanes]
                    if not self.reverse:
                        self.snd[h, j, i, 16:17] = a[:, lanes]
                        self.snd[h, j, i, 17:18] = ad[:, lanes]
            for d in FAR8:
                c = lax.rem(self.z + d, NZ)
                dev = device(self.x, self.y, c, self.k)
                remote(
                    self.snd.at[h, c, :, self.rows], self.rcv.at[h, self.z, :, self.rows],
                    self.s_send.at[1], self.s_one.at[h], dev,
                ).start()
            self.rcv[h, self.z] = self.snd[h, self.z]

    @staticmethod
    def step(carry, ref, decays, c):
        s, t = carry
        a, ad = decays[*c, :, 16:17, :], decays[*c, :, 17:18, :]
        return a * s + ref[*c, :, 0:8, :], a * t + (ad * s + ref[*c, :, 8:16, :])

    def order(self, count):
        return range(count - 1, -1, -1) if self.reverse else range(count)

    def row_total(self, h):
        arrived(self.rcv.at[h, pl.ds(0, NZ - 1), :, self.rows], self.s_one.at[h], self.mate)
        carry = (jnp.zeros((LANES, 8, 128), F32),) * 2
        for c in self.order(NZ):
            carry = self.step(carry, self.rcv, self.decays.rcv, (h, c))
        self.tot[h, :, 0:8, :], self.tot[h, :, 8:16, :] = carry
        if not self.reverse:
            a, ad = self.rcv[h, 0, :, 16:17, :], self.rcv[h, 0, :, 17:18, :]
            for c in range(1, NZ):
                b, bd = self.rcv[h, c, :, 16:17, :], self.rcv[h, c, :, 17:18, :]
                a, ad = a * b, ad * b + a * bd
            self.tot[h, :, 16:17, :], self.tot[h, :, 17:18, :] = a, ad
        for d in FAR4:
            dev = device(self.x, lax.rem(self.y + d, NY), self.z, self.k)
            remote(
                self.tot.at[h, :, self.rows], self.tots.at[h, self.y, :, self.rows],
                self.s_send.at[2], self.s_row.at[h], dev,
            ).start()
        self.tots[h, self.y] = self.tot[h]

    def start_two(self, h):
        arrived(self.tots.at[h, pl.ds(0, NY - 1), :, self.rows], self.s_row.at[h], self.mate)
        carry = (jnp.zeros((LANES, 8, 128), F32),) * 2
        for row in self.order(NY):
            after = self.step(carry, self.tots, self.decays.tots, (h, row))
            ahead = (row > self.y) if self.reverse else (row < self.y)
            carry = tuple(jnp.where(ahead, new, old) for new, old in zip(after, carry))
        for c in self.order(NZ):
            self.snd2[h, c, :, 0:8, :], self.snd2[h, c, :, 8:16, :] = carry
            carry = self.step(carry, self.rcv, self.decays.rcv, (h, c))
        for d in FAR8:
            c = lax.rem(self.z + d, NZ)
            dev = device(self.x, self.y, c, self.k)
            remote(self.snd2.at[h, c], self.rcv2.at[h, self.z], self.s_send.at[3], self.s_two.at[h], dev).start()
        self.rcv2[h, self.z] = self.snd2[h, self.z]

    def wait_two(self, h):
        arrived(self.rcv2.at[h, pl.ds(0, NZ - 1)], self.s_two.at[h], self.mate)

    def assemble(self, a, ad, base, base_first):
        s, t = (
            jnp.concatenate(
                [jnp.concatenate([self.rcv2[i // LANES, j, i % LANES, rows] for j in range(NZ)], 0) for i in range(2 * LANES)], 1
            )
            for rows in (slice(0, 8), slice(8, 16))
        )
        next_s = a * s + base[0:64]
        next_t = a * t + ad * s + base[64:128]
        mine_is_base = self.first if base_first else jnp.logical_not(self.first)
        self.other[0:64, :] = jnp.where(mine_is_base, next_s, s)
        self.other[64:128, :] = jnp.where(mine_is_base, next_t, t)
        self.back().start()
        self.st[self.k, 0:64, :] = jnp.where(mine_is_base, s, next_s)
        self.st[self.k, 64:128, :] = jnp.where(mine_is_base, t, next_t)

    def drain(self):
        self.to_mate().wait_send()
        sent(self.snd.at[:, pl.ds(0, NZ - 1), :, self.rows], self.s_send.at[1], self.mate)
        sent(self.tots.at[:, pl.ds(0, NY - 1), :, self.rows], self.s_send.at[2], self.mate)
        sent(self.snd2.at[:, pl.ds(0, NZ - 1)], self.s_send.at[3], self.mate)
        self.back().wait_send()


def reduce(dp, ext_t, full, g2, m01, m2, a0, a1, a2, r0, r1, r2, b0, b1, b2, q0, q1, q2, c0, c1, c2, p0, p1, p2,
           e2, s_send, s_mate, s_a, s_b, s_c, s_e, out_ref):
    x, y, z, k, chip = place()
    mate = device(x, y, z, 1 - k)
    holder = lax.rem(z, 2) == k

    def x_to(d):
        return device(lax.rem(x + d, NX), y, z, k)

    def y_to(d):
        return device(x, lax.rem(y + d, NY), z, k)

    def z_to(d):
        return device(x, y, lax.rem(z + d, NZ), k)

    both = jnp.concatenate(split(dp), 1)
    low_half = iota((8, 128), 1) < 64
    block_rows = NY * NZ * 16

    order = FAR4 + (0,)

    def settle(i):
        xb = lax.rem(x + order[i], NX)
        arrived(m01.at[:, xb], s_mate.at[i], mate)
        a0[xb] = full[0, xb, :, :, k] + m01[0, xb]
        if i < NX - 1:
            remote(a0.at[xb], r0.at[i], s_send.at[2], s_a.at[0], x_to(order[i])).start()
        a1[xb] = full[1, xb, :, :, k] + m01[1, xb]
        for d in FAR4:
            remote(a1.at[xb, lax.rem(y + d, NY)], r1.at[d - 1, xb], s_send.at[3], s_a.at[1], y_to(d)).start()
        arrived(m2.at[xb], s_mate.at[NX + i], mate)
        a2[xb] = g2[k, xb] + m2[xb]

    for i in range(NX):
        xb = lax.rem(x + order[i], NX)
        rows = ext_t[pl.ds(pl.multiple_of(xb * block_rows, block_rows), block_rows), :]
        part = dg(rows, both, 1, 0)
        part = part[:, :WIDE] + part[:, WIDE:]
        full[0, xb] = part[:, 0:128].reshape(NY, NZ, 2, 8, 128)
        full[1, xb] = part[:, 128:256].reshape(NY, NZ, 2, 8, 128)
        steps = part[:, 256:384].reshape(NY, NZ // 2, 2, 2, 8, 128)
        for zp in range(2):
            g2[zp, xb] = jnp.where(low_half, steps[:, :, zp, 0], steps[:, :, zp, 1])
        for tile in range(2):
            remote(full.at[tile, xb, :, :, 1 - k], m01.at[tile, xb], s_send.at[0], s_mate.at[i], mate).start()
        remote(g2.at[1 - k, xb], m2.at[xb], s_send.at[1], s_mate.at[NX + i], mate).start()
        if i > 1:
            settle(i - 2)
    settle(NX - 2)
    settle(NX - 1)

    zsend = []
    for i in range(NZ // 2):
        target = 2 * i + k
        gap = lax.rem(z - target + NZ, NZ)
        zsend.append((target != z, remote(a2.at[:, :, i], r2.at[gap], s_send.at[4 + i], s_a.at[2], device(x, y, target, k))))
        pl.when(zsend[-1][0])(zsend[-1][1].start)

    arrived(r0, s_a.at[0], mate)
    b0[...] = (a0[x] + r0[0]) + (r0[1] + r0[2])
    for d in FAR4:
        remote(b0.at[lax.rem(y + d, NY)], q0.at[d - 1], s_send.at[8], s_b.at[0], y_to(d)).start()
    arrived(r1, s_a.at[1], mate)
    b1[...] = (a1[:, y] + r1[0]) + (r1[1] + r1[2])
    for d in FAR4:
        remote(b1.at[lax.rem(x + d, NX)], q1.at[d - 1], s_send.at[9], s_b.at[1], x_to(d)).start()

    @pl.when(holder)
    def _():
        arrived(r2.at[pl.ds(1, NZ - 1)], s_a.at[2], mate)
        total = a2[:, :, z // 2] + ((r2[1] + r2[2]) + (r2[3] + r2[4]))
        b2[...] = total + ((r2[5] + r2[6]) + r2[7])
        for d in FAR4:
            remote(b2.at[lax.rem(x + d, NX)], q2.at[d - 1], s_send.at[10], s_b.at[2], x_to(d)).start()

    arrived(q0, s_b.at[0], mate)
    c0[...] = (b0[y] + q0[0]) + (q0[1] + q0[2])
    for d in FAR8:
        remote(c0.at[lax.rem(z + d, NZ)], p0.at[d - 1], s_send.at[11], s_c.at[0], z_to(d)).start()

    arrived(q1, s_b.at[1], mate)
    c1[...] = (b1[x] + q1[0]) + (q1[1] + q1[2])
    for d in FAR8:
        remote(c1.at[lax.rem(z + d, NZ)], p1.at[d - 1], s_send.at[13], s_c.at[1], z_to(d)).start()
    last = remote(c2.at[y], e2, s_send.at[14], s_e, mate)

    @pl.when(holder)
    def _():
        arrived(q2, s_b.at[2], mate)
        c2[...] = (b2[x] + q2[0]) + (q2[1] + q2[2])
        for d in FAR4:
            for core in range(2):
                row = lax.rem(y + d, NY)
                remote(c2.at[row], p2.at[d - 1], s_send.at[12], s_c.at[2], device(x, row, z, core)).start()
        last.start()
        e2[...] = c2[y]

    sent(m01, s_send.at[0], mate)
    sent(m2, s_send.at[1], mate)
    sent(r0, s_send.at[2], mate)
    sent(r1, s_send.at[3], mate)
    for used, copy in zsend:
        pl.when(used)(copy.wait_send)
    sent(q0, s_send.at[8], mate)
    sent(q1, s_send.at[9], mate)
    arrived(p0, s_c.at[0], mate)
    out_ref[:, 0:128] = c0[z] + ((p0[0] + p0[1]) + (p0[2] + p0[3])) + ((p0[4] + p0[5]) + p0[6])
    arrived(p1, s_c.at[1], mate)
    out_ref[:, 128:256] = c1[z] + ((p1[0] + p1[1]) + (p1[2] + p1[3])) + ((p1[4] + p1[5]) + p1[6])
    arrived(p2, s_c.at[2], mate)

    @pl.when(jnp.logical_not(holder))
    def _():
        remote(c2.at[y], e2, s_send.at[14], s_e, mate).wait_recv()

    steps = (e2[...] + p2[0]) + (p2[1] + p2[2])
    out_ref[:, 256:384] = jnp.where(k == 0, steps, roll64(steps))
    sent(p0, s_send.at[11], mate)
    sent(p1, s_send.at[13], mate)

    @pl.when(holder)
    def _():
        sent(q2, s_send.at[10], mate)
        sent(p1.at[pl.ds(0, 6)], s_send.at[12], mate)
        last.wait_send()


def everything(scale, sw_hbm, sd_hbm, tw_hbm, td_hbm, tok_ref, v_hbm, u_hbm, conv_hbm, bias_hbm, rate_hbm,
               out_ref, v_ref, u_ref, sw_ref, sd_ref, tw_ref, td_ref, conv_ref, bias_ref, rate_ref, wbuf, ext, ext_t, proj,
               forward_scratch, backward_scratch, rows_ref, row1_ref, row2_ref, colq_ref, colqd_ref, zp_ref, reduce_scratch,
               s_in, gather_sems, forward_sems, backward_sems, reduce_sems):
    entered = enter()
    pairs = [
        (sw_hbm, sw_ref), (sd_hbm, sd_ref), (tw_hbm, tw_ref), (td_hbm, td_ref), (tok_ref, ext.at[pl.ds(0, L)]),
        (v_hbm, v_ref), (u_hbm, u_ref), (conv_hbm, conv_ref), (bias_hbm, bias_ref), (rate_hbm, rate_ref),
    ]
    local = [pltpu.make_async_copy(src, dst, s_in.at[i]) for i, (src, dst) in enumerate(pairs)]
    for c in local:
        c.start()
    x, y, z, k, _ = place()
    ext_t[:, L + HALO :] = jnp.zeros((ext_t.shape[0], L - HALO), BF16)
    for c in local[0:4]:
        c.wait()
    wbuf[x, y, z, k, :, 0:128] = sw_ref[...]
    wbuf[x, y, z, k, :, 128:256] = sd_ref[...]
    rows = sw_ref.shape[0]
    wbuf[x, y, z, k, :, 256:384] = jnp.concatenate(
        [tw_ref[...].astype(F32), td_ref[...].astype(F32), jnp.zeros((rows, 128 - 2 * H), F32)], 1
    ).astype(BF16)
    local[4].wait()
    ext_t[:, 0:L] = ext[0:L, :].T
    for c in local[5:]:
        c.wait()
    entered()
    drain_gather = gather(wbuf, ext, ext_t, proj, tok_ref, *gather_sems)

    rate = rate_ref[...]
    ft = features(lambda row, lane, lanes: proj[row : row + L, lane : lane + lanes], conv_ref[...], bias_ref[...], rate)
    wts = weights_of(ft)
    pp = pair_parts(ft)
    we, wde, decay, decayd = forward_streams(wts, v_ref[...])
    fw = Half(*forward_scratch, None, *forward_sems)
    bw = Half(*backward_scratch, fw, *backward_sems)
    row = iota((8, HP), 0)
    dec = jnp.where(row == 0, decay, jnp.where(row == 1, decayd, 0.0))
    states = forward_states(pp, we, wde)
    for half in range(2):
        lanes = slice(HALF * half, HALF * half + HALF)
        fw.loc[half, 0:128, :] = states[:, lanes]
        fw.loc[half, 128:136, :] = dec[:, lanes]
    fw.to_mate().start()
    eu, edu = backward_streams(wts, u_ref[...])
    states = backward_states(pp, eu, edu)
    for half in range(2):
        bw.loc[half] = states[:, HALF * half : HALF * half + HALF]
    bw.to_mate().start()

    fw.to_mate().wait_recv()
    one0, one1 = fw.cores()
    a0, ad0 = one0[128:129], one0[129:130]
    a1, ad1 = one1[128:129], one1[129:130]
    a, ad = a0 * a1, ad0 * a1 + a0 * ad1
    fw.start_one(
        a1 * one0[0:64] + one1[0:64], a1 * one0[64:128] + ad1 * one0[0:64] + one1[64:128], a, ad
    )
    bw.to_mate().wait_recv()
    one0, one1 = bw.cores()
    bw.start_one(
        a0 * one1[0:64] + one0[0:64], a0 * one1[64:128] + ad0 * one1[0:64] + one0[64:128], a, ad
    )

    def tile(ref):
        return lambda i: ref[:, pl.ds(pl.multiple_of(i * 128, 128), 128)]

    g, gd = intra_setup(ft, pp, rows_ref, row1_ref, row2_ref)
    zero = jnp.zeros((L, L), F32)

    def block_terms(first, last, carry):
        return intra(
            ft, g, gd, tile(v_ref), tile(u_ref), rows_ref, row1_ref, row2_ref, colq_ref, colqd_ref, first, last, carry
        )

    carry = block_terms(0, 4, (zero, zero))
    fw.row_total(0)
    carry = block_terms(4, 6, carry)
    fw.row_total(1)
    carry = block_terms(6, 7, carry)
    fw.start_two(0)
    bw.row_total(0)
    fw.start_two(1)
    carry = block_terms(7, 8, carry)
    bw.row_total(1)
    bw.start_two(0)
    pairs = intra_pairs(pp, *carry)
    bw.start_two(1)
    e_split = split(jnp.concatenate([eu, edu], 0))
    w_split = split(jnp.concatenate([we, wde], 0))
    fw.wait_two(0)
    fw.wait_two(1)
    fw.assemble(a0, ad0, fw.cores()[0], True)
    fw.back_in().wait_recv()
    xf = jnp.concatenate([fw.st[0], fw.st[1]], 1)
    from_forward = finish_forward(pp, e_split, u_ref[...], xf)
    colq, colqd = colq_ref[...].T, colqd_ref[...].T
    bw.wait_two(0)
    bw.wait_two(1)
    bw.assemble(a1, ad1, bw.cores()[1], False)
    bw.back_in().wait_recv()
    xb = jnp.concatenate([bw.st[0], bw.st[1]], 1)
    from_backward = finish_backward(pp, w_split, v_ref[...], xb)
    dz, dzd, dq, dqd = finish(
        ft, wts, pairs, row1_ref[...], row2_ref[...], colq, colqd,
        from_forward, from_backward, xf, xb, rate, scale,
    )
    zp_ref[...] = jnp.zeros(zp_ref.shape, F32)
    zp_ref[HALO : HALO + L, 0:128] = dz
    zp_ref[HALO : HALO + L, 128:256] = dzd
    conv = conv_ref[...]

    def spread(first_row, count, lanes):
        total = conv[0:1, :] * zp_ref[first_row + 3 : first_row + 3 + count, lanes]
        for tap in range(1, KCONV):
            total = total + conv[tap : tap + 1, :] * zp_ref[first_row + 3 - tap : first_row + 3 - tap + count, lanes]
        return total

    pad = jnp.zeros((128 - HALO, 128), F32)
    columns = []
    for half in range(2):
        lanes = slice(128 * half, 128 * half + 128)
        columns.append(jnp.concatenate([spread(HALO, L, lanes), spread(0, HALO, lanes), pad], 0))
    both = jnp.concatenate([dq, dqd, dq, dqd], 1)
    columns.append(jnp.concatenate([both, jnp.zeros((128, 128), F32)], 0))
    dp = jnp.concatenate(columns, 1)
    drain_gather()
    fw.drain()
    bw.drain()
    reduce(dp, ext_t, *reduce_scratch, *reduce_sems, out_ref)


def split_outputs(sums_ref, o_sel, o_step, o_selh, o_steph):
    o_sel[...] = sums_ref[:, 0:128]
    o_selh[...] = sums_ref[:, 128:256]
    o_step[...] = sums_ref[:, 256 : 256 + H]
    o_steph[...] = sums_ref[:, 256 + H : 256 + 2 * H]


def vmem(shape, dtype=F32):
    return pltpu.VMEM(shape, dtype)


def dma(*shape):
    return pltpu.SemaphoreType.DMA(shape)


def body(tokens, values, cotangent, sel_weight, step_weight, sel_dir, step_dir, conv_weight, step_bias, decay_rate):
    own_tokens, v, u = tokens[0], values[0], cotangent[0]
    depth = own_tokens.shape[1]
    rows = sel_weight.shape[0]
    scale = 1.0 / math.sqrt(NX * CHIPS * 2 * L)
    spec = pl.BlockSpec(memory_space=pltpu.VMEM)
    hbm = pl.BlockSpec(memory_space=pl.ANY)
    tiles = NX * NY * NZ
    reduce_scratch = (
        [vmem((2, NX, NY, NZ, 2, 8, 128)), vmem((2, NX, NY, NZ // 2, 8, 128)),
         vmem((2, NX, NY, NZ, 8, 128)), vmem((NX, NY, NZ // 2, 8, 128))]
        + [vmem((NX, NY, NZ, 8, 128))] * 2 + [vmem((NX, NY, NZ // 2, 8, 128))]
        + [vmem((3, NY, NZ, 8, 128)), vmem((3, NX, NZ, 8, 128)), vmem((NZ, NX, NY, 8, 128))]
        + [vmem((NY, NZ, 8, 128)), vmem((NX, NZ, 8, 128)), vmem((NX, NY, 8, 128))]
        + [vmem((3, NZ, 8, 128)), vmem((3, NZ, 8, 128)), vmem((3, NY, 8, 128))]
        + [vmem((NZ, 8, 128)), vmem((NZ, 8, 128)), vmem((NY, 8, 128))]
        + [vmem((7, 8, 128)), vmem((7, 8, 128)), vmem((3, 8, 128))]
        + [vmem((8, 128))]
    )

    def scan_scratch():
        return (
            [vmem((2, NZ, LANES, 24, 128))] * 2 + [vmem((2, LANES, 24, 128)), vmem((2, NY, LANES, 24, 128))]
            + [vmem((2, NZ, LANES, 16, 128))] * 2 + [vmem((128, HALF)), vmem((2, 128, HALF))]
        )

    scratch = [
        vmem((L, HP), BF16), vmem((L, HP), BF16),
        vmem((rows, 128), BF16), vmem((rows, 128), BF16), vmem((rows, H), BF16), vmem((rows, H), BF16),
        vmem((KCONV, 128)), vmem((1, H)), vmem((1, H)),
        vmem((NX, NY, NZ, 2, rows, WIDE), BF16),
        vmem((L + HALO, depth), BF16), vmem((depth, 2 * L), BF16), vmem((HALO + L, WIDE)),
        [vmem((2, 136, HALF)), vmem((136, HALF))] + scan_scratch(),
        [vmem((2, 128, HALF)), vmem((128, HALF))] + scan_scratch(),
        vmem((3 * H, L)), vmem((L, L)), vmem((L, L)), vmem((H, L)), vmem((H, L)), vmem((HALO + L + 8, 256)),
        reduce_scratch,
        dma(10),
        [dma(5), dma(), dma(), dma(NX * NY), dma(NX * NY)],
        [dma(5), dma(2), dma(2), dma(2), dma(2)],
        [dma(5), dma(2), dma(2), dma(2), dma(2)],
        [dma(15), dma(2 * NX), dma(3), dma(3), dma(3), dma()],
    ]
    sums = pl.pallas_call(
        functools.partial(everything, scale),
        out_shape=jax.ShapeDtypeStruct((rows, WIDE), F32),
        in_specs=[hbm] * 10,
        out_specs=spec,
        scratch_shapes=scratch,
        compiler_params=pltpu.CompilerParams(
            vmem_limit_bytes=VMEM_LIMIT, collective_id=0, has_side_effects=True
        ),
    )(sel_weight, sel_dir, step_weight, step_dir, own_tokens, v, u, conv_weight, step_bias[None, :], decay_rate[None, :])
    return pl.pallas_call(
        split_outputs,
        out_shape=[
            jax.ShapeDtypeStruct((rows, 128), F32), jax.ShapeDtypeStruct((rows, H), F32),
            jax.ShapeDtypeStruct((rows, 128), F32), jax.ShapeDtypeStruct((rows, H), F32),
        ],
        in_specs=[spec],
        out_specs=[spec] * 4,
    )(sums)


def solution(mesh):
    shards = P(("dp", "seq"), None)
    stream = P("dp", "seq", None)
    return jax.shard_map(
        body,
        mesh=mesh,
        in_specs=(stream, stream, stream, shards, shards, shards, shards, P(), P(), P()),
        out_specs=(shards, shards, shards, shards),
        check_vma=False,
    )
```

```python
import functools
import math

import jax
import jax.numpy as jnp
from jax import lax
from jax.experimental import pallas as pl
from jax.experimental.pallas import tpu as pltpu
from jax.sharding import PartitionSpec as P

N = 64
P_SIZE = 32
H = 32
KCONV = 4
L = 128
HALO = 16
HP = H * P_SIZE
HALF = HP // 2
WIDE = 384
NX, NY, NZ = 4, 4, 8
CHIPS = NY * NZ
MESH = pl.DeviceIdType.MESH
F32 = jnp.float32
BF16 = jnp.bfloat16
VMEM_LIMIT = 56 * 1024 * 1024


def roll64(x):
    return pltpu.roll(x, 64, 1)


def split(x):
    high = x.astype(BF16)
    low = (x - high.astype(F32)).astype(BF16)
    return high, low


def split3(x):
    high = x.astype(BF16)
    rest = x - high.astype(F32)
    mid = rest.astype(BF16)
    low = (rest - mid.astype(F32)).astype(BF16)
    return high, mid, low


def dg(a, b, ca, cb):
    return lax.dot_general(a, b, (((ca,), (cb,)), ((), ())), preferred_element_type=F32)


def dot_split(a, b, ca, cb):
    return dot_parts(split(a), split(b), ca, cb)


def dot_parts(a, b, ca, cb):
    (ah, al), (bh, bl) = a, b
    return dg(ah, bh, ca, cb) + (dg(ah, bl, ca, cb) + dg(al, bh, ca, cb))


def dot_left(a, b, ca, cb):
    ah, al = split(a)
    return dg(ah, b, ca, cb) + dg(al, b, ca, cb)


def iota(shape, dim):
    return lax.broadcasted_iota(jnp.int32, shape, dim)


def low_lanes():
    return iota((L, 128), 1) < 64


def head_spread():
    return (iota((H, HP), 0) == iota((H, HP), 1) // P_SIZE).astype(F32).astype(BF16)


def triangle(reverse):
    row, column = iota((L, L), 0), iota((L, L), 1)
    keep = (column >= row) if reverse else (row >= column)
    return keep.astype(F32).astype(BF16)


def cumulate(x, reverse):
    tri = triangle(reverse)
    a, b, c = split3(x)
    return dg(tri, a, 1, 0) + (dg(tri, b, 1, 0) + dg(tri, c, 1, 0))


def features(proj, conv2, bias, rate):
    z = jnp.zeros((L, 128), F32)
    zd = jnp.zeros((L, 128), F32)
    for k in range(KCONV):
        rows = HALO - (KCONV - 1) + k
        z = z + conv2[k : k + 1, :128] * proj(rows, 0, 128)
        zd = zd + conv2[k : k + 1, :128] * proj(rows, 128, 128)
    sg = jax.nn.sigmoid(z)
    act = z * sg
    first = sg * (1.0 + z * (1.0 - sg))
    second = sg * (1.0 - sg) * (2.0 + z * (1.0 - 2.0 * sg))
    actd = first * zd
    steps = proj(HALO, 256, 128)
    q = steps[:, :H] + bias
    qd = steps[:, H : 2 * H]
    delta = jnp.maximum(q, 0.0) + jnp.log1p(jnp.exp(-jnp.abs(q)))
    sq = jax.nn.sigmoid(q)
    deltad = sq * qd
    cum = cumulate(-(delta * rate), False)
    cumd = cumulate(-(deltad * rate), False)
    return dict(
        zd=zd, act=act, actd=actd, first=first, second=second,
        qd=qd, sq=sq, delta=delta, deltad=deltad, cum=cum, cumd=cumd,
    )


def weights_of(ft):
    cum, cumd = ft["cum"], ft["cumd"]
    last, lastd = cum[L - 1 :, :], cumd[L - 1 :, :]
    e = jnp.exp(cum)
    ed = e * cumd
    f = jnp.exp(last - cum)
    fd = f * (lastd - cumd)
    w = f * ft["delta"]
    wd = fd * ft["delta"] + f * ft["deltad"]
    return e, ed, f, fd, w, wd


def pair_parts(ft):
    act, actd = ft["act"], ft["actd"]
    actr, actdr = roll64(act), roll64(actd)
    m = low_lanes()
    return dict(
        b_bd=jnp.where(m, act, actdr),
        o_b=jnp.where(m, 0.0, actr),
        c_cd=jnp.where(m, actr, actd),
        o_c=jnp.where(m, 0.0, act),
        b_o=jnp.where(m, act, 0.0),
        bd_b=jnp.where(m, actd, actr),
        c_o=jnp.where(m, actr, 0.0),
        cd_c=jnp.where(m, actdr, act),
        b_c=act,
        c_b=actr,
    )


def spread_rows(rows):
    return dot_left(rows, head_spread(), 1, 0)


def forward_streams(wts, values):
    e, ed, _, _, w, wd = wts
    v = values.astype(F32)
    last = jnp.concatenate([jnp.broadcast_to(row[L - 1 :, :], (8, H)) for row in (e, ed)], 0)
    last = spread_rows(last)
    return spread_rows(w) * v, spread_rows(wd) * v, last[0:8], last[8:16]


def backward_streams(wts, cotangent):
    u = cotangent.astype(F32)
    return spread_rows(wts[0]) * u, spread_rows(wts[1]) * u


def forward_states(pp, we, wde):
    left = jnp.concatenate([pp["b_bd"], pp["o_b"]], 0)
    return dot_split(left, jnp.concatenate([we, wde], 0), 0, 0)


def backward_states(pp, eu, edu):
    left = jnp.concatenate([pp["c_cd"], pp["o_c"]], 0)
    return dot_split(left, jnp.concatenate([eu, edu], 0), 0, 0)


def intra_setup(ft, pp, rows_ref, row1_ref, row2_ref):
    g = dot_split(pp["c_o"], pp["b_c"], 1, 1)
    gd = dot_split(pp["cd_c"], pp["b_bd"], 1, 1)
    eta = ft["deltad"] - ft["delta"] * ft["cumd"]
    rows_ref[0:H, :] = ft["cum"].T
    rows_ref[H : 2 * H, :] = ft["delta"].T
    rows_ref[2 * H : 3 * H, :] = eta.T
    row1_ref[...] = jnp.zeros((L, L), F32)
    row2_ref[...] = jnp.zeros((L, L), F32)
    return g, gd


def intra(ft, g, gd, v_of, u_of, rows_ref, row1_ref, row2_ref, colq_ref, colqd_ref, first, last, carry):
    parts = split3(ft["cum"])
    partsd = split(ft["cumd"])
    row, lane = iota((L, L), 0), iota((L, L), 1)
    causal = row >= lane

    def one(i, carry):
        dgm, dgd = carry
        pick = (iota((H, 512), 0) == (4 * i + iota((H, 512), 1) // 128)).astype(F32).astype(BF16)
        ct4 = dg(parts[0], pick, 1, 0) + (dg(parts[1], pick, 1, 0) + dg(parts[2], pick, 1, 0))
        cd4 = dg(partsd[0], pick, 1, 0) + dg(partsd[1], pick, 1, 0)
        v_tile, u_tile = v_of(i), u_of(i)
        row1, row2 = row1_ref[...], row2_ref[...]
        for j in range(4):
            h = 4 * i + j
            mask = (iota((L, 128), 1) // P_SIZE == j).astype(F32)
            w = dg((u_tile.astype(F32) * mask).astype(BF16), v_tile, 1, 1)
            ct = ct4[:, 128 * j : 128 * j + 128]
            cd = cd4[:, 128 * j : 128 * j + 128]
            cs = rows_ref[pl.ds(h, 1), :]
            ds = rows_ref[pl.ds(H + h, 1), :]
            et = rows_ref[pl.ds(2 * H + h, 1), :]
            x = jnp.exp(jnp.where(causal, ct - cs, -1e30)) * w
            xd = x * ds
            dgm = dgm + xd
            dgd = dgd + (x * et + cd * xd)
            q = x * g
            xgd = x * gd
            colq_ref[pl.ds(h, 1), :] = jnp.sum(q, axis=0, keepdims=True)
            colqd_ref[pl.ds(h, 1), :] = jnp.sum(xgd + q * cd, axis=0, keepdims=True)
            r1 = jnp.sum(q * ds, axis=1, keepdims=True)
            r2 = jnp.sum(xgd * ds + q * et, axis=1, keepdims=True)
            here = lane == h
            row1 = jnp.where(here, r1, row1)
            row2 = jnp.where(here, r2, row2)
        row1_ref[...] = row1
        row2_ref[...] = row2
        return dgm, dgd

    return lax.fori_loop(first, last, one, carry)


def intra_pairs(pp, dgm, dgd):
    return (
        dot_split(dgm, pp["b_bd"], 1, 0),
        dot_split(dgd, pp["b_c"], 1, 0),
        dot_split(dgm, pp["c_cd"], 0, 0),
        dot_split(dgd, pp["c_b"], 0, 0),
    )


def head_sums(x):
    return dot_left(x, head_spread(), 1, 1)


def finish_forward(pp, e_split, cotangent, xf):
    u = cotangent.astype(F32)
    x_split = split(xf)
    zz = dot_parts(split(jnp.concatenate([pp["c_o"], pp["cd_c"]], 0)), x_split, 1, 0)
    return head_sums(zz[:L] * u), head_sums(zz[L:] * u), dot_parts(e_split, x_split, 1, 1)


def finish_backward(pp, w_split, values, xb):
    v = values.astype(F32)
    x_split = split(xb)
    yy = dot_parts(split(jnp.concatenate([pp["b_o"], pp["bd_b"]], 0)), x_split, 1, 0)
    return head_sums(yy[:L] * v), head_sums(yy[L:] * v), dot_parts(w_split, x_split, 1, 1)


def finish(ft, wts, pairs, row1, row2, colq, colqd, from_forward, from_backward, xf, xb, rate, scale):
    e, ed, f, fd, w, wd = wts
    g, gdot, pc = from_forward
    kk, kdot, pb = from_backward
    kap = jnp.sum(xb[:64] * xf[:64], axis=0, keepdims=True)
    kapd = jnp.sum(xb[64:] * xf[:64] + xb[:64] * xf[64:], axis=0, keepdims=True)
    both = head_sums(jnp.concatenate([jnp.broadcast_to(kap, (8, HP)), jnp.broadcast_to(kapd, (8, HP))], 0))
    kap, kapd = both[0:1], both[8:9]

    m = low_lanes()
    t1, t2, t3, t4 = pairs
    pair_c = t1 + pc[:L] + jnp.where(m, 0.0, roll64(t2 + pc[L:]))
    pair_b = t3 + pb[:L] + jnp.where(m, 0.0, roll64(t4 + pb[L:]))
    dact = jnp.where(m, pair_b, roll64(pair_c))
    dactd = jnp.where(m, roll64(pair_b), pair_c)
    dz = scale * (ft["first"] * dact)
    dzd = scale * (ft["second"] * ft["zd"] * dact + ft["first"] * dactd)

    delta, deltad, cum, cumd = ft["delta"], ft["deltad"], ft["cum"], ft["cumd"]
    colqd = colqd - cumd * colq
    row1, row2 = row1[:, :H], row2[:, :H]
    row2 = row2 + cumd * row1
    wk = w * kk
    wkd = wd * kk + w * kdot
    dc = row1 - delta * colq + e * g - wk
    dcd = row2 - (deltad * colq + delta * colqd) + ed * g + e * gdot - wkd
    el, edl = e[L - 1 :, :], ed[L - 1 :, :]
    extra = el * kap + jnp.sum(wk, axis=0, keepdims=True)
    extrad = edl * kap + el * kapd + jnp.sum(wkd, axis=0, keepdims=True)
    ddelta = colq + f * kk - rate * (cumulate(dc, True) + extra)
    ddeltad = colqd + fd * kk + f * kdot - rate * (cumulate(dcd, True) + extrad)
    sq = ft["sq"]
    dq = scale * (sq * ddelta)
    dqd = scale * (sq * (1.0 - sq) * ft["qd"] * ddelta + sq * ddeltad)
    return dz, dzd, dq, dqd


def place():
    x = lax.axis_index("dp")
    s = lax.axis_index("seq")
    chip = s // 2
    return x, chip // NZ, lax.rem(chip, NZ), lax.rem(s, 2), chip


def device(x, y, z, k):
    return (x, (y * NZ + z) * 2 + k)


def remote(src, dst, send_sem, recv_sem, dev):
    return pltpu.make_async_remote_copy(
        src_ref=src, dst_ref=dst, send_sem=send_sem, recv_sem=recv_sem,
        device_id=dev, device_id_type=MESH,
    )


def arrived(dst, sem, dev):
    remote(dst, dst, sem, sem, dev).wait_recv()


def sent(src, sem, dev):
    remote(src, src, sem, sem, dev).wait_send()


FAR4 = (2, 1, 3)
LANES = HALF // 256
FAR8 = (4, 3, 5, 2, 6, 1, 7)


def enter():
    x, y, z, k, chip = place()
    s = 2 * chip + k
    seq = CHIPS * 2
    partners = [device(x, y, lax.rem(z + d, NZ), k) for d in FAR8]
    partners += [device(lax.rem(x + d, NX), y, z, k) for d in FAR4]
    partners += [device(x, lax.rem(y + d, NY), z, k) for d in FAR4]
    partners += [(x, lax.rem(s + 1, seq)), (x, lax.rem(s + seq - 1, seq)), device(x, y, z, 1 - k)]
    barrier = pltpu.get_barrier_semaphore()
    for dev in partners:
        pl.semaphore_signal(barrier, inc=1, device_id=dev, device_id_type=MESH)
    return lambda: pl.semaphore_wait(barrier, len(partners))


def gather(wbuf, ext, ext_t, proj, tok_ref, s_send, s_halo, s_z, s_slab, s_swap):
    x, y, z, k, chip = place()
    s = 2 * chip + k
    mate = device(x, y, z, 1 - k)
    own = wbuf.at[x, y, z, k]
    for d in FAR8:
        remote(own, own, s_send.at[0], s_z, device(x, y, lax.rem(z + d, NZ), k)).start()
    halo = remote(
        tok_ref.at[pl.ds(L - HALO, HALO)], ext.at[pl.ds(L, HALO)], s_send.at[4], s_halo,
        (x, lax.rem(s + 1, 2 * CHIPS)),
    )
    halo.start()
    arrived(wbuf.at[x, y, pl.ds(0, NZ - 1), k], s_z, mate)

    def slab_copy(sx, sy, tx, ty, sem):
        ref = wbuf.at[sx, sy, :, k]
        return remote(ref, ref, s_send.at[sem], s_slab.at[sx * NY + sy], device(tx, ty, z, k))

    def swap(sx, sy, kk):
        ref = wbuf.at[sx, sy, :, kk]
        return remote(ref, ref, s_send.at[3], s_swap.at[sx * NY + sy], mate)

    def near(d):
        return lax.rem(x + d * k, NX), lax.rem(y + d * (1 - k), NY)

    def far(d):
        return lax.rem(x + d * (1 - k), NX), lax.rem(y + d * k, NY)

    for d in FAR4:
        slab_copy(x, y, *near(d), 1).start()
    for d in FAR4:
        slab_copy(x, y, *far(d), 2).start()
    swap(x, y, k).start()
    for d in (1, 3, 2):
        sx, sy = near(d)
        slab_copy(sx, sy, x, y, 1).wait_recv()
        for t in FAR4:
            slab_copy(sx, sy, *far(t), 2).start()
        swap(sx, sy, k).start()
    halo.wait_recv()

    @pl.when(s == 0)
    def _():
        ext[L : L + HALO, :] = jnp.zeros((HALO, ext.shape[1]), BF16)

    ext_t[:, L : L + HALO] = ext[L:, :].T
    for e in (0, 1, 3, 2):
        for d in (1, 3, 2):
            fx, fy = far(d)
            sx = lax.rem(fx + e * k, NX)
            sy = lax.rem(fy + e * (1 - k), NY)
            slab_copy(sx, sy, x, y, 2).wait_recv()
            swap(sx, sy, k).start()
    depth = ext.shape[1] // NX
    total = jnp.zeros((L + HALO, WIDE), F32)
    for d in range(NX):
        sx = lax.rem(x + d, NX)
        for sy in range(NY):
            swap(sx, sy, 1 - k).wait_recv()
        at = pl.multiple_of(sx * depth, depth)
        weights = wbuf[sx].astype(F32).reshape(depth, WIDE).astype(BF16)
        total = total + dg(ext[0 : L + HALO, pl.ds(at, depth)], weights, 1, 0)
    proj[HALO:, :] = total[0:L]
    proj[0:HALO, :] = total[L:]

    def drain():
        sent(wbuf.at[0, 0, pl.ds(0, NZ - 1), 0], s_send.at[0], mate)
        sent(wbuf.at[0, pl.ds(0, NY - 1), :, 0], s_send.at[1], mate)
        sent(wbuf.at[pl.ds(0, NX - 1), :, :, 0], s_send.at[2], mate)
        sent(wbuf.at[:, :, :, 0], s_send.at[3], mate)
        halo.wait_send()

    return drain


class Half:
    def __init__(self, loc, part, snd, rcv, tot, tots, snd2, rcv2, other, st, decays, s_send, s_mate, s_one, s_row, s_two):
        self.loc, self.part, self.snd, self.rcv, self.tot, self.tots = loc, part, snd, rcv, tot, tots
        self.snd2, self.rcv2, self.other, self.st = snd2, rcv2, other, st
        self.reverse = decays is not None
        self.decays = decays if self.reverse else self
        self.rows = pl.ds(0, 16 if self.reverse else 18)
        self.s_send, self.s_mate, self.s_one, self.s_row, self.s_two = s_send, s_mate, s_one, s_row, s_two
        self.x, self.y, self.z, self.k, self.chip = place()
        self.mate = device(self.x, self.y, self.z, 1 - self.k)
        self.first = self.k == 0

    def to_mate(self):
        return remote(self.loc.at[1 - self.k], self.part, self.s_send.at[0], self.s_mate.at[0], self.mate)

    def back(self):
        return remote(self.other, self.st.at[self.k], self.s_send.at[4], self.s_mate.at[1], self.mate)

    def back_in(self):
        return remote(self.other, self.st.at[1 - self.k], self.s_send.at[4], self.s_mate.at[1], self.mate)

    def cores(self):
        own, other = self.loc[self.k], self.part[...]
        return jnp.where(self.first, own, other), jnp.where(self.first, other, own)

    def start_one(self, s, t, a, ad):
        for h in range(2):
            for j in range(NZ):
                rows = slice(8 * j, 8 * j + 8)
                for i in range(LANES):
                    at = 128 * (LANES * h + i)
                    lanes = slice(at, at + 128)
                    self.snd[h, j, i, 0:8] = s[rows, lanes]
                    self.snd[h, j, i, 8:16] = t[rows, lanes]
                    if not self.reverse:
                        self.snd[h, j, i, 16:17] = a[:, lanes]
                        self.snd[h, j, i, 17:18] = ad[:, lanes]
            for d in FAR8:
                c = lax.rem(self.z + d, NZ)
                dev = device(self.x, self.y, c, self.k)
                remote(
                    self.snd.at[h, c, :, self.rows], self.rcv.at[h, self.z, :, self.rows],
                    self.s_send.at[1], self.s_one.at[h], dev,
                ).start()
            self.rcv[h, self.z] = self.snd[h, self.z]

    @staticmethod
    def step(carry, ref, decays, c):
        s, t = carry
        a, ad = decays[*c, :, 16:17, :], decays[*c, :, 17:18, :]
        return a * s + ref[*c, :, 0:8, :], a * t + (ad * s + ref[*c, :, 8:16, :])

    def order(self, count):
        return range(count - 1, -1, -1) if self.reverse else range(count)

    def row_total(self, h):
        arrived(self.rcv.at[h, pl.ds(0, NZ - 1), :, self.rows], self.s_one.at[h], self.mate)
        carry = (jnp.zeros((LANES, 8, 128), F32),) * 2
        for c in self.order(NZ):
            carry = self.step(carry, self.rcv, self.decays.rcv, (h, c))
        self.tot[h, :, 0:8, :], self.tot[h, :, 8:16, :] = carry
        if not self.reverse:
            a, ad = self.rcv[h, 0, :, 16:17, :], self.rcv[h, 0, :, 17:18, :]
            for c in range(1, NZ):
                b, bd = self.rcv[h, c, :, 16:17, :], self.rcv[h, c, :, 17:18, :]
                a, ad = a * b, ad * b + a * bd
            self.tot[h, :, 16:17, :], self.tot[h, :, 17:18, :] = a, ad
        for d in FAR4:
            dev = device(self.x, lax.rem(self.y + d, NY), self.z, self.k)
            remote(
                self.tot.at[h, :, self.rows], self.tots.at[h, self.y, :, self.rows],
                self.s_send.at[2], self.s_row.at[h], dev,
            ).start()
        self.tots[h, self.y] = self.tot[h]

    def start_two(self, h):
        arrived(self.tots.at[h, pl.ds(0, NY - 1), :, self.rows], self.s_row.at[h], self.mate)
        carry = (jnp.zeros((LANES, 8, 128), F32),) * 2
        for row in self.order(NY):
            after = self.step(carry, self.tots, self.decays.tots, (h, row))
            ahead = (row > self.y) if self.reverse else (row < self.y)
            carry = tuple(jnp.where(ahead, new, old) for new, old in zip(after, carry))
        for c in self.order(NZ):
            self.snd2[h, c, :, 0:8, :], self.snd2[h, c, :, 8:16, :] = carry
            carry = self.step(carry, self.rcv, self.decays.rcv, (h, c))
        for d in FAR8:
            c = lax.rem(self.z + d, NZ)
            dev = device(self.x, self.y, c, self.k)
            remote(self.snd2.at[h, c], self.rcv2.at[h, self.z], self.s_send.at[3], self.s_two.at[h], dev).start()
        self.rcv2[h, self.z] = self.snd2[h, self.z]

    def wait_two(self, h):
        arrived(self.rcv2.at[h, pl.ds(0, NZ - 1)], self.s_two.at[h], self.mate)

    def assemble(self, a, ad, base, base_first):
        s, t = (
            jnp.concatenate(
                [jnp.concatenate([self.rcv2[i // LANES, j, i % LANES, rows] for j in range(NZ)], 0) for i in range(2 * LANES)], 1
            )
            for rows in (slice(0, 8), slice(8, 16))
        )
        next_s = a * s + base[0:64]
        next_t = a * t + ad * s + base[64:128]
        mine_is_base = self.first if base_first else jnp.logical_not(self.first)
        self.other[0:64, :] = jnp.where(mine_is_base, next_s, s)
        self.other[64:128, :] = jnp.where(mine_is_base, next_t, t)
        self.back().start()
        self.st[self.k, 0:64, :] = jnp.where(mine_is_base, s, next_s)
        self.st[self.k, 64:128, :] = jnp.where(mine_is_base, t, next_t)

    def drain(self):
        self.to_mate().wait_send()
        sent(self.snd.at[:, pl.ds(0, NZ - 1), :, self.rows], self.s_send.at[1], self.mate)
        sent(self.tots.at[:, pl.ds(0, NY - 1), :, self.rows], self.s_send.at[2], self.mate)
        sent(self.snd2.at[:, pl.ds(0, NZ - 1)], self.s_send.at[3], self.mate)
        self.back().wait_send()


def reduce(dp, ext_t, full, g2, m01, m2, a0, a1, a2, r0, r1, r2, b0, b1, b2, q0, q1, q2, c0, c1, c2, p0, p1, p2,
           e2, s_send, s_mate, s_a, s_b, s_c, s_e, out_ref):
    x, y, z, k, chip = place()
    mate = device(x, y, z, 1 - k)
    holder = lax.rem(z, 2) == k

    def x_to(d):
        return device(lax.rem(x + d, NX), y, z, k)

    def y_to(d):
        return device(x, lax.rem(y + d, NY), z, k)

    def z_to(d):
        return device(x, y, lax.rem(z + d, NZ), k)

    both = jnp.concatenate(split(dp), 1)
    low_half = iota((8, 128), 1) < 64
    block_rows = NY * NZ * 16

    order = FAR4 + (0,)

    def settle(i):
        xb = lax.rem(x + order[i], NX)
        arrived(m01.at[:, xb], s_mate.at[i], mate)
        a0[xb] = full[0, xb, :, :, k] + m01[0, xb]
        if i < NX - 1:
            remote(a0.at[xb], r0.at[i], s_send.at[2], s_a.at[0], x_to(order[i])).start()
        a1[xb] = full[1, xb, :, :, k] + m01[1, xb]
        for d in FAR4:
            remote(a1.at[xb, lax.rem(y + d, NY)], r1.at[d - 1, xb], s_send.at[3], s_a.at[1], y_to(d)).start()
        arrived(m2.at[xb], s_mate.at[NX + i], mate)
        a2[xb] = g2[k, xb] + m2[xb]

    for i in range(NX):
        xb = lax.rem(x + order[i], NX)
        rows = ext_t[pl.ds(pl.multiple_of(xb * block_rows, block_rows), block_rows), :]
        part = dg(rows, both, 1, 0)
        part = part[:, :WIDE] + part[:, WIDE:]
        full[0, xb] = part[:, 0:128].reshape(NY, NZ, 2, 8, 128)
        full[1, xb] = part[:, 128:256].reshape(NY, NZ, 2, 8, 128)
        steps = part[:, 256:384].reshape(NY, NZ // 2, 2, 2, 8, 128)
        for zp in range(2):
            g2[zp, xb] = jnp.where(low_half, steps[:, :, zp, 0], steps[:, :, zp, 1])
        for tile in range(2):
            remote(full.at[tile, xb, :, :, 1 - k], m01.at[tile, xb], s_send.at[0], s_mate.at[i], mate).start()
        remote(g2.at[1 - k, xb], m2.at[xb], s_send.at[1], s_mate.at[NX + i], mate).start()
    for i in range(NX):
        settle(i)

    zsend = []
    for i in range(NZ // 2):
        target = 2 * i + k
        gap = lax.rem(z - target + NZ, NZ)
        zsend.append((target != z, remote(a2.at[:, :, i], r2.at[gap], s_send.at[4 + i], s_a.at[2], device(x, y, target, k))))
        pl.when(zsend[-1][0])(zsend[-1][1].start)

    arrived(r0, s_a.at[0], mate)
    b0[...] = (a0[x] + r0[0]) + (r0[1] + r0[2])
    for d in FAR4:
        remote(b0.at[lax.rem(y + d, NY)], q0.at[d - 1], s_send.at[8], s_b.at[0], y_to(d)).start()
    arrived(r1, s_a.at[1], mate)
    b1[...] = (a1[:, y] + r1[0]) + (r1[1] + r1[2])
    for d in FAR4:
        remote(b1.at[lax.rem(x + d, NX)], q1.at[d - 1], s_send.at[9], s_b.at[1], x_to(d)).start()

    @pl.when(holder)
    def _():
        arrived(r2.at[pl.ds(1, NZ - 1)], s_a.at[2], mate)
        total = a2[:, :, z // 2] + ((r2[1] + r2[2]) + (r2[3] + r2[4]))
        b2[...] = total + ((r2[5] + r2[6]) + r2[7])
        for d in FAR4:
            remote(b2.at[lax.rem(x + d, NX)], q2.at[d - 1], s_send.at[10], s_b.at[2], x_to(d)).start()

    arrived(q0, s_b.at[0], mate)
    c0[...] = (b0[y] + q0[0]) + (q0[1] + q0[2])
    for d in FAR8:
        remote(c0.at[lax.rem(z + d, NZ)], p0.at[d - 1], s_send.at[11], s_c.at[0], z_to(d)).start()

    arrived(q1, s_b.at[1], mate)
    c1[...] = (b1[x] + q1[0]) + (q1[1] + q1[2])
    for d in FAR8:
        remote(c1.at[lax.rem(z + d, NZ)], p1.at[d - 1], s_send.at[13], s_c.at[1], z_to(d)).start()
    last = remote(c2.at[y], e2, s_send.at[14], s_e, mate)

    @pl.when(holder)
    def _():
        arrived(q2, s_b.at[2], mate)
        c2[...] = (b2[x] + q2[0]) + (q2[1] + q2[2])
        for d in FAR4:
            for core in range(2):
                row = lax.rem(y + d, NY)
                remote(c2.at[row], p2.at[d - 1], s_send.at[12], s_c.at[2], device(x, row, z, core)).start()
        last.start()
        e2[...] = c2[y]

    sent(m01, s_send.at[0], mate)
    sent(m2, s_send.at[1], mate)
    sent(r0, s_send.at[2], mate)
    sent(r1, s_send.at[3], mate)
    for used, copy in zsend:
        pl.when(used)(copy.wait_send)
    sent(q0, s_send.at[8], mate)
    sent(q1, s_send.at[9], mate)
    arrived(p0, s_c.at[0], mate)
    out_ref[:, 0:128] = c0[z] + ((p0[0] + p0[1]) + (p0[2] + p0[3])) + ((p0[4] + p0[5]) + p0[6])
    arrived(p1, s_c.at[1], mate)
    out_ref[:, 128:256] = c1[z] + ((p1[0] + p1[1]) + (p1[2] + p1[3])) + ((p1[4] + p1[5]) + p1[6])
    arrived(p2, s_c.at[2], mate)

    @pl.when(jnp.logical_not(holder))
    def _():
        remote(c2.at[y], e2, s_send.at[14], s_e, mate).wait_recv()

    steps = (e2[...] + p2[0]) + (p2[1] + p2[2])
    out_ref[:, 256:384] = jnp.where(k == 0, steps, roll64(steps))
    sent(p0, s_send.at[11], mate)
    sent(p1, s_send.at[13], mate)

    @pl.when(holder)
    def _():
        sent(q2, s_send.at[10], mate)
        sent(p1.at[pl.ds(0, 6)], s_send.at[12], mate)
        last.wait_send()


def everything(scale, sw_hbm, sd_hbm, tw_hbm, td_hbm, tok_ref, v_hbm, u_hbm, conv_hbm, bias_hbm, rate_hbm,
               out_ref, v_ref, u_ref, sw_ref, sd_ref, tw_ref, td_ref, conv_ref, bias_ref, rate_ref, wbuf, ext, ext_t, proj,
               forward_scratch, backward_scratch, rows_ref, row1_ref, row2_ref, colq_ref, colqd_ref, zp_ref, reduce_scratch,
               s_in, gather_sems, forward_sems, backward_sems, reduce_sems):
    entered = enter()
    pairs = [
        (sw_hbm, sw_ref), (sd_hbm, sd_ref), (tw_hbm, tw_ref), (td_hbm, td_ref), (tok_ref, ext.at[pl.ds(0, L)]),
        (v_hbm, v_ref), (u_hbm, u_ref), (conv_hbm, conv_ref), (bias_hbm, bias_ref), (rate_hbm, rate_ref),
    ]
    local = [pltpu.make_async_copy(src, dst, s_in.at[i]) for i, (src, dst) in enumerate(pairs)]
    for c in local:
        c.start()
    x, y, z, k, _ = place()
    ext_t[:, L + HALO :] = jnp.zeros((ext_t.shape[0], L - HALO), BF16)
    for c in local[0:4]:
        c.wait()
    wbuf[x, y, z, k, :, 0:128] = sw_ref[...]
    wbuf[x, y, z, k, :, 128:256] = sd_ref[...]
    rows = sw_ref.shape[0]
    wbuf[x, y, z, k, :, 256:384] = jnp.concatenate(
        [tw_ref[...].astype(F32), td_ref[...].astype(F32), jnp.zeros((rows, 128 - 2 * H), F32)], 1
    ).astype(BF16)
    local[4].wait()
    ext_t[:, 0:L] = ext[0:L, :].T
    for c in local[5:]:
        c.wait()
    entered()
    drain_gather = gather(wbuf, ext, ext_t, proj, tok_ref, *gather_sems)

    rate = rate_ref[...]
    ft = features(lambda row, lane, lanes: proj[row : row + L, lane : lane + lanes], conv_ref[...], bias_ref[...], rate)
    wts = weights_of(ft)
    pp = pair_parts(ft)
    we, wde, decay, decayd = forward_streams(wts, v_ref[...])
    fw = Half(*forward_scratch, None, *forward_sems)
    bw = Half(*backward_scratch, fw, *backward_sems)
    row = iota((8, HP), 0)
    dec = jnp.where(row == 0, decay, jnp.where(row == 1, decayd, 0.0))
    states = forward_states(pp, we, wde)
    for half in range(2):
        lanes = slice(HALF * half, HALF * half + HALF)
        fw.loc[half, 0:128, :] = states[:, lanes]
        fw.loc[half, 128:136, :] = dec[:, lanes]
    fw.to_mate().start()
    eu, edu = backward_streams(wts, u_ref[...])
    states = backward_states(pp, eu, edu)
    for half in range(2):
        bw.loc[half] = states[:, HALF * half : HALF * half + HALF]
    bw.to_mate().start()

    fw.to_mate().wait_recv()
    one0, one1 = fw.cores()
    a0, ad0 = one0[128:129], one0[129:130]
    a1, ad1 = one1[128:129], one1[129:130]
    a, ad = a0 * a1, ad0 * a1 + a0 * ad1
    fw.start_one(
        a1 * one0[0:64] + one1[0:64], a1 * one0[64:128] + ad1 * one0[0:64] + one1[64:128], a, ad
    )
    bw.to_mate().wait_recv()
    one0, one1 = bw.cores()
    bw.start_one(
        a0 * one1[0:64] + one0[0:64], a0 * one1[64:128] + ad0 * one1[0:64] + one0[64:128], a, ad
    )

    def tile(ref):
        return lambda i: ref[:, pl.ds(pl.multiple_of(i * 128, 128), 128)]

    g, gd = intra_setup(ft, pp, rows_ref, row1_ref, row2_ref)
    zero = jnp.zeros((L, L), F32)

    def block_terms(first, last, carry):
        return intra(
            ft, g, gd, tile(v_ref), tile(u_ref), rows_ref, row1_ref, row2_ref, colq_ref, colqd_ref, first, last, carry
        )

    carry = block_terms(0, 4, (zero, zero))
    fw.row_total(0)
    carry = block_terms(4, 6, carry)
    fw.row_total(1)
    carry = block_terms(6, 7, carry)
    fw.start_two(0)
    bw.row_total(0)
    fw.start_two(1)
    carry = block_terms(7, 8, carry)
    bw.row_total(1)
    bw.start_two(0)
    pairs = intra_pairs(pp, *carry)
    bw.start_two(1)
    e_split = split(jnp.concatenate([eu, edu], 0))
    w_split = split(jnp.concatenate([we, wde], 0))
    fw.wait_two(0)
    fw.wait_two(1)
    fw.assemble(a0, ad0, fw.cores()[0], True)
    fw.back_in().wait_recv()
    xf = jnp.concatenate([fw.st[0], fw.st[1]], 1)
    from_forward = finish_forward(pp, e_split, u_ref[...], xf)
    colq, colqd = colq_ref[...].T, colqd_ref[...].T
    bw.wait_two(0)
    bw.wait_two(1)
    bw.assemble(a1, ad1, bw.cores()[1], False)
    bw.back_in().wait_recv()
    xb = jnp.concatenate([bw.st[0], bw.st[1]], 1)
    from_backward = finish_backward(pp, w_split, v_ref[...], xb)
    dz, dzd, dq, dqd = finish(
        ft, wts, pairs, row1_ref[...], row2_ref[...], colq, colqd,
        from_forward, from_backward, xf, xb, rate, scale,
    )
    zp_ref[...] = jnp.zeros(zp_ref.shape, F32)
    zp_ref[HALO : HALO + L, 0:128] = dz
    zp_ref[HALO : HALO + L, 128:256] = dzd
    conv = conv_ref[...]

    def spread(first_row, count, lanes):
        total = conv[0:1, :] * zp_ref[first_row + 3 : first_row + 3 + count, lanes]
        for tap in range(1, KCONV):
            total = total + conv[tap : tap + 1, :] * zp_ref[first_row + 3 - tap : first_row + 3 - tap + count, lanes]
        return total

    pad = jnp.zeros((128 - HALO, 128), F32)
    columns = []
    for half in range(2):
        lanes = slice(128 * half, 128 * half + 128)
        columns.append(jnp.concatenate([spread(HALO, L, lanes), spread(0, HALO, lanes), pad], 0))
    both = jnp.concatenate([dq, dqd, dq, dqd], 1)
    columns.append(jnp.concatenate([both, jnp.zeros((128, 128), F32)], 0))
    dp = jnp.concatenate(columns, 1)
    drain_gather()
    fw.drain()
    bw.drain()
    reduce(dp, ext_t, *reduce_scratch, *reduce_sems, out_ref)


def split_outputs(sums_ref, o_sel, o_step, o_selh, o_steph):
    o_sel[...] = sums_ref[:, 0:128]
    o_selh[...] = sums_ref[:, 128:256]
    o_step[...] = sums_ref[:, 256 : 256 + H]
    o_steph[...] = sums_ref[:, 256 + H : 256 + 2 * H]


def vmem(shape, dtype=F32):
    return pltpu.VMEM(shape, dtype)


def dma(*shape):
    return pltpu.SemaphoreType.DMA(shape)


def body(tokens, values, cotangent, sel_weight, step_weight, sel_dir, step_dir, conv_weight, step_bias, decay_rate):
    own_tokens, v, u = tokens[0], values[0], cotangent[0]
    depth = own_tokens.shape[1]
    rows = sel_weight.shape[0]
    scale = 1.0 / math.sqrt(NX * CHIPS * 2 * L)
    spec = pl.BlockSpec(memory_space=pltpu.VMEM)
    hbm = pl.BlockSpec(memory_space=pl.ANY)
    tiles = NX * NY * NZ
    reduce_scratch = (
        [vmem((2, NX, NY, NZ, 2, 8, 128)), vmem((2, NX, NY, NZ // 2, 8, 128)),
         vmem((2, NX, NY, NZ, 8, 128)), vmem((NX, NY, NZ // 2, 8, 128))]
        + [vmem((NX, NY, NZ, 8, 128))] * 2 + [vmem((NX, NY, NZ // 2, 8, 128))]
        + [vmem((3, NY, NZ, 8, 128)), vmem((3, NX, NZ, 8, 128)), vmem((NZ, NX, NY, 8, 128))]
        + [vmem((NY, NZ, 8, 128)), vmem((NX, NZ, 8, 128)), vmem((NX, NY, 8, 128))]
        + [vmem((3, NZ, 8, 128)), vmem((3, NZ, 8, 128)), vmem((3, NY, 8, 128))]
        + [vmem((NZ, 8, 128)), vmem((NZ, 8, 128)), vmem((NY, 8, 128))]
        + [vmem((7, 8, 128)), vmem((7, 8, 128)), vmem((3, 8, 128))]
        + [vmem((8, 128))]
    )

    def scan_scratch():
        return (
            [vmem((2, NZ, LANES, 24, 128))] * 2 + [vmem((2, LANES, 24, 128)), vmem((2, NY, LANES, 24, 128))]
            + [vmem((2, NZ, LANES, 16, 128))] * 2 + [vmem((128, HALF)), vmem((2, 128, HALF))]
        )

    scratch = [
        vmem((L, HP), BF16), vmem((L, HP), BF16),
        vmem((rows, 128), BF16), vmem((rows, 128), BF16), vmem((rows, H), BF16), vmem((rows, H), BF16),
        vmem((KCONV, 128)), vmem((1, H)), vmem((1, H)),
        vmem((NX, NY, NZ, 2, rows, WIDE), BF16),
        vmem((L + HALO, depth), BF16), vmem((depth, 2 * L), BF16), vmem((HALO + L, WIDE)),
        [vmem((2, 136, HALF)), vmem((136, HALF))] + scan_scratch(),
        [vmem((2, 128, HALF)), vmem((128, HALF))] + scan_scratch(),
        vmem((3 * H, L)), vmem((L, L)), vmem((L, L)), vmem((H, L)), vmem((H, L)), vmem((HALO + L + 8, 256)),
        reduce_scratch,
        dma(10),
        [dma(5), dma(), dma(), dma(NX * NY), dma(NX * NY)],
        [dma(5), dma(2), dma(2), dma(2), dma(2)],
        [dma(5), dma(2), dma(2), dma(2), dma(2)],
        [dma(15), dma(2 * NX), dma(3), dma(3), dma(3), dma()],
    ]
    sums = pl.pallas_call(
        functools.partial(everything, scale),
        out_shape=jax.ShapeDtypeStruct((rows, WIDE), F32),
        in_specs=[hbm] * 10,
        out_specs=spec,
        scratch_shapes=scratch,
        compiler_params=pltpu.CompilerParams(
            vmem_limit_bytes=VMEM_LIMIT, collective_id=0, has_side_effects=True
        ),
    )(sel_weight, sel_dir, step_weight, step_dir, own_tokens, v, u, conv_weight, step_bias[None, :], decay_rate[None, :])
    return pl.pallas_call(
        split_outputs,
        out_shape=[
            jax.ShapeDtypeStruct((rows, 128), F32), jax.ShapeDtypeStruct((rows, H), F32),
            jax.ShapeDtypeStruct((rows, 128), F32), jax.ShapeDtypeStruct((rows, H), F32),
        ],
        in_specs=[spec],
        out_specs=[spec] * 4,
    )(sums)


def solution(mesh):
    shards = P(("dp", "seq"), None)
    stream = P("dp", "seq", None)
    return jax.shard_map(
        body,
        mesh=mesh,
        in_specs=(stream, stream, stream, shards, shards, shards, shards, P(), P(), P()),
        out_specs=(shards, shards, shards, shards),
        check_vma=False,
    )
```

```python
import functools
import math

import jax
import jax.numpy as jnp
from jax import lax
from jax.experimental import pallas as pl
from jax.experimental.pallas import tpu as pltpu
from jax.sharding import PartitionSpec as P

N = 64
P_SIZE = 32
H = 32
KCONV = 4
L = 128
HALO = 16
HP = H * P_SIZE
HALF = HP // 2
WIDE = 384
NX, NY, NZ = 4, 4, 8
CHIPS = NY * NZ
MESH = pl.DeviceIdType.MESH
F32 = jnp.float32
BF16 = jnp.bfloat16
VMEM_LIMIT = 56 * 1024 * 1024


def roll64(x):
    return pltpu.roll(x, 64, 1)


def split(x):
    high = x.astype(BF16)
    low = (x - high.astype(F32)).astype(BF16)
    return high, low


def split3(x):
    high = x.astype(BF16)
    rest = x - high.astype(F32)
    mid = rest.astype(BF16)
    low = (rest - mid.astype(F32)).astype(BF16)
    return high, mid, low


def dg(a, b, ca, cb):
    return lax.dot_general(a, b, (((ca,), (cb,)), ((), ())), preferred_element_type=F32)


def dot_split(a, b, ca, cb):
    return dot_parts(split(a), split(b), ca, cb)


def dot_parts(a, b, ca, cb):
    (ah, al), (bh, bl) = a, b
    return dg(ah, bh, ca, cb) + (dg(ah, bl, ca, cb) + dg(al, bh, ca, cb))


def dot_left(a, b, ca, cb):
    ah, al = split(a)
    return dg(ah, b, ca, cb) + dg(al, b, ca, cb)


def iota(shape, dim):
    return lax.broadcasted_iota(jnp.int32, shape, dim)


def low_lanes():
    return iota((L, 128), 1) < 64


def head_spread():
    return (iota((H, HP), 0) == iota((H, HP), 1) // P_SIZE).astype(F32).astype(BF16)


def triangle(reverse):
    row, column = iota((L, L), 0), iota((L, L), 1)
    keep = (column >= row) if reverse else (row >= column)
    return keep.astype(F32).astype(BF16)


def cumulate(x, reverse):
    tri = triangle(reverse)
    a, b, c = split3(x)
    return dg(tri, a, 1, 0) + (dg(tri, b, 1, 0) + dg(tri, c, 1, 0))


def features(proj, conv2, bias, rate):
    z = jnp.zeros((L, 128), F32)
    zd = jnp.zeros((L, 128), F32)
    for k in range(KCONV):
        rows = HALO - (KCONV - 1) + k
        z = z + conv2[k : k + 1, :128] * proj(rows, 0, 128)
        zd = zd + conv2[k : k + 1, :128] * proj(rows, 128, 128)
    sg = jax.nn.sigmoid(z)
    act = z * sg
    first = sg * (1.0 + z * (1.0 - sg))
    second = sg * (1.0 - sg) * (2.0 + z * (1.0 - 2.0 * sg))
    actd = first * zd
    steps = proj(HALO, 256, 128)
    q = steps[:, :H] + bias
    qd = steps[:, H : 2 * H]
    delta = jnp.maximum(q, 0.0) + jnp.log1p(jnp.exp(-jnp.abs(q)))
    sq = jax.nn.sigmoid(q)
    deltad = sq * qd
    cum = cumulate(-(delta * rate), False)
    cumd = cumulate(-(deltad * rate), False)
    return dict(
        zd=zd, act=act, actd=actd, first=first, second=second,
        qd=qd, sq=sq, delta=delta, deltad=deltad, cum=cum, cumd=cumd,
    )


def weights_of(ft):
    cum, cumd = ft["cum"], ft["cumd"]
    last, lastd = cum[L - 1 :, :], cumd[L - 1 :, :]
    e = jnp.exp(cum)
    ed = e * cumd
    f = jnp.exp(last - cum)
    fd = f * (lastd - cumd)
    w = f * ft["delta"]
    wd = fd * ft["delta"] + f * ft["deltad"]
    return e, ed, f, fd, w, wd


def pair_parts(ft):
    act, actd = ft["act"], ft["actd"]
    actr, actdr = roll64(act), roll64(actd)
    m = low_lanes()
    return dict(
        b_bd=jnp.where(m, act, actdr),
        o_b=jnp.where(m, 0.0, actr),
        c_cd=jnp.where(m, actr, actd),
        o_c=jnp.where(m, 0.0, act),
        b_o=jnp.where(m, act, 0.0),
        bd_b=jnp.where(m, actd, actr),
        c_o=jnp.where(m, actr, 0.0),
        cd_c=jnp.where(m, actdr, act),
        b_c=act,
        c_b=actr,
    )


def spread_rows(rows):
    return dot_left(rows, head_spread(), 1, 0)


def forward_streams(wts, values):
    e, ed, _, _, w, wd = wts
    v = values.astype(F32)
    last = jnp.concatenate([jnp.broadcast_to(row[L - 1 :, :], (8, H)) for row in (e, ed)], 0)
    last = spread_rows(last)
    return spread_rows(w) * v, spread_rows(wd) * v, last[0:8], last[8:16]


def backward_streams(wts, cotangent):
    u = cotangent.astype(F32)
    return spread_rows(wts[0]) * u, spread_rows(wts[1]) * u


def forward_states(pp, we, wde):
    left = jnp.concatenate([pp["b_bd"], pp["o_b"]], 0)
    return dot_split(left, jnp.concatenate([we, wde], 0), 0, 0)


def backward_states(pp, eu, edu):
    left = jnp.concatenate([pp["c_cd"], pp["o_c"]], 0)
    return dot_split(left, jnp.concatenate([eu, edu], 0), 0, 0)


def intra_setup(ft, pp, rows_ref, row1_ref, row2_ref):
    g = dot_split(pp["c_o"], pp["b_c"], 1, 1)
    gd = dot_split(pp["cd_c"], pp["b_bd"], 1, 1)
    eta = ft["deltad"] - ft["delta"] * ft["cumd"]
    rows_ref[0:H, :] = ft["cum"].T
    rows_ref[H : 2 * H, :] = ft["delta"].T
    rows_ref[2 * H : 3 * H, :] = eta.T
    row1_ref[...] = jnp.zeros((L, L), F32)
    row2_ref[...] = jnp.zeros((L, L), F32)
    return g, gd


def intra(ft, g, gd, v_of, u_of, rows_ref, row1_ref, row2_ref, colq_ref, colqd_ref, first, last, carry):
    parts = split3(ft["cum"])
    partsd = split(ft["cumd"])
    row, lane = iota((L, L), 0), iota((L, L), 1)
    causal = row >= lane

    def one(i, carry):
        dgm, dgd = carry
        pick = (iota((H, 512), 0) == (4 * i + iota((H, 512), 1) // 128)).astype(F32).astype(BF16)
        ct4 = dg(parts[0], pick, 1, 0) + (dg(parts[1], pick, 1, 0) + dg(parts[2], pick, 1, 0))
        cd4 = dg(partsd[0], pick, 1, 0) + dg(partsd[1], pick, 1, 0)
        v_tile, u_tile = v_of(i), u_of(i)
        row1, row2 = row1_ref[...], row2_ref[...]
        for j in range(4):
            h = 4 * i + j
            mask = (iota((L, 128), 1) // P_SIZE == j).astype(F32)
            w = dg((u_tile.astype(F32) * mask).astype(BF16), v_tile, 1, 1)
            ct = ct4[:, 128 * j : 128 * j + 128]
            cd = cd4[:, 128 * j : 128 * j + 128]
            cs = rows_ref[pl.ds(h, 1), :]
            ds = rows_ref[pl.ds(H + h, 1), :]
            et = rows_ref[pl.ds(2 * H + h, 1), :]
            x = jnp.exp(jnp.where(causal, ct - cs, -1e30)) * w
            xd = x * ds
            dgm = dgm + xd
            dgd = dgd + (x * et + cd * xd)
            q = x * g
            xgd = x * gd
            colq_ref[pl.ds(h, 1), :] = jnp.sum(q, axis=0, keepdims=True)
            colqd_ref[pl.ds(h, 1), :] = jnp.sum(xgd + q * cd, axis=0, keepdims=True)
            r1 = jnp.sum(q * ds, axis=1, keepdims=True)
            r2 = jnp.sum(xgd * ds + q * et, axis=1, keepdims=True)
            here = lane == h
            row1 = jnp.where(here, r1, row1)
            row2 = jnp.where(here, r2, row2)
        row1_ref[...] = row1
        row2_ref[...] = row2
        return dgm, dgd

    return lax.fori_loop(first, last, one, carry)


def intra_pairs(pp, dgm, dgd):
    return (
        dot_split(dgm, pp["b_bd"], 1, 0),
        dot_split(dgd, pp["b_c"], 1, 0),
        dot_split(dgm, pp["c_cd"], 0, 0),
        dot_split(dgd, pp["c_b"], 0, 0),
    )


def head_sums(x):
    return dot_left(x, head_spread(), 1, 1)


def finish_forward(pp, e_split, cotangent, xf):
    u = cotangent.astype(F32)
    x_split = split(xf)
    zz = dot_parts(split(jnp.concatenate([pp["c_o"], pp["cd_c"]], 0)), x_split, 1, 0)
    return head_sums(zz[:L] * u), head_sums(zz[L:] * u), dot_parts(e_split, x_split, 1, 1)


def finish_backward(pp, w_split, values, xb):
    v = values.astype(F32)
    x_split = split(xb)
    yy = dot_parts(split(jnp.concatenate([pp["b_o"], pp["bd_b"]], 0)), x_split, 1, 0)
    return head_sums(yy[:L] * v), head_sums(yy[L:] * v), dot_parts(w_split, x_split, 1, 1)


def finish(ft, wts, pairs, row1, row2, colq, colqd, from_forward, from_backward, xf, xb, rate, scale):
    e, ed, f, fd, w, wd = wts
    g, gdot, pc = from_forward
    kk, kdot, pb = from_backward
    kap = jnp.sum(xb[:64] * xf[:64], axis=0, keepdims=True)
    kapd = jnp.sum(xb[64:] * xf[:64] + xb[:64] * xf[64:], axis=0, keepdims=True)
    both = head_sums(jnp.concatenate([jnp.broadcast_to(kap, (8, HP)), jnp.broadcast_to(kapd, (8, HP))], 0))
    kap, kapd = both[0:1], both[8:9]

    m = low_lanes()
    t1, t2, t3, t4 = pairs
    pair_c = t1 + pc[:L] + jnp.where(m, 0.0, roll64(t2 + pc[L:]))
    pair_b = t3 + pb[:L] + jnp.where(m, 0.0, roll64(t4 + pb[L:]))
    dact = jnp.where(m, pair_b, roll64(pair_c))
    dactd = jnp.where(m, roll64(pair_b), pair_c)
    dz = scale * (ft["first"] * dact)
    dzd = scale * (ft["second"] * ft["zd"] * dact + ft["first"] * dactd)

    delta, deltad, cum, cumd = ft["delta"], ft["deltad"], ft["cum"], ft["cumd"]
    colqd = colqd - cumd * colq
    row1, row2 = row1[:, :H], row2[:, :H]
    row2 = row2 + cumd * row1
    wk = w * kk
    wkd = wd * kk + w * kdot
    dc = row1 - delta * colq + e * g - wk
    dcd = row2 - (deltad * colq + delta * colqd) + ed * g + e * gdot - wkd
    el, edl = e[L - 1 :, :], ed[L - 1 :, :]
    extra = el * kap + jnp.sum(wk, axis=0, keepdims=True)
    extrad = edl * kap + el * kapd + jnp.sum(wkd, axis=0, keepdims=True)
    ddelta = colq + f * kk - rate * (cumulate(dc, True) + extra)
    ddeltad = colqd + fd * kk + f * kdot - rate * (cumulate(dcd, True) + extrad)
    sq = ft["sq"]
    dq = scale * (sq * ddelta)
    dqd = scale * (sq * (1.0 - sq) * ft["qd"] * ddelta + sq * ddeltad)
    return dz, dzd, dq, dqd


def place():
    x = lax.axis_index("dp")
    s = lax.axis_index("seq")
    chip = s // 2
    return x, chip // NZ, lax.rem(chip, NZ), lax.rem(s, 2), chip


def device(x, y, z, k):
    return (x, (y * NZ + z) * 2 + k)


def remote(src, dst, send_sem, recv_sem, dev):
    return pltpu.make_async_remote_copy(
        src_ref=src, dst_ref=dst, send_sem=send_sem, recv_sem=recv_sem,
        device_id=dev, device_id_type=MESH,
    )


def arrived(dst, sem, dev):
    remote(dst, dst, sem, sem, dev).wait_recv()


def sent(src, sem, dev):
    remote(src, src, sem, sem, dev).wait_send()


FAR4 = (2, 1, 3)
LANES = HALF // 256
FAR8 = (4, 3, 5, 2, 6, 1, 7)


def enter():
    x, y, z, k, chip = place()
    s = 2 * chip + k
    seq = CHIPS * 2
    partners = [device(x, y, lax.rem(z + d, NZ), k) for d in FAR8]
    partners += [device(lax.rem(x + d, NX), y, z, k) for d in FAR4]
    partners += [device(x, lax.rem(y + d, NY), z, k) for d in FAR4]
    partners += [(x, lax.rem(s + 1, seq)), (x, lax.rem(s + seq - 1, seq)), device(x, y, z, 1 - k)]
    barrier = pltpu.get_barrier_semaphore()
    for dev in partners:
        pl.semaphore_signal(barrier, inc=1, device_id=dev, device_id_type=MESH)
    return lambda: pl.semaphore_wait(barrier, len(partners))


def gather(wbuf, ext, ext_t, proj, tok_ref, s_send, s_halo, s_z, s_slab, s_swap):
    x, y, z, k, chip = place()
    s = 2 * chip + k
    mate = device(x, y, z, 1 - k)
    own = wbuf.at[x, y, z, k]
    for d in FAR8:
        remote(own, own, s_send.at[0], s_z, device(x, y, lax.rem(z + d, NZ), k)).start()
    halo = remote(
        tok_ref.at[pl.ds(L - HALO, HALO)], ext.at[pl.ds(L, HALO)], s_send.at[4], s_halo,
        (x, lax.rem(s + 1, 2 * CHIPS)),
    )
    halo.start()
    arrived(wbuf.at[x, y, pl.ds(0, NZ - 1), k], s_z, mate)

    def slab_copy(sx, sy, tx, ty, sem):
        ref = wbuf.at[sx, sy, :, k]
        return remote(ref, ref, s_send.at[sem], s_slab.at[sx * NY + sy], device(tx, ty, z, k))

    def swap(sx, sy, kk):
        ref = wbuf.at[sx, sy, :, kk]
        return remote(ref, ref, s_send.at[3], s_swap.at[sx * NY + sy], mate)

    def near(d):
        return lax.rem(x + d * k, NX), lax.rem(y + d * (1 - k), NY)

    def far(d):
        return lax.rem(x + d * (1 - k), NX), lax.rem(y + d * k, NY)

    for d in FAR4:
        slab_copy(x, y, *near(d), 1).start()
    for d in FAR4:
        slab_copy(x, y, *far(d), 2).start()
    swap(x, y, k).start()
    for d in (1, 3, 2):
        sx, sy = near(d)
        slab_copy(sx, sy, x, y, 1).wait_recv()
        for t in FAR4:
            slab_copy(sx, sy, *far(t), 2).start()
        swap(sx, sy, k).start()
    halo.wait_recv()

    @pl.when(s == 0)
    def _():
        ext[L : L + HALO, :] = jnp.zeros((HALO, ext.shape[1]), BF16)

    ext_t[:, L : L + HALO] = ext[L:, :].T
    for e in (0, 1, 3, 2):
        for d in (1, 3, 2):
            fx, fy = far(d)
            sx = lax.rem(fx + e * k, NX)
            sy = lax.rem(fy + e * (1 - k), NY)
            slab_copy(sx, sy, x, y, 2).wait_recv()
            swap(sx, sy, k).start()
    depth = ext.shape[1] // NX
    total = jnp.zeros((L + HALO, WIDE), F32)
    for d in range(NX):
        sx = lax.rem(x + d, NX)
        for sy in range(NY):
            swap(sx, sy, 1 - k).wait_recv()
        at = pl.multiple_of(sx * depth, depth)
        weights = wbuf[sx].astype(F32).reshape(depth, WIDE).astype(BF16)
        total = total + dg(ext[0 : L + HALO, pl.ds(at, depth)], weights, 1, 0)
    proj[HALO:, :] = total[0:L]
    proj[0:HALO, :] = total[L:]

    def drain():
        sent(wbuf.at[0, 0, pl.ds(0, NZ - 1), 0], s_send.at[0], mate)
        sent(wbuf.at[0, pl.ds(0, NY - 1), :, 0], s_send.at[1], mate)
        sent(wbuf.at[pl.ds(0, NX - 1), :, :, 0], s_send.at[2], mate)
        sent(wbuf.at[:, :, :, 0], s_send.at[3], mate)
        halo.wait_send()

    return drain


class Half:
    def __init__(self, loc, part, snd, rcv, tot, tots, snd2, rcv2, other, st, decays, s_send, s_mate, s_one, s_row, s_two):
        self.loc, self.part, self.snd, self.rcv, self.tot, self.tots = loc, part, snd, rcv, tot, tots
        self.snd2, self.rcv2, self.other, self.st = snd2, rcv2, other, st
        self.reverse = decays is not None
        self.decays = decays if self.reverse else self
        self.rows = pl.ds(0, 16 if self.reverse else 18)
        self.s_send, self.s_mate, self.s_one, self.s_row, self.s_two = s_send, s_mate, s_one, s_row, s_two
        self.x, self.y, self.z, self.k, self.chip = place()
        self.mate = device(self.x, self.y, self.z, 1 - self.k)
        self.first = self.k == 0

    def to_mate(self):
        return remote(self.loc.at[1 - self.k], self.part, self.s_send.at[0], self.s_mate.at[0], self.mate)

    def back(self):
        return remote(self.other, self.st.at[self.k], self.s_send.at[4], self.s_mate.at[1], self.mate)

    def back_in(self):
        return remote(self.other, self.st.at[1 - self.k], self.s_send.at[4], self.s_mate.at[1], self.mate)

    def cores(self):
        own, other = self.loc[self.k], self.part[...]
        return jnp.where(self.first, own, other), jnp.where(self.first, other, own)

    def start_one(self, s, t, a, ad):
        for h in range(2):
            for j in range(NZ):
                rows = slice(8 * j, 8 * j + 8)
                for i in range(LANES):
                    at = 128 * (LANES * h + i)
                    lanes = slice(at, at + 128)
                    self.snd[h, j, i, 0:8] = s[rows, lanes]
                    self.snd[h, j, i, 8:16] = t[rows, lanes]
                    if not self.reverse:
                        self.snd[h, j, i, 16:17] = a[:, lanes]
                        self.snd[h, j, i, 17:18] = ad[:, lanes]
            for d in FAR8:
                c = lax.rem(self.z + d, NZ)
                dev = device(self.x, self.y, c, self.k)
                remote(
                    self.snd.at[h, c, :, self.rows], self.rcv.at[h, self.z, :, self.rows],
                    self.s_send.at[1], self.s_one.at[h], dev,
                ).start()
            self.rcv[h, self.z] = self.snd[h, self.z]

    @staticmethod
    def step(carry, ref, decays, c):
        s, t = carry
        a, ad = decays[*c, :, 16:17, :], decays[*c, :, 17:18, :]
        return a * s + ref[*c, :, 0:8, :], a * t + (ad * s + ref[*c, :, 8:16, :])

    def order(self, count):
        return range(count - 1, -1, -1) if self.reverse else range(count)

    def row_total(self, h):
        arrived(self.rcv.at[h, pl.ds(0, NZ - 1), :, self.rows], self.s_one.at[h], self.mate)
        carry = (jnp.zeros((LANES, 8, 128), F32),) * 2
        for c in self.order(NZ):
            carry = self.step(carry, self.rcv, self.decays.rcv, (h, c))
        self.tot[h, :, 0:8, :], self.tot[h, :, 8:16, :] = carry
        if not self.reverse:
            a, ad = self.rcv[h, 0, :, 16:17, :], self.rcv[h, 0, :, 17:18, :]
            for c in range(1, NZ):
                b, bd = self.rcv[h, c, :, 16:17, :], self.rcv[h, c, :, 17:18, :]
                a, ad = a * b, ad * b + a * bd
            self.tot[h, :, 16:17, :], self.tot[h, :, 17:18, :] = a, ad
        for d in FAR4:
            dev = device(self.x, lax.rem(self.y + d, NY), self.z, self.k)
            remote(
                self.tot.at[h, :, self.rows], self.tots.at[h, self.y, :, self.rows],
                self.s_send.at[2], self.s_row.at[h], dev,
            ).start()
        self.tots[h, self.y] = self.tot[h]

    def start_two(self, h):
        arrived(self.tots.at[h, pl.ds(0, NY - 1), :, self.rows], self.s_row.at[h], self.mate)
        carry = (jnp.zeros((LANES, 8, 128), F32),) * 2
        for row in self.order(NY):
            after = self.step(carry, self.tots, self.decays.tots, (h, row))
            ahead = (row > self.y) if self.reverse else (row < self.y)
            carry = tuple(jnp.where(ahead, new, old) for new, old in zip(after, carry))
        for c in self.order(NZ):
            self.snd2[h, c, :, 0:8, :], self.snd2[h, c, :, 8:16, :] = carry
            carry = self.step(carry, self.rcv, self.decays.rcv, (h, c))
        for d in FAR8:
            c = lax.rem(self.z + d, NZ)
            dev = device(self.x, self.y, c, self.k)
            remote(self.snd2.at[h, c], self.rcv2.at[h, self.z], self.s_send.at[3], self.s_two.at[h], dev).start()
        self.rcv2[h, self.z] = self.snd2[h, self.z]

    def wait_two(self, h):
        arrived(self.rcv2.at[h, pl.ds(0, NZ - 1)], self.s_two.at[h], self.mate)

    def assemble(self, a, ad, base, base_first):
        s, t = (
            jnp.concatenate(
                [jnp.concatenate([self.rcv2[i // LANES, j, i % LANES, rows] for j in range(NZ)], 0) for i in range(2 * LANES)], 1
            )
            for rows in (slice(0, 8), slice(8, 16))
        )
        next_s = a * s + base[0:64]
        next_t = a * t + ad * s + base[64:128]
        mine_is_base = self.first if base_first else jnp.logical_not(self.first)
        self.other[0:64, :] = jnp.where(mine_is_base, next_s, s)
        self.other[64:128, :] = jnp.where(mine_is_base, next_t, t)
        self.back().start()
        self.st[self.k, 0:64, :] = jnp.where(mine_is_base, s, next_s)
        self.st[self.k, 64:128, :] = jnp.where(mine_is_base, t, next_t)

    def drain(self):
        self.to_mate().wait_send()
        sent(self.snd.at[:, pl.ds(0, NZ - 1), :, self.rows], self.s_send.at[1], self.mate)
        sent(self.tots.at[:, pl.ds(0, NY - 1), :, self.rows], self.s_send.at[2], self.mate)
        sent(self.snd2.at[:, pl.ds(0, NZ - 1)], self.s_send.at[3], self.mate)
        self.back().wait_send()


def reduce(dp, ext_t, full, g2, m01, m2, a0, a1, a2, r0, r1, r2, b0, b1, b2, q0, q1, q2, c0, c1, c2, p0, p1, p2,
           e2, s_send, s_mate, s_a, s_b, s_c, s_e, out_ref, drains):
    x, y, z, k, chip = place()
    mate = device(x, y, z, 1 - k)
    holder = lax.rem(z, 2) == k

    def x_to(d):
        return device(lax.rem(x + d, NX), y, z, k)

    def y_to(d):
        return device(x, lax.rem(y + d, NY), z, k)

    def z_to(d):
        return device(x, y, lax.rem(z + d, NZ), k)

    both = jnp.concatenate(split(dp), 1)
    low_half = iota((8, 128), 1) < 64
    block_rows = NY * NZ * 16

    order = FAR4 + (0,)

    def settle(i):
        xb = lax.rem(x + order[i], NX)
        arrived(m01.at[:, xb], s_mate.at[i], mate)
        a0[xb] = full[0, xb, :, :, k] + m01[0, xb]
        if i < NX - 1:
            remote(a0.at[xb], r0.at[i], s_send.at[2], s_a.at[0], x_to(order[i])).start()
        a1[xb] = full[1, xb, :, :, k] + m01[1, xb]
        for d in FAR4:
            remote(a1.at[xb, lax.rem(y + d, NY)], r1.at[d - 1, xb], s_send.at[3], s_a.at[1], y_to(d)).start()
        arrived(m2.at[xb], s_mate.at[NX + i], mate)
        a2[xb] = g2[k, xb] + m2[xb]

    for i in range(NX):
        xb = lax.rem(x + order[i], NX)
        rows = ext_t[pl.ds(pl.multiple_of(xb * block_rows, block_rows), block_rows), :]
        part = dg(rows, both, 1, 0)
        part = part[:, :WIDE] + part[:, WIDE:]
        full[0, xb] = part[:, 0:128].reshape(NY, NZ, 2, 8, 128)
        full[1, xb] = part[:, 128:256].reshape(NY, NZ, 2, 8, 128)
        steps = part[:, 256:384].reshape(NY, NZ // 2, 2, 2, 8, 128)
        for zp in range(2):
            g2[zp, xb] = jnp.where(low_half, steps[:, :, zp, 0], steps[:, :, zp, 1])
        for tile in range(2):
            remote(full.at[tile, xb, :, :, 1 - k], m01.at[tile, xb], s_send.at[0], s_mate.at[i], mate).start()
        remote(g2.at[1 - k, xb], m2.at[xb], s_send.at[1], s_mate.at[NX + i], mate).start()
        if i > 1:
            settle(i - 2)
    settle(NX - 2)
    settle(NX - 1)

    zsend = []
    for i in range(NZ // 2):
        target = 2 * i + k
        gap = lax.rem(z - target + NZ, NZ)
        zsend.append((target != z, remote(a2.at[:, :, i], r2.at[gap], s_send.at[4 + i], s_a.at[2], device(x, y, target, k))))
        pl.when(zsend[-1][0])(zsend[-1][1].start)

    arrived(r0, s_a.at[0], mate)
    b0[...] = (a0[x] + r0[0]) + (r0[1] + r0[2])
    for d in FAR4:
        remote(b0.at[lax.rem(y + d, NY)], q0.at[d - 1], s_send.at[8], s_b.at[0], y_to(d)).start()
    arrived(r1, s_a.at[1], mate)
    b1[...] = (a1[:, y] + r1[0]) + (r1[1] + r1[2])
    for d in FAR4:
        remote(b1.at[lax.rem(x + d, NX)], q1.at[d - 1], s_send.at[9], s_b.at[1], x_to(d)).start()

    @pl.when(holder)
    def _():
        arrived(r2.at[pl.ds(1, NZ - 1)], s_a.at[2], mate)
        total = a2[:, :, z // 2] + ((r2[1] + r2[2]) + (r2[3] + r2[4]))
        b2[...] = total + ((r2[5] + r2[6]) + r2[7])
        for d in FAR4:
            remote(b2.at[lax.rem(x + d, NX)], q2.at[d - 1], s_send.at[10], s_b.at[2], x_to(d)).start()

    arrived(q0, s_b.at[0], mate)
    c0[...] = (b0[y] + q0[0]) + (q0[1] + q0[2])
    for d in FAR8:
        remote(c0.at[lax.rem(z + d, NZ)], p0.at[d - 1], s_send.at[11], s_c.at[0], z_to(d)).start()

    arrived(q1, s_b.at[1], mate)
    c1[...] = (b1[x] + q1[0]) + (q1[1] + q1[2])
    for d in FAR8:
        remote(c1.at[lax.rem(z + d, NZ)], p1.at[d - 1], s_send.at[13], s_c.at[1], z_to(d)).start()
    last = remote(c2.at[y], e2, s_send.at[14], s_e, mate)

    @pl.when(holder)
    def _():
        arrived(q2, s_b.at[2], mate)
        c2[...] = (b2[x] + q2[0]) + (q2[1] + q2[2])
        for d in FAR4:
            for core in range(2):
                row = lax.rem(y + d, NY)
                remote(c2.at[row], p2.at[d - 1], s_send.at[12], s_c.at[2], device(x, row, z, core)).start()
        last.start()
        e2[...] = c2[y]

    for drain in drains:
        drain()
    sent(m01, s_send.at[0], mate)
    sent(m2, s_send.at[1], mate)
    sent(r0, s_send.at[2], mate)
    sent(r1, s_send.at[3], mate)
    for used, copy in zsend:
        pl.when(used)(copy.wait_send)
    sent(q0, s_send.at[8], mate)
    sent(q1, s_send.at[9], mate)
    arrived(p0, s_c.at[0], mate)
    out_ref[:, 0:128] = c0[z] + ((p0[0] + p0[1]) + (p0[2] + p0[3])) + ((p0[4] + p0[5]) + p0[6])
    arrived(p1, s_c.at[1], mate)
    out_ref[:, 128:256] = c1[z] + ((p1[0] + p1[1]) + (p1[2] + p1[3])) + ((p1[4] + p1[5]) + p1[6])
    arrived(p2, s_c.at[2], mate)

    @pl.when(jnp.logical_not(holder))
    def _():
        remote(c2.at[y], e2, s_send.at[14], s_e, mate).wait_recv()

    steps = (e2[...] + p2[0]) + (p2[1] + p2[2])
    out_ref[:, 256:384] = jnp.where(k == 0, steps, roll64(steps))
    sent(p0, s_send.at[11], mate)
    sent(p1, s_send.at[13], mate)

    @pl.when(holder)
    def _():
        sent(q2, s_send.at[10], mate)
        sent(p1.at[pl.ds(0, 6)], s_send.at[12], mate)
        last.wait_send()


def everything(scale, sw_hbm, sd_hbm, tw_hbm, td_hbm, tok_ref, v_hbm, u_hbm, conv_hbm, bias_hbm, rate_hbm,
               out_ref, v_ref, u_ref, sw_ref, sd_ref, tw_ref, td_ref, conv_ref, bias_ref, rate_ref, wbuf, ext, ext_t, proj,
               forward_scratch, backward_scratch, rows_ref, row1_ref, row2_ref, colq_ref, colqd_ref, zp_ref, reduce_scratch,
               s_in, gather_sems, forward_sems, backward_sems, reduce_sems):
    entered = enter()
    pairs = [
        (sw_hbm, sw_ref), (sd_hbm, sd_ref), (tw_hbm, tw_ref), (td_hbm, td_ref), (tok_ref, ext.at[pl.ds(0, L)]),
        (v_hbm, v_ref), (u_hbm, u_ref), (conv_hbm, conv_ref), (bias_hbm, bias_ref), (rate_hbm, rate_ref),
    ]
    local = [pltpu.make_async_copy(src, dst, s_in.at[i]) for i, (src, dst) in enumerate(pairs)]
    for c in local:
        c.start()
    x, y, z, k, _ = place()
    ext_t[:, L + HALO :] = jnp.zeros((ext_t.shape[0], L - HALO), BF16)
    for c in local[0:4]:
        c.wait()
    wbuf[x, y, z, k, :, 0:128] = sw_ref[...]
    wbuf[x, y, z, k, :, 128:256] = sd_ref[...]
    rows = sw_ref.shape[0]
    wbuf[x, y, z, k, :, 256:384] = jnp.concatenate(
        [tw_ref[...].astype(F32), td_ref[...].astype(F32), jnp.zeros((rows, 128 - 2 * H), F32)], 1
    ).astype(BF16)
    local[4].wait()
    ext_t[:, 0:L] = ext[0:L, :].T
    for c in local[5:]:
        c.wait()
    entered()
    drain_gather = gather(wbuf, ext, ext_t, proj, tok_ref, *gather_sems)

    rate = rate_ref[...]
    ft = features(lambda row, lane, lanes: proj[row : row + L, lane : lane + lanes], conv_ref[...], bias_ref[...], rate)
    wts = weights_of(ft)
    pp = pair_parts(ft)
    we, wde, decay, decayd = forward_streams(wts, v_ref[...])
    fw = Half(*forward_scratch, None, *forward_sems)
    bw = Half(*backward_scratch, fw, *backward_sems)
    row = iota((8, HP), 0)
    dec = jnp.where(row == 0, decay, jnp.where(row == 1, decayd, 0.0))
    states = forward_states(pp, we, wde)
    for half in range(2):
        lanes = slice(HALF * half, HALF * half + HALF)
        fw.loc[half, 0:128, :] = states[:, lanes]
        fw.loc[half, 128:136, :] = dec[:, lanes]
    fw.to_mate().start()
    eu, edu = backward_streams(wts, u_ref[...])
    states = backward_states(pp, eu, edu)
    for half in range(2):
        bw.loc[half] = states[:, HALF * half : HALF * half + HALF]
    bw.to_mate().start()

    fw.to_mate().wait_recv()
    one0, one1 = fw.cores()
    a0, ad0 = one0[128:129], one0[129:130]
    a1, ad1 = one1[128:129], one1[129:130]
    a, ad = a0 * a1, ad0 * a1 + a0 * ad1
    fw.start_one(
        a1 * one0[0:64] + one1[0:64], a1 * one0[64:128] + ad1 * one0[0:64] + one1[64:128], a, ad
    )
    bw.to_mate().wait_recv()
    one0, one1 = bw.cores()
    bw.start_one(
        a0 * one1[0:64] + one0[0:64], a0 * one1[64:128] + ad0 * one1[0:64] + one0[64:128], a, ad
    )

    def tile(ref):
        return lambda i: ref[:, pl.ds(pl.multiple_of(i * 128, 128), 128)]

    g, gd = intra_setup(ft, pp, rows_ref, row1_ref, row2_ref)
    zero = jnp.zeros((L, L), F32)

    def block_terms(first, last, carry):
        return intra(
            ft, g, gd, tile(v_ref), tile(u_ref), rows_ref, row1_ref, row2_ref, colq_ref, colqd_ref, first, last, carry
        )

    carry = block_terms(0, 4, (zero, zero))
    fw.row_total(0)
    carry = block_terms(4, 6, carry)
    fw.row_total(1)
    carry = block_terms(6, 7, carry)
    fw.start_two(0)
    bw.row_total(0)
    fw.start_two(1)
    carry = block_terms(7, 8, carry)
    bw.row_total(1)
    bw.start_two(0)
    pairs = intra_pairs(pp, *carry)
    bw.start_two(1)
    e_split = split(jnp.concatenate([eu, edu], 0))
    w_split = split(jnp.concatenate([we, wde], 0))
    fw.wait_two(0)
    fw.wait_two(1)
    fw.assemble(a0, ad0, fw.cores()[0], True)
    fw.back_in().wait_recv()
    xf = jnp.concatenate([fw.st[0], fw.st[1]], 1)
    from_forward = finish_forward(pp, e_split, u_ref[...], xf)
    colq, colqd = colq_ref[...].T, colqd_ref[...].T
    bw.wait_two(0)
    bw.wait_two(1)
    bw.assemble(a1, ad1, bw.cores()[1], False)
    bw.back_in().wait_recv()
    xb = jnp.concatenate([bw.st[0], bw.st[1]], 1)
    from_backward = finish_backward(pp, w_split, v_ref[...], xb)
    dz, dzd, dq, dqd = finish(
        ft, wts, pairs, row1_ref[...], row2_ref[...], colq, colqd,
        from_forward, from_backward, xf, xb, rate, scale,
    )
    zp_ref[...] = jnp.zeros(zp_ref.shape, F32)
    zp_ref[HALO : HALO + L, 0:128] = dz
    zp_ref[HALO : HALO + L, 128:256] = dzd
    conv = conv_ref[...]

    def spread(first_row, count, lanes):
        total = conv[0:1, :] * zp_ref[first_row + 3 : first_row + 3 + count, lanes]
        for tap in range(1, KCONV):
            total = total + conv[tap : tap + 1, :] * zp_ref[first_row + 3 - tap : first_row + 3 - tap + count, lanes]
        return total

    pad = jnp.zeros((128 - HALO, 128), F32)
    columns = []
    for half in range(2):
        lanes = slice(128 * half, 128 * half + 128)
        columns.append(jnp.concatenate([spread(HALO, L, lanes), spread(0, HALO, lanes), pad], 0))
    both = jnp.concatenate([dq, dqd, dq, dqd], 1)
    columns.append(jnp.concatenate([both, jnp.zeros((128, 128), F32)], 0))
    dp = jnp.concatenate(columns, 1)
    reduce(dp, ext_t, *reduce_scratch, *reduce_sems, out_ref, (drain_gather, fw.drain, bw.drain))


def split_outputs(sums_ref, o_sel, o_step, o_selh, o_steph):
    o_sel[...] = sums_ref[:, 0:128]
    o_selh[...] = sums_ref[:, 128:256]
    o_step[...] = sums_ref[:, 256 : 256 + H]
    o_steph[...] = sums_ref[:, 256 + H : 256 + 2 * H]


def vmem(shape, dtype=F32):
    return pltpu.VMEM(shape, dtype)


def dma(*shape):
    return pltpu.SemaphoreType.DMA(shape)


def body(tokens, values, cotangent, sel_weight, step_weight, sel_dir, step_dir, conv_weight, step_bias, decay_rate):
    own_tokens, v, u = tokens[0], values[0], cotangent[0]
    depth = own_tokens.shape[1]
    rows = sel_weight.shape[0]
    scale = 1.0 / math.sqrt(NX * CHIPS * 2 * L)
    spec = pl.BlockSpec(memory_space=pltpu.VMEM)
    hbm = pl.BlockSpec(memory_space=pl.ANY)
    tiles = NX * NY * NZ
    reduce_scratch = (
        [vmem((2, NX, NY, NZ, 2, 8, 128)), vmem((2, NX, NY, NZ // 2, 8, 128)),
         vmem((2, NX, NY, NZ, 8, 128)), vmem((NX, NY, NZ // 2, 8, 128))]
        + [vmem((NX, NY, NZ, 8, 128))] * 2 + [vmem((NX, NY, NZ // 2, 8, 128))]
        + [vmem((3, NY, NZ, 8, 128)), vmem((3, NX, NZ, 8, 128)), vmem((NZ, NX, NY, 8, 128))]
        + [vmem((NY, NZ, 8, 128)), vmem((NX, NZ, 8, 128)), vmem((NX, NY, 8, 128))]
        + [vmem((3, NZ, 8, 128)), vmem((3, NZ, 8, 128)), vmem((3, NY, 8, 128))]
        + [vmem((NZ, 8, 128)), vmem((NZ, 8, 128)), vmem((NY, 8, 128))]
        + [vmem((7, 8, 128)), vmem((7, 8, 128)), vmem((3, 8, 128))]
        + [vmem((8, 128))]
    )

    def scan_scratch():
        return (
            [vmem((2, NZ, LANES, 24, 128))] * 2 + [vmem((2, LANES, 24, 128)), vmem((2, NY, LANES, 24, 128))]
            + [vmem((2, NZ, LANES, 16, 128))] * 2 + [vmem((128, HALF)), vmem((2, 128, HALF))]
        )

    scratch = [
        vmem((L, HP), BF16), vmem((L, HP), BF16),
        vmem((rows, 128), BF16), vmem((rows, 128), BF16), vmem((rows, H), BF16), vmem((rows, H), BF16),
        vmem((KCONV, 128)), vmem((1, H)), vmem((1, H)),
        vmem((NX, NY, NZ, 2, rows, WIDE), BF16),
        vmem((L + HALO, depth), BF16), vmem((depth, 2 * L), BF16), vmem((HALO + L, WIDE)),
        [vmem((2, 136, HALF)), vmem((136, HALF))] + scan_scratch(),
        [vmem((2, 128, HALF)), vmem((128, HALF))] + scan_scratch(),
        vmem((3 * H, L)), vmem((L, L)), vmem((L, L)), vmem((H, L)), vmem((H, L)), vmem((HALO + L + 8, 256)),
        reduce_scratch,
        dma(10),
        [dma(5), dma(), dma(), dma(NX * NY), dma(NX * NY)],
        [dma(5), dma(2), dma(2), dma(2), dma(2)],
        [dma(5), dma(2), dma(2), dma(2), dma(2)],
        [dma(15), dma(2 * NX), dma(3), dma(3), dma(3), dma()],
    ]
    sums = pl.pallas_call(
        functools.partial(everything, scale),
        out_shape=jax.ShapeDtypeStruct((rows, WIDE), F32),
        in_specs=[hbm] * 10,
        out_specs=spec,
        scratch_shapes=scratch,
        compiler_params=pltpu.CompilerParams(
            vmem_limit_bytes=VMEM_LIMIT, collective_id=0, has_side_effects=True
        ),
    )(sel_weight, sel_dir, step_weight, step_dir, own_tokens, v, u, conv_weight, step_bias[None, :], decay_rate[None, :])
    return pl.pallas_call(
        split_outputs,
        out_shape=[
            jax.ShapeDtypeStruct((rows, 128), F32), jax.ShapeDtypeStruct((rows, H), F32),
            jax.ShapeDtypeStruct((rows, 128), F32), jax.ShapeDtypeStruct((rows, H), F32),
        ],
        in_specs=[spec],
        out_specs=[spec] * 4,
    )(sums)


def solution(mesh):
    shards = P(("dp", "seq"), None)
    stream = P("dp", "seq", None)
    return jax.shard_map(
        body,
        mesh=mesh,
        in_specs=(stream, stream, stream, shards, shards, shards, shards, P(), P(), P()),
        out_specs=(shards, shards, shards, shards),
        check_vma=False,
    )
```
